32 devices in a mesh: dp: 8 (over z, x), fsdp: 4 (over y, core).
Axes of the slice: x: 2, y: 2, z: 4, core: 2. Of those that a mesh axis runs over, the one named last changes fastest.
Arguments:
- layer_input: bfloat16 [2, 32, 709, 768], P(None, ('dp', 'fsdp')), may hold values from -6 to 6
- text_lengths: int32 [2, 32], P(None, ('dp', 'fsdp')), may hold values from 40 to 512, as said below
- pos_buckets: int32 [2, 32, 709, 709], P(None, ('dp', 'fsdp')), may hold values from 0 to 31
- box_buckets: int32 [2, 32, 2, 709, 709], P(None, ('dp', 'fsdp')), may hold values from 0 to 63
- w_qkv: bfloat16 [768, 2304], P(('dp', 'fsdp')), may hold values from -0.21875 to 0.21875
- w_out: bfloat16 [768, 768], P(('dp', 'fsdp')), may hold values from -1.75 to 1.75
- w_up: bfloat16 [768, 3072], P(('dp', 'fsdp')), may hold values from -0.21875 to 0.21875
- w_down: bfloat16 [3072, 768], P(('dp', 'fsdp')), may hold values from -0.109375 to 0.109375
- norm_gains: bfloat16 [2, 768], P(None, ('dp', 'fsdp')), may hold values from 0.5 to 1.5
- norm_shifts: bfloat16 [2, 768], P(None, ('dp', 'fsdp')), may hold values from -1.75 to 1.75
- proj_biases: bfloat16 [4, 768], P(None, ('dp', 'fsdp')), may hold values from -1.75 to 1.75
- up_bias: bfloat16 [3072], P(('dp', 'fsdp')), may hold values from -1.75 to 1.75
- rel_tables: bfloat16 [160, 12], P('fsdp'), may hold values from -32 to 32
- cotangent: bfloat16 [2, 32, 709, 768], P(None, ('dp', 'fsdp')), may hold values from -6 to 6
Outputs:
- layer_output: bfloat16 [2, 32, 709, 768], P(None, ('dp', 'fsdp'))
- input_grad: float32 [2, 32, 709, 768], P(None, ('dp', 'fsdp'))
- grad_w_qkv: float32 [768, 2304], P(('dp', 'fsdp'))
- grad_w_out: float32 [768, 768], P(('dp', 'fsdp'))
- grad_w_up: float32 [768, 3072], P(('dp', 'fsdp'))
- grad_w_down: float32 [3072, 768], P(('dp', 'fsdp'))
- grad_gains: float32 [2, 768], P(None, ('dp', 'fsdp'))
- grad_shifts: float32 [2, 768], P(None, ('dp', 'fsdp'))
- grad_biases: float32 [4, 768], P(None, ('dp', 'fsdp'))
- grad_up_bias: float32 [3072], P(('dp', 'fsdp'))
- grad_tables: float32 [160, 12], P('fsdp')
The draws below stay inside these ranges and needn't reach their ends.
Inputs may be any that keep to these rules, and one draw needn't show every extreme that they name: `text_lengths`: text slots at and past a document's length are padding keys; the image slots are always real.
All inputs are finite; a program needn't handle non-finite values.
Results may differ from the reference program's by a relative error of at most 0.013.
Values may be sent and summed in bfloat16 or wider, within the bound.
A program may use at most 384 MiB of HBM per device.

```python
import jax
import jax.numpy as jnp
from jax import lax

D = 768
HEADS = 12
HEAD_DIM = 64
FF = 3072
POS_BINS = 32
BOX_BINS = 64
TEXT_SLOTS = 512
MICRO = 2
SEQ = 709
DOCS = 32


def draw_text_lengths(key, part):
    low_end = max(1, TEXT_SLOTS * 5 // 64)
    first_key, pick_key = jax.random.split(key)
    lengths = jax.random.randint(first_key, (MICRO, DOCS), low_end, TEXT_SLOTS + 1)
    chosen = jax.random.randint(pick_key, (), 0, DOCS)
    return lengths.at[0, chosen].set(TEXT_SLOTS).astype(jnp.int32)


def with_ends(values, stream_key, low, largest):
    place = [jax.random.randint(jax.random.fold_in(stream_key, axis), (), 0, length) for axis, length in enumerate(values.shape)]
    longest = values.shape.index(max(values.shape))
    next_to = place[:longest] + [(place[longest] + 1) % values.shape[longest]] + place[longest + 1:]
    return values.at[tuple(place)].set(low).at[tuple(next_to)].set(largest)


def shard_levels(key, shape, shards, least, high):
    gain, own = 1.0, jax.random.fold_in(key, 6)
    for position, blocks in shards:
        draws = jnp.exp(jax.random.uniform(jax.random.fold_in(own, position), (blocks,), jnp.float32, least / len(shards), high / len(shards)))
        gain = gain * jnp.repeat(draws, shape[position] // blocks).reshape([-1 if axis == position else 1 for axis in range(len(shape))])
    return gain


def centred(stream_key, shape, width, bound, cuts=(), kind=jnp.bfloat16):
    values = width * jax.random.normal(stream_key, shape, jnp.float32)
    if cuts:
        values = values * shard_levels(stream_key, shape, cuts, -0.22, 0.18)
    return jnp.clip(values, -bound, bound).astype(kind)


def setup_inputs(seed: int = 0) -> dict:
    seeds = jax.random.split(jax.random.key(seed), 15)
    return {
        "layer_input": centred(seeds[0], (MICRO, DOCS, SEQ, D), 1.0, 6.0, ((1, 32),)),
        "text_lengths": draw_text_lengths(jax.random.fold_in(seeds[14], 71), 0),
        "pos_buckets": with_ends(jax.random.randint(seeds[2], (MICRO, DOCS, SEQ, SEQ), 0, POS_BINS), jax.random.fold_in(seeds[2], 1), 0, POS_BINS - 1).astype(jnp.int32),
        "box_buckets": with_ends(jax.random.randint(seeds[3], (MICRO, DOCS, 2, SEQ, SEQ), 0, BOX_BINS), jax.random.fold_in(seeds[3], 1), 0, BOX_BINS - 1).astype(jnp.int32),
        "w_qkv": centred(seeds[4], (D, 3 * D), D ** -0.5, 0.21875, ((0, 32),)),
        "w_out": centred(seeds[5], (D, D), (D // 64) ** -0.5, 1.75, ((0, 32),)),
        "w_up": centred(seeds[6], (D, FF), D ** -0.5, 0.21875, ((0, 32),)),
        "w_down": centred(seeds[7], (FF, D), FF ** -0.5, 0.109375, ((0, 32),)),
        "norm_gains": jnp.clip(1.0 + 0.1 * jax.random.normal(seeds[8], (2, D), jnp.float32), 0.5, 1.5).astype(jnp.bfloat16),
        "norm_shifts": centred(seeds[9], (2, D), 0.3, 1.75, ((1, 32),)),
        "proj_biases": centred(seeds[10], (4, D), 0.3, 1.75, ((1, 32),)),
        "up_bias": centred(seeds[11], (FF,), 0.3, 1.75, ((0, 32),)),
        "rel_tables": centred(seeds[12], (POS_BINS + 2 * BOX_BINS, HEADS), 6.0, 32.0, ((0, 4),)),
        "cotangent": centred(seeds[13], (MICRO, DOCS, SEQ, D), 1.0, 6.0, ((1, 32),)),
    }


HIGH = lax.Precision.HIGHEST
NEG_FILL = -1000000000.0
NORM_EPS = 1e-05

@jax.custom_vjp
def low(v):
    return lax.optimization_barrier(v.astype(jnp.bfloat16)).astype(jnp.float32)

@jax.custom_vjp
def low_back(v):
    return v

def low_keep(v):
    return (low(v), None)

def low_pass(kept, grad):
    return (grad,)

def back_keep(v):
    return (v, None)

def back_low(kept, grad):
    return (low(grad),)
low.defvjp(low_keep, low_pass)
low_back.defvjp(back_keep, back_low)

def matmul_hi(left, right):
    return jnp.dot(left, right, precision=HIGH)

def normalize(rows_in, gain_row, shift_row):
    centre = rows_in - lax.optimization_barrier(jnp.mean(rows_in, axis=-1, keepdims=True))
    inv_std = lax.rsqrt(lax.optimization_barrier(jnp.mean(centre * centre, axis=-1, keepdims=True)) + NORM_EPS)
    return centre * inv_std * gain_row + shift_row

def layer_doc(params, tables, doc_rows, length, pos_idx, box_idx):
    w_qkv, w_out, w_up, w_down, norm_gains, norm_shifts, proj_biases, up_bias = params
    heads = D // HEAD_DIM
    projected = matmul_hi(doc_rows, w_qkv)
    queries = low_back(low(projected[:, :D] + proj_biases[0]))
    key_rows = low_back(low(projected[:, D:2 * D]))
    values = low_back(low(projected[:, 2 * D:] + proj_biases[1]))
    query_heads = queries.reshape(SEQ, heads, HEAD_DIM)
    key_heads = key_rows.reshape(SEQ, heads, HEAD_DIM)
    value_heads = values.reshape(SEQ, heads, HEAD_DIM)
    raw_scores = low_back(jnp.einsum('ihd,jhd->hij', query_heads, key_heads, precision=HIGH))
    table_t = tables.T
    bias_terms = table_t[:, pos_idx] + table_t[:, POS_BINS + box_idx[0]] + table_t[:, POS_BINS + BOX_BINS + box_idx[1]]
    scores = (raw_scores + bias_terms) * 0.125
    slots = jnp.arange(SEQ, dtype=jnp.int32)
    key_valid = (slots >= TEXT_SLOTS) | (slots < length)
    scores = jnp.where(key_valid[None, None, :], scores, NEG_FILL)
    top_score = lax.optimization_barrier(jnp.max(scores, axis=-1, keepdims=True))
    log_total = top_score + jnp.log(lax.optimization_barrier(jnp.sum(jnp.exp(scores - top_score), axis=-1, keepdims=True)))
    attn_probs = low(jnp.exp(scores - log_total))
    attended = jnp.einsum('hij,jhd->ihd', attn_probs, value_heads, precision=HIGH).reshape(SEQ, D)
    attended = low_back(low(attended))
    branch = low_back(matmul_hi(attended, w_out) + proj_biases[2])
    hidden = normalize(doc_rows + branch, norm_gains[0], norm_shifts[0])
    upper = low_back(matmul_hi(low(hidden), w_up) + up_bias)
    active = low(jax.nn.gelu(upper, approximate=False))
    ffn_out = low_back(matmul_hi(active, w_down) + proj_biases[3])
    return normalize(hidden + ffn_out, norm_gains[1], norm_shifts[1])

def reference(layer_input, text_lengths, pos_buckets, box_buckets, w_qkv, w_out, w_up, w_down, norm_gains, norm_shifts, proj_biases, up_bias, rel_tables, cotangent):
    params = (w_qkv.astype(jnp.float32), w_out.astype(jnp.float32), w_up.astype(jnp.float32), w_down.astype(jnp.float32), norm_gains.astype(jnp.float32), norm_shifts.astype(jnp.float32), proj_biases.astype(jnp.float32), up_bias.astype(jnp.float32))
    tables = rel_tables.astype(jnp.float32)
    doc_total = MICRO * DOCS
    input_rows = layer_input.astype(jnp.float32).reshape(doc_total, SEQ, D)
    lengths = text_lengths.reshape(doc_total)
    pos_all = pos_buckets.reshape(doc_total, SEQ, SEQ)
    box_all = box_buckets.reshape(doc_total, 2, SEQ, SEQ)
    one_doc = jax.checkpoint(layer_doc)

    def forward(params_in, tables_in, rows_in):

        def per_doc(doc_item):
            return one_doc(params_in, tables_in, doc_item[0], doc_item[1], doc_item[2], doc_item[3])
        return lax.map(per_doc, (rows_in, lengths, pos_all, box_all))
    result, pullback = jax.vjp(forward, params, tables, input_rows)
    grad_params, grad_tables, grad_rows = pullback(cotangent.astype(jnp.float32).reshape(doc_total, SEQ, D))
    return (result.astype(jnp.bfloat16).reshape(MICRO, DOCS, SEQ, D), grad_rows.reshape(MICRO, DOCS, SEQ, D), grad_params[0], grad_params[1], grad_params[2], grad_params[3], grad_params[4], grad_params[5], grad_params[6], grad_params[7], grad_tables)
```

```python
from functools import partial

import jax
import jax.numpy as jnp
from jax import lax
from jax.experimental import pallas as pl
from jax.experimental.pallas import tpu as pltpu
from jax.sharding import PartitionSpec as P

HEAD_DIM = 64
POS_BINS = 32
BOX_BINS = 64
TEXT_SLOTS = 512
NEG_FILL = -1000000000.0
NORM_EPS = 1e-05
BLOCK = 256
DENSE_BLOCK = 384
LANES = 128
HALF = 32
SCALE = 0.125
F32 = jnp.float32
BF16 = jnp.bfloat16
VMEM_LIMIT = 58 << 20


def dot(left, right):
    return jnp.dot(left, right, preferred_element_type=F32)


def dot_nt(left, right):
    return lax.dot_general(left, right, (((1,), (1,)), ((), ())), preferred_element_type=F32)


def params(count):
    return pltpu.CompilerParams(
        dimension_semantics=("arbitrary",) * count, vmem_limit_bytes=VMEM_LIMIT
    )


def resident(shape):
    zeros = (0,) * len(shape)
    return pl.BlockSpec(shape, lambda *_: zeros, pipeline_mode=pl.Buffered(1))


def live_rows(values, rows, first):
    row = first + lax.broadcasted_iota(jnp.int32, (values.shape[0], 1), 0)
    return jnp.where(row < rows, values, jnp.zeros_like(values))


def bias_kernel(rows, len_ref, tab_ref, pos_ref, box_ref, out_ref):
    heads, chunks = out_ref.shape[1], out_ref.shape[3] // LANES
    block = pl.program_id(1)
    length = len_ref[pl.program_id(0)]
    steps = jnp.minimum(BLOCK, (rows + 7) // 8 * 8 - block * BLOCK) // 8

    def fill(step, carry):
        at = pl.ds(pl.multiple_of(step * 8, 8), 8)
        for chunk in range(chunks):
            cols = slice(chunk * LANES, (chunk + 1) * LANES)
            picks = (
                box_ref[0, 0, 0, at, cols] & (BOX_BINS - 1),
                (box_ref[0, 0, 1, at, cols] & (BOX_BINS - 1)) | BOX_BINS,
                pos_ref[0, 0, at, cols] & (POS_BINS - 1),
            )
            slot = chunk * LANES + lax.broadcasted_iota(jnp.int32, (8, LANES), 1)
            valid = ((slot >= TEXT_SLOTS) & (slot < rows)) | (slot < length)
            totals = [None] * heads
            for which, pick in enumerate(picks):
                for head in range(heads):
                    line = head + (heads if which == 2 else 0)
                    entries = jnp.broadcast_to(tab_ref[line : line + 1, :], (8, LANES))
                    term = jnp.take_along_axis(entries, pick, axis=1)
                    totals[head] = term if which == 0 else totals[head] + term
            for head in range(heads):
                out_ref[0, head, at, cols] = jnp.where(valid, totals[head], NEG_FILL)
        return carry

    def blank(step, carry):
        at = pl.ds(pl.multiple_of(step * 8, 8), 8)
        for head in range(heads):
            out_ref[0, head, at, :] = jnp.zeros((8, chunks * LANES), F32)
        return carry

    lax.fori_loop(0, steps, fill, 0)
    lax.fori_loop(steps, BLOCK // 8, blank, 0)


def bias_rows(lengths, entries, pos_buckets, box_buckets, heads):
    docs, rows = pos_buckets.shape[0], pos_buckets.shape[2]
    padded = pl.cdiv(rows, BLOCK) * BLOCK
    return pl.pallas_call(
        partial(bias_kernel, rows),
        out_shape=jax.ShapeDtypeStruct((docs, heads, padded, padded), F32),
        grid=(docs, padded // BLOCK),
        in_specs=[
            pl.BlockSpec(memory_space=pltpu.SMEM),
            resident(entries.shape),
            pl.BlockSpec((1, 1, BLOCK, padded), lambda d, i: (d, 0, i, 0)),
            pl.BlockSpec((1, 1, 2, BLOCK, padded), lambda d, i: (d, 0, 0, i, 0)),
        ],
        out_specs=pl.BlockSpec((1, heads, BLOCK, padded), lambda d, i: (d, 0, i, 0)),
        compiler_params=params(2),
        cost_estimate=pl.CostEstimate(
            flops=3 * docs * heads * rows * rows,
            transcendentals=0,
            bytes_accessed=docs * padded * padded * (4 * heads + 12),
        ),
        name="bias_rows",
    )(lengths, entries, pos_buckets, box_buckets)


def project_kernel(rows, x_ref, w_ref, vec_ref, out_ref):
    width = x_ref.shape[3]
    block = live_rows(x_ref[0, 0], rows, pl.program_id(1) * x_ref.shape[2])
    queries = dot(block, w_ref[:, :width]) + vec_ref[4:5, :]
    out_ref[0, :, :width] = queries.astype(BF16) * BF16(SCALE)
    out_ref[0, :, width : 2 * width] = dot(block, w_ref[:, width : 2 * width]).astype(BF16)
    values = dot(block, w_ref[:, 2 * width :]) + vec_ref[5:6, :]
    out_ref[0, :, 2 * width :] = values.astype(BF16)


def project(layer_input, w_qkv, vectors):
    docs, unused, rows, width = layer_input.shape
    padded = pl.cdiv(rows, BLOCK) * BLOCK
    return pl.pallas_call(
        partial(project_kernel, rows),
        out_shape=jax.ShapeDtypeStruct((docs, padded, 3 * width), BF16),
        grid=(docs, padded // DENSE_BLOCK),
        in_specs=[
            pl.BlockSpec((1, 1, DENSE_BLOCK, width), lambda d, i: (d, 0, i, 0)),
            resident(w_qkv.shape),
            resident(vectors.shape),
        ],
        out_specs=pl.BlockSpec((1, DENSE_BLOCK, 3 * width), lambda d, i: (d, i, 0)),
        compiler_params=params(2),
        name="project",
    )(layer_input, w_qkv, vectors)


def attend_kernel(q_ref, k_ref, v_ref, bias_ref, probs_ref, out_ref):
    lane = lax.broadcasted_iota(jnp.int32, (1, LANES), 1)
    for pair in range(q_ref.shape[2] // LANES):
        cols = slice(pair * LANES, (pair + 1) * LANES)
        queries, key_rows, values = q_ref[0, :, cols], k_ref[0, :, cols], v_ref[0, :, cols]
        total = None
        for half in range(2):
            head = 2 * pair + half
            keep = (lane < HEAD_DIM) if half == 0 else (lane >= HEAD_DIM)
            scores = dot_nt(jnp.where(keep, queries, BF16(0)), key_rows) + bias_ref[0, head]
            top = jnp.max(scores, axis=-1, keepdims=True)
            powers = jnp.exp(scores - top)
            share = 1.0 / jnp.sum(powers, axis=-1, keepdims=True)
            probs = (powers * share).astype(BF16)
            probs_ref[0, head] = probs
            part = dot(probs, jnp.where(keep, values, BF16(0)))
            total = part if half == 0 else total + part
        out_ref[0, :, cols] = total.astype(BF16)


def attend(qkv, bias):
    docs, padded, width = qkv.shape[0], qkv.shape[1], qkv.shape[2] // 3
    heads = bias.shape[1]
    return pl.pallas_call(
        attend_kernel,
        out_shape=(
            jax.ShapeDtypeStruct((docs, heads, padded, padded), BF16),
            jax.ShapeDtypeStruct((docs, padded, width), BF16),
        ),
        grid=(docs, padded // BLOCK),
        in_specs=[
            pl.BlockSpec((1, BLOCK, width), lambda d, i: (d, i, 0)),
            pl.BlockSpec((1, padded, width), lambda d, i: (d, 0, 1)),
            pl.BlockSpec((1, padded, width), lambda d, i: (d, 0, 2)),
            pl.BlockSpec((1, heads, BLOCK, padded), lambda d, i: (d, 0, i, 0)),
        ],
        out_specs=(
            pl.BlockSpec((1, heads, BLOCK, padded), lambda d, i: (d, 0, i, 0)),
            pl.BlockSpec((1, BLOCK, width), lambda d, i: (d, i, 0)),
        ),
        compiler_params=params(2),
        name="attend",
    )(qkv, qkv, qkv, bias)


def norm(rows_in):
    centre = rows_in - jnp.mean(rows_in, axis=-1, keepdims=True)
    inv_std = lax.rsqrt(jnp.mean(centre * centre, axis=-1, keepdims=True) + NORM_EPS)
    return centre * inv_std, inv_std


def norm_back(grad_in, normed, inv_std, gain_row):
    scaled = grad_in * gain_row
    return inv_std * (
        scaled
        - jnp.mean(scaled, axis=-1, keepdims=True)
        - normed * jnp.mean(scaled * normed, axis=-1, keepdims=True)
    )


def dense_kernel(
    rows, x_ref, o_ref, cot_ref, wo_ref, wu_ref, wd_ref, vec_ref, upb_ref,
    y_ref, dr_ref, h_ref, g_ref, du_ref, df_ref, db_ref, do_ref, sums_ref, upsum_ref,
    slope_ref,
):
    width, hidden = wu_ref.shape
    first = pl.program_id(1) * x_ref.shape[2]
    vec = vec_ref[...]

    @pl.when((pl.program_id(0) == 0) & (pl.program_id(1) == 0))
    def _():
        sums_ref[...] = jnp.zeros_like(sums_ref)
        upsum_ref[...] = jnp.zeros_like(upsum_ref)

    tok = live_rows(x_ref[0, 0], rows, first).astype(F32)
    normed_one, inv_one = norm(tok + dot(o_ref[0], wo_ref[...]) + vec[6:7])
    state = normed_one * vec[0:1] + vec[2:3]
    low = state.astype(BF16)
    h_ref[0] = low
    second = state + vec[7:8]
    for part in range(hidden // width):
        cols = slice(part * width, (part + 1) * width)
        upper = dot(low, wu_ref[:, cols]) + upb_ref[:, cols]
        cdf = 0.5 * (1.0 + lax.erf(upper * (0.5**0.5)))
        slope_ref[:, cols] = cdf + upper * (jnp.exp(-0.5 * upper * upper) * 0.3989422804014327)
        active = (upper * cdf).astype(BF16)
        g_ref[0, :, cols] = active
        second = second + dot(active, wd_ref[cols, :])
    normed_two, inv_two = norm(second)
    y_ref[0, 0] = (normed_two * vec[1:2] + vec[3:4]).astype(BF16)
    grad = live_rows(cot_ref[0, 0], rows, first).astype(F32)
    sums_ref[1:2, :] += jnp.sum(grad * normed_two, axis=0, keepdims=True)
    sums_ref[3:4, :] += jnp.sum(grad, axis=0, keepdims=True)
    d_two = norm_back(grad, normed_two, inv_two, vec[1:2])
    d_ffn = d_two.astype(BF16)
    df_ref[0] = d_ffn
    sums_ref[7:8, :] += jnp.sum(d_ffn.astype(F32), axis=0, keepdims=True)
    back = d_two
    for part in range(hidden // width):
        cols = slice(part * width, (part + 1) * width)
        d_upper = (dot_nt(d_ffn, wd_ref[cols, :]) * slope_ref[:, cols]).astype(BF16)
        du_ref[0, :, cols] = d_upper
        upsum_ref[:, cols] += jnp.sum(d_upper.astype(F32), axis=0, keepdims=True)
        back = back + dot_nt(d_upper, wu_ref[:, cols])
    sums_ref[0:1, :] += jnp.sum(back * normed_one, axis=0, keepdims=True)
    sums_ref[2:3, :] += jnp.sum(back, axis=0, keepdims=True)
    d_one = norm_back(back, normed_one, inv_one, vec[0:1])
    dr_ref[0] = d_one
    d_branch = d_one.astype(BF16)
    db_ref[0] = d_branch
    sums_ref[6:7, :] += jnp.sum(d_branch.astype(F32), axis=0, keepdims=True)
    do_ref[0] = dot_nt(d_branch, wo_ref[...]).astype(BF16)


def dense(layer_input, attended, cotangent, w_out, w_up, w_down, vectors, up_row):
    docs, unused, rows, width = layer_input.shape
    padded, hidden = attended.shape[1], w_up.shape[1]
    ragged = pl.BlockSpec((1, 1, DENSE_BLOCK, width), lambda d, i: (d, 0, i, 0))
    narrow = pl.BlockSpec((1, DENSE_BLOCK, width), lambda d, i: (d, i, 0))
    wide = pl.BlockSpec((1, DENSE_BLOCK, hidden), lambda d, i: (d, i, 0))

    def rows_of(columns, dtype):
        return jax.ShapeDtypeStruct((docs, padded, columns), dtype)

    return pl.pallas_call(
        partial(dense_kernel, rows),
        out_shape=(
            jax.ShapeDtypeStruct(layer_input.shape, BF16),
            rows_of(width, F32),
            rows_of(width, BF16),
            rows_of(hidden, BF16),
            rows_of(hidden, BF16),
            rows_of(width, BF16),
            rows_of(width, BF16),
            rows_of(width, BF16),
            jax.ShapeDtypeStruct((8, width), F32),
            jax.ShapeDtypeStruct((1, hidden), F32),
        ),
        grid=(docs, padded // DENSE_BLOCK),
        in_specs=[
            ragged, narrow, ragged,
            resident(w_out.shape), resident(w_up.shape), resident(w_down.shape),
            resident(vectors.shape), resident(up_row.shape),
        ],
        out_specs=(
            ragged, narrow, narrow, wide, wide, narrow, narrow, narrow,
            pl.BlockSpec((8, width), lambda d, i: (0, 0)),
            pl.BlockSpec((1, hidden), lambda d, i: (0, 0)),
        ),
        scratch_shapes=[pltpu.VMEM((DENSE_BLOCK, hidden), F32)],
        compiler_params=params(2),
        name="dense",
    )(layer_input, attended, cotangent, w_out, w_up, w_down, vectors, up_row)


def attend_back_kernel(
    rows, q_ref, k_ref, v_ref, probs_ref, do_ref, pos_ref, box_ref, dm_ref, bins_ref,
    dk_ref, dv_ref, ds_ref,
):
    block, width = pl.program_id(1), q_ref.shape[2]
    padded = k_ref.shape[1]
    lane = lax.broadcasted_iota(jnp.int32, (1, LANES), 1)

    @pl.when((pl.program_id(0) == 0) & (block == 0))
    def _():
        bins_ref[...] = jnp.zeros_like(bins_ref)
        ds_ref[...] = jnp.zeros_like(ds_ref)

    @pl.when(block == 0)
    def _():
        dk_ref[...] = jnp.zeros_like(dk_ref)
        dv_ref[...] = jnp.zeros_like(dv_ref)

    own = pl.ds(pl.multiple_of(block * BLOCK, BLOCK), BLOCK)
    for pair in range(width // LANES):
        cols = slice(pair * LANES, (pair + 1) * LANES)
        queries, key_rows, values = q_ref[0, :, cols], k_ref[0, :, cols], v_ref[0, :, cols]
        grads = do_ref[0, :, cols]
        turned_q, turned_g = queries.T, grads.T
        total = None
        for half in range(2):
            head = 2 * pair + half
            keep = (lane < HEAD_DIM) if half == 0 else (lane >= HEAD_DIM)
            part = slice(half * HEAD_DIM, (half + 1) * HEAD_DIM)
            lines = slice(head * HEAD_DIM, (head + 1) * HEAD_DIM)
            low = probs_ref[0, head]
            probs = low.astype(F32)
            dprobs = dot_nt(jnp.where(keep, grads, BF16(0)), values)
            delta = jnp.sum(probs * dprobs, axis=-1, keepdims=True)
            dscore = probs * (dprobs - delta)
            for chunk in range(padded // LANES):
                ds_ref[chunk, pl.ds(head, BLOCK, stride=16), :] = dscore[
                    :, chunk * LANES : (chunk + 1) * LANES
                ]
            dlow = dscore.astype(BF16)
            piece = dot(dlow, jnp.where(keep, key_rows, BF16(0)))
            total = piece if half == 0 else total + piece
            dk_ref[lines, :] += dot(turned_q[part, :], dlow)
            dv_ref[lines, :] += dot(turned_g[part, :], low)
        dm_ref[0, own, cols] = (total * SCALE).astype(BF16)

    group = 8
    low_bins = lax.broadcasted_iota(jnp.int32, (HALF, padded), 0).astype(BF16)

    def hits(picks, bins):
        return jnp.where(low_bins[:bins] == picks.astype(BF16), BF16(1), BF16(0))

    def count(step, carry):
        left, right = [], []
        for line in range(group):
            row = step * group + line
            at = pl.ds(row, 1)
            pick_x = box_ref[0, 0, 0, at, :] & (BOX_BINS - 1)
            pick_y = box_ref[0, 0, 1, at, :] & (BOX_BINS - 1)
            pick_p = pos_ref[0, 0, at, :] & (POS_BINS - 1)
            here = pl.ds(pl.multiple_of(row * 16, 16), 16)
            base = jnp.concatenate(
                [ds_ref[chunk, here, :] for chunk in range(padded // LANES)], axis=1
            )
            left.append(
                jnp.concatenate(
                    [
                        base.astype(BF16),
                        (base * (pick_x >> 5).astype(F32)).astype(BF16),
                        (base * (pick_y >> 5).astype(F32)).astype(BF16),
                        (base * (pick_p >> 4).astype(F32)).astype(BF16),
                    ],
                    axis=0,
                )
            )
            right.append(
                jnp.concatenate(
                    [
                        hits(pick_x & (HALF - 1), HALF),
                        hits(pick_y & (HALF - 1), HALF),
                        hits(pick_p & (HALF // 2 - 1), HALF // 2),
                    ],
                    axis=0,
                )
            )
        sums = dot_nt(jnp.concatenate(left, axis=1), jnp.concatenate(right, axis=1))
        bins_ref[:, : sums.shape[1]] += sums
        return carry

    live = jnp.minimum(BLOCK, (rows + group - 1) // group * group - block * BLOCK)
    lax.fori_loop(0, live // group, count, 0)

    @pl.when(block == pl.num_programs(1) - 1)
    def _():
        dm_ref[0, :, width : 2 * width] = dk_ref[...].astype(BF16).T
        dm_ref[0, :, 2 * width :] = dv_ref[...].astype(BF16).T


def attend_back(qkv, probs, d_attended, pos_buckets, box_buckets):
    docs, padded, width = qkv.shape[0], qkv.shape[1], qkv.shape[2] // 3
    heads, rows = probs.shape[1], pos_buckets.shape[2]
    return pl.pallas_call(
        partial(attend_back_kernel, rows),
        out_shape=(
            jax.ShapeDtypeStruct((docs, padded, 3 * width), BF16),
            jax.ShapeDtypeStruct((64, LANES), F32),
        ),
        grid=(docs, padded // BLOCK),
        in_specs=[
            pl.BlockSpec((1, BLOCK, width), lambda d, i: (d, i, 0)),
            pl.BlockSpec((1, padded, width), lambda d, i: (d, 0, 1)),
            pl.BlockSpec((1, padded, width), lambda d, i: (d, 0, 2)),
            pl.BlockSpec((1, heads, BLOCK, padded), lambda d, i: (d, 0, i, 0)),
            pl.BlockSpec((1, BLOCK, width), lambda d, i: (d, i, 0)),
            pl.BlockSpec((1, 1, BLOCK, padded), lambda d, i: (d, 0, i, 0)),
            pl.BlockSpec((1, 1, 2, BLOCK, padded), lambda d, i: (d, 0, 0, i, 0)),
        ],
        out_specs=(
            pl.BlockSpec((1, padded, 3 * width), lambda d, i: (d, 0, 0)),
            pl.BlockSpec((64, LANES), lambda d, i: (0, 0)),
        ),
        scratch_shapes=[
            pltpu.VMEM((width, padded), F32),
            pltpu.VMEM((width, padded), F32),
            pltpu.VMEM((padded // LANES, BLOCK * 16, LANES), F32),
        ],
        compiler_params=params(2),
        name="attend_back",
    )(qkv, qkv, qkv, probs, d_attended, pos_buckets, box_buckets)


def table_entries(table):
    heads = table.shape[1]
    lines = table.astype(F32).T * SCALE
    boxes = lines[:, POS_BINS:]
    spots = jnp.pad(lines[:, :POS_BINS], ((0, 0), (0, LANES - POS_BINS)))
    return jnp.concatenate([boxes, spots], axis=0).reshape(2 * heads, LANES)


def table_grad(bins, heads):
    base, upper = bins[:heads], (bins[16 : 16 + heads], bins[32 : 32 + heads], bins[48 : 48 + heads])
    pieces = []
    for which, (first, size) in enumerate(((0, HALF), (HALF, HALF), (2 * HALF, HALF // 2))):
        high = upper[which][:, first : first + size]
        pieces.append(jnp.concatenate([base[:, first : first + size] - high, high], axis=1))
    return jnp.concatenate([pieces[2], pieces[0], pieces[1]], axis=1).T * SCALE


def local_step(lengths, pos_buckets, box_buckets, layer_input, cotangent, weights, vectors, up_row, table):
    w_qkv, w_out, w_up, w_down = weights
    heads, width = table.shape[1], layer_input.shape[3]
    docs, rows = layer_input.shape[0], layer_input.shape[2]
    bias = bias_rows(lengths, table_entries(table), pos_buckets, box_buckets, heads)
    qkv = project(layer_input, w_qkv, vectors)
    probs, attended = attend(qkv, bias)
    result, d_one, low, active, d_upper, d_ffn, d_branch, d_attended, sums, up_sum = dense(
        layer_input, attended, cotangent, w_out, w_up, w_down, vectors, up_row
    )

    def across(left, right):
        left, right = (item.reshape(-1, item.shape[-1]) for item in (left, right))
        return lax.dot_general(left, right, (((0,), (0,)), ((), ())), preferred_element_type=F32)

    d_down = across(active, d_ffn)
    d_up = across(low, d_upper)
    d_out = across(attended, d_branch)
    d_mixed, bins = attend_back(qkv, probs, d_attended, pos_buckets, box_buckets)
    padded = d_mixed.shape[1]
    tok = jnp.pad(layer_input[:, 0], ((0, 0), (0, padded - rows), (0, 0)))
    d_qkv = across(tok, d_mixed)
    flat = d_mixed.reshape(docs * padded, 3 * width)
    back = dot_nt(flat, w_qkv).reshape(docs, padded, width)
    input_grad = (d_one + back)[:, None, :rows]
    mixed_sum = jnp.sum(flat.astype(F32), axis=0)
    return (
        result, input_grad, d_qkv, d_out, d_up, d_down, sums, up_sum, mixed_sum,
        table_grad(bins, heads),
    )


def body(
    layer_input, text_lengths, pos_buckets, box_buckets, w_qkv, w_out, w_up, w_down,
    norm_gains, norm_shifts, proj_biases, up_bias, rel_tables, cotangent,
):
    axes = ("dp", "fsdp")
    width = layer_input.shape[3]
    hidden = w_up.shape[1]
    table = lax.all_gather(rel_tables, "fsdp", axis=0, tiled=True)
    own = norm_gains.shape[1]
    small = jnp.concatenate(
        [
            jnp.concatenate([norm_gains, norm_shifts, proj_biases], axis=0).reshape(-1),
            up_bias,
        ]
    )
    every = lax.all_gather(small, axes, axis=0)
    devices = every.shape[0]
    vectors = every[:, : 8 * own].reshape(devices, 8, own)
    vectors = jnp.transpose(vectors, (1, 0, 2)).reshape(8, width).astype(F32)
    up_row = every[:, 8 * own :].reshape(1, hidden).astype(F32)
    weights = tuple(
        lax.all_gather(item, axes, axis=0, tiled=True) for item in (w_qkv, w_out, w_up, w_down)
    )
    (
        result, input_grad, d_qkv, d_out, d_up, d_down, sums, up_sum, mixed_sum, d_table,
    ) = local_step(
        text_lengths[:, 0], pos_buckets, box_buckets, layer_input, cotangent, weights, vectors,
        up_row, table,
    )
    shards = [
        lax.psum_scatter(item.astype(BF16), axes, scatter_dimension=0, tiled=True).astype(F32)
        for item in (d_qkv, d_out, d_up, d_down)
    ]
    sums = sums.at[4].set(mixed_sum[:width]).at[5].set(mixed_sum[2 * width :])
    sums, up_sum, d_table = lax.psum((sums, up_sum, d_table), axes)
    place = lax.axis_index(axes)
    sums = lax.dynamic_slice_in_dim(sums, place * own, own, 1)
    up_sum = lax.dynamic_slice_in_dim(up_sum[0], place * up_bias.shape[0], up_bias.shape[0], 0)
    table_rows = rel_tables.shape[0]
    d_table = lax.dynamic_slice_in_dim(d_table, lax.axis_index("fsdp") * table_rows, table_rows, 0)
    return (
        result, input_grad, *shards, sums[0:2], sums[2:4], sums[4:8], up_sum, d_table,
    )


def solution(mesh):
    both = ("dp", "fsdp")
    docs = P(None, both, None, None)
    return jax.shard_map(
        body,
        mesh=mesh,
        in_specs=(
            docs, P(None, both), docs, P(None, both, None, None, None),
            P(both, None), P(both, None), P(both, None), P(both, None),
            P(None, both), P(None, both), P(None, both), P(both), P("fsdp", None), docs,
        ),
        out_specs=(
            docs, docs, P(both, None), P(both, None), P(both, None), P(both, None),
            P(None, both), P(None, both), P(None, both), P(both), P("fsdp", None),
        ),
        check_vma=False,
    )
```

```python
from functools import partial

import jax
import jax.numpy as jnp
from jax import lax
from jax.experimental import pallas as pl
from jax.experimental.pallas import tpu as pltpu
from jax.sharding import PartitionSpec as P

HEAD_DIM = 64
POS_BINS = 32
BOX_BINS = 64
TEXT_SLOTS = 512
NEG_FILL = -1000000000.0
NORM_EPS = 1e-05
BLOCK = 256
DENSE_BLOCK = 384
LANES = 128
HALF = 32
SCALE = 0.125
F32 = jnp.float32
BF16 = jnp.bfloat16
VMEM_LIMIT = 58 << 20


def dot(left, right):
    return jnp.dot(left, right, preferred_element_type=F32)


def dot_nt(left, right):
    return lax.dot_general(left, right, (((1,), (1,)), ((), ())), preferred_element_type=F32)


def params(count):
    return pltpu.CompilerParams(
        dimension_semantics=("arbitrary",) * count, vmem_limit_bytes=VMEM_LIMIT
    )


def resident(shape):
    zeros = (0,) * len(shape)
    return pl.BlockSpec(shape, lambda *_: zeros, pipeline_mode=pl.Buffered(1))


def columns(shape, place):
    return pl.BlockSpec(shape, lambda *_: (0, place), pipeline_mode=pl.Buffered(1))


def live_rows(values, rows, first):
    row = first + lax.broadcasted_iota(jnp.int32, (values.shape[0], 1), 0)
    return jnp.where(row < rows, values, jnp.zeros_like(values))


def bias_kernel(rows, len_ref, tab_ref, pos_ref, box_ref, out_ref):
    heads, chunks = out_ref.shape[1], out_ref.shape[3] // LANES
    block = pl.program_id(1)
    length = len_ref[pl.program_id(0)]
    steps = jnp.minimum(BLOCK, (rows + 7) // 8 * 8 - block * BLOCK) // 8

    def fill(step, carry):
        at = pl.ds(pl.multiple_of(step * 8, 8), 8)
        for chunk in range(chunks):
            cols = slice(chunk * LANES, (chunk + 1) * LANES)
            picks = (
                box_ref[0, 0, 0, at, cols] & (BOX_BINS - 1),
                (box_ref[0, 0, 1, at, cols] & (BOX_BINS - 1)) | BOX_BINS,
                pos_ref[0, 0, at, cols] & (POS_BINS - 1),
            )
            slot = chunk * LANES + lax.broadcasted_iota(jnp.int32, (8, LANES), 1)
            valid = ((slot >= TEXT_SLOTS) & (slot < rows)) | (slot < length)
            totals = [None] * heads
            for which, pick in enumerate(picks):
                for head in range(heads):
                    line = head + (heads if which == 2 else 0)
                    entries = jnp.broadcast_to(tab_ref[line : line + 1, :], (8, LANES))
                    term = jnp.take_along_axis(entries, pick, axis=1)
                    totals[head] = term if which == 0 else totals[head] + term
            for head in range(heads):
                out_ref[0, head, at, cols] = jnp.where(valid, totals[head], NEG_FILL)
        return carry

    def blank(step, carry):
        at = pl.ds(pl.multiple_of(step * 8, 8), 8)
        for head in range(heads):
            out_ref[0, head, at, :] = jnp.zeros((8, chunks * LANES), F32)
        return carry

    lax.fori_loop(0, steps, fill, 0)
    lax.fori_loop(steps, BLOCK // 8, blank, 0)


def bias_rows(lengths, entries, pos_buckets, box_buckets, heads):
    docs, rows = pos_buckets.shape[0], pos_buckets.shape[2]
    padded = pl.cdiv(rows, BLOCK) * BLOCK
    return pl.pallas_call(
        partial(bias_kernel, rows),
        out_shape=jax.ShapeDtypeStruct((docs, heads, padded, padded), F32),
        grid=(docs, padded // BLOCK),
        in_specs=[
            pl.BlockSpec(memory_space=pltpu.SMEM),
            resident(entries.shape),
            pl.BlockSpec((1, 1, BLOCK, padded), lambda d, i: (d, 0, i, 0)),
            pl.BlockSpec((1, 1, 2, BLOCK, padded), lambda d, i: (d, 0, 0, i, 0)),
        ],
        out_specs=pl.BlockSpec((1, heads, BLOCK, padded), lambda d, i: (d, 0, i, 0)),
        compiler_params=params(2),
        cost_estimate=pl.CostEstimate(
            flops=3 * docs * heads * rows * rows,
            transcendentals=0,
            bytes_accessed=docs * padded * padded * (4 * heads + 12),
        ),
        name="bias_rows",
    )(lengths, entries, pos_buckets, box_buckets)


def project_kernel(rows, x_ref, w_ref, vec_ref, out_ref, tok_ref):
    width = x_ref.shape[3]
    block = live_rows(x_ref[0, 0], rows, pl.program_id(1) * x_ref.shape[2])
    tok_ref[0] = block
    queries = dot(block, w_ref[:, :width]) + vec_ref[4:5, :]
    out_ref[0, :, :width] = queries.astype(BF16) * BF16(SCALE)
    out_ref[0, :, width : 2 * width] = dot(block, w_ref[:, width : 2 * width]).astype(BF16)
    values = dot(block, w_ref[:, 2 * width :]) + vec_ref[5:6, :]
    out_ref[0, :, 2 * width :] = values.astype(BF16)


def project(layer_input, w_mixed, vectors):
    docs, unused, rows, width = layer_input.shape
    padded = pl.cdiv(rows, BLOCK) * BLOCK
    return pl.pallas_call(
        partial(project_kernel, rows),
        out_shape=(
            jax.ShapeDtypeStruct((docs, padded, 3 * width), BF16),
            jax.ShapeDtypeStruct((docs, padded, width), BF16),
        ),
        grid=(docs, padded // DENSE_BLOCK),
        in_specs=[
            pl.BlockSpec((1, 1, DENSE_BLOCK, width), lambda d, i: (d, 0, i, 0)),
            columns((width, 3 * width), 0),
            resident(vectors.shape),
        ],
        out_specs=(
            pl.BlockSpec((1, DENSE_BLOCK, 3 * width), lambda d, i: (d, i, 0)),
            pl.BlockSpec((1, DENSE_BLOCK, width), lambda d, i: (d, i, 0)),
        ),
        compiler_params=params(2),
        name="project",
    )(layer_input, w_mixed, vectors)


def attend_kernel(q_ref, k_ref, v_ref, bias_ref, probs_ref, out_ref):
    lane = lax.broadcasted_iota(jnp.int32, (1, LANES), 1)
    for pair in range(q_ref.shape[2] // LANES):
        cols = slice(pair * LANES, (pair + 1) * LANES)
        queries, key_rows, values = q_ref[0, :, cols], k_ref[0, :, cols], v_ref[0, :, cols]
        total = None
        for half in range(2):
            head = 2 * pair + half
            keep = (lane < HEAD_DIM) if half == 0 else (lane >= HEAD_DIM)
            scores = dot_nt(jnp.where(keep, queries, BF16(0)), key_rows) + bias_ref[0, head]
            top = jnp.max(scores, axis=-1, keepdims=True)
            powers = jnp.exp(scores - top)
            share = 1.0 / jnp.sum(powers, axis=-1, keepdims=True)
            probs = (powers * share).astype(BF16)
            probs_ref[0, head] = probs
            part = dot(probs, jnp.where(keep, values, BF16(0)))
            total = part if half == 0 else total + part
        out_ref[0, :, cols] = total.astype(BF16)


def attend(qkv, bias):
    docs, padded, width = qkv.shape[0], qkv.shape[1], qkv.shape[2] // 3
    heads = bias.shape[1]
    return pl.pallas_call(
        attend_kernel,
        out_shape=(
            jax.ShapeDtypeStruct((docs, heads, padded, padded), BF16),
            jax.ShapeDtypeStruct((docs, padded, width), BF16),
        ),
        grid=(docs, padded // BLOCK),
        in_specs=[
            pl.BlockSpec((1, BLOCK, width), lambda d, i: (d, i, 0)),
            pl.BlockSpec((1, padded, width), lambda d, i: (d, 0, 1)),
            pl.BlockSpec((1, padded, width), lambda d, i: (d, 0, 2)),
            pl.BlockSpec((1, heads, BLOCK, padded), lambda d, i: (d, 0, i, 0)),
        ],
        out_specs=(
            pl.BlockSpec((1, heads, BLOCK, padded), lambda d, i: (d, 0, i, 0)),
            pl.BlockSpec((1, BLOCK, width), lambda d, i: (d, i, 0)),
        ),
        compiler_params=params(2),
        name="attend",
    )(qkv, qkv, qkv, bias)


def norm(rows_in):
    centre = rows_in - jnp.mean(rows_in, axis=-1, keepdims=True)
    inv_std = lax.rsqrt(jnp.mean(centre * centre, axis=-1, keepdims=True) + NORM_EPS)
    return centre * inv_std, inv_std


def norm_back(grad_in, normed, inv_std, gain_row):
    scaled = grad_in * gain_row
    return inv_std * (
        scaled
        - jnp.mean(scaled, axis=-1, keepdims=True)
        - normed * jnp.mean(scaled * normed, axis=-1, keepdims=True)
    )


def dense_kernel(
    rows, x_ref, o_ref, cot_ref, wo_ref, wu_ref, wd_ref, vec_ref, upb_ref,
    y_ref, dr_ref, h_ref, g_ref, du_ref, df_ref, db_ref, do_ref, sums_ref, upsum_ref,
    slope_ref,
):
    width, hidden = wu_ref.shape
    first = pl.program_id(1) * x_ref.shape[2]
    vec = vec_ref[...]

    @pl.when((pl.program_id(0) == 0) & (pl.program_id(1) == 0))
    def _():
        sums_ref[...] = jnp.zeros_like(sums_ref)
        upsum_ref[...] = jnp.zeros_like(upsum_ref)

    tok = live_rows(x_ref[0, 0], rows, first).astype(F32)
    normed_one, inv_one = norm(tok + dot(o_ref[0], wo_ref[...]) + vec[6:7])
    state = normed_one * vec[0:1] + vec[2:3]
    low = state.astype(BF16)
    h_ref[0] = low
    second = state + vec[7:8]
    for part in range(hidden // width):
        cols = slice(part * width, (part + 1) * width)
        upper = dot(low, wu_ref[:, cols]) + upb_ref[:, cols]
        cdf = 0.5 * (1.0 + lax.erf(upper * (0.5**0.5)))
        slope_ref[:, cols] = cdf + upper * (jnp.exp(-0.5 * upper * upper) * 0.3989422804014327)
        active = (upper * cdf).astype(BF16)
        g_ref[0, :, cols] = active
        second = second + dot(active, wd_ref[cols, :])
    normed_two, inv_two = norm(second)
    y_ref[0, 0] = (normed_two * vec[1:2] + vec[3:4]).astype(BF16)
    grad = live_rows(cot_ref[0, 0], rows, first).astype(F32)
    sums_ref[1:2, :] += jnp.sum(grad * normed_two, axis=0, keepdims=True)
    sums_ref[3:4, :] += jnp.sum(grad, axis=0, keepdims=True)
    d_two = norm_back(grad, normed_two, inv_two, vec[1:2])
    d_ffn = d_two.astype(BF16)
    df_ref[0] = d_ffn
    sums_ref[7:8, :] += jnp.sum(d_ffn.astype(F32), axis=0, keepdims=True)
    back = d_two
    for part in range(hidden // width):
        cols = slice(part * width, (part + 1) * width)
        d_upper = (dot_nt(d_ffn, wd_ref[cols, :]) * slope_ref[:, cols]).astype(BF16)
        du_ref[0, :, cols] = d_upper
        upsum_ref[:, cols] += jnp.sum(d_upper.astype(F32), axis=0, keepdims=True)
        back = back + dot_nt(d_upper, wu_ref[:, cols])
    sums_ref[0:1, :] += jnp.sum(back * normed_one, axis=0, keepdims=True)
    sums_ref[2:3, :] += jnp.sum(back, axis=0, keepdims=True)
    d_one = norm_back(back, normed_one, inv_one, vec[0:1])
    dr_ref[0] = d_one
    d_branch = d_one.astype(BF16)
    db_ref[0] = d_branch
    sums_ref[6:7, :] += jnp.sum(d_branch.astype(F32), axis=0, keepdims=True)
    do_ref[0] = dot_nt(d_branch, wo_ref[...]).astype(BF16)


def dense(layer_input, attended, cotangent, w_mixed, w_down, vectors, up_row):
    docs, unused, rows, width = layer_input.shape
    padded, hidden = attended.shape[1], w_down.shape[0]
    ragged = pl.BlockSpec((1, 1, DENSE_BLOCK, width), lambda d, i: (d, 0, i, 0))
    narrow = pl.BlockSpec((1, DENSE_BLOCK, width), lambda d, i: (d, i, 0))
    wide = pl.BlockSpec((1, DENSE_BLOCK, hidden), lambda d, i: (d, i, 0))

    def rows_of(columns, dtype):
        return jax.ShapeDtypeStruct((docs, padded, columns), dtype)

    return pl.pallas_call(
        partial(dense_kernel, rows),
        out_shape=(
            jax.ShapeDtypeStruct(layer_input.shape, BF16),
            rows_of(width, F32),
            rows_of(width, BF16),
            rows_of(hidden, BF16),
            rows_of(hidden, BF16),
            rows_of(width, BF16),
            rows_of(width, BF16),
            rows_of(width, BF16),
            jax.ShapeDtypeStruct((8, width), F32),
            jax.ShapeDtypeStruct((1, hidden), F32),
        ),
        grid=(docs, padded // DENSE_BLOCK),
        in_specs=[
            ragged, narrow, ragged,
            columns((width, width), 3), columns((width, hidden), 4 * width // hidden),
            resident(w_down.shape),
            resident(vectors.shape), resident(up_row.shape),
        ],
        out_specs=(
            ragged, narrow, narrow, wide, wide, narrow, narrow, narrow,
            pl.BlockSpec((8, width), lambda d, i: (0, 0)),
            pl.BlockSpec((1, hidden), lambda d, i: (0, 0)),
        ),
        scratch_shapes=[pltpu.VMEM((DENSE_BLOCK, hidden), F32)],
        compiler_params=params(2),
        name="dense",
    )(layer_input, attended, cotangent, w_mixed, w_mixed, w_down, vectors, up_row)


def attend_back_kernel(
    rows, q_ref, k_ref, v_ref, probs_ref, do_ref, pos_ref, box_ref, dm_ref, bins_ref,
    dk_ref, dv_ref, ds_ref,
):
    block, width = pl.program_id(1), q_ref.shape[2]
    padded = k_ref.shape[1]
    lane = lax.broadcasted_iota(jnp.int32, (1, LANES), 1)

    @pl.when((pl.program_id(0) == 0) & (block == 0))
    def _():
        bins_ref[...] = jnp.zeros_like(bins_ref)
        ds_ref[...] = jnp.zeros_like(ds_ref)

    @pl.when(block == 0)
    def _():
        dk_ref[...] = jnp.zeros_like(dk_ref)
        dv_ref[...] = jnp.zeros_like(dv_ref)

    own = pl.ds(pl.multiple_of(block * BLOCK, BLOCK), BLOCK)
    for pair in range(width // LANES):
        cols = slice(pair * LANES, (pair + 1) * LANES)
        queries, key_rows, values = q_ref[0, :, cols], k_ref[0, :, cols], v_ref[0, :, cols]
        grads = do_ref[0, :, cols]
        turned_q, turned_g = queries.T, grads.T
        total = None
        for half in range(2):
            head = 2 * pair + half
            keep = (lane < HEAD_DIM) if half == 0 else (lane >= HEAD_DIM)
            part = slice(half * HEAD_DIM, (half + 1) * HEAD_DIM)
            lines = slice(head * HEAD_DIM, (head + 1) * HEAD_DIM)
            low = probs_ref[0, head]
            probs = low.astype(F32)
            dprobs = dot_nt(jnp.where(keep, grads, BF16(0)), values)
            delta = jnp.sum(probs * dprobs, axis=-1, keepdims=True)
            dscore = probs * (dprobs - delta)
            for chunk in range(padded // LANES):
                ds_ref[chunk, pl.ds(head, BLOCK, stride=16), :] = dscore[
                    :, chunk * LANES : (chunk + 1) * LANES
                ]
            dlow = dscore.astype(BF16)
            piece = dot(dlow, jnp.where(keep, key_rows, BF16(0)))
            total = piece if half == 0 else total + piece
            dk_ref[lines, :] += dot(turned_q[part, :], dlow)
            dv_ref[lines, :] += dot(turned_g[part, :], low)
        dm_ref[0, own, cols] = (total * SCALE).astype(BF16)

    group = 16
    low_bins = lax.broadcasted_iota(jnp.int32, (HALF, padded), 0).astype(BF16)

    def hits(picks, bins):
        return jnp.where(low_bins[:bins] == picks.astype(BF16), BF16(1), BF16(0))

    def count(step, carry):
        left, right = [], []
        for line in range(group):
            row = step * group + line
            at = pl.ds(row, 1)
            pick_x = box_ref[0, 0, 0, at, :] & (BOX_BINS - 1)
            pick_y = box_ref[0, 0, 1, at, :] & (BOX_BINS - 1)
            pick_p = pos_ref[0, 0, at, :] & (POS_BINS - 1)
            here = pl.ds(pl.multiple_of(row * 16, 16), 16)
            base = jnp.concatenate(
                [ds_ref[chunk, here, :] for chunk in range(padded // LANES)], axis=1
            )
            left.append(
                jnp.concatenate(
                    [
                        base.astype(BF16),
                        (base * (pick_x >> 5).astype(F32)).astype(BF16),
                        (base * (pick_y >> 5).astype(F32)).astype(BF16),
                        (base * (pick_p >> 4).astype(F32)).astype(BF16),
                    ],
                    axis=0,
                )
            )
            right.append(
                jnp.concatenate(
                    [
                        hits(pick_x & (HALF - 1), HALF),
                        hits(pick_y & (HALF - 1), HALF),
                        hits(pick_p & (HALF // 2 - 1), HALF // 2),
                    ],
                    axis=0,
                )
            )
        sums = dot_nt(jnp.concatenate(left, axis=1), jnp.concatenate(right, axis=1))
        bins_ref[:, : sums.shape[1]] += sums
        return carry

    live = jnp.minimum(BLOCK, (rows + group - 1) // group * group - block * BLOCK)
    lax.fori_loop(0, live // group, count, 0)

    @pl.when(block == pl.num_programs(1) - 1)
    def _():
        dm_ref[0, :, width : 2 * width] = dk_ref[...].astype(BF16).T
        dm_ref[0, :, 2 * width :] = dv_ref[...].astype(BF16).T


def attend_back(qkv, probs, d_attended, pos_buckets, box_buckets):
    docs, padded, width = qkv.shape[0], qkv.shape[1], qkv.shape[2] // 3
    heads, rows = probs.shape[1], pos_buckets.shape[2]
    return pl.pallas_call(
        partial(attend_back_kernel, rows),
        out_shape=(
            jax.ShapeDtypeStruct((docs, padded, 3 * width), BF16),
            jax.ShapeDtypeStruct((64, LANES), F32),
        ),
        grid=(docs, padded // BLOCK),
        in_specs=[
            pl.BlockSpec((1, BLOCK, width), lambda d, i: (d, i, 0)),
            pl.BlockSpec((1, padded, width), lambda d, i: (d, 0, 1)),
            pl.BlockSpec((1, padded, width), lambda d, i: (d, 0, 2)),
            pl.BlockSpec((1, heads, BLOCK, padded), lambda d, i: (d, 0, i, 0)),
            pl.BlockSpec((1, BLOCK, width), lambda d, i: (d, i, 0)),
            pl.BlockSpec((1, 1, BLOCK, padded), lambda d, i: (d, 0, i, 0)),
            pl.BlockSpec((1, 1, 2, BLOCK, padded), lambda d, i: (d, 0, 0, i, 0)),
        ],
        out_specs=(
            pl.BlockSpec((1, padded, 3 * width), lambda d, i: (d, 0, 0)),
            pl.BlockSpec((64, LANES), lambda d, i: (0, 0)),
        ),
        scratch_shapes=[
            pltpu.VMEM((width, padded), F32),
            pltpu.VMEM((width, padded), F32),
            pltpu.VMEM((padded // LANES, BLOCK * 16, LANES), F32),
        ],
        compiler_params=params(2),
        name="attend_back",
    )(qkv, qkv, qkv, probs, d_attended, pos_buckets, box_buckets)


def table_entries(table):
    heads = table.shape[1]
    lines = table.astype(F32).T * SCALE
    boxes = lines[:, POS_BINS:]
    spots = jnp.pad(lines[:, :POS_BINS], ((0, 0), (0, LANES - POS_BINS)))
    return jnp.concatenate([boxes, spots], axis=0).reshape(2 * heads, LANES)


def table_grad(bins, heads):
    base, upper = bins[:heads], (bins[16 : 16 + heads], bins[32 : 32 + heads], bins[48 : 48 + heads])
    pieces = []
    for which, (first, size) in enumerate(((0, HALF), (HALF, HALF), (2 * HALF, HALF // 2))):
        high = upper[which][:, first : first + size]
        pieces.append(jnp.concatenate([base[:, first : first + size] - high, high], axis=1))
    return jnp.concatenate([pieces[2], pieces[0], pieces[1]], axis=1).T * SCALE


def branch_up_grads(attended, d_branch, low, d_upper):
    rows, width = attended.shape
    parts = 1 + d_upper.shape[1] // width

    def kernel(a_ref, b_ref, l_ref, u_ref, out_ref, turned_ref):
        part = pl.program_id(0)

        @pl.when(part == 0)
        def _():
            out_ref[...] = dot(a_ref[...].T, b_ref[...]).astype(BF16)
            turned_ref[...] = l_ref[...].T

        @pl.when(part > 0)
        def _():
            out_ref[...] = dot(turned_ref[...], u_ref[...]).astype(BF16)

    return pl.pallas_call(
        kernel,
        out_shape=jax.ShapeDtypeStruct((width, parts * width), BF16),
        grid=(parts,),
        in_specs=[
            resident((rows, width)),
            resident((rows, width)),
            resident((rows, width)),
            pl.BlockSpec((rows, width), lambda p: (0, jnp.maximum(p - 1, 0))),
        ],
        out_specs=pl.BlockSpec((width, width), lambda p: (0, p)),
        scratch_shapes=[pltpu.VMEM((width, rows), BF16)],
        compiler_params=params(1),
        cost_estimate=pl.CostEstimate(
            flops=2 * rows * width * width * parts, transcendentals=0,
            bytes_accessed=2 * rows * width * (parts + 3),
        ),
        name="branch_up_grads",
    )(attended, d_branch, low, d_upper)


def down_grads(active, d_ffn):
    rows, width = d_ffn.shape
    parts = active.shape[1] // width

    def kernel(g_ref, f_ref, out_ref):
        out_ref[...] = dot(g_ref[...].T, f_ref[...]).astype(BF16)

    return pl.pallas_call(
        kernel,
        out_shape=jax.ShapeDtypeStruct((parts * width, width), BF16),
        grid=(parts,),
        in_specs=[pl.BlockSpec((rows, width), lambda p: (0, p)), resident((rows, width))],
        out_specs=pl.BlockSpec((width, width), lambda p: (p, 0)),
        compiler_params=params(1),
        cost_estimate=pl.CostEstimate(
            flops=2 * rows * width * width * parts, transcendentals=0,
            bytes_accessed=2 * rows * width * (parts + 2),
        ),
        name="down_grads",
    )(active, d_ffn)


def mixed_grads(tok, d_mixed):
    rows, width = tok.shape
    parts = d_mixed.shape[1] // width

    def kernel(t_ref, m_ref, out_ref, turned_ref):
        @pl.when(pl.program_id(0) == 0)
        def _():
            turned_ref[...] = t_ref[...].T

        out_ref[...] = dot(turned_ref[...], m_ref[...]).astype(BF16)

    return pl.pallas_call(
        kernel,
        out_shape=jax.ShapeDtypeStruct((width, parts * width), BF16),
        grid=(parts,),
        in_specs=[resident((rows, width)), pl.BlockSpec((rows, width), lambda p: (0, p))],
        out_specs=pl.BlockSpec((width, width), lambda p: (0, p)),
        scratch_shapes=[pltpu.VMEM((width, rows), BF16)],
        compiler_params=params(1),
        cost_estimate=pl.CostEstimate(
            flops=2 * rows * width * width * parts, transcendentals=0,
            bytes_accessed=2 * rows * width * (parts + 2),
        ),
        name="mixed_grads",
    )(tok, d_mixed)


def input_grads(d_mixed, d_one, w_mixed, rows):
    docs, padded, width = d_one.shape

    def kernel(m_ref, d_ref, w_ref, out_ref, sum_ref):
        @pl.when((pl.program_id(0) == 0) & (pl.program_id(1) == 0))
        def _():
            sum_ref[...] = jnp.zeros_like(sum_ref)

        block = m_ref[0]
        out_ref[0, 0] = d_ref[0] + dot_nt(block, w_ref[...])
        sum_ref[...] += jnp.sum(block.astype(F32), axis=0, keepdims=True)

    return pl.pallas_call(
        kernel,
        out_shape=(
            jax.ShapeDtypeStruct((docs, 1, rows, width), F32),
            jax.ShapeDtypeStruct((1, 3 * width), F32),
        ),
        grid=(docs, padded // DENSE_BLOCK),
        in_specs=[
            pl.BlockSpec((1, DENSE_BLOCK, 3 * width), lambda d, i: (d, i, 0)),
            pl.BlockSpec((1, DENSE_BLOCK, width), lambda d, i: (d, i, 0)),
            columns((width, 3 * width), 0),
        ],
        out_specs=(
            pl.BlockSpec((1, 1, DENSE_BLOCK, width), lambda d, i: (d, 0, i, 0)),
            pl.BlockSpec((1, 3 * width), lambda d, i: (0, 0)),
        ),
        compiler_params=params(2),
        name="input_grads",
    )(d_mixed, d_one, w_mixed)


def reduce_kernel(
    dims, grad_ref, small_ref, out_ref, sums_ref,
    got_c, one, got_xa, got_yb, two_a, two_b, got_ya, got_xb, three, got_z,
    sums, got_s, send_sems, recv_sems,
):
    deep, across, along, cores = dims
    dp, fsdp = lax.axis_index("dp"), lax.axis_index("fsdp")
    z, x = dp // across, dp % across
    y, c = fsdp // cores, fsdp % cores
    width = grad_ref.shape[5]
    cut = width // LANES // 2 * LANES
    lower, upper = slice(0, cut), slice(cut, width)

    def peer(axis, step):
        place = [z, x, y, c]
        place[axis] = (place[axis] + step) % dims[axis]
        return place[axis], (place[0] * across + place[1], place[2] * cores + place[3])

    barrier = pltpu.get_barrier_semaphore()
    partners = 0
    for axis in range(4):
        for step in range(1, dims[axis]):
            pl.semaphore_signal(
                barrier, inc=1, device_id=peer(axis, step)[1], device_id_type=pl.DeviceIdType.MESH
            )
            partners += 1
    pl.semaphore_wait(barrier, partners)

    def exchange(stage, axis, source, target):
        copies = []
        for step in range(1, dims[axis]):
            place, device = peer(axis, step)
            copies.append(
                pltpu.make_async_remote_copy(
                    src_ref=source(place),
                    dst_ref=target(step - 1),
                    send_sem=send_sems.at[stage, step - 1],
                    recv_sem=recv_sems.at[stage, step - 1],
                    device_id=device,
                    device_id_type=pl.DeviceIdType.MESH,
                )
            )
        for copy in copies:
            copy.start()
        return copies

    def finish(copies):
        for copy in copies:
            copy.wait()

    def joined(own, others):
        total = own.astype(F32)
        for other in others:
            total = total + other.astype(F32)
        return total

    def small_step(stage, axis, level):
        own = small_ref if level == 0 else sums.at[level - 1]
        first = sum(dims[later] - 1 for later in (3, 1, 2, 0)[:level])
        return exchange(stage, axis, lambda place: own, lambda slot: got_s.at[first + slot])

    def small_join(axis, level):
        own = small_ref if level == 0 else sums.at[level - 1]
        first = sum(dims[later] - 1 for later in (3, 1, 2, 0)[:level])
        return joined(own[...], [got_s[first + slot] for slot in range(dims[axis] - 1)])

    copies_c = exchange(0, 3, lambda t: grad_ref.at[:, :, :, t], lambda slot: got_c.at[slot])
    copies_s = small_step(7, 3, 0)
    finish(copies_s)
    finish(copies_c)
    sums[0] = small_join(3, 0)
    copies_s = small_step(8, 1, 1)

    def add_cores(k, carry):
        for i in range(across):
            for j in range(along):
                one[k, i, j] = joined(
                    grad_ref[k, i, j, c], [got_c[s, k, i, j] for s in range(cores - 1)]
                ).astype(BF16)
        return carry

    lax.fori_loop(0, deep, add_cores, 0)
    copies_xa = exchange(1, 1, lambda t: one.at[:, t, :, :, lower], lambda slot: got_xa.at[slot])
    copies_yb = exchange(2, 2, lambda t: one.at[:, :, t, :, upper], lambda slot: got_yb.at[slot])
    finish(copies_s)
    sums[1] = small_join(1, 1)
    copies_s = small_step(9, 2, 2)
    finish(copies_xa)

    def add_xa(k, carry):
        for j in range(along):
            two_a[k, j] = joined(
                one[k, x, j, :, lower], [got_xa[s, k, j] for s in range(across - 1)]
            ).astype(BF16)
        return carry

    lax.fori_loop(0, deep, add_xa, 0)
    copies_ya = exchange(3, 2, lambda t: two_a.at[:, t], lambda slot: got_ya.at[slot])
    finish(copies_yb)

    def add_yb(k, carry):
        for i in range(across):
            two_b[k, i] = joined(
                one[k, i, y, :, upper], [got_yb[s, k, i] for s in range(along - 1)]
            ).astype(BF16)
        return carry

    lax.fori_loop(0, deep, add_yb, 0)
    copies_xb = exchange(4, 1, lambda t: two_b.at[:, t], lambda slot: got_xb.at[slot])
    finish(copies_s)
    sums[2] = small_join(2, 2)
    copies_s = small_step(10, 0, 3)
    finish(copies_ya)

    def add_ya(k, carry):
        three[k, :, lower] = joined(
            two_a[k, y], [got_ya[s, k] for s in range(along - 1)]
        ).astype(BF16)
        return carry

    lax.fori_loop(0, deep, add_ya, 0)
    copies_za = exchange(
        5, 0, lambda t: three.at[t, :, lower], lambda slot: got_z.at[slot, :, lower]
    )
    finish(copies_xb)

    def add_xb(k, carry):
        three[k, :, upper] = joined(
            two_b[k, x], [got_xb[s, k] for s in range(across - 1)]
        ).astype(BF16)
        return carry

    lax.fori_loop(0, deep, add_xb, 0)
    copies_zb = exchange(
        6, 0, lambda t: three.at[t, :, upper], lambda slot: got_z.at[slot, :, upper]
    )
    finish(copies_s)
    sums_ref[...] = small_join(0, 3)
    finish(copies_za)
    finish(copies_zb)
    out_ref[...] = joined(three[z], [got_z[s] for s in range(deep - 1)])


def reduce_tail(grad, small, dp, fsdp):
    across = 1 << ((dp.bit_length() - 1) // 2)
    across = across if dp % across == 0 else 1
    cores = 2 if fsdp % 2 == 0 else 1
    dims = (dp // across, across, fsdp // cores, cores)
    deep, across, along, cores = dims
    width = grad.shape[1]
    rows = grad.shape[0] // (dp * fsdp)
    cut = width // LANES // 2 * LANES
    rest = width - cut
    slots = sum(dims) - 4
    vmem = pl.BlockSpec(memory_space=pltpu.VMEM)
    most = max(max(dims) - 1, 1)

    def held(*shape):
        return pltpu.VMEM(tuple(max(item, 1) for item in shape), BF16)

    return pl.pallas_call(
        partial(reduce_kernel, dims),
        out_shape=(
            jax.ShapeDtypeStruct((rows, width), F32),
            jax.ShapeDtypeStruct(small.shape, F32),
        ),
        in_specs=[vmem, vmem],
        out_specs=(vmem, vmem),
        scratch_shapes=[
            held(cores - 1, deep, across, along, rows, width),
            held(deep, across, along, rows, width),
            held(across - 1, deep, along, rows, cut),
            held(along - 1, deep, across, rows, rest),
            held(deep, along, rows, cut),
            held(deep, across, rows, rest),
            held(along - 1, deep, rows, cut),
            held(across - 1, deep, rows, rest),
            held(deep, rows, width),
            held(deep - 1, rows, width),
            pltpu.VMEM((3,) + small.shape, F32),
            pltpu.VMEM((slots,) + small.shape, F32),
            pltpu.SemaphoreType.DMA((11, most)),
            pltpu.SemaphoreType.DMA((11, most)),
        ],
        compiler_params=pltpu.CompilerParams(
            collective_id=0, has_side_effects=True, vmem_limit_bytes=VMEM_LIMIT
        ),
        name="reduce_tail",
    )(grad.reshape(deep, across, along, cores, rows, width), small)


def local_step(lengths, pos_buckets, box_buckets, layer_input, cotangent, w_mixed, w_down, vectors, up_row, table):
    heads, width = table.shape[1], layer_input.shape[3]
    docs, rows = layer_input.shape[0], layer_input.shape[2]
    bias = bias_rows(lengths, table_entries(table), pos_buckets, box_buckets, heads)
    qkv, tok = project(layer_input, w_mixed, vectors)
    probs, attended = attend(qkv, bias)
    result, d_one, low, active, d_upper, d_ffn, d_branch, d_attended, sums, up_sum = dense(
        layer_input, attended, cotangent, w_mixed, w_down, vectors, up_row
    )

    def flat(item):
        return item.reshape(-1, item.shape[-1])

    d_down = down_grads(flat(active), flat(d_ffn))
    d_branch_up = branch_up_grads(flat(attended), flat(d_branch), flat(low), flat(d_upper))
    d_mixed, bins = attend_back(qkv, probs, d_attended, pos_buckets, box_buckets)
    d_qkv = mixed_grads(flat(tok), flat(d_mixed))
    input_grad, mixed_sum = input_grads(d_mixed, d_one, w_mixed, rows)
    sums = jnp.concatenate(
        [sums[:4], mixed_sum[:, :width], mixed_sum[:, 2 * width :], sums[6:]], axis=0
    )
    return (
        result, input_grad, d_qkv, d_branch_up, d_down, sums, up_sum, bins,
    )


def body(
    layer_input, text_lengths, pos_buckets, box_buckets, w_qkv, w_out, w_up, w_down,
    norm_gains, norm_shifts, proj_biases, up_bias, rel_tables, cotangent,
):
    axes = ("dp", "fsdp")
    width, hidden = layer_input.shape[3], w_up.shape[1]
    own = norm_gains.shape[1]
    table = lax.all_gather(rel_tables, "fsdp", axis=0, tiled=True)
    heads = table.shape[1]
    small = jnp.concatenate(
        [norm_gains.T, norm_shifts.T, proj_biases.T, up_bias.reshape(own, hidden // width)], axis=1
    )
    small = jnp.pad(small, ((0, 0), (0, LANES - small.shape[1])))
    w_mixed = lax.all_gather(
        jnp.concatenate([w_qkv, w_out, w_up, small], axis=1), axes, axis=0, tiled=True
    )
    w_down = lax.all_gather(w_down, axes, axis=0, tiled=True)
    small = w_mixed[:, 4 * width + hidden :].astype(F32)
    vectors = small[:, :8].T
    up_row = small[:, 8 : 8 + hidden // width].reshape(1, hidden)
    result, input_grad, d_qkv, d_branch_up, d_down, sums, up_sum, bins = local_step(
        text_lengths[:, 0], pos_buckets, box_buckets, layer_input, cotangent, w_mixed, w_down,
        vectors, up_row, table,
    )
    d_down = lax.psum_scatter(d_down, axes, scatter_dimension=0, tiled=True).astype(F32)
    d_branch_up = lax.psum_scatter(d_branch_up, axes, scatter_dimension=0, tiled=True).astype(F32)
    packed = jnp.concatenate(
        [sums.reshape(-1, LANES), up_sum.reshape(-1, LANES), bins], axis=0
    )
    d_qkv, packed = reduce_tail(d_qkv, packed, lax.axis_size("dp"), lax.axis_size("fsdp"))
    lines = 8 * width // LANES
    place = lax.axis_index(axes)
    sums = lax.dynamic_slice_in_dim(packed[:lines].reshape(8, width), place * own, own, 1)
    up_sum = packed[lines : lines + hidden // LANES].reshape(hidden)
    up_sum = lax.dynamic_slice_in_dim(up_sum, place * up_bias.shape[0], up_bias.shape[0], 0)
    d_table = table_grad(packed[lines + hidden // LANES :], heads)
    table_rows = rel_tables.shape[0]
    d_table = lax.dynamic_slice_in_dim(d_table, lax.axis_index("fsdp") * table_rows, table_rows, 0)
    return (
        result, input_grad, d_qkv, d_branch_up[:, :width], d_branch_up[:, width:], d_down,
        sums[0:2], sums[2:4], sums[4:8], up_sum, d_table,
    )


def solution(mesh):
    both = ("dp", "fsdp")
    docs = P(None, both, None, None)
    return jax.shard_map(
        body,
        mesh=mesh,
        in_specs=(
            docs, P(None, both), docs, P(None, both, None, None, None),
            P(both, None), P(both, None), P(both, None), P(both, None),
            P(None, both), P(None, both), P(None, both), P(both), P("fsdp", None), docs,
        ),
        out_specs=(
            docs, docs, P(both, None), P(both, None), P(both, None), P(both, None),
            P(None, both), P(None, both), P(None, both), P(both), P("fsdp", None),
        ),
        check_vma=False,
    )
```

```python
from functools import partial

import jax
import jax.numpy as jnp
from jax import lax
from jax.experimental import pallas as pl
from jax.experimental.pallas import tpu as pltpu
from jax.sharding import PartitionSpec as P

HEAD_DIM = 64
POS_BINS = 32
BOX_BINS = 64
TEXT_SLOTS = 512
NEG_FILL = -1000000000.0
NORM_EPS = 1e-05
BLOCK = 256
DENSE_BLOCK = 384
LANES = 128
HALF = 32
SPLIT = 1
LINES = 1
SCALE = 0.125
F32 = jnp.float32
BF16 = jnp.bfloat16
VMEM_LIMIT = 58 << 20


def dot(left, right):
    return jnp.dot(left, right, preferred_element_type=F32)


def dot_nt(left, right):
    return lax.dot_general(left, right, (((1,), (1,)), ((), ())), preferred_element_type=F32)


def params(count):
    return pltpu.CompilerParams(
        dimension_semantics=("arbitrary",) * count, vmem_limit_bytes=VMEM_LIMIT
    )


def resident(shape):
    zeros = (0,) * len(shape)
    return pl.BlockSpec(shape, lambda *_: zeros, pipeline_mode=pl.Buffered(1))


def columns(shape, place):
    return pl.BlockSpec(shape, lambda *_: (0, place), pipeline_mode=pl.Buffered(1))


def live_rows(values, rows, first):
    row = first + lax.broadcasted_iota(jnp.int32, (values.shape[0], 1), 0)
    return jnp.where(row < rows, values, jnp.zeros_like(values))


def bias_kernel(rows, len_ref, tab_ref, pos_ref, box_ref, out_ref):
    heads, chunks = out_ref.shape[1], out_ref.shape[3] // LANES
    block = pl.program_id(1)
    length = len_ref[pl.program_id(0)]
    steps = jnp.minimum(BLOCK, (rows + 7) // 8 * 8 - block * BLOCK) // 8

    def fill(step, carry):
        at = pl.ds(pl.multiple_of(step * 8, 8), 8)
        for chunk in range(chunks):
            cols = slice(chunk * LANES, (chunk + 1) * LANES)
            picks = (
                box_ref[0, 0, 0, at, cols] & (BOX_BINS - 1),
                (box_ref[0, 0, 1, at, cols] & (BOX_BINS - 1)) | BOX_BINS,
                pos_ref[0, 0, at, cols] & (POS_BINS - 1),
            )
            slot = chunk * LANES + lax.broadcasted_iota(jnp.int32, (8, LANES), 1)
            valid = ((slot >= TEXT_SLOTS) & (slot < rows)) | (slot < length)
            totals = [None] * heads
            for which, pick in enumerate(picks):
                for head in range(heads):
                    line = head + (heads if which == 2 else 0)
                    entries = jnp.broadcast_to(tab_ref[line : line + 1, :], (8, LANES))
                    term = jnp.take_along_axis(entries, pick, axis=1)
                    totals[head] = term if which == 0 else totals[head] + term
            for head in range(heads):
                out_ref[0, head, at, cols] = jnp.where(valid, totals[head], NEG_FILL)
        return carry

    def blank(step, carry):
        at = pl.ds(pl.multiple_of(step * 8, 8), 8)
        for head in range(heads):
            out_ref[0, head, at, :] = jnp.zeros((8, chunks * LANES), F32)
        return carry

    lax.fori_loop(0, steps, fill, 0)
    lax.fori_loop(steps, BLOCK // 8, blank, 0)


def bias_rows(lengths, entries, pos_buckets, box_buckets, heads):
    docs, rows = pos_buckets.shape[0], pos_buckets.shape[2]
    padded = pl.cdiv(rows, BLOCK) * BLOCK
    return pl.pallas_call(
        partial(bias_kernel, rows),
        out_shape=jax.ShapeDtypeStruct((docs, heads, padded, padded), F32),
        grid=(docs, padded // BLOCK),
        in_specs=[
            pl.BlockSpec(memory_space=pltpu.SMEM),
            resident(entries.shape),
            pl.BlockSpec((1, 1, BLOCK, padded), lambda d, i: (d, 0, i, 0)),
            pl.BlockSpec((1, 1, 2, BLOCK, padded), lambda d, i: (d, 0, 0, i, 0)),
        ],
        out_specs=pl.BlockSpec((1, heads, BLOCK, padded), lambda d, i: (d, 0, i, 0)),
        compiler_params=params(2),
        cost_estimate=pl.CostEstimate(
            flops=3 * docs * heads * rows * rows,
            transcendentals=0,
            bytes_accessed=docs * padded * padded * (4 * heads + 12),
        ),
        name="bias_rows",
    )(lengths, entries, pos_buckets, box_buckets)


def project_kernel(rows, x_ref, w_ref, vec_ref, out_ref, tok_ref):
    width = x_ref.shape[3]
    block = live_rows(x_ref[0, 0], rows, pl.program_id(1) * x_ref.shape[2])
    tok_ref[0] = block
    queries = dot(block, w_ref[:, :width]) + vec_ref[4:5, :]
    out_ref[0, :, :width] = queries.astype(BF16) * BF16(SCALE)
    out_ref[0, :, width : 2 * width] = dot(block, w_ref[:, width : 2 * width]).astype(BF16)
    values = dot(block, w_ref[:, 2 * width :]) + vec_ref[5:6, :]
    out_ref[0, :, 2 * width :] = values.astype(BF16)


def project(layer_input, w_mixed, vectors):
    docs, unused, rows, width = layer_input.shape
    padded = pl.cdiv(rows, BLOCK) * BLOCK
    return pl.pallas_call(
        partial(project_kernel, rows),
        out_shape=(
            jax.ShapeDtypeStruct((docs, padded, 3 * width), BF16),
            jax.ShapeDtypeStruct((docs, padded, width), BF16),
        ),
        grid=(docs, padded // DENSE_BLOCK),
        in_specs=[
            pl.BlockSpec((1, 1, DENSE_BLOCK, width), lambda d, i: (d, 0, i, 0)),
            columns((width, 3 * width), 0),
            resident(vectors.shape),
        ],
        out_specs=(
            pl.BlockSpec((1, DENSE_BLOCK, 3 * width), lambda d, i: (d, i, 0)),
            pl.BlockSpec((1, DENSE_BLOCK, width), lambda d, i: (d, i, 0)),
        ),
        compiler_params=params(2),
        name="project",
    )(layer_input, w_mixed, vectors)


def attend_kernel(q_ref, k_ref, v_ref, bias_ref, probs_ref, out_ref):
    lane = lax.broadcasted_iota(jnp.int32, (1, LANES), 1)
    for pair in range(q_ref.shape[2] // LANES):
        cols = slice(pair * LANES, (pair + 1) * LANES)
        queries, key_rows, values = q_ref[0, :, cols], k_ref[0, :, cols], v_ref[0, :, cols]
        total = None
        for half in range(2):
            head = 2 * pair + half
            keep = (lane < HEAD_DIM) if half == 0 else (lane >= HEAD_DIM)
            scores = dot_nt(jnp.where(keep, queries, BF16(0)), key_rows) + bias_ref[0, head]
            top = jnp.max(scores, axis=-1, keepdims=True)
            powers = jnp.exp(scores - top)
            share = 1.0 / jnp.sum(powers, axis=-1, keepdims=True)
            probs = (powers * share).astype(BF16)
            probs_ref[0, head] = probs
            part = dot(probs, jnp.where(keep, values, BF16(0)))
            total = part if half == 0 else total + part
        out_ref[0, :, cols] = total.astype(BF16)


def attend(qkv, bias):
    docs, padded, width = qkv.shape[0], qkv.shape[1], qkv.shape[2] // 3
    heads = bias.shape[1]
    return pl.pallas_call(
        attend_kernel,
        out_shape=(
            jax.ShapeDtypeStruct((docs, heads, padded, padded), BF16),
            jax.ShapeDtypeStruct((docs, padded, width), BF16),
        ),
        grid=(docs, padded // BLOCK),
        in_specs=[
            pl.BlockSpec((1, BLOCK, width), lambda d, i: (d, i, 0)),
            pl.BlockSpec((1, padded, width), lambda d, i: (d, 0, 1)),
            pl.BlockSpec((1, padded, width), lambda d, i: (d, 0, 2)),
            pl.BlockSpec((1, heads, BLOCK, padded), lambda d, i: (d, 0, i, 0)),
        ],
        out_specs=(
            pl.BlockSpec((1, heads, BLOCK, padded), lambda d, i: (d, 0, i, 0)),
            pl.BlockSpec((1, BLOCK, width), lambda d, i: (d, i, 0)),
        ),
        compiler_params=params(2),
        name="attend",
    )(qkv, qkv, qkv, bias)


def norm(rows_in):
    centre = rows_in - jnp.mean(rows_in, axis=-1, keepdims=True)
    inv_std = lax.rsqrt(jnp.mean(centre * centre, axis=-1, keepdims=True) + NORM_EPS)
    return centre * inv_std, inv_std


def norm_back(grad_in, normed, inv_std, gain_row):
    scaled = grad_in * gain_row
    return inv_std * (
        scaled
        - jnp.mean(scaled, axis=-1, keepdims=True)
        - normed * jnp.mean(scaled * normed, axis=-1, keepdims=True)
    )


def dense_kernel(
    rows, x_ref, o_ref, cot_ref, wo_ref, wu_ref, wd_ref, vec_ref, upb_ref,
    y_ref, dr_ref, h_ref, g_ref, du_ref, df_ref, db_ref, do_ref, sums_ref, upsum_ref,
    slope_ref,
):
    width, hidden = wu_ref.shape
    first = pl.program_id(1) * x_ref.shape[2]
    vec = vec_ref[...]

    @pl.when((pl.program_id(0) == 0) & (pl.program_id(1) == 0))
    def _():
        sums_ref[...] = jnp.zeros_like(sums_ref)
        upsum_ref[...] = jnp.zeros_like(upsum_ref)

    tok = live_rows(x_ref[0, 0], rows, first).astype(F32)
    normed_one, inv_one = norm(tok + dot(o_ref[0], wo_ref[...]) + vec[6:7])
    state = normed_one * vec[0:1] + vec[2:3]
    low = state.astype(BF16)
    h_ref[0] = low
    second = state + vec[7:8]
    for part in range(hidden // width):
        cols = slice(part * width, (part + 1) * width)
        upper = dot(low, wu_ref[:, cols]) + upb_ref[:, cols]
        cdf = 0.5 * (1.0 + lax.erf(upper * (0.5**0.5)))
        slope_ref[:, cols] = cdf + upper * (jnp.exp(-0.5 * upper * upper) * 0.3989422804014327)
        active = (upper * cdf).astype(BF16)
        g_ref[0, :, cols] = active
        second = second + dot(active, wd_ref[cols, :])
    normed_two, inv_two = norm(second)
    y_ref[0, 0] = (normed_two * vec[1:2] + vec[3:4]).astype(BF16)
    grad = live_rows(cot_ref[0, 0], rows, first).astype(F32)
    sums_ref[1:2, :] += jnp.sum(grad * normed_two, axis=0, keepdims=True)
    sums_ref[3:4, :] += jnp.sum(grad, axis=0, keepdims=True)
    d_two = norm_back(grad, normed_two, inv_two, vec[1:2])
    d_ffn = d_two.astype(BF16)
    df_ref[0] = d_ffn
    sums_ref[7:8, :] += jnp.sum(d_ffn.astype(F32), axis=0, keepdims=True)
    back = d_two
    for part in range(hidden // width):
        cols = slice(part * width, (part + 1) * width)
        d_upper = (dot_nt(d_ffn, wd_ref[cols, :]) * slope_ref[:, cols]).astype(BF16)
        du_ref[0, :, cols] = d_upper
        upsum_ref[:, cols] += jnp.sum(d_upper.astype(F32), axis=0, keepdims=True)
        back = back + dot_nt(d_upper, wu_ref[:, cols])
    sums_ref[0:1, :] += jnp.sum(back * normed_one, axis=0, keepdims=True)
    sums_ref[2:3, :] += jnp.sum(back, axis=0, keepdims=True)
    d_one = norm_back(back, normed_one, inv_one, vec[0:1])
    dr_ref[0] = d_one
    d_branch = d_one.astype(BF16)
    db_ref[0] = d_branch
    sums_ref[6:7, :] += jnp.sum(d_branch.astype(F32), axis=0, keepdims=True)
    do_ref[0] = dot_nt(d_branch, wo_ref[...]).astype(BF16)


def dense(layer_input, attended, cotangent, w_mixed, w_down, vectors, up_row):
    docs, unused, rows, width = layer_input.shape
    padded, hidden = attended.shape[1], w_down.shape[0]
    ragged = pl.BlockSpec((1, 1, DENSE_BLOCK, width), lambda d, i: (d, 0, i, 0))
    narrow = pl.BlockSpec((1, DENSE_BLOCK, width), lambda d, i: (d, i, 0))
    wide = pl.BlockSpec((1, DENSE_BLOCK, hidden), lambda d, i: (d, i, 0))

    def rows_of(columns, dtype):
        return jax.ShapeDtypeStruct((docs, padded, columns), dtype)

    return pl.pallas_call(
        partial(dense_kernel, rows),
        out_shape=(
            jax.ShapeDtypeStruct(layer_input.shape, BF16),
            rows_of(width, F32),
            rows_of(width, BF16),
            rows_of(hidden, BF16),
            rows_of(hidden, BF16),
            rows_of(width, BF16),
            rows_of(width, BF16),
            rows_of(width, BF16),
            jax.ShapeDtypeStruct((8, width), F32),
            jax.ShapeDtypeStruct((1, hidden), F32),
        ),
        grid=(docs, padded // DENSE_BLOCK),
        in_specs=[
            ragged, narrow, ragged,
            columns((width, width), 3), columns((width, hidden), 4 * width // hidden),
            resident(w_down.shape),
            resident(vectors.shape), resident(up_row.shape),
        ],
        out_specs=(
            ragged, narrow, narrow, wide, wide, narrow, narrow, narrow,
            pl.BlockSpec((8, width), lambda d, i: (0, 0)),
            pl.BlockSpec((1, hidden), lambda d, i: (0, 0)),
        ),
        scratch_shapes=[pltpu.VMEM((DENSE_BLOCK, hidden), F32)],
        compiler_params=params(2),
        name="dense",
    )(layer_input, attended, cotangent, w_mixed, w_mixed, w_down, vectors, up_row)


def attend_back_kernel(
    rows, q_ref, k_ref, v_ref, probs_ref, do_ref, pos_ref, box_ref, dm_ref, bins_ref,
    dk_ref, dv_ref, ds_ref, acc_ref, picks_ref,
):
    block, width = pl.program_id(1), q_ref.shape[2]
    padded = k_ref.shape[1]
    lane = lax.broadcasted_iota(jnp.int32, (1, LANES), 1)

    @pl.when((pl.program_id(0) == 0) & (block == 0))
    def _():
        acc_ref[...] = jnp.zeros_like(acc_ref)
        ds_ref[...] = jnp.zeros_like(ds_ref)

    @pl.when(block == 0)
    def _():
        dk_ref[...] = jnp.zeros_like(dk_ref)
        dv_ref[...] = jnp.zeros_like(dv_ref)

    own = pl.ds(pl.multiple_of(block * BLOCK, BLOCK), BLOCK)
    for pair in range(width // LANES):
        cols = slice(pair * LANES, (pair + 1) * LANES)
        queries, key_rows, values = q_ref[0, :, cols], k_ref[0, :, cols], v_ref[0, :, cols]
        grads = do_ref[0, :, cols]
        turned_q, turned_g = queries.T, grads.T
        total = None
        for half in range(2):
            head = 2 * pair + half
            keep = (lane < HEAD_DIM) if half == 0 else (lane >= HEAD_DIM)
            part = slice(half * HEAD_DIM, (half + 1) * HEAD_DIM)
            lines = slice(head * HEAD_DIM, (head + 1) * HEAD_DIM)
            low = probs_ref[0, head]
            probs = low.astype(F32)
            dprobs = dot_nt(jnp.where(keep, grads, BF16(0)), values)
            delta = jnp.sum(probs * dprobs, axis=-1, keepdims=True)
            dscore = probs * (dprobs - delta)
            for chunk in range(padded // LANES):
                ds_ref[chunk, pl.ds(head, BLOCK, stride=16), :] = dscore[
                    :, chunk * LANES : (chunk + 1) * LANES
                ]
            dlow = dscore.astype(BF16)
            piece = dot(dlow, jnp.where(keep, key_rows, BF16(0)))
            total = piece if half == 0 else total + piece
            dk_ref[lines, :] += dot(turned_q[part, :], dlow)
            dv_ref[lines, :] += dot(turned_g[part, :], low)
        dm_ref[0, own, cols] = (total * SCALE).astype(BF16)

    group = 32
    low_bins = lax.broadcasted_iota(jnp.int32, (HALF, LANES), 0).astype(BF16)

    def hits(picks, bins):
        low = picks.astype(BF16)
        return jnp.concatenate(
            [
                jnp.where(low_bins[first : first + 16] == low, BF16(1), BF16(0))
                for first in range(0, bins, 16)
            ],
            axis=0,
        )

    for place, (picks, bits) in enumerate(
        (
            (box_ref[0, 0, 0], BOX_BINS),
            (box_ref[0, 0, 1], BOX_BINS),
            (pos_ref[0, 0], POS_BINS),
        )
    ):
        half = bits // 2
        for chunk in range(padded // LANES):
            part = picks[:, chunk * LANES : (chunk + 1) * LANES] & (bits - 1)
            picks_ref[2 * place, chunk] = (part & (half - 1)).astype(F32)
            picks_ref[2 * place + 1, chunk] = (part >> (half.bit_length() - 1)).astype(F32)

    def count(step, carry):
        total = None
        for line in range(0, group, LINES):
            left, right = [], []
            for own in range(LINES):
                row = step * group + line + own
                here = pl.ds(pl.multiple_of(row * 16, 16), 16)
                again = pl.ds(row, 16, stride=0)
                for chunk in range(padded // LANES):
                    base = ds_ref[chunk, here, :]
                    left.append(
                        jnp.concatenate(
                            [base.astype(BF16)]
                            + [
                                (base * picks_ref[2 * place + 1, chunk, again, :]).astype(BF16)
                                for place in range(3)
                            ],
                            axis=0,
                        )
                    )
                    right.append(
                        jnp.concatenate(
                            [
                                hits(picks_ref[2 * place, chunk, again, :], bins)
                                for place, bins in enumerate((HALF, HALF, HALF // 2))
                            ],
                            axis=0,
                        )
                    )
            part = dot_nt(jnp.concatenate(left, axis=1), jnp.concatenate(right, axis=1))
            total = part if total is None else total + part
        acc_ref[0, :, : total.shape[1]] += total
        return carry

    live = jnp.minimum(BLOCK, (rows + group - 1) // group * group - block * BLOCK)
    lax.fori_loop(0, live // group, count, 0)

    @pl.when(block == pl.num_programs(1) - 1)
    def _():
        dm_ref[0, :, width : 2 * width] = dk_ref[...].astype(BF16).T
        dm_ref[0, :, 2 * width :] = dv_ref[...].astype(BF16).T
        bins_ref[...] = jnp.sum(acc_ref[...], axis=0)


def attend_back(qkv, probs, d_attended, pos_buckets, box_buckets):
    docs, padded, width = qkv.shape[0], qkv.shape[1], qkv.shape[2] // 3
    heads, rows = probs.shape[1], pos_buckets.shape[2]
    return pl.pallas_call(
        partial(attend_back_kernel, rows),
        out_shape=(
            jax.ShapeDtypeStruct((docs, padded, 3 * width), BF16),
            jax.ShapeDtypeStruct((64, LANES), F32),
        ),
        grid=(docs, padded // BLOCK),
        in_specs=[
            pl.BlockSpec((1, BLOCK, width), lambda d, i: (d, i, 0)),
            pl.BlockSpec((1, padded, width), lambda d, i: (d, 0, 1)),
            pl.BlockSpec((1, padded, width), lambda d, i: (d, 0, 2)),
            pl.BlockSpec((1, heads, BLOCK, padded), lambda d, i: (d, 0, i, 0)),
            pl.BlockSpec((1, BLOCK, width), lambda d, i: (d, i, 0)),
            pl.BlockSpec((1, 1, BLOCK, padded), lambda d, i: (d, 0, i, 0)),
            pl.BlockSpec((1, 1, 2, BLOCK, padded), lambda d, i: (d, 0, 0, i, 0)),
        ],
        out_specs=(
            pl.BlockSpec((1, padded, 3 * width), lambda d, i: (d, 0, 0)),
            pl.BlockSpec((64, LANES), lambda d, i: (0, 0)),
        ),
        scratch_shapes=[
            pltpu.VMEM((width, padded), F32),
            pltpu.VMEM((width, padded), F32),
            pltpu.VMEM((padded // LANES, BLOCK * 16, LANES), F32),
            pltpu.VMEM((SPLIT, 64, LANES), F32),
            pltpu.VMEM((6, padded // LANES, BLOCK, LANES), F32),
        ],
        compiler_params=params(2),
        name="attend_back",
    )(qkv, qkv, qkv, probs, d_attended, pos_buckets, box_buckets)


def table_entries(table):
    heads = table.shape[1]
    lines = table.astype(F32).T * SCALE
    boxes = lines[:, POS_BINS:]
    spots = jnp.pad(lines[:, :POS_BINS], ((0, 0), (0, LANES - POS_BINS)))
    return jnp.concatenate([boxes, spots], axis=0).reshape(2 * heads, LANES)


def table_grad(bins, heads):
    base, upper = bins[:heads], (bins[16 : 16 + heads], bins[32 : 32 + heads], bins[48 : 48 + heads])
    pieces = []
    for which, (first, size) in enumerate(((0, HALF), (HALF, HALF), (2 * HALF, HALF // 2))):
        high = upper[which][:, first : first + size]
        pieces.append(jnp.concatenate([base[:, first : first + size] - high, high], axis=1))
    return jnp.concatenate([pieces[2], pieces[0], pieces[1]], axis=1).T * SCALE


def branch_up_grads(attended, d_branch, low, d_upper):
    rows, width = attended.shape
    parts = 1 + d_upper.shape[1] // width

    def kernel(a_ref, b_ref, l_ref, u_ref, out_ref, turned_ref):
        part = pl.program_id(0)

        @pl.when(part == 0)
        def _():
            out_ref[...] = dot(a_ref[...].T, b_ref[...]).astype(BF16)
            turned_ref[...] = l_ref[...].T

        @pl.when(part > 0)
        def _():
            out_ref[...] = dot(turned_ref[...], u_ref[...]).astype(BF16)

    return pl.pallas_call(
        kernel,
        out_shape=jax.ShapeDtypeStruct((width, parts * width), BF16),
        grid=(parts,),
        in_specs=[
            resident((rows, width)),
            resident((rows, width)),
            resident((rows, width)),
            pl.BlockSpec((rows, width), lambda p: (0, jnp.maximum(p - 1, 0))),
        ],
        out_specs=pl.BlockSpec((width, width), lambda p: (0, p)),
        scratch_shapes=[pltpu.VMEM((width, rows), BF16)],
        compiler_params=params(1),
        cost_estimate=pl.CostEstimate(
            flops=2 * rows * width * width * parts, transcendentals=0,
            bytes_accessed=2 * rows * width * (parts + 3),
        ),
        name="branch_up_grads",
    )(attended, d_branch, low, d_upper)


def down_grads(active, d_ffn):
    rows, width = d_ffn.shape
    parts = active.shape[1] // width

    def kernel(g_ref, f_ref, out_ref):
        out_ref[...] = dot(g_ref[...].T, f_ref[...]).astype(BF16)

    return pl.pallas_call(
        kernel,
        out_shape=jax.ShapeDtypeStruct((parts * width, width), BF16),
        grid=(parts,),
        in_specs=[pl.BlockSpec((rows, width), lambda p: (0, p)), resident((rows, width))],
        out_specs=pl.BlockSpec((width, width), lambda p: (p, 0)),
        compiler_params=params(1),
        cost_estimate=pl.CostEstimate(
            flops=2 * rows * width * width * parts, transcendentals=0,
            bytes_accessed=2 * rows * width * (parts + 2),
        ),
        name="down_grads",
    )(active, d_ffn)


ORDERS = ((3, 1, 2, 0), (3, 2, 1, 0), (3, 1, 2, 0))
MESH = pl.DeviceIdType.MESH


def remaining(part, level):
    return [axis for axis in range(4) if axis not in ORDERS[part][:level]]


def tail_kernel(
    dims, w_ref, tok_ref, mixed_ref, one_ref, small_ref, grad_ref, sums_ref, input_ref, *scratch
):
    parts, width = len(ORDERS), tok_ref.shape[1]
    holders = [scratch[8 * part : 8 * part + 4] for part in range(parts)]
    inboxes = [scratch[8 * part + 4 : 8 * part + 8] for part in range(parts)]
    (
        tok, turned, mixed, weights, kept, stage, own_sums, got_sums,
        send_sems, recv_sems, load_sems, keep_sems, store_sems,
    ) = scratch[8 * parts :]
    deep, across, along, cores = dims
    dp, fsdp = lax.axis_index("dp"), lax.axis_index("fsdp")
    mine = (dp // across, dp % across, fsdp // cores, fsdp % cores)
    docs, padded = one_ref.shape[0], one_ref.shape[1]
    rows, block = input_ref.shape[1], kept.shape[1]
    own_lines = small_ref.shape[0]

    def peer(axis, step):
        place = list(mine)
        place[axis] = (place[axis] + step) % dims[axis]
        return place[axis], (place[0] * across + place[1], place[2] * cores + place[3])

    loads = [pltpu.make_async_copy(tok_ref, tok, load_sems.at[0])]
    for part in range(parts):
        loads.append(
            pltpu.make_async_copy(
                mixed_ref.at[:, pl.ds(part * width, width)], mixed.at[part], load_sems.at[1 + part]
            )
        )
    loads.append(
        pltpu.make_async_copy(
            w_ref.at[:, pl.ds(0, parts * width)], weights, load_sems.at[1 + parts]
        )
    )
    for load in loads:
        load.start()

    barrier = pltpu.get_barrier_semaphore()
    partners = 0
    for axis in range(4):
        for step in range(1, dims[axis]):
            pl.semaphore_signal(barrier, inc=1, device_id=peer(axis, step)[1], device_id_type=MESH)
            partners += 1
    pl.semaphore_wait(barrier, partners)

    flying = {}

    def launch(lane, axis, source, target):
        copies = []
        for step in range(1, dims[axis]):
            place, device = peer(axis, step)
            copies.append(
                pltpu.make_async_remote_copy(
                    src_ref=source(place),
                    dst_ref=target(step - 1),
                    send_sem=send_sems.at[lane, step - 1],
                    recv_sem=recv_sems.at[lane, step - 1],
                    device_id=device,
                    device_id_type=MESH,
                )
            )
        for copy in copies:
            copy.start()
        flying[lane] = copies

    def land(lane):
        for copy in flying.pop(lane):
            copy.wait()

    def joined(own, others):
        total = own.astype(F32)
        for other in others:
            total = total + other.astype(F32)
        return total

    def send(part, level):
        axis, axes = ORDERS[part][level], remaining(part, level)

        def source(place):
            return holders[part][level].at[
                tuple(place if item == axis else slice(None) for item in axes)
            ]

        launch(4 * part + level, axis, source, lambda slot: inboxes[part][level].at[slot])

    def join(part, level):
        land(4 * part + level)
        axis, axes = ORDERS[part][level], remaining(part, level)
        source, box = holders[part][level], inboxes[part][level]
        left = [item for item in axes if item != axis]
        count = dims[axis] - 1
        if not left:
            grad_ref[:, part * width : (part + 1) * width] = joined(
                source[mine[axis]], [box[slot] for slot in range(count)]
            )
            return
        spots = [()]
        for item in left[1:]:
            spots = [spot + (place,) for spot in spots for place in range(dims[item])]

        def add(k, carry):
            for spot in spots:
                there = (k,) + spot
                where = dict(zip(left, there))
                where[axis] = mine[axis]
                own = tuple(where[item] for item in axes)
                holders[part][level + 1][there] = joined(
                    source[own], [box[(slot,) + there] for slot in range(count)]
                ).astype(BF16)
            return carry

        lax.fori_loop(0, dims[left[0]], add, 0)
        send(part, level + 1)

    small_order = (3, 1, 2, 0)

    def small_send(level):
        axis = small_order[level]
        first = sum(dims[item] - 1 for item in small_order[:level])
        launch(
            4 * parts + level, axis,
            lambda place: own_sums.at[level], lambda slot: got_sums.at[first + slot],
        )

    def small_join(level):
        land(4 * parts + level)
        axis = small_order[level]
        first = sum(dims[item] - 1 for item in small_order[:level])
        total = joined(
            own_sums[level], [got_sums[first + slot] for slot in range(dims[axis] - 1)]
        )
        if level == 3:
            sums_ref[...] = total
        else:
            own_sums[level + 1] = total
            small_send(level + 1)

    spans = [(doc, first) for doc in range(docs) for first in range(0, padded, block)]

    def keep(step):
        doc, first = spans[step]
        return pltpu.make_async_copy(
            one_ref.at[doc, pl.ds(first, block), :], kept.at[step % 2], keep_sems.at[step % 2]
        )

    def store(step):
        doc, first = spans[step]
        count = min(block, rows - first)
        return pltpu.make_async_copy(
            stage.at[step % 2, pl.ds(0, count)],
            input_ref.at[doc, pl.ds(first, count)],
            store_sems.at[step % 2],
        )

    def input_step(step):
        doc, first = spans[step]
        if step == 0:
            loads[1 + parts].wait()
            keep(0).start()
        if step + 1 < len(spans):
            keep(step + 1).start()
        keep(step).wait()
        if step >= 2:
            store(step - 2).wait()
        at = pl.ds(doc * padded + first, block)
        total = kept[step % 2]
        for part in range(parts):
            total = total + dot_nt(
                mixed[part, at, :], weights[:, part * width : (part + 1) * width]
            )
        stage[step % 2, :, 0, :] = total
        store(step).start()

    loads[0].wait()
    turned[...] = tok[...].T
    ones = jnp.ones((16, tok.shape[0]), BF16)
    own_sums[0, 0:own_lines] = small_ref[...]

    def multiply(part):
        loads[1 + part].wait()
        rest = holders[part][0].shape
        block_rows = dot(turned[...], mixed[part]).astype(BF16)
        holders[part][0][...] = block_rows.reshape(rest)
        line = dot(ones, mixed[part])[0:8]
        share = 8 * width // LANES // 8
        for chunk in range(share):
            own_sums[0, pl.ds(own_lines + (part * share + chunk) * 8, 8)] = line[
                :, chunk * LANES : (chunk + 1) * LANES
            ]
        send(part, 0)

    multiply(0)
    multiply(1)
    multiply(2)
    small_send(0)
    join(0, 0)
    input_step(0)
    join(1, 0)
    join(0, 1)
    small_join(0)
    join(2, 0)
    join(1, 1)
    input_step(1)
    join(0, 2)
    small_join(1)
    join(2, 1)
    join(1, 2)
    input_step(2)
    small_join(2)
    join(2, 2)
    input_step(3)
    join(0, 3)
    join(1, 3)
    join(2, 3)
    small_join(3)
    for step in range(max(len(spans) - 2, 0), len(spans)):
        store(step).wait()


def split_mesh(dp, fsdp):
    across = 1 << ((dp.bit_length() - 1) // 2)
    across = across if dp % across == 0 else 1
    cores = 2 if fsdp % 2 == 0 else 1
    return dp // across, across, fsdp // cores, cores


def tail(w_mixed, tok, d_mixed, d_one, small, rows, dims):
    docs, padded, width = d_one.shape
    parts = len(ORDERS)
    devices = dims[0] * dims[1] * dims[2] * dims[3]
    own = width // devices
    lines = small.shape[0] + parts * 8 * width // LANES
    any_space = pl.BlockSpec(memory_space=pl.ANY)
    vmem = pl.BlockSpec(memory_space=pltpu.VMEM)
    scratch = []
    for part in range(parts):
        boxes = []
        for level in range(4):
            axes = remaining(part, level)
            axis = ORDERS[part][level]
            scratch.append(pltpu.VMEM(tuple(dims[item] for item in axes) + (own, width), BF16))
            boxes.append(
                pltpu.VMEM(
                    (max(dims[axis] - 1, 1),)
                    + tuple(dims[item] for item in axes if item != axis)
                    + (own, width),
                    BF16,
                )
            )
        scratch += boxes
    most = max(max(dims) - 1, 1)
    flat = docs * padded
    scratch += [
        pltpu.VMEM((flat, width), BF16),
        pltpu.VMEM((width, flat), BF16),
        pltpu.VMEM((parts, flat, width), BF16),
        pltpu.VMEM((width, parts * width), BF16),
        pltpu.VMEM((2, DENSE_BLOCK, width), F32),
        pltpu.VMEM((2, DENSE_BLOCK, 1, width), F32),
        pltpu.VMEM((4, lines, LANES), F32),
        pltpu.VMEM((sum(dims) - 4, lines, LANES), F32),
        pltpu.SemaphoreType.DMA((4 * parts + 4, most)),
        pltpu.SemaphoreType.DMA((4 * parts + 4, most)),
        pltpu.SemaphoreType.DMA((parts + 2,)),
        pltpu.SemaphoreType.DMA((2,)),
        pltpu.SemaphoreType.DMA((2,)),
    ]
    return pl.pallas_call(
        partial(tail_kernel, dims),
        out_shape=(
            jax.ShapeDtypeStruct((own, parts * width), F32),
            jax.ShapeDtypeStruct((lines, LANES), F32),
            jax.ShapeDtypeStruct((docs, rows, 1, width), F32),
        ),
        in_specs=[any_space, any_space, any_space, any_space, vmem],
        out_specs=(vmem, vmem, any_space),
        scratch_shapes=scratch,
        compiler_params=pltpu.CompilerParams(
            collective_id=0, has_side_effects=True, vmem_limit_bytes=VMEM_LIMIT
        ),
        name="tail",
    )(w_mixed, tok, d_mixed, d_one, small)


def small_results(packed, width, hidden, heads):
    lines, more = 8 * width // LANES, hidden // LANES
    sums = packed[:lines].reshape(8, width)
    up_sum = packed[lines : lines + more].reshape(hidden)
    d_table = table_grad(packed[lines + more : lines + more + 64], heads)
    mixed = packed[lines + more + 64 :].reshape(3, width // LANES, 8, LANES)[:, :, 0]
    mixed = mixed.reshape(3, width)
    d_biases = jnp.concatenate([mixed[0:1], mixed[2:3], sums[6:8]], axis=0)
    return sums[0:2], sums[2:4], d_biases, up_sum, d_table


def local_step(lengths, pos_buckets, box_buckets, layer_input, cotangent, w_mixed, w_down, vectors, up_row, table):
    heads, width = table.shape[1], layer_input.shape[3]
    docs, rows = layer_input.shape[0], layer_input.shape[2]
    bias = bias_rows(lengths, table_entries(table), pos_buckets, box_buckets, heads)
    qkv, tok = project(layer_input, w_mixed, vectors)
    probs, attended = attend(qkv, bias)
    result, d_one, low, active, d_upper, d_ffn, d_branch, d_attended, sums, up_sum = dense(
        layer_input, attended, cotangent, w_mixed, w_down, vectors, up_row
    )

    def flat(item):
        return item.reshape(-1, item.shape[-1])

    d_down = down_grads(flat(active), flat(d_ffn))
    d_branch_up = branch_up_grads(flat(attended), flat(d_branch), flat(low), flat(d_upper))
    d_mixed, bins = attend_back(qkv, probs, d_attended, pos_buckets, box_buckets)
    packed = jnp.concatenate(
        [sums.reshape(-1, LANES), up_sum.reshape(-1, LANES), bins], axis=0
    )
    return result, d_branch_up, d_down, (w_mixed, flat(tok), flat(d_mixed), d_one, packed, rows)


def body(
    layer_input, text_lengths, pos_buckets, box_buckets, w_qkv, w_out, w_up, w_down,
    norm_gains, norm_shifts, proj_biases, up_bias, rel_tables, cotangent,
):
    axes = ("dp", "fsdp")
    width, hidden = layer_input.shape[3], w_up.shape[1]
    own = norm_gains.shape[1]
    table = lax.all_gather(rel_tables, "fsdp", axis=0, tiled=True)
    heads = table.shape[1]
    small = jnp.concatenate(
        [norm_gains.T, norm_shifts.T, proj_biases.T, up_bias.reshape(own, hidden // width)], axis=1
    )
    small = jnp.pad(small, ((0, 0), (0, LANES - small.shape[1])))
    w_mixed = lax.all_gather(
        jnp.concatenate([w_qkv, w_out, w_up, small], axis=1), axes, axis=0, tiled=True
    )
    w_down = lax.all_gather(w_down, axes, axis=0, tiled=True)
    small = w_mixed[:, 4 * width + hidden :].astype(F32)
    vectors = small[:, :8].T
    up_row = small[:, 8 : 8 + hidden // width].reshape(1, hidden)
    result, d_branch_up, d_down, rest = local_step(
        text_lengths[:, 0], pos_buckets, box_buckets, layer_input, cotangent, w_mixed, w_down,
        vectors, up_row, table,
    )
    d_down = lax.psum_scatter(d_down, axes, scatter_dimension=0, tiled=True).astype(F32)
    d_branch_up = lax.psum_scatter(d_branch_up, axes, scatter_dimension=0, tiled=True).astype(F32)
    d_qkv, packed, input_grad = tail(
        *rest, split_mesh(lax.axis_size("dp"), lax.axis_size("fsdp"))
    )
    d_gains, d_shifts, d_biases, up_sum, d_table = small_results(packed, width, hidden, heads)
    place = lax.axis_index(axes)
    d_gains, d_shifts, d_biases = (
        lax.dynamic_slice_in_dim(item, place * own, own, 1)
        for item in (d_gains, d_shifts, d_biases)
    )
    up_sum = lax.dynamic_slice_in_dim(up_sum, place * up_bias.shape[0], up_bias.shape[0], 0)
    table_rows = rel_tables.shape[0]
    d_table = lax.dynamic_slice_in_dim(d_table, lax.axis_index("fsdp") * table_rows, table_rows, 0)
    return (
        result, jnp.transpose(input_grad, (0, 2, 1, 3)), d_qkv, d_branch_up[:, :width], d_branch_up[:, width:], d_down,
        d_gains, d_shifts, d_biases, up_sum, d_table,
    )


def solution(mesh):
    both = ("dp", "fsdp")
    docs = P(None, both, None, None)
    return jax.shard_map(
        body,
        mesh=mesh,
        in_specs=(
            docs, P(None, both), docs, P(None, both, None, None, None),
            P(both, None), P(both, None), P(both, None), P(both, None),
            P(None, both), P(None, both), P(None, both), P(both), P("fsdp", None), docs,
        ),
        out_specs=(
            docs, docs, P(both, None), P(both, None), P(both, None), P(both, None),
            P(None, both), P(None, both), P(None, both), P(both), P("fsdp", None),
        ),
        check_vma=False,
    )
```

```python
from functools import partial

import jax
import jax.numpy as jnp
from jax import lax
from jax.experimental import pallas as pl
from jax.experimental.pallas import tpu as pltpu
from jax.sharding import PartitionSpec as P

HEAD_DIM = 64
POS_BINS = 32
BOX_BINS = 64
TEXT_SLOTS = 512
NEG_FILL = -1000000000.0
NORM_EPS = 1e-05
BLOCK = 256
DENSE_BLOCK = 384
LANES = 128
HALF = 32
SPLIT = 1
LINES = 1
SCALE = 0.125
F32 = jnp.float32
BF16 = jnp.bfloat16
VMEM_LIMIT = 58 << 20


def dot(left, right):
    return jnp.dot(left, right, preferred_element_type=F32)


def dot_nt(left, right):
    return lax.dot_general(left, right, (((1,), (1,)), ((), ())), preferred_element_type=F32)


def params(count):
    return pltpu.CompilerParams(
        dimension_semantics=("arbitrary",) * count, vmem_limit_bytes=VMEM_LIMIT
    )


def resident(shape):
    zeros = (0,) * len(shape)
    return pl.BlockSpec(shape, lambda *_: zeros, pipeline_mode=pl.Buffered(1))


def columns(shape, place):
    return pl.BlockSpec(shape, lambda *_: (0, place), pipeline_mode=pl.Buffered(1))


def live_rows(values, rows, first):
    row = first + lax.broadcasted_iota(jnp.int32, (values.shape[0], 1), 0)
    return jnp.where(row < rows, values, jnp.zeros_like(values))


def bias_kernel(rows, len_ref, tab_ref, pos_ref, box_ref, out_ref):
    heads, chunks = out_ref.shape[1], out_ref.shape[3] // LANES
    block = pl.program_id(1)
    length = len_ref[pl.program_id(0)]
    steps = jnp.minimum(BLOCK, (rows + 7) // 8 * 8 - block * BLOCK) // 8

    def fill(step, carry):
        at = pl.ds(pl.multiple_of(step * 8, 8), 8)
        for chunk in range(chunks):
            cols = slice(chunk * LANES, (chunk + 1) * LANES)
            picks = (
                box_ref[0, 0, 0, at, cols] & (BOX_BINS - 1),
                (box_ref[0, 0, 1, at, cols] & (BOX_BINS - 1)) | BOX_BINS,
                pos_ref[0, 0, at, cols] & (POS_BINS - 1),
            )
            slot = chunk * LANES + lax.broadcasted_iota(jnp.int32, (8, LANES), 1)
            valid = ((slot >= TEXT_SLOTS) & (slot < rows)) | (slot < length)
            totals = [None] * heads
            for which, pick in enumerate(picks):
                for head in range(heads):
                    line = head + (heads if which == 2 else 0)
                    entries = jnp.broadcast_to(tab_ref[line : line + 1, :], (8, LANES))
                    term = jnp.take_along_axis(entries, pick, axis=1)
                    totals[head] = term if which == 0 else totals[head] + term
            for head in range(heads):
                out_ref[0, head, at, cols] = jnp.where(valid, totals[head], NEG_FILL)
        return carry

    def blank(step, carry):
        at = pl.ds(pl.multiple_of(step * 8, 8), 8)
        for head in range(heads):
            out_ref[0, head, at, :] = jnp.zeros((8, chunks * LANES), F32)
        return carry

    lax.fori_loop(0, steps, fill, 0)
    lax.fori_loop(steps, BLOCK // 8, blank, 0)


def bias_rows(lengths, entries, pos_buckets, box_buckets, heads):
    docs, rows = pos_buckets.shape[0], pos_buckets.shape[2]
    padded = pl.cdiv(rows, BLOCK) * BLOCK
    return pl.pallas_call(
        partial(bias_kernel, rows),
        out_shape=jax.ShapeDtypeStruct((docs, heads, padded, padded), F32),
        grid=(docs, padded // BLOCK),
        in_specs=[
            pl.BlockSpec(memory_space=pltpu.SMEM),
            resident(entries.shape),
            pl.BlockSpec((1, 1, BLOCK, padded), lambda d, i: (d, 0, i, 0)),
            pl.BlockSpec((1, 1, 2, BLOCK, padded), lambda d, i: (d, 0, 0, i, 0)),
        ],
        out_specs=pl.BlockSpec((1, heads, BLOCK, padded), lambda d, i: (d, 0, i, 0)),
        compiler_params=params(2),
        cost_estimate=pl.CostEstimate(
            flops=3 * docs * heads * rows * rows,
            transcendentals=0,
            bytes_accessed=docs * padded * padded * (4 * heads + 12),
        ),
        name="bias_rows",
    )(lengths, entries, pos_buckets, box_buckets)


def project_kernel(rows, x_ref, w_ref, vec_ref, out_ref, tok_ref):
    width = x_ref.shape[3]
    block = live_rows(x_ref[0, 0], rows, pl.program_id(1) * x_ref.shape[2])
    tok_ref[0] = block
    queries = dot(block, w_ref[:, :width]) + vec_ref[4:5, :]
    out_ref[0, :, :width] = queries.astype(BF16) * BF16(SCALE)
    out_ref[0, :, width : 2 * width] = dot(block, w_ref[:, width : 2 * width]).astype(BF16)
    values = dot(block, w_ref[:, 2 * width :]) + vec_ref[5:6, :]
    out_ref[0, :, 2 * width :] = values.astype(BF16)


def project(layer_input, w_mixed, vectors):
    docs, unused, rows, width = layer_input.shape
    padded = pl.cdiv(rows, BLOCK) * BLOCK
    return pl.pallas_call(
        partial(project_kernel, rows),
        out_shape=(
            jax.ShapeDtypeStruct((docs, padded, 3 * width), BF16),
            jax.ShapeDtypeStruct((docs, padded, width), BF16),
        ),
        grid=(docs, padded // DENSE_BLOCK),
        in_specs=[
            pl.BlockSpec((1, 1, DENSE_BLOCK, width), lambda d, i: (d, 0, i, 0)),
            columns((width, 3 * width), 0),
            resident(vectors.shape),
        ],
        out_specs=(
            pl.BlockSpec((1, DENSE_BLOCK, 3 * width), lambda d, i: (d, i, 0)),
            pl.BlockSpec((1, DENSE_BLOCK, width), lambda d, i: (d, i, 0)),
        ),
        compiler_params=params(2),
        name="project",
    )(layer_input, w_mixed, vectors)


def attend_kernel(q_ref, k_ref, v_ref, bias_ref, probs_ref, out_ref):
    lane = lax.broadcasted_iota(jnp.int32, (1, LANES), 1)
    for pair in range(q_ref.shape[2] // LANES):
        cols = slice(pair * LANES, (pair + 1) * LANES)
        queries, key_rows, values = q_ref[0, :, cols], k_ref[0, :, cols], v_ref[0, :, cols]
        total = None
        for half in range(2):
            head = 2 * pair + half
            keep = (lane < HEAD_DIM) if half == 0 else (lane >= HEAD_DIM)
            scores = dot_nt(jnp.where(keep, queries, BF16(0)), key_rows) + bias_ref[0, head]
            top = jnp.max(scores, axis=-1, keepdims=True)
            powers = jnp.exp(scores - top)
            share = 1.0 / jnp.sum(powers, axis=-1, keepdims=True)
            probs = (powers * share).astype(BF16)
            probs_ref[0, head] = probs
            part = dot(probs, jnp.where(keep, values, BF16(0)))
            total = part if half == 0 else total + part
        out_ref[0, :, cols] = total.astype(BF16)


def attend(qkv, bias):
    docs, padded, width = qkv.shape[0], qkv.shape[1], qkv.shape[2] // 3
    heads = bias.shape[1]
    return pl.pallas_call(
        attend_kernel,
        out_shape=(
            jax.ShapeDtypeStruct((docs, heads, padded, padded), BF16),
            jax.ShapeDtypeStruct((docs, padded, width), BF16),
        ),
        grid=(docs, padded // BLOCK),
        in_specs=[
            pl.BlockSpec((1, BLOCK, width), lambda d, i: (d, i, 0)),
            pl.BlockSpec((1, padded, width), lambda d, i: (d, 0, 1)),
            pl.BlockSpec((1, padded, width), lambda d, i: (d, 0, 2)),
            pl.BlockSpec((1, heads, BLOCK, padded), lambda d, i: (d, 0, i, 0)),
        ],
        out_specs=(
            pl.BlockSpec((1, heads, BLOCK, padded), lambda d, i: (d, 0, i, 0)),
            pl.BlockSpec((1, BLOCK, width), lambda d, i: (d, i, 0)),
        ),
        compiler_params=params(2),
        name="attend",
    )(qkv, qkv, qkv, bias)


def norm(rows_in):
    centre = rows_in - jnp.mean(rows_in, axis=-1, keepdims=True)
    inv_std = lax.rsqrt(jnp.mean(centre * centre, axis=-1, keepdims=True) + NORM_EPS)
    return centre * inv_std, inv_std


def norm_back(grad_in, normed, inv_std, gain_row):
    scaled = grad_in * gain_row
    return inv_std * (
        scaled
        - jnp.mean(scaled, axis=-1, keepdims=True)
        - normed * jnp.mean(scaled * normed, axis=-1, keepdims=True)
    )


def dense_kernel(
    rows, x_ref, o_ref, cot_ref, wo_ref, wu_ref, wd_ref, vec_ref, upb_ref,
    y_ref, dr_ref, h_ref, g_ref, du_ref, df_ref, db_ref, do_ref, sums_ref, upsum_ref,
    slope_ref,
):
    width, hidden = wu_ref.shape
    first = pl.program_id(1) * x_ref.shape[2]
    vec = vec_ref[...]

    @pl.when((pl.program_id(0) == 0) & (pl.program_id(1) == 0))
    def _():
        sums_ref[...] = jnp.zeros_like(sums_ref)
        upsum_ref[...] = jnp.zeros_like(upsum_ref)

    tok = live_rows(x_ref[0, 0], rows, first).astype(F32)
    normed_one, inv_one = norm(tok + dot(o_ref[0], wo_ref[...]) + vec[6:7])
    state = normed_one * vec[0:1] + vec[2:3]
    low = state.astype(BF16)
    h_ref[0] = low
    second = state + vec[7:8]
    for part in range(hidden // width):
        cols = slice(part * width, (part + 1) * width)
        upper = dot(low, wu_ref[:, cols]) + upb_ref[:, cols]
        cdf = 0.5 * (1.0 + lax.erf(upper * (0.5**0.5)))
        slope_ref[:, cols] = cdf + upper * (jnp.exp(-0.5 * upper * upper) * 0.3989422804014327)
        active = (upper * cdf).astype(BF16)
        g_ref[0, :, cols] = active
        second = second + dot(active, wd_ref[cols, :])
    normed_two, inv_two = norm(second)
    y_ref[0, 0] = (normed_two * vec[1:2] + vec[3:4]).astype(BF16)
    grad = live_rows(cot_ref[0, 0], rows, first).astype(F32)
    sums_ref[1:2, :] += jnp.sum(grad * normed_two, axis=0, keepdims=True)
    sums_ref[3:4, :] += jnp.sum(grad, axis=0, keepdims=True)
    d_two = norm_back(grad, normed_two, inv_two, vec[1:2])
    d_ffn = d_two.astype(BF16)
    df_ref[0] = d_ffn
    sums_ref[7:8, :] += jnp.sum(d_ffn.astype(F32), axis=0, keepdims=True)
    back = d_two
    for part in range(hidden // width):
        cols = slice(part * width, (part + 1) * width)
        d_upper = (dot_nt(d_ffn, wd_ref[cols, :]) * slope_ref[:, cols]).astype(BF16)
        du_ref[0, :, cols] = d_upper
        upsum_ref[:, cols] += jnp.sum(d_upper.astype(F32), axis=0, keepdims=True)
        back = back + dot_nt(d_upper, wu_ref[:, cols])
    sums_ref[0:1, :] += jnp.sum(back * normed_one, axis=0, keepdims=True)
    sums_ref[2:3, :] += jnp.sum(back, axis=0, keepdims=True)
    d_one = norm_back(back, normed_one, inv_one, vec[0:1])
    dr_ref[0] = d_one
    d_branch = d_one.astype(BF16)
    db_ref[0] = d_branch
    sums_ref[6:7, :] += jnp.sum(d_branch.astype(F32), axis=0, keepdims=True)
    do_ref[0] = dot_nt(d_branch, wo_ref[...]).astype(BF16)


def dense(layer_input, attended, cotangent, w_mixed, w_down, vectors, up_row):
    docs, unused, rows, width = layer_input.shape
    padded, hidden = attended.shape[1], w_down.shape[0]
    ragged = pl.BlockSpec((1, 1, DENSE_BLOCK, width), lambda d, i: (d, 0, i, 0))
    narrow = pl.BlockSpec((1, DENSE_BLOCK, width), lambda d, i: (d, i, 0))
    wide = pl.BlockSpec((1, DENSE_BLOCK, hidden), lambda d, i: (d, i, 0))

    def rows_of(columns, dtype):
        return jax.ShapeDtypeStruct((docs, padded, columns), dtype)

    return pl.pallas_call(
        partial(dense_kernel, rows),
        out_shape=(
            jax.ShapeDtypeStruct(layer_input.shape, BF16),
            rows_of(width, F32),
            rows_of(width, BF16),
            rows_of(hidden, BF16),
            rows_of(hidden, BF16),
            rows_of(width, BF16),
            rows_of(width, BF16),
            rows_of(width, BF16),
            jax.ShapeDtypeStruct((8, width), F32),
            jax.ShapeDtypeStruct((1, hidden), F32),
        ),
        grid=(docs, padded // DENSE_BLOCK),
        in_specs=[
            ragged, narrow, ragged,
            columns((width, width), 3), columns((width, hidden), 4 * width // hidden),
            resident(w_down.shape),
            resident(vectors.shape), resident(up_row.shape),
        ],
        out_specs=(
            ragged, narrow, narrow, wide, wide, narrow, narrow, narrow,
            pl.BlockSpec((8, width), lambda d, i: (0, 0)),
            pl.BlockSpec((1, hidden), lambda d, i: (0, 0)),
        ),
        scratch_shapes=[pltpu.VMEM((DENSE_BLOCK, hidden), F32)],
        compiler_params=params(2),
        name="dense",
    )(layer_input, attended, cotangent, w_mixed, w_mixed, w_down, vectors, up_row)


def attend_back_kernel(
    rows, q_ref, k_ref, v_ref, probs_ref, do_ref, pos_ref, box_ref, dm_ref, bins_ref,
    dk_ref, dv_ref, ds_ref, acc_ref, picks_ref,
):
    block, width = pl.program_id(1), q_ref.shape[2]
    padded = k_ref.shape[1]
    lane = lax.broadcasted_iota(jnp.int32, (1, LANES), 1)

    @pl.when((pl.program_id(0) == 0) & (block == 0))
    def _():
        acc_ref[...] = jnp.zeros_like(acc_ref)
        ds_ref[...] = jnp.zeros_like(ds_ref)

    @pl.when(block == 0)
    def _():
        dk_ref[...] = jnp.zeros_like(dk_ref)
        dv_ref[...] = jnp.zeros_like(dv_ref)

    own = pl.ds(pl.multiple_of(block * BLOCK, BLOCK), BLOCK)
    for pair in range(width // LANES):
        cols = slice(pair * LANES, (pair + 1) * LANES)
        queries, key_rows, values = q_ref[0, :, cols], k_ref[0, :, cols], v_ref[0, :, cols]
        grads = do_ref[0, :, cols]
        turned_q, turned_g = queries.T, grads.T
        total = None
        for half in range(2):
            head = 2 * pair + half
            keep = (lane < HEAD_DIM) if half == 0 else (lane >= HEAD_DIM)
            part = slice(half * HEAD_DIM, (half + 1) * HEAD_DIM)
            lines = slice(head * HEAD_DIM, (head + 1) * HEAD_DIM)
            low = probs_ref[0, head]
            probs = low.astype(F32)
            dprobs = dot_nt(jnp.where(keep, grads, BF16(0)), values)
            delta = jnp.sum(probs * dprobs, axis=-1, keepdims=True)
            dscore = probs * (dprobs - delta)
            for chunk in range(padded // LANES):
                ds_ref[chunk, pl.ds(head, BLOCK, stride=16), :] = dscore[
                    :, chunk * LANES : (chunk + 1) * LANES
                ]
            dlow = dscore.astype(BF16)
            piece = dot(dlow, jnp.where(keep, key_rows, BF16(0)))
            total = piece if half == 0 else total + piece
            dk_ref[lines, :] += dot(turned_q[part, :], dlow)
            dv_ref[lines, :] += dot(turned_g[part, :], low)
        dm_ref[0, own, cols] = (total * SCALE).astype(BF16)

    group = 32
    low_bins = lax.broadcasted_iota(jnp.int32, (HALF, LANES), 0).astype(BF16)

    def hits(picks, bins):
        low = picks.astype(BF16)
        return jnp.concatenate(
            [
                jnp.where(low_bins[first : first + 16] == low, BF16(1), BF16(0))
                for first in range(0, bins, 16)
            ],
            axis=0,
        )

    for place, (picks, bits) in enumerate(
        (
            (box_ref[0, 0, 0], BOX_BINS),
            (box_ref[0, 0, 1], BOX_BINS),
            (pos_ref[0, 0], POS_BINS),
        )
    ):
        half = bits // 2
        for chunk in range(padded // LANES):
            part = picks[:, chunk * LANES : (chunk + 1) * LANES] & (bits - 1)
            picks_ref[2 * place, chunk] = (part & (half - 1)).astype(F32)
            picks_ref[2 * place + 1, chunk] = (part >> (half.bit_length() - 1)).astype(F32)

    def count(step, carry):
        total = None
        for line in range(0, group, LINES):
            left, right = [], []
            for own in range(LINES):
                row = step * group + line + own
                here = pl.ds(pl.multiple_of(row * 16, 16), 16)
                again = pl.ds(row, 16, stride=0)
                for chunk in range(padded // LANES):
                    base = ds_ref[chunk, here, :]
                    left.append(
                        jnp.concatenate(
                            [base.astype(BF16)]
                            + [
                                (base * picks_ref[2 * place + 1, chunk, again, :]).astype(BF16)
                                for place in range(3)
                            ],
                            axis=0,
                        )
                    )
                    right.append(
                        jnp.concatenate(
                            [
                                hits(picks_ref[2 * place, chunk, again, :], bins)
                                for place, bins in enumerate((HALF, HALF, HALF // 2))
                            ],
                            axis=0,
                        )
                    )
            part = dot_nt(jnp.concatenate(left, axis=1), jnp.concatenate(right, axis=1))
            total = part if total is None else total + part
        acc_ref[0, :, : total.shape[1]] += total
        return carry

    live = jnp.minimum(BLOCK, (rows + group - 1) // group * group - block * BLOCK)
    lax.fori_loop(0, live // group, count, 0)

    @pl.when(block == pl.num_programs(1) - 1)
    def _():
        dm_ref[0, :, width : 2 * width] = dk_ref[...].astype(BF16).T
        dm_ref[0, :, 2 * width :] = dv_ref[...].astype(BF16).T
        bins_ref[...] = jnp.sum(acc_ref[...], axis=0)


def attend_back(qkv, probs, d_attended, pos_buckets, box_buckets):
    docs, padded, width = qkv.shape[0], qkv.shape[1], qkv.shape[2] // 3
    heads, rows = probs.shape[1], pos_buckets.shape[2]
    return pl.pallas_call(
        partial(attend_back_kernel, rows),
        out_shape=(
            jax.ShapeDtypeStruct((docs, padded, 3 * width), BF16),
            jax.ShapeDtypeStruct((64, LANES), F32),
        ),
        grid=(docs, padded // BLOCK),
        in_specs=[
            pl.BlockSpec((1, BLOCK, width), lambda d, i: (d, i, 0)),
            pl.BlockSpec((1, padded, width), lambda d, i: (d, 0, 1)),
            pl.BlockSpec((1, padded, width), lambda d, i: (d, 0, 2)),
            pl.BlockSpec((1, heads, BLOCK, padded), lambda d, i: (d, 0, i, 0)),
            pl.BlockSpec((1, BLOCK, width), lambda d, i: (d, i, 0)),
            pl.BlockSpec((1, 1, BLOCK, padded), lambda d, i: (d, 0, i, 0)),
            pl.BlockSpec((1, 1, 2, BLOCK, padded), lambda d, i: (d, 0, 0, i, 0)),
        ],
        out_specs=(
            pl.BlockSpec((1, padded, 3 * width), lambda d, i: (d, 0, 0)),
            pl.BlockSpec((64, LANES), lambda d, i: (0, 0)),
        ),
        scratch_shapes=[
            pltpu.VMEM((width, padded), F32),
            pltpu.VMEM((width, padded), F32),
            pltpu.VMEM((padded // LANES, BLOCK * 16, LANES), F32),
            pltpu.VMEM((SPLIT, 64, LANES), F32),
            pltpu.VMEM((6, padded // LANES, BLOCK, LANES), F32),
        ],
        compiler_params=params(2),
        name="attend_back",
    )(qkv, qkv, qkv, probs, d_attended, pos_buckets, box_buckets)


def table_entries(table):
    heads = table.shape[1]
    lines = table.astype(F32).T * SCALE
    boxes = lines[:, POS_BINS:]
    spots = jnp.pad(lines[:, :POS_BINS], ((0, 0), (0, LANES - POS_BINS)))
    return jnp.concatenate([boxes, spots], axis=0).reshape(2 * heads, LANES)


def table_grad(bins, heads):
    base, upper = bins[:heads], (bins[16 : 16 + heads], bins[32 : 32 + heads], bins[48 : 48 + heads])
    pieces = []
    for which, (first, size) in enumerate(((0, HALF), (HALF, HALF), (2 * HALF, HALF // 2))):
        high = upper[which][:, first : first + size]
        pieces.append(jnp.concatenate([base[:, first : first + size] - high, high], axis=1))
    return jnp.concatenate([pieces[2], pieces[0], pieces[1]], axis=1).T * SCALE


def weight_grads(attended, d_branch, low, d_upper, active, d_ffn, devices):
    rows, width = attended.shape
    own, fold = width // devices, d_upper.shape[1] // width
    share = devices // fold
    steps = 1 + 2 * fold

    def kernel(a_ref, b_ref, l_ref, u_ref, g_ref, f_ref, out_ref, turned_ref, stage_ref, sems):
        step = pl.program_id(0)
        slot = step % 2

        def flat_copy(where, spot):
            cols = pl.ds(pl.multiple_of(where * width, width), width)
            return pltpu.make_async_copy(
                stage_ref.at[spot], out_ref.at[:, :, cols], sems.at[spot, 0]
            )

        def fold_copy(where, spot, part):
            block = where - 1 - fold
            cols = pl.ds((1 + fold + part) * width, width)
            return pltpu.make_async_copy(
                stage_ref.at[spot].reshape(share, fold, own, width).at[:, part],
                out_ref.at[pl.ds(block * share, share), :, cols],
                sems.at[spot, part],
            )

        def wait_for(where, spot):
            @pl.when(where <= fold)
            def _():
                flat_copy(where, spot).wait()

            @pl.when(where > fold)
            def _():
                for part in range(fold):
                    fold_copy(where, spot, part).wait()

        @pl.when(step >= 2)
        def _():
            wait_for(step - 2, slot)

        def put(value):
            stage_ref[slot] = value.astype(BF16).reshape(devices, own, width)

        @pl.when(step == 0)
        def _():
            put(dot(a_ref[...].T, b_ref[...]))
            turned_ref[...] = l_ref[...].T

        @pl.when((step > 0) & (step <= fold))
        def _():
            put(dot(turned_ref[...], u_ref[...]))

        @pl.when(step > fold)
        def _():
            put(dot(g_ref[...].T, f_ref[...]))

        @pl.when(step <= fold)
        def _():
            flat_copy(step, slot).start()

        @pl.when(step > fold)
        def _():
            for part in range(fold):
                fold_copy(step, slot, part).start()

        @pl.when(step == steps - 1)
        def _():
            wait_for(step - 1, 1 - slot)
            wait_for(step, slot)

    return pl.pallas_call(
        kernel,
        out_shape=jax.ShapeDtypeStruct((devices, own, (1 + 2 * fold) * width), BF16),
        grid=(steps,),
        in_specs=[
            resident((rows, width)),
            resident((rows, width)),
            resident((rows, width)),
            pl.BlockSpec((rows, width), lambda p: (0, jnp.clip(p - 1, 0, fold - 1))),
            pl.BlockSpec((rows, width), lambda p: (0, jnp.clip(p - 1 - fold, 0, fold - 1))),
            resident((rows, width)),
        ],
        out_specs=pl.BlockSpec(memory_space=pl.ANY),
        scratch_shapes=[
            pltpu.VMEM((width, rows), BF16),
            pltpu.VMEM((2, devices, own, width), BF16),
            pltpu.SemaphoreType.DMA((2, fold)),
        ],
        compiler_params=params(1),
        cost_estimate=pl.CostEstimate(
            flops=2 * rows * width * width * steps, transcendentals=0,
            bytes_accessed=2 * rows * width * (steps + 3),
        ),
        name="weight_grads",
    )(attended, d_branch, low, d_upper, active, d_ffn)


ORDERS = ((3, 1, 2, 0), (3, 2, 1, 0), (3, 1, 2, 0))
MESH = pl.DeviceIdType.MESH


def remaining(part, level):
    return [axis for axis in range(4) if axis not in ORDERS[part][:level]]


def tail_kernel(
    dims, w_ref, tok_ref, mixed_ref, one_ref, small_ref, grad_ref, sums_ref, input_ref, *scratch
):
    parts, width = len(ORDERS), tok_ref.shape[1]
    holders = [scratch[8 * part : 8 * part + 4] for part in range(parts)]
    inboxes = [scratch[8 * part + 4 : 8 * part + 8] for part in range(parts)]
    (
        tok, turned, mixed, weights, kept, stage, own_sums, got_sums,
        send_sems, recv_sems, load_sems, keep_sems, store_sems,
    ) = scratch[8 * parts :]
    deep, across, along, cores = dims
    dp, fsdp = lax.axis_index("dp"), lax.axis_index("fsdp")
    mine = (dp // across, dp % across, fsdp // cores, fsdp % cores)
    docs, padded = one_ref.shape[0], one_ref.shape[1]
    rows, block = input_ref.shape[1], kept.shape[1]
    own_lines = small_ref.shape[0]

    def peer(axis, step):
        place = list(mine)
        place[axis] = (place[axis] + step) % dims[axis]
        return place[axis], (place[0] * across + place[1], place[2] * cores + place[3])

    loads = [pltpu.make_async_copy(tok_ref, tok, load_sems.at[0])]
    for part in range(parts):
        loads.append(
            pltpu.make_async_copy(
                mixed_ref.at[:, pl.ds(part * width, width)], mixed.at[part], load_sems.at[1 + part]
            )
        )
    loads.append(
        pltpu.make_async_copy(
            w_ref.at[:, pl.ds(0, parts * width)], weights, load_sems.at[1 + parts]
        )
    )
    for load in loads:
        load.start()

    barrier = pltpu.get_barrier_semaphore()
    partners = 0
    for axis in range(4):
        for step in range(1, dims[axis]):
            pl.semaphore_signal(barrier, inc=1, device_id=peer(axis, step)[1], device_id_type=MESH)
            partners += 1
    pl.semaphore_wait(barrier, partners)

    flying = {}

    def launch(lane, axis, source, target):
        copies = []
        for step in range(1, dims[axis]):
            place, device = peer(axis, step)
            copies.append(
                pltpu.make_async_remote_copy(
                    src_ref=source(place),
                    dst_ref=target(step - 1),
                    send_sem=send_sems.at[lane, step - 1],
                    recv_sem=recv_sems.at[lane, step - 1],
                    device_id=device,
                    device_id_type=MESH,
                )
            )
        for copy in copies:
            copy.start()
        flying[lane] = copies

    def land(lane):
        for copy in flying.pop(lane):
            copy.wait()

    def joined(own, others):
        total = own.astype(F32)
        for other in others:
            total = total + other.astype(F32)
        return total

    def send(part, level):
        axis, axes = ORDERS[part][level], remaining(part, level)

        def source(place):
            return holders[part][level].at[
                tuple(place if item == axis else slice(None) for item in axes)
            ]

        launch(4 * part + level, axis, source, lambda slot: inboxes[part][level].at[slot])

    def join(part, level):
        land(4 * part + level)
        axis, axes = ORDERS[part][level], remaining(part, level)
        source, box = holders[part][level], inboxes[part][level]
        left = [item for item in axes if item != axis]
        count = dims[axis] - 1
        if not left:
            grad_ref[:, part * width : (part + 1) * width] = joined(
                source[mine[axis]], [box[slot] for slot in range(count)]
            )
            return
        spots = [()]
        for item in left[1:]:
            spots = [spot + (place,) for spot in spots for place in range(dims[item])]

        def add(k, carry):
            for spot in spots:
                there = (k,) + spot
                where = dict(zip(left, there))
                where[axis] = mine[axis]
                own = tuple(where[item] for item in axes)
                holders[part][level + 1][there] = joined(
                    source[own], [box[(slot,) + there] for slot in range(count)]
                ).astype(BF16)
            return carry

        lax.fori_loop(0, dims[left[0]], add, 0)
        send(part, level + 1)

    small_order = (3, 1, 2, 0)

    def small_send(level):
        axis = small_order[level]
        first = sum(dims[item] - 1 for item in small_order[:level])
        launch(
            4 * parts + level, axis,
            lambda place: own_sums.at[level], lambda slot: got_sums.at[first + slot],
        )

    def small_join(level):
        land(4 * parts + level)
        axis = small_order[level]
        first = sum(dims[item] - 1 for item in small_order[:level])
        total = joined(
            own_sums[level], [got_sums[first + slot] for slot in range(dims[axis] - 1)]
        )
        if level == 3:
            sums_ref[...] = total
        else:
            own_sums[level + 1] = total
            small_send(level + 1)

    spans = [(doc, first) for doc in range(docs) for first in range(0, padded, block)]

    def keep(step):
        doc, first = spans[step]
        return pltpu.make_async_copy(
            one_ref.at[doc, pl.ds(first, block), :], kept.at[step % 2], keep_sems.at[step % 2]
        )

    def store(step):
        doc, first = spans[step]
        count = min(block, rows - first)
        return pltpu.make_async_copy(
            stage.at[step % 2, pl.ds(0, count)],
            input_ref.at[doc, pl.ds(first, count)],
            store_sems.at[step % 2],
        )

    def input_step(step):
        doc, first = spans[step]
        if step == 0:
            loads[1 + parts].wait()
            keep(0).start()
        if step + 1 < len(spans):
            keep(step + 1).start()
        keep(step).wait()
        if step >= 2:
            store(step - 2).wait()
        at = pl.ds(doc * padded + first, block)
        total = kept[step % 2]
        for part in range(parts):
            total = total + dot_nt(
                mixed[part, at, :], weights[:, part * width : (part + 1) * width]
            )
        stage[step % 2, :, 0, :] = total
        store(step).start()

    loads[0].wait()
    turned[...] = tok[...].T
    ones = jnp.ones((16, tok.shape[0]), BF16)
    own_sums[0, 0:own_lines] = small_ref[...]

    def multiply(part):
        loads[1 + part].wait()
        rest = holders[part][0].shape
        block_rows = dot(turned[...], mixed[part]).astype(BF16)
        holders[part][0][...] = block_rows.reshape(rest)
        line = dot(ones, mixed[part])[0:8]
        share = 8 * width // LANES // 8
        for chunk in range(share):
            own_sums[0, pl.ds(own_lines + (part * share + chunk) * 8, 8)] = line[
                :, chunk * LANES : (chunk + 1) * LANES
            ]
        send(part, 0)

    multiply(0)
    multiply(1)
    multiply(2)
    small_send(0)
    join(0, 0)
    input_step(0)
    join(1, 0)
    join(0, 1)
    small_join(0)
    join(2, 0)
    join(1, 1)
    input_step(1)
    join(0, 2)
    small_join(1)
    join(2, 1)
    join(1, 2)
    input_step(2)
    small_join(2)
    join(2, 2)
    input_step(3)
    join(0, 3)
    join(1, 3)
    join(2, 3)
    small_join(3)
    for step in range(max(len(spans) - 2, 0), len(spans)):
        store(step).wait()


def split_mesh(dp, fsdp):
    across = 1 << ((dp.bit_length() - 1) // 2)
    across = across if dp % across == 0 else 1
    cores = 2 if fsdp % 2 == 0 else 1
    return dp // across, across, fsdp // cores, cores


def tail(w_mixed, tok, d_mixed, d_one, small, rows, dims):
    docs, padded, width = d_one.shape
    parts = len(ORDERS)
    devices = dims[0] * dims[1] * dims[2] * dims[3]
    own = width // devices
    lines = small.shape[0] + parts * 8 * width // LANES
    any_space = pl.BlockSpec(memory_space=pl.ANY)
    vmem = pl.BlockSpec(memory_space=pltpu.VMEM)
    scratch = []
    for part in range(parts):
        boxes = []
        for level in range(4):
            axes = remaining(part, level)
            axis = ORDERS[part][level]
            scratch.append(pltpu.VMEM(tuple(dims[item] for item in axes) + (own, width), BF16))
            boxes.append(
                pltpu.VMEM(
                    (max(dims[axis] - 1, 1),)
                    + tuple(dims[item] for item in axes if item != axis)
                    + (own, width),
                    BF16,
                )
            )
        scratch += boxes
    most = max(max(dims) - 1, 1)
    flat = docs * padded
    scratch += [
        pltpu.VMEM((flat, width), BF16),
        pltpu.VMEM((width, flat), BF16),
        pltpu.VMEM((parts, flat, width), BF16),
        pltpu.VMEM((width, parts * width), BF16),
        pltpu.VMEM((2, DENSE_BLOCK, width), F32),
        pltpu.VMEM((2, DENSE_BLOCK, 1, width), F32),
        pltpu.VMEM((4, lines, LANES), F32),
        pltpu.VMEM((sum(dims) - 4, lines, LANES), F32),
        pltpu.SemaphoreType.DMA((4 * parts + 4, most)),
        pltpu.SemaphoreType.DMA((4 * parts + 4, most)),
        pltpu.SemaphoreType.DMA((parts + 2,)),
        pltpu.SemaphoreType.DMA((2,)),
        pltpu.SemaphoreType.DMA((2,)),
    ]
    return pl.pallas_call(
        partial(tail_kernel, dims),
        out_shape=(
            jax.ShapeDtypeStruct((own, parts * width), F32),
            jax.ShapeDtypeStruct((lines, LANES), F32),
            jax.ShapeDtypeStruct((docs, rows, 1, width), F32),
        ),
        in_specs=[any_space, any_space, any_space, any_space, vmem],
        out_specs=(vmem, vmem, any_space),
        scratch_shapes=scratch,
        compiler_params=pltpu.CompilerParams(
            collective_id=0, has_side_effects=True, vmem_limit_bytes=VMEM_LIMIT
        ),
        name="tail",
    )(w_mixed, tok, d_mixed, d_one, small)


def small_results(packed, width, hidden, heads):
    lines, more = 8 * width // LANES, hidden // LANES
    sums = packed[:lines].reshape(8, width)
    up_sum = packed[lines : lines + more].reshape(hidden)
    d_table = table_grad(packed[lines + more : lines + more + 64], heads)
    mixed = packed[lines + more + 64 :].reshape(3, width // LANES, 8, LANES)[:, :, 0]
    mixed = mixed.reshape(3, width)
    d_biases = jnp.concatenate([mixed[0:1], mixed[2:3], sums[6:8]], axis=0)
    return sums[0:2], sums[2:4], d_biases, up_sum, d_table


def local_step(devices, lengths, pos_buckets, box_buckets, layer_input, cotangent, w_mixed, w_down, vectors, up_row, table):
    heads, width = table.shape[1], layer_input.shape[3]
    docs, rows = layer_input.shape[0], layer_input.shape[2]
    bias = bias_rows(lengths, table_entries(table), pos_buckets, box_buckets, heads)
    qkv, tok = project(layer_input, w_mixed, vectors)
    probs, attended = attend(qkv, bias)
    result, d_one, low, active, d_upper, d_ffn, d_branch, d_attended, sums, up_sum = dense(
        layer_input, attended, cotangent, w_mixed, w_down, vectors, up_row
    )

    def flat(item):
        return item.reshape(-1, item.shape[-1])

    d_weights = weight_grads(
        flat(attended), flat(d_branch), flat(low), flat(d_upper), flat(active), flat(d_ffn), devices
    )
    d_mixed, bins = attend_back(qkv, probs, d_attended, pos_buckets, box_buckets)
    packed = jnp.concatenate(
        [sums.reshape(-1, LANES), up_sum.reshape(-1, LANES), bins], axis=0
    )
    return result, d_weights, (w_mixed, flat(tok), flat(d_mixed), d_one, packed, rows)


def body(
    layer_input, text_lengths, pos_buckets, box_buckets, w_qkv, w_out, w_up, w_down,
    norm_gains, norm_shifts, proj_biases, up_bias, rel_tables, cotangent,
):
    axes = ("dp", "fsdp")
    width, hidden = layer_input.shape[3], w_up.shape[1]
    own = norm_gains.shape[1]
    table = lax.all_gather(rel_tables, "fsdp", axis=0, tiled=True)
    heads = table.shape[1]
    small = jnp.concatenate(
        [norm_gains.T, norm_shifts.T, proj_biases.T, up_bias.reshape(own, hidden // width)], axis=1
    )
    small = jnp.pad(small, ((0, 0), (0, LANES - small.shape[1])))
    w_mixed = lax.all_gather(
        jnp.concatenate([w_qkv, w_out, w_up, small], axis=1), axes, axis=0, tiled=True
    )
    w_down = lax.all_gather(w_down, axes, axis=0, tiled=True)
    small = w_mixed[:, 4 * width + hidden :].astype(F32)
    vectors = small[:, :8].T
    up_row = small[:, 8 : 8 + hidden // width].reshape(1, hidden)
    devices = width // own
    result, d_weights, rest = local_step(
        devices, text_lengths[:, 0], pos_buckets, box_buckets, layer_input, cotangent, w_mixed, w_down,
        vectors, up_row, table,
    )
    d_weights = lax.psum_scatter(
        d_weights.reshape(width, -1), axes, scatter_dimension=0, tiled=True
    ).astype(F32)
    d_down = [d_weights[:, first : first + width] for first in range(width + hidden, width + 2 * hidden, width)]
    d_down = jnp.concatenate(d_down, axis=0)
    d_qkv, packed, input_grad = tail(
        *rest, split_mesh(lax.axis_size("dp"), lax.axis_size("fsdp"))
    )
    d_gains, d_shifts, d_biases, up_sum, d_table = small_results(packed, width, hidden, heads)
    place = lax.axis_index(axes)
    d_gains, d_shifts, d_biases = (
        lax.dynamic_slice_in_dim(item, place * own, own, 1)
        for item in (d_gains, d_shifts, d_biases)
    )
    up_sum = lax.dynamic_slice_in_dim(up_sum, place * up_bias.shape[0], up_bias.shape[0], 0)
    table_rows = rel_tables.shape[0]
    d_table = lax.dynamic_slice_in_dim(d_table, lax.axis_index("fsdp") * table_rows, table_rows, 0)
    return (
        result, jnp.transpose(input_grad, (0, 2, 1, 3)), d_qkv, d_weights[:, :width], d_weights[:, width : width + hidden], d_down,
        d_gains, d_shifts, d_biases, up_sum, d_table,
    )


def solution(mesh):
    both = ("dp", "fsdp")
    docs = P(None, both, None, None)
    return jax.shard_map(
        body,
        mesh=mesh,
        in_specs=(
            docs, P(None, both), docs, P(None, both, None, None, None),
            P(both, None), P(both, None), P(both, None), P(both, None),
            P(None, both), P(None, both), P(None, both), P(both), P("fsdp", None), docs,
        ),
        out_specs=(
            docs, docs, P(both, None), P(both, None), P(both, None), P(both, None),
            P(None, both), P(None, both), P(None, both), P(both), P("fsdp", None),
        ),
        check_vma=False,
    )
```

```python
from functools import partial

import jax
import jax.numpy as jnp
from jax import lax
from jax.experimental import pallas as pl
from jax.experimental.pallas import tpu as pltpu
from jax.sharding import PartitionSpec as P

HEAD_DIM = 64
POS_BINS = 32
BOX_BINS = 64
TEXT_SLOTS = 512
NEG_FILL = -1000000000.0
NORM_EPS = 1e-05
BLOCK = 256
DENSE_BLOCK = 384
LANES = 128
HALF = 32
SPLIT = 1
LINES = 1
SCALE = 0.125
F32 = jnp.float32
BF16 = jnp.bfloat16
VMEM_LIMIT = 58 << 20


def dot(left, right):
    return jnp.dot(left, right, preferred_element_type=F32)


def dot_nt(left, right):
    return lax.dot_general(left, right, (((1,), (1,)), ((), ())), preferred_element_type=F32)


def params(count):
    return pltpu.CompilerParams(
        dimension_semantics=("arbitrary",) * count, vmem_limit_bytes=VMEM_LIMIT
    )


def resident(shape):
    zeros = (0,) * len(shape)
    return pl.BlockSpec(shape, lambda *_: zeros, pipeline_mode=pl.Buffered(1))


def columns(shape, place):
    return pl.BlockSpec(shape, lambda *_: (0, place), pipeline_mode=pl.Buffered(1))


def live_rows(values, rows, first):
    row = first + lax.broadcasted_iota(jnp.int32, (values.shape[0], 1), 0)
    return jnp.where(row < rows, values, jnp.zeros_like(values))


def bias_kernel(rows, len_ref, tab_ref, pos_ref, box_ref, out_ref):
    heads, chunks = out_ref.shape[1], out_ref.shape[3] // LANES
    block = pl.program_id(1)
    length = len_ref[pl.program_id(0)]
    steps = jnp.minimum(BLOCK, (rows + 7) // 8 * 8 - block * BLOCK) // 8

    def fill(step, carry):
        at = pl.ds(pl.multiple_of(step * 8, 8), 8)
        for chunk in range(chunks):
            cols = slice(chunk * LANES, (chunk + 1) * LANES)
            picks = (
                box_ref[0, 0, 0, at, cols] & (BOX_BINS - 1),
                (box_ref[0, 0, 1, at, cols] & (BOX_BINS - 1)) | BOX_BINS,
                pos_ref[0, 0, at, cols] & (POS_BINS - 1),
            )
            slot = chunk * LANES + lax.broadcasted_iota(jnp.int32, (8, LANES), 1)
            valid = ((slot >= TEXT_SLOTS) & (slot < rows)) | (slot < length)
            totals = [None] * heads
            for which, pick in enumerate(picks):
                for head in range(heads):
                    line = head + (heads if which == 2 else 0)
                    entries = jnp.broadcast_to(tab_ref[line : line + 1, :], (8, LANES))
                    term = jnp.take_along_axis(entries, pick, axis=1)
                    totals[head] = term if which == 0 else totals[head] + term
            for head in range(heads):
                out_ref[0, head, at, cols] = jnp.where(valid, totals[head], NEG_FILL)
        return carry

    def blank(step, carry):
        at = pl.ds(pl.multiple_of(step * 8, 8), 8)
        for head in range(heads):
            out_ref[0, head, at, :] = jnp.zeros((8, chunks * LANES), F32)
        return carry

    lax.fori_loop(0, steps, fill, 0)
    lax.fori_loop(steps, BLOCK // 8, blank, 0)


def bias_rows(lengths, entries, pos_buckets, box_buckets, heads):
    docs, rows = pos_buckets.shape[0], pos_buckets.shape[2]
    padded = pl.cdiv(rows, BLOCK) * BLOCK
    return pl.pallas_call(
        partial(bias_kernel, rows),
        out_shape=jax.ShapeDtypeStruct((docs, heads, padded, padded), F32),
        grid=(docs, padded // BLOCK),
        in_specs=[
            pl.BlockSpec(memory_space=pltpu.SMEM),
            resident(entries.shape),
            pl.BlockSpec((1, 1, BLOCK, padded), lambda d, i: (d, 0, i, 0)),
            pl.BlockSpec((1, 1, 2, BLOCK, padded), lambda d, i: (d, 0, 0, i, 0)),
        ],
        out_specs=pl.BlockSpec((1, heads, BLOCK, padded), lambda d, i: (d, 0, i, 0)),
        compiler_params=params(2),
        cost_estimate=pl.CostEstimate(
            flops=3 * docs * heads * rows * rows,
            transcendentals=0,
            bytes_accessed=docs * padded * padded * (4 * heads + 12),
        ),
        name="bias_rows",
    )(lengths, entries, pos_buckets, box_buckets)


def project_kernel(rows, x_ref, w_ref, vec_ref, out_ref, tok_ref):
    width = x_ref.shape[3]
    block = live_rows(x_ref[0, 0], rows, pl.program_id(1) * x_ref.shape[2])
    tok_ref[...] = block.T
    queries = dot(block, w_ref[:, :width]) + vec_ref[4:5, :]
    out_ref[0, :, :width] = queries.astype(BF16) * BF16(SCALE)
    out_ref[0, :, width : 2 * width] = dot(block, w_ref[:, width : 2 * width]).astype(BF16)
    values = dot(block, w_ref[:, 2 * width :]) + vec_ref[5:6, :]
    out_ref[0, :, 2 * width :] = values.astype(BF16)


def project(layer_input, w_mixed, vectors):
    docs, unused, rows, width = layer_input.shape
    padded = pl.cdiv(rows, BLOCK) * BLOCK
    return pl.pallas_call(
        partial(project_kernel, rows),
        out_shape=(
            jax.ShapeDtypeStruct((docs, padded, 3 * width), BF16),
            jax.ShapeDtypeStruct((width, docs * padded), BF16),
        ),
        grid=(docs, padded // DENSE_BLOCK),
        in_specs=[
            pl.BlockSpec((1, 1, DENSE_BLOCK, width), lambda d, i: (d, 0, i, 0)),
            columns((width, 3 * width), 0),
            resident(vectors.shape),
        ],
        out_specs=(
            pl.BlockSpec((1, DENSE_BLOCK, 3 * width), lambda d, i: (d, i, 0)),
            pl.BlockSpec((width, DENSE_BLOCK), lambda d, i: (0, d * (padded // DENSE_BLOCK) + i)),
        ),
        compiler_params=params(2),
        name="project",
    )(layer_input, w_mixed, vectors)


def attend_kernel(q_ref, k_ref, v_ref, bias_ref, probs_ref, out_ref):
    lane = lax.broadcasted_iota(jnp.int32, (1, LANES), 1)
    for pair in range(q_ref.shape[2] // LANES):
        cols = slice(pair * LANES, (pair + 1) * LANES)
        queries, key_rows, values = q_ref[0, :, cols], k_ref[0, :, cols], v_ref[0, :, cols]
        total = None
        for half in range(2):
            head = 2 * pair + half
            keep = (lane < HEAD_DIM) if half == 0 else (lane >= HEAD_DIM)
            scores = dot_nt(jnp.where(keep, queries, BF16(0)), key_rows) + bias_ref[0, head]
            top = jnp.max(scores, axis=-1, keepdims=True)
            powers = jnp.exp(scores - top)
            share = 1.0 / jnp.sum(powers, axis=-1, keepdims=True)
            probs = (powers * share).astype(BF16)
            probs_ref[0, head] = probs
            part = dot(probs, jnp.where(keep, values, BF16(0)))
            total = part if half == 0 else total + part
        out_ref[0, :, cols] = total.astype(BF16)


def attend(qkv, bias):
    docs, padded, width = qkv.shape[0], qkv.shape[1], qkv.shape[2] // 3
    heads = bias.shape[1]
    return pl.pallas_call(
        attend_kernel,
        out_shape=(
            jax.ShapeDtypeStruct((docs, heads, padded, padded), BF16),
            jax.ShapeDtypeStruct((docs, padded, width), BF16),
        ),
        grid=(docs, padded // BLOCK),
        in_specs=[
            pl.BlockSpec((1, BLOCK, width), lambda d, i: (d, i, 0)),
            pl.BlockSpec((1, padded, width), lambda d, i: (d, 0, 1)),
            pl.BlockSpec((1, padded, width), lambda d, i: (d, 0, 2)),
            pl.BlockSpec((1, heads, BLOCK, padded), lambda d, i: (d, 0, i, 0)),
        ],
        out_specs=(
            pl.BlockSpec((1, heads, BLOCK, padded), lambda d, i: (d, 0, i, 0)),
            pl.BlockSpec((1, BLOCK, width), lambda d, i: (d, i, 0)),
        ),
        compiler_params=params(2),
        name="attend",
    )(qkv, qkv, qkv, bias)


def norm(rows_in):
    centre = rows_in - jnp.mean(rows_in, axis=-1, keepdims=True)
    inv_std = lax.rsqrt(jnp.mean(centre * centre, axis=-1, keepdims=True) + NORM_EPS)
    return centre * inv_std, inv_std


def norm_back(grad_in, normed, inv_std, gain_row):
    scaled = grad_in * gain_row
    return inv_std * (
        scaled
        - jnp.mean(scaled, axis=-1, keepdims=True)
        - normed * jnp.mean(scaled * normed, axis=-1, keepdims=True)
    )


def dense_kernel(
    rows, x_ref, o_ref, cot_ref, wo_ref, wu_ref, wd_ref, vec_ref, upb_ref,
    y_ref, dr_ref, h_ref, g_ref, du_ref, df_ref, db_ref, do_ref, sums_ref, upsum_ref,
    slope_ref,
):
    width, hidden = wu_ref.shape
    first = pl.program_id(1) * x_ref.shape[2]
    vec = vec_ref[...]

    @pl.when((pl.program_id(0) == 0) & (pl.program_id(1) == 0))
    def _():
        sums_ref[...] = jnp.zeros_like(sums_ref)
        upsum_ref[...] = jnp.zeros_like(upsum_ref)

    tok = live_rows(x_ref[0, 0], rows, first).astype(F32)
    normed_one, inv_one = norm(tok + dot(o_ref[0], wo_ref[...]) + vec[6:7])
    state = normed_one * vec[0:1] + vec[2:3]
    low = state.astype(BF16)
    h_ref[0] = low
    second = state + vec[7:8]
    for part in range(hidden // width):
        cols = slice(part * width, (part + 1) * width)
        upper = dot(low, wu_ref[:, cols]) + upb_ref[:, cols]
        cdf = 0.5 * (1.0 + lax.erf(upper * (0.5**0.5)))
        slope_ref[:, cols] = cdf + upper * (jnp.exp(-0.5 * upper * upper) * 0.3989422804014327)
        active = (upper * cdf).astype(BF16)
        g_ref[0, :, cols] = active
        second = second + dot(active, wd_ref[cols, :])
    normed_two, inv_two = norm(second)
    y_ref[0, 0] = (normed_two * vec[1:2] + vec[3:4]).astype(BF16)
    grad = live_rows(cot_ref[0, 0], rows, first).astype(F32)
    sums_ref[1:2, :] += jnp.sum(grad * normed_two, axis=0, keepdims=True)
    sums_ref[3:4, :] += jnp.sum(grad, axis=0, keepdims=True)
    d_two = norm_back(grad, normed_two, inv_two, vec[1:2])
    d_ffn = d_two.astype(BF16)
    df_ref[0] = d_ffn
    sums_ref[7:8, :] += jnp.sum(d_ffn.astype(F32), axis=0, keepdims=True)
    back = d_two
    for part in range(hidden // width):
        cols = slice(part * width, (part + 1) * width)
        d_upper = (dot_nt(d_ffn, wd_ref[cols, :]) * slope_ref[:, cols]).astype(BF16)
        du_ref[0, :, cols] = d_upper
        upsum_ref[:, cols] += jnp.sum(d_upper.astype(F32), axis=0, keepdims=True)
        back = back + dot_nt(d_upper, wu_ref[:, cols])
    sums_ref[0:1, :] += jnp.sum(back * normed_one, axis=0, keepdims=True)
    sums_ref[2:3, :] += jnp.sum(back, axis=0, keepdims=True)
    d_one = norm_back(back, normed_one, inv_one, vec[0:1])
    dr_ref[0] = d_one
    d_branch = d_one.astype(BF16)
    db_ref[0] = d_branch
    sums_ref[6:7, :] += jnp.sum(d_branch.astype(F32), axis=0, keepdims=True)
    do_ref[0] = dot_nt(d_branch, wo_ref[...]).astype(BF16)


def dense(layer_input, attended, cotangent, w_mixed, w_down, vectors, up_row):
    docs, unused, rows, width = layer_input.shape
    padded, hidden = attended.shape[1], w_down.shape[0]
    ragged = pl.BlockSpec((1, 1, DENSE_BLOCK, width), lambda d, i: (d, 0, i, 0))
    narrow = pl.BlockSpec((1, DENSE_BLOCK, width), lambda d, i: (d, i, 0))
    wide = pl.BlockSpec((1, DENSE_BLOCK, hidden), lambda d, i: (d, i, 0))

    def rows_of(columns, dtype):
        return jax.ShapeDtypeStruct((docs, padded, columns), dtype)

    return pl.pallas_call(
        partial(dense_kernel, rows),
        out_shape=(
            jax.ShapeDtypeStruct(layer_input.shape, BF16),
            rows_of(width, F32),
            rows_of(width, BF16),
            rows_of(hidden, BF16),
            rows_of(hidden, BF16),
            rows_of(width, BF16),
            rows_of(width, BF16),
            rows_of(width, BF16),
            jax.ShapeDtypeStruct((8, width), F32),
            jax.ShapeDtypeStruct((1, hidden), F32),
        ),
        grid=(docs, padded // DENSE_BLOCK),
        in_specs=[
            ragged, narrow, ragged,
            columns((width, width), 3), columns((width, hidden), 4 * width // hidden),
            resident(w_down.shape),
            resident(vectors.shape), resident(up_row.shape),
        ],
        out_specs=(
            ragged, narrow, narrow, wide, wide, narrow, narrow, narrow,
            pl.BlockSpec((8, width), lambda d, i: (0, 0)),
            pl.BlockSpec((1, hidden), lambda d, i: (0, 0)),
        ),
        scratch_shapes=[pltpu.VMEM((DENSE_BLOCK, hidden), F32)],
        compiler_params=params(2),
        name="dense",
    )(layer_input, attended, cotangent, w_mixed, w_mixed, w_down, vectors, up_row)


def attend_back_kernel(
    rows, q_ref, k_ref, v_ref, probs_ref, do_ref, pos_ref, box_ref, dm_ref, bins_ref, line_ref,
    dk_ref, dv_ref, ds_ref, acc_ref, picks_ref,
):
    block, width = pl.program_id(1), q_ref.shape[2]
    padded = k_ref.shape[1]
    lane = lax.broadcasted_iota(jnp.int32, (1, LANES), 1)

    @pl.when((pl.program_id(0) == 0) & (block == 0))
    def _():
        acc_ref[...] = jnp.zeros_like(acc_ref)
        line_ref[...] = jnp.zeros_like(line_ref)
        ds_ref[...] = jnp.zeros_like(ds_ref)

    @pl.when(block == 0)
    def _():
        dk_ref[...] = jnp.zeros_like(dk_ref)
        dv_ref[...] = jnp.zeros_like(dv_ref)

    own = pl.ds(pl.multiple_of(block * BLOCK, BLOCK), BLOCK)
    for pair in range(width // LANES):
        cols = slice(pair * LANES, (pair + 1) * LANES)
        queries, key_rows, values = q_ref[0, :, cols], k_ref[0, :, cols], v_ref[0, :, cols]
        grads = do_ref[0, :, cols]
        turned_q, turned_g = queries.T, grads.T
        total = None
        for half in range(2):
            head = 2 * pair + half
            keep = (lane < HEAD_DIM) if half == 0 else (lane >= HEAD_DIM)
            part = slice(half * HEAD_DIM, (half + 1) * HEAD_DIM)
            lines = slice(head * HEAD_DIM, (head + 1) * HEAD_DIM)
            low = probs_ref[0, head]
            probs = low.astype(F32)
            dprobs = dot_nt(jnp.where(keep, grads, BF16(0)), values)
            delta = jnp.sum(probs * dprobs, axis=-1, keepdims=True)
            dscore = probs * (dprobs - delta)
            for chunk in range(padded // LANES):
                ds_ref[chunk, pl.ds(head, BLOCK, stride=16), :] = dscore[
                    :, chunk * LANES : (chunk + 1) * LANES
                ]
            dlow = dscore.astype(BF16)
            piece = dot(dlow, jnp.where(keep, key_rows, BF16(0)))
            total = piece if half == 0 else total + piece
            dk_ref[lines, :] += dot(turned_q[part, :], dlow)
            dv_ref[lines, :] += dot(turned_g[part, :], low)
        dm_ref[0, own, cols] = (total * SCALE).astype(BF16)

    group = 32
    low_bins = lax.broadcasted_iota(jnp.int32, (HALF, LANES), 0).astype(BF16)

    def hits(picks, bins):
        low = picks.astype(BF16)
        return jnp.concatenate(
            [
                jnp.where(low_bins[first : first + 16] == low, BF16(1), BF16(0))
                for first in range(0, bins, 16)
            ],
            axis=0,
        )

    for place, (picks, bits) in enumerate(
        (
            (box_ref[0, 0, 0], BOX_BINS),
            (box_ref[0, 0, 1], BOX_BINS),
            (pos_ref[0, 0], POS_BINS),
        )
    ):
        half = bits // 2
        for chunk in range(padded // LANES):
            part = picks[:, chunk * LANES : (chunk + 1) * LANES] & (bits - 1)
            picks_ref[2 * place, chunk] = (part & (half - 1)).astype(F32)
            picks_ref[2 * place + 1, chunk] = (part >> (half.bit_length() - 1)).astype(F32)

    def count(step, carry):
        total = None
        for line in range(0, group, LINES):
            left, right = [], []
            for own in range(LINES):
                row = step * group + line + own
                here = pl.ds(pl.multiple_of(row * 16, 16), 16)
                again = pl.ds(row, 16, stride=0)
                for chunk in range(padded // LANES):
                    base = ds_ref[chunk, here, :]
                    left.append(
                        jnp.concatenate(
                            [base.astype(BF16)]
                            + [
                                (base * picks_ref[2 * place + 1, chunk, again, :]).astype(BF16)
                                for place in range(3)
                            ],
                            axis=0,
                        )
                    )
                    right.append(
                        jnp.concatenate(
                            [
                                hits(picks_ref[2 * place, chunk, again, :], bins)
                                for place, bins in enumerate((HALF, HALF, HALF // 2))
                            ],
                            axis=0,
                        )
                    )
            part = dot_nt(jnp.concatenate(left, axis=1), jnp.concatenate(right, axis=1))
            total = part if total is None else total + part
        acc_ref[0, :, : total.shape[1]] += total
        return carry

    live = jnp.minimum(BLOCK, (rows + group - 1) // group * group - block * BLOCK)
    lax.fori_loop(0, live // group, count, 0)

    @pl.when(block == pl.num_programs(1) - 1)
    def _():
        dm_ref[0, :, width : 2 * width] = dk_ref[...].astype(BF16).T
        dm_ref[0, :, 2 * width :] = dv_ref[...].astype(BF16).T
        bins_ref[...] = jnp.sum(acc_ref[...], axis=0)
        line_ref[...] += dot(jnp.ones((16, padded), BF16), dm_ref[0])[0:8]


def attend_back(qkv, probs, d_attended, pos_buckets, box_buckets):
    docs, padded, width = qkv.shape[0], qkv.shape[1], qkv.shape[2] // 3
    heads, rows = probs.shape[1], pos_buckets.shape[2]
    return pl.pallas_call(
        partial(attend_back_kernel, rows),
        out_shape=(
            jax.ShapeDtypeStruct((docs, padded, 3 * width), BF16),
            jax.ShapeDtypeStruct((64, LANES), F32),
            jax.ShapeDtypeStruct((8, 3 * width), F32),
        ),
        grid=(docs, padded // BLOCK),
        in_specs=[
            pl.BlockSpec((1, BLOCK, width), lambda d, i: (d, i, 0)),
            pl.BlockSpec((1, padded, width), lambda d, i: (d, 0, 1)),
            pl.BlockSpec((1, padded, width), lambda d, i: (d, 0, 2)),
            pl.BlockSpec((1, heads, BLOCK, padded), lambda d, i: (d, 0, i, 0)),
            pl.BlockSpec((1, BLOCK, width), lambda d, i: (d, i, 0)),
            pl.BlockSpec((1, 1, BLOCK, padded), lambda d, i: (d, 0, i, 0)),
            pl.BlockSpec((1, 1, 2, BLOCK, padded), lambda d, i: (d, 0, 0, i, 0)),
        ],
        out_specs=(
            pl.BlockSpec((1, padded, 3 * width), lambda d, i: (d, 0, 0)),
            pl.BlockSpec((64, LANES), lambda d, i: (0, 0)),
            pl.BlockSpec((8, 3 * width), lambda d, i: (0, 0)),
        ),
        scratch_shapes=[
            pltpu.VMEM((width, padded), F32),
            pltpu.VMEM((width, padded), F32),
            pltpu.VMEM((padded // LANES, BLOCK * 16, LANES), F32),
            pltpu.VMEM((SPLIT, 64, LANES), F32),
            pltpu.VMEM((6, padded // LANES, BLOCK, LANES), F32),
        ],
        compiler_params=params(2),
        name="attend_back",
    )(qkv, qkv, qkv, probs, d_attended, pos_buckets, box_buckets)


def table_entries(table):
    heads = table.shape[1]
    lines = table.astype(F32).T * SCALE
    boxes = lines[:, POS_BINS:]
    spots = jnp.pad(lines[:, :POS_BINS], ((0, 0), (0, LANES - POS_BINS)))
    return jnp.concatenate([boxes, spots], axis=0).reshape(2 * heads, LANES)


def table_grad(bins, heads):
    base, upper = bins[:heads], (bins[16 : 16 + heads], bins[32 : 32 + heads], bins[48 : 48 + heads])
    pieces = []
    for which, (first, size) in enumerate(((0, HALF), (HALF, HALF), (2 * HALF, HALF // 2))):
        high = upper[which][:, first : first + size]
        pieces.append(jnp.concatenate([base[:, first : first + size] - high, high], axis=1))
    return jnp.concatenate([pieces[2], pieces[0], pieces[1]], axis=1).T * SCALE


def weight_grads(attended, d_branch, low, d_upper, active, d_ffn, devices):
    rows, width = attended.shape
    own, fold = width // devices, d_upper.shape[1] // width
    share = devices // fold
    steps = 1 + 2 * fold

    def kernel(a_ref, b_ref, l_ref, u_ref, g_ref, f_ref, out_ref, turned_ref, stage_ref, sems):
        step = pl.program_id(0)
        slot = step % 2

        def flat_copy(where, spot):
            cols = pl.ds(pl.multiple_of(where * width, width), width)
            return pltpu.make_async_copy(
                stage_ref.at[spot], out_ref.at[:, :, cols], sems.at[spot, 0]
            )

        def fold_copy(where, spot, part):
            block = where - 1 - fold
            cols = pl.ds((1 + fold + part) * width, width)
            return pltpu.make_async_copy(
                stage_ref.at[spot].reshape(share, fold, own, width).at[:, part],
                out_ref.at[pl.ds(block * share, share), :, cols],
                sems.at[spot, part],
            )

        def wait_for(where, spot):
            @pl.when(where <= fold)
            def _():
                flat_copy(where, spot).wait()

            @pl.when(where > fold)
            def _():
                for part in range(fold):
                    fold_copy(where, spot, part).wait()

        @pl.when(step >= 2)
        def _():
            wait_for(step - 2, slot)

        def put(value):
            stage_ref[slot] = value.astype(BF16).reshape(devices, own, width)

        @pl.when(step == 0)
        def _():
            put(dot(a_ref[...].T, b_ref[...]))
            turned_ref[...] = l_ref[...].T

        @pl.when((step > 0) & (step <= fold))
        def _():
            put(dot(turned_ref[...], u_ref[...]))

        @pl.when(step > fold)
        def _():
            put(dot(g_ref[...].T, f_ref[...]))

        @pl.when(step <= fold)
        def _():
            flat_copy(step, slot).start()

        @pl.when(step > fold)
        def _():
            for part in range(fold):
                fold_copy(step, slot, part).start()

        @pl.when(step == steps - 1)
        def _():
            wait_for(step - 1, 1 - slot)
            wait_for(step, slot)

    return pl.pallas_call(
        kernel,
        out_shape=jax.ShapeDtypeStruct((devices, own, (1 + 2 * fold) * width), BF16),
        grid=(steps,),
        in_specs=[
            resident((rows, width)),
            resident((rows, width)),
            resident((rows, width)),
            pl.BlockSpec((rows, width), lambda p: (0, jnp.clip(p - 1, 0, fold - 1))),
            pl.BlockSpec((rows, width), lambda p: (0, jnp.clip(p - 1 - fold, 0, fold - 1))),
            resident((rows, width)),
        ],
        out_specs=pl.BlockSpec(memory_space=pl.ANY),
        scratch_shapes=[
            pltpu.VMEM((width, rows), BF16),
            pltpu.VMEM((2, devices, own, width), BF16),
            pltpu.SemaphoreType.DMA((2, fold)),
        ],
        compiler_params=params(1),
        cost_estimate=pl.CostEstimate(
            flops=2 * rows * width * width * steps, transcendentals=0,
            bytes_accessed=2 * rows * width * (steps + 3),
        ),
        name="weight_grads",
    )(attended, d_branch, low, d_upper, active, d_ffn)


ORDERS = ((3, 1, 2, 0), (3, 2, 1, 0)) * 3
MATRICES = 3
TABLE_LINES = 64
MESH = pl.DeviceIdType.MESH


def remaining(part, level):
    return [axis for axis in range(4) if axis not in ORDERS[part][:level]]


def tail_kernel(
    dims, w_ref, tok_ref, mixed_ref, one_ref, small_ref, grad_ref, sums_ref, input_ref, *scratch
):
    parts, width = len(ORDERS), tok_ref.shape[0]
    cut = MATRICES * width // parts
    holders = [scratch[8 * part : 8 * part + 4] for part in range(parts)]
    inboxes = [scratch[8 * part + 4 : 8 * part + 8] for part in range(parts)]
    (
        turned, mixed, weights, kept, stage, own_sums, got_sums,
        send_sems, recv_sems, load_sems, keep_sems, store_sems,
    ) = scratch[8 * parts :]
    deep, across, along, cores = dims
    dp, fsdp = lax.axis_index("dp"), lax.axis_index("fsdp")
    mine = (dp // across, dp % across, fsdp // cores, fsdp % cores)
    docs, padded = one_ref.shape[0], one_ref.shape[1]
    rows, block = input_ref.shape[1], kept.shape[1]
    own_lines = sums_ref.shape[0] - TABLE_LINES

    def peer(axis, step):
        place = list(mine)
        place[axis] = (place[axis] + step) % dims[axis]
        return place[axis], (place[0] * across + place[1], place[2] * cores + place[3])

    loads = [pltpu.make_async_copy(tok_ref, turned, load_sems.at[0])]
    for part in range(MATRICES):
        loads.append(
            pltpu.make_async_copy(
                mixed_ref.at[:, pl.ds(part * width, width)], mixed.at[part], load_sems.at[1 + part]
            )
        )
    loads.append(
        pltpu.make_async_copy(
            w_ref.at[:, pl.ds(0, MATRICES * width)], weights, load_sems.at[1 + MATRICES]
        )
    )
    for load in loads:
        load.start()

    barrier = pltpu.get_barrier_semaphore()
    partners = 0
    for axis in range(4):
        for step in range(1, dims[axis]):
            pl.semaphore_signal(barrier, inc=1, device_id=peer(axis, step)[1], device_id_type=MESH)
            partners += 1
    pl.semaphore_wait(barrier, partners)

    flying = {}

    def launch(lane, axis, source, target):
        copies = []
        for step in range(1, dims[axis]):
            place, device = peer(axis, step)
            copies.append(
                pltpu.make_async_remote_copy(
                    src_ref=source(place),
                    dst_ref=target(step - 1),
                    send_sem=send_sems.at[lane, step - 1],
                    recv_sem=recv_sems.at[lane, step - 1],
                    device_id=device,
                    device_id_type=MESH,
                )
            )
        for copy in copies:
            copy.start()
        flying[lane] = copies

    def land(lane):
        for copy in flying.pop(lane):
            copy.wait()

    def joined(own, others):
        total = own.astype(F32)
        for other in others:
            total = total + other.astype(F32)
        return total

    def send(part, level):
        axis, axes = ORDERS[part][level], remaining(part, level)

        def source(place):
            return holders[part][level].at[
                tuple(place if item == axis else slice(None) for item in axes)
            ]

        launch(4 * part + level, axis, source, lambda slot: inboxes[part][level].at[slot])

    def join(part, level):
        land(4 * part + level)
        axis, axes = ORDERS[part][level], remaining(part, level)
        source, box = holders[part][level], inboxes[part][level]
        left = [item for item in axes if item != axis]
        count = dims[axis] - 1
        if not left:
            grad_ref[:, part * cut : (part + 1) * cut] = joined(
                source[mine[axis]], [box[slot] for slot in range(count)]
            )
            return
        spots = [()]
        for item in left[1:]:
            spots = [spot + (place,) for spot in spots for place in range(dims[item])]

        def add(k, carry):
            for spot in spots:
                there = (k,) + spot
                where = dict(zip(left, there))
                where[axis] = mine[axis]
                own = tuple(where[item] for item in axes)
                holders[part][level + 1][there] = joined(
                    source[own], [box[(slot,) + there] for slot in range(count)]
                ).astype(BF16)
            return carry

        lax.fori_loop(0, dims[left[0]], add, 0)
        send(part, level + 1)

    small_order = (3, 1, 2, 0)
    own_bins = deep * own_lines

    def small_send(level):
        axis, lane = small_order[level], 4 * parts + level
        if level < 3:
            launch(lane, axis, lambda place: own_sums.at[level], lambda slot: got_sums.at[level, slot])
            return
        launch(
            lane, axis,
            lambda place: own_sums.at[3, pl.ds(pl.multiple_of(place * own_lines, 8), own_lines)],
            lambda slot: got_sums.at[3, slot, pl.ds(0, own_lines)],
        )
        launch(
            lane + 1, axis,
            lambda place: own_sums.at[3, pl.ds(own_bins, TABLE_LINES)],
            lambda slot: got_sums.at[3, slot, pl.ds(own_bins, TABLE_LINES)],
        )

    def small_join(level):
        axis, lane = small_order[level], 4 * parts + level
        land(lane)
        slots = range(dims[axis] - 1)
        if level < 3:
            own_sums[level + 1] = joined(own_sums[level], [got_sums[level, slot] for slot in slots])
            small_send(level + 1)
            return
        land(lane + 1)
        here = pl.ds(pl.multiple_of(mine[0] * own_lines, 8), own_lines)
        sums_ref[0:own_lines] = joined(
            own_sums[3, here], [got_sums[3, slot, 0:own_lines] for slot in slots]
        )
        last = slice(own_bins, own_bins + TABLE_LINES)
        sums_ref[own_lines:] = joined(own_sums[3, last], [got_sums[3, slot, last] for slot in slots])

    spans = [(doc, first) for doc in range(docs) for first in range(0, padded, block)]

    def keep(step):
        doc, first = spans[step]
        return pltpu.make_async_copy(
            one_ref.at[doc, pl.ds(first, block), :], kept.at[step % 2], keep_sems.at[step % 2]
        )

    def store(step):
        doc, first = spans[step]
        count = min(block, rows - first)
        return pltpu.make_async_copy(
            stage.at[step % 2, pl.ds(0, count)],
            input_ref.at[doc, pl.ds(first, count)],
            store_sems.at[step % 2],
        )

    def input_step(step):
        doc, first = spans[step]
        if step == 0:
            loads[1 + MATRICES].wait()
            keep(0).start()
        if step + 1 < len(spans):
            keep(step + 1).start()
        keep(step).wait()
        if step >= 2:
            store(step - 2).wait()
        at = pl.ds(doc * padded + first, block)
        total = kept[step % 2]
        for part in range(MATRICES):
            total = total + dot_nt(
                mixed[part, at, :], weights[:, part * width : (part + 1) * width]
            )
        stage[step % 2, :, 0, :] = total
        store(step).start()

    loads[0].wait()
    own_sums[0] = small_ref[...]
    small_send(0)

    def multiply(matrix):
        loads[1 + matrix].wait()
        for part in range(matrix * parts // MATRICES, (matrix + 1) * parts // MATRICES):
            first = part * cut - matrix * width
            block_rows = dot(turned[...], mixed[matrix, :, first : first + cut]).astype(BF16)
            holders[part][0][...] = block_rows.reshape(holders[part][0].shape)
            send(part, 0)

    multiply(0)
    small_join(0)
    multiply(1)
    join(0, 0)
    join(1, 0)
    multiply(2)
    small_join(1)
    join(2, 0)
    join(3, 0)
    join(0, 1)
    join(1, 1)
    join(4, 0)
    join(5, 0)
    small_join(2)
    input_step(0)
    join(2, 1)
    join(3, 1)
    join(0, 2)
    join(1, 2)
    input_step(1)
    join(4, 1)
    join(5, 1)
    join(2, 2)
    join(3, 2)
    input_step(2)
    small_join(3)
    join(4, 2)
    join(5, 2)
    input_step(3)
    for part in range(parts):
        join(part, 3)
    for step in range(max(len(spans) - 2, 0), len(spans)):
        store(step).wait()


def split_mesh(dp, fsdp):
    across = 1 << ((dp.bit_length() - 1) // 2)
    across = across if dp % across == 0 else 1
    cores = 2 if fsdp % 2 == 0 else 1
    return dp // across, across, fsdp // cores, cores


def tail(w_mixed, tok, d_mixed, d_one, small, rows, dims):
    docs, padded, width = d_one.shape
    parts = len(ORDERS)
    cut = MATRICES * width // parts
    devices = dims[0] * dims[1] * dims[2] * dims[3]
    own = width // devices
    lines = (small.shape[0] - TABLE_LINES) // dims[0] + TABLE_LINES
    any_space = pl.BlockSpec(memory_space=pl.ANY)
    vmem = pl.BlockSpec(memory_space=pltpu.VMEM)
    scratch = []
    for part in range(parts):
        boxes = []
        for level in range(4):
            axes = remaining(part, level)
            axis = ORDERS[part][level]
            scratch.append(pltpu.VMEM(tuple(dims[item] for item in axes) + (own, cut), BF16))
            boxes.append(
                pltpu.VMEM(
                    (max(dims[axis] - 1, 1),)
                    + tuple(dims[item] for item in axes if item != axis)
                    + (own, cut),
                    BF16,
                )
            )
        scratch += boxes
    most = max(max(dims) - 1, 1)
    flat = docs * padded
    scratch += [
        pltpu.VMEM((width, flat), BF16),
        pltpu.VMEM((MATRICES, flat, width), BF16),
        pltpu.VMEM((width, MATRICES * width), BF16),
        pltpu.VMEM((2, DENSE_BLOCK, width), F32),
        pltpu.VMEM((2, DENSE_BLOCK, 1, width), F32),
        pltpu.VMEM((4,) + small.shape, F32),
        pltpu.VMEM((4, most) + small.shape, F32),
        pltpu.SemaphoreType.DMA((4 * parts + 5, most)),
        pltpu.SemaphoreType.DMA((4 * parts + 5, most)),
        pltpu.SemaphoreType.DMA((MATRICES + 2,)),
        pltpu.SemaphoreType.DMA((2,)),
        pltpu.SemaphoreType.DMA((2,)),
    ]
    return pl.pallas_call(
        partial(tail_kernel, dims),
        out_shape=(
            jax.ShapeDtypeStruct((own, MATRICES * width), F32),
            jax.ShapeDtypeStruct((lines, LANES), F32),
            jax.ShapeDtypeStruct((docs, rows, 1, width), F32),
        ),
        in_specs=[any_space, any_space, any_space, any_space, vmem],
        out_specs=(vmem, vmem, any_space),
        scratch_shapes=scratch,
        compiler_params=pltpu.CompilerParams(
            collective_id=0, has_side_effects=True, vmem_limit_bytes=VMEM_LIMIT
        ),
        name="tail",
    )(w_mixed, tok, d_mixed, d_one, small)


def packed_sums(sums, up_sum, bins, deep):
    width, hidden = sums.shape[1], up_sum.shape[1]
    sums = jnp.transpose(sums.reshape(8, deep, width // deep), (1, 0, 2)).reshape(deep, -1)
    lines = jnp.concatenate([sums, up_sum.reshape(deep, hidden // deep)], axis=1)
    share = pl.cdiv(lines.shape[1], 8 * LANES) * 8 * LANES
    lines = jnp.pad(lines, ((0, 0), (0, share - lines.shape[1])))
    return jnp.concatenate([lines.reshape(-1, LANES), bins], axis=0)


def small_results(packed, width, hidden, heads, deep, own, rank):
    flat = packed[:-TABLE_LINES].reshape(-1)
    count, more = 8 * width // deep, hidden // deep
    sums = lax.dynamic_slice_in_dim(flat[:count].reshape(8, -1), rank * own, own, 1)
    fold = hidden // width * own
    up_sum = lax.dynamic_slice_in_dim(flat[count : count + more], rank * fold, fold, 0)
    return sums, up_sum, table_grad(packed[-TABLE_LINES:], heads)


def local_step(dims, lengths, pos_buckets, box_buckets, layer_input, cotangent, w_mixed, w_down, vectors, up_row, table):
    heads, width = table.shape[1], layer_input.shape[3]
    docs, rows = layer_input.shape[0], layer_input.shape[2]
    bias = bias_rows(lengths, table_entries(table), pos_buckets, box_buckets, heads)
    qkv, tok = project(layer_input, w_mixed, vectors)
    probs, attended = attend(qkv, bias)
    result, d_one, low, active, d_upper, d_ffn, d_branch, d_attended, sums, up_sum = dense(
        layer_input, attended, cotangent, w_mixed, w_down, vectors, up_row
    )

    def flat(item):
        return item.reshape(-1, item.shape[-1])

    d_weights = weight_grads(
        flat(attended), flat(d_branch), flat(low), flat(d_upper), flat(active), flat(d_ffn), dims[0] * dims[1] * dims[2] * dims[3]
    )
    d_mixed, bins, line = attend_back(qkv, probs, d_attended, pos_buckets, box_buckets)
    sums = jnp.concatenate(
        [sums[:4], line[:1, :width], line[:1, 2 * width :], sums[6:]], axis=0
    )
    packed = packed_sums(sums, up_sum, bins, dims[0])
    return result, d_weights, (w_mixed, tok, flat(d_mixed), d_one, packed, rows, dims)


def body(
    layer_input, text_lengths, pos_buckets, box_buckets, w_qkv, w_out, w_up, w_down,
    norm_gains, norm_shifts, proj_biases, up_bias, rel_tables, cotangent,
):
    axes = ("dp", "fsdp")
    width, hidden = layer_input.shape[3], w_up.shape[1]
    own = norm_gains.shape[1]
    table = lax.all_gather(rel_tables, "fsdp", axis=0, tiled=True)
    heads = table.shape[1]
    small = jnp.concatenate(
        [norm_gains.T, norm_shifts.T, proj_biases.T, up_bias.reshape(own, hidden // width)], axis=1
    )
    small = jnp.pad(small, ((0, 0), (0, LANES - small.shape[1])))
    w_mixed = lax.all_gather(
        jnp.concatenate([w_qkv, w_out, w_up, small], axis=1), axes, axis=0, tiled=True
    )
    w_down = lax.all_gather(w_down, axes, axis=0, tiled=True)
    small = w_mixed[:, 4 * width + hidden :].astype(F32)
    vectors = small[:, :8].T
    up_row = small[:, 8 : 8 + hidden // width].reshape(1, hidden)
    dims = split_mesh(lax.axis_size("dp"), lax.axis_size("fsdp"))
    result, d_weights, rest = local_step(
        dims, text_lengths[:, 0], pos_buckets, box_buckets, layer_input, cotangent, w_mixed, w_down,
        vectors, up_row, table,
    )
    d_weights = lax.psum_scatter(
        d_weights.reshape(width, -1), axes, scatter_dimension=0, tiled=True
    ).astype(F32)
    d_down = [d_weights[:, first : first + width] for first in range(width + hidden, width + 2 * hidden, width)]
    d_down = jnp.concatenate(d_down, axis=0)
    d_qkv, packed, input_grad = tail(*rest)
    rank = lax.axis_index(axes) % (width // own // dims[0])
    sums, up_sum, d_table = small_results(packed, width, hidden, heads, dims[0], own, rank)
    table_rows = rel_tables.shape[0]
    d_table = lax.dynamic_slice_in_dim(d_table, lax.axis_index("fsdp") * table_rows, table_rows, 0)
    return (
        result, jnp.transpose(input_grad, (0, 2, 1, 3)), d_qkv, d_weights[:, :width], d_weights[:, width : width + hidden], d_down,
        sums[0:2], sums[2:4], sums[4:8], up_sum, d_table,
    )


def solution(mesh):
    both = ("dp", "fsdp")
    docs = P(None, both, None, None)
    return jax.shard_map(
        body,
        mesh=mesh,
        in_specs=(
            docs, P(None, both), docs, P(None, both, None, None, None),
            P(both, None), P(both, None), P(both, None), P(both, None),
            P(None, both), P(None, both), P(None, both), P(both), P("fsdp", None), docs,
        ),
        out_specs=(
            docs, docs, P(both, None), P(both, None), P(both, None), P(both, None),
            P(None, both), P(None, both), P(None, both), P(both), P("fsdp", None),
        ),
        check_vma=False,
    )
```

```python
from functools import partial

import jax
import jax.numpy as jnp
from jax import lax
from jax.experimental import pallas as pl
from jax.experimental.pallas import tpu as pltpu
from jax.sharding import PartitionSpec as P

HEAD_DIM = 64
POS_BINS = 32
BOX_BINS = 64
TEXT_SLOTS = 512
NEG_FILL = -1000000000.0
NORM_EPS = 1e-05
BLOCK = 256
DENSE_BLOCK = 384
LANES = 128
HALF = 32
SPLIT = 1
LINES = 1
SCALE = 0.125
F32 = jnp.float32
BF16 = jnp.bfloat16
VMEM_LIMIT = 58 << 20


def dot(left, right):
    return jnp.dot(left, right, preferred_element_type=F32)


def dot_nt(left, right):
    return lax.dot_general(left, right, (((1,), (1,)), ((), ())), preferred_element_type=F32)


def params(count):
    return pltpu.CompilerParams(
        dimension_semantics=("arbitrary",) * count, vmem_limit_bytes=VMEM_LIMIT
    )


def resident(shape):
    zeros = (0,) * len(shape)
    return pl.BlockSpec(shape, lambda *_: zeros, pipeline_mode=pl.Buffered(1))


def columns(shape, place):
    return pl.BlockSpec(shape, lambda *_: (0, place), pipeline_mode=pl.Buffered(1))


def live_rows(values, rows, first):
    row = first + lax.broadcasted_iota(jnp.int32, (values.shape[0], 1), 0)
    return jnp.where(row < rows, values, jnp.zeros_like(values))


def bias_kernel(rows, len_ref, tab_ref, pos_ref, box_ref, out_ref):
    heads, chunks = out_ref.shape[1], out_ref.shape[3] // LANES
    block = pl.program_id(1)
    length = len_ref[pl.program_id(0)]
    steps = jnp.minimum(BLOCK, (rows + 7) // 8 * 8 - block * BLOCK) // 8

    def fill(step, carry):
        at = pl.ds(pl.multiple_of(step * 8, 8), 8)
        for chunk in range(chunks):
            cols = slice(chunk * LANES, (chunk + 1) * LANES)
            picks = (
                box_ref[0, 0, 0, at, cols] & (BOX_BINS - 1),
                (box_ref[0, 0, 1, at, cols] & (BOX_BINS - 1)) | BOX_BINS,
                pos_ref[0, 0, at, cols] & (POS_BINS - 1),
            )
            slot = chunk * LANES + lax.broadcasted_iota(jnp.int32, (8, LANES), 1)
            valid = ((slot >= TEXT_SLOTS) & (slot < rows)) | (slot < length)
            totals = [None] * heads
            for which, pick in enumerate(picks):
                for head in range(heads):
                    line = head + (heads if which == 2 else 0)
                    entries = jnp.broadcast_to(tab_ref[line : line + 1, :], (8, LANES))
                    term = jnp.take_along_axis(entries, pick, axis=1)
                    totals[head] = term if which == 0 else totals[head] + term
            for head in range(heads):
                out_ref[0, head, at, cols] = jnp.where(valid, totals[head], NEG_FILL)
        return carry

    def blank(step, carry):
        at = pl.ds(pl.multiple_of(step * 8, 8), 8)
        for head in range(heads):
            out_ref[0, head, at, :] = jnp.zeros((8, chunks * LANES), F32)
        return carry

    lax.fori_loop(0, steps, fill, 0)
    lax.fori_loop(steps, BLOCK // 8, blank, 0)


def bias_rows(lengths, entries, pos_buckets, box_buckets, heads):
    docs, rows = pos_buckets.shape[0], pos_buckets.shape[2]
    padded = pl.cdiv(rows, BLOCK) * BLOCK
    return pl.pallas_call(
        partial(bias_kernel, rows),
        out_shape=jax.ShapeDtypeStruct((docs, heads, padded, padded), F32),
        grid=(docs, padded // BLOCK),
        in_specs=[
            pl.BlockSpec(memory_space=pltpu.SMEM),
            resident(entries.shape),
            pl.BlockSpec((1, 1, BLOCK, padded), lambda d, i: (d, 0, i, 0)),
            pl.BlockSpec((1, 1, 2, BLOCK, padded), lambda d, i: (d, 0, 0, i, 0)),
        ],
        out_specs=pl.BlockSpec((1, heads, BLOCK, padded), lambda d, i: (d, 0, i, 0)),
        compiler_params=params(2),
        cost_estimate=pl.CostEstimate(
            flops=3 * docs * heads * rows * rows,
            transcendentals=0,
            bytes_accessed=docs * padded * padded * (4 * heads + 12),
        ),
        name="bias_rows",
    )(lengths, entries, pos_buckets, box_buckets)


def project_kernel(rows, x_ref, w_ref, vec_ref, out_ref, tok_ref):
    width = x_ref.shape[3]
    block = live_rows(x_ref[0, 0], rows, pl.program_id(1) * x_ref.shape[2])
    tok_ref[...] = block.T
    queries = dot(block, w_ref[:, :width]) + vec_ref[4:5, :]
    out_ref[0, :, :width] = queries.astype(BF16) * BF16(SCALE)
    out_ref[0, :, width : 2 * width] = dot(block, w_ref[:, width : 2 * width]).astype(BF16)
    values = dot(block, w_ref[:, 2 * width :]) + vec_ref[5:6, :]
    out_ref[0, :, 2 * width :] = values.astype(BF16)


def project(layer_input, w_mixed, vectors):
    docs, unused, rows, width = layer_input.shape
    padded = pl.cdiv(rows, BLOCK) * BLOCK
    return pl.pallas_call(
        partial(project_kernel, rows),
        out_shape=(
            jax.ShapeDtypeStruct((docs, padded, 3 * width), BF16),
            jax.ShapeDtypeStruct((width, docs * padded), BF16),
        ),
        grid=(docs, padded // DENSE_BLOCK),
        in_specs=[
            pl.BlockSpec((1, 1, DENSE_BLOCK, width), lambda d, i: (d, 0, i, 0)),
            columns((width, 3 * width), 0),
            resident(vectors.shape),
        ],
        out_specs=(
            pl.BlockSpec((1, DENSE_BLOCK, 3 * width), lambda d, i: (d, i, 0)),
            pl.BlockSpec((width, DENSE_BLOCK), lambda d, i: (0, d * (padded // DENSE_BLOCK) + i)),
        ),
        compiler_params=params(2),
        name="project",
    )(layer_input, w_mixed, vectors)


def attend_kernel(q_ref, k_ref, v_ref, bias_ref, probs_ref, out_ref, turned_ref):
    lane = lax.broadcasted_iota(jnp.int32, (1, LANES), 1)
    for pair in range(q_ref.shape[2] // LANES):
        cols = slice(pair * LANES, (pair + 1) * LANES)
        queries, key_rows, values = q_ref[0, :, cols], k_ref[0, :, cols], v_ref[0, :, cols]
        total = None
        for half in range(2):
            head = 2 * pair + half
            keep = (lane < HEAD_DIM) if half == 0 else (lane >= HEAD_DIM)
            scores = dot_nt(jnp.where(keep, queries, BF16(0)), key_rows) + bias_ref[0, head]
            top = jnp.max(scores, axis=-1, keepdims=True)
            powers = jnp.exp(scores - top)
            share = 1.0 / jnp.sum(powers, axis=-1, keepdims=True)
            probs = (powers * share).astype(BF16)
            probs_ref[0, head] = probs
            part = dot(probs, jnp.where(keep, values, BF16(0)))
            total = part if half == 0 else total + part
        low = total.astype(BF16)
        out_ref[0, :, cols] = low
        turned_ref[cols, :] = low.T


def attend(qkv, bias):
    docs, padded, width = qkv.shape[0], qkv.shape[1], qkv.shape[2] // 3
    heads = bias.shape[1]
    return pl.pallas_call(
        attend_kernel,
        out_shape=(
            jax.ShapeDtypeStruct((docs, heads, padded, padded), BF16),
            jax.ShapeDtypeStruct((docs, padded, width), BF16),
            jax.ShapeDtypeStruct((width, docs * padded), BF16),
        ),
        grid=(docs, padded // BLOCK),
        in_specs=[
            pl.BlockSpec((1, BLOCK, width), lambda d, i: (d, i, 0)),
            pl.BlockSpec((1, padded, width), lambda d, i: (d, 0, 1)),
            pl.BlockSpec((1, padded, width), lambda d, i: (d, 0, 2)),
            pl.BlockSpec((1, heads, BLOCK, padded), lambda d, i: (d, 0, i, 0)),
        ],
        out_specs=(
            pl.BlockSpec((1, heads, BLOCK, padded), lambda d, i: (d, 0, i, 0)),
            pl.BlockSpec((1, BLOCK, width), lambda d, i: (d, i, 0)),
            pl.BlockSpec((width, BLOCK), lambda d, i: (0, d * (padded // BLOCK) + i)),
        ),
        compiler_params=params(2),
        name="attend",
    )(qkv, qkv, qkv, bias)


def norm(rows_in):
    centre = rows_in - jnp.mean(rows_in, axis=-1, keepdims=True)
    inv_std = lax.rsqrt(jnp.mean(centre * centre, axis=-1, keepdims=True) + NORM_EPS)
    return centre * inv_std, inv_std


def norm_back(grad_in, normed, inv_std, gain_row):
    scaled = grad_in * gain_row
    return inv_std * (
        scaled
        - jnp.mean(scaled, axis=-1, keepdims=True)
        - normed * jnp.mean(scaled * normed, axis=-1, keepdims=True)
    )


def dense_kernel(
    rows, x_ref, o_ref, cot_ref, wo_ref, wu_ref, wd_ref, vec_ref, upb_ref,
    y_ref, dr_ref, left_ref, du_ref, df_ref, db_ref, do_ref, sums_ref, upsum_ref,
    slope_ref,
):
    width, hidden = wu_ref.shape
    first = pl.program_id(1) * x_ref.shape[2]
    vec = vec_ref[...]

    @pl.when((pl.program_id(0) == 0) & (pl.program_id(1) == 0))
    def _():
        sums_ref[...] = jnp.zeros_like(sums_ref)
        upsum_ref[...] = jnp.zeros_like(upsum_ref)

    tok = live_rows(x_ref[0, 0], rows, first).astype(F32)
    normed_one, inv_one = norm(tok + dot(o_ref[0], wo_ref[...]) + vec[6:7])
    state = normed_one * vec[0:1] + vec[2:3]
    low = state.astype(BF16)
    left_ref[0:width, :] = low.T
    second = state + vec[7:8]
    for part in range(hidden // width):
        cols = slice(part * width, (part + 1) * width)
        upper = dot(low, wu_ref[:, cols]) + upb_ref[:, cols]
        cdf = 0.5 * (1.0 + lax.erf(upper * (0.5**0.5)))
        slope_ref[:, cols] = cdf + upper * (jnp.exp(-0.5 * upper * upper) * 0.3989422804014327)
        active = (upper * cdf).astype(BF16)
        left_ref[(part + 1) * width : (part + 2) * width, :] = active.T
        second = second + dot(active, wd_ref[cols, :])
    normed_two, inv_two = norm(second)
    y_ref[0, 0] = (normed_two * vec[1:2] + vec[3:4]).astype(BF16)
    grad = live_rows(cot_ref[0, 0], rows, first).astype(F32)
    sums_ref[1:2, :] += jnp.sum(grad * normed_two, axis=0, keepdims=True)
    sums_ref[3:4, :] += jnp.sum(grad, axis=0, keepdims=True)
    d_two = norm_back(grad, normed_two, inv_two, vec[1:2])
    d_ffn = d_two.astype(BF16)
    df_ref[0] = d_ffn
    sums_ref[7:8, :] += jnp.sum(d_ffn.astype(F32), axis=0, keepdims=True)
    back = d_two
    for part in range(hidden // width):
        cols = slice(part * width, (part + 1) * width)
        d_upper = (dot_nt(d_ffn, wd_ref[cols, :]) * slope_ref[:, cols]).astype(BF16)
        du_ref[0, :, cols] = d_upper
        upsum_ref[:, cols] += jnp.sum(d_upper.astype(F32), axis=0, keepdims=True)
        back = back + dot_nt(d_upper, wu_ref[:, cols])
    sums_ref[0:1, :] += jnp.sum(back * normed_one, axis=0, keepdims=True)
    sums_ref[2:3, :] += jnp.sum(back, axis=0, keepdims=True)
    d_one = norm_back(back, normed_one, inv_one, vec[0:1])
    dr_ref[0] = d_one
    d_branch = d_one.astype(BF16)
    db_ref[0] = d_branch
    sums_ref[6:7, :] += jnp.sum(d_branch.astype(F32), axis=0, keepdims=True)
    do_ref[0] = dot_nt(d_branch, wo_ref[...]).astype(BF16)


def dense(layer_input, attended, cotangent, w_mixed, w_down, vectors, up_row):
    docs, unused, rows, width = layer_input.shape
    padded, hidden = attended.shape[1], w_down.shape[0]
    ragged = pl.BlockSpec((1, 1, DENSE_BLOCK, width), lambda d, i: (d, 0, i, 0))
    narrow = pl.BlockSpec((1, DENSE_BLOCK, width), lambda d, i: (d, i, 0))
    wide = pl.BlockSpec((1, DENSE_BLOCK, hidden), lambda d, i: (d, i, 0))

    def turned(lines):
        return pl.BlockSpec(
            (lines, DENSE_BLOCK), lambda d, i: (0, d * (padded // DENSE_BLOCK) + i)
        )

    def rows_of(columns, dtype):
        return jax.ShapeDtypeStruct((docs, padded, columns), dtype)

    return pl.pallas_call(
        partial(dense_kernel, rows),
        out_shape=(
            jax.ShapeDtypeStruct(layer_input.shape, BF16),
            rows_of(width, F32),
            jax.ShapeDtypeStruct((width + hidden, docs * padded), BF16),
            rows_of(hidden, BF16),
            rows_of(width, BF16),
            rows_of(width, BF16),
            rows_of(width, BF16),
            jax.ShapeDtypeStruct((8, width), F32),
            jax.ShapeDtypeStruct((1, hidden), F32),
        ),
        grid=(docs, padded // DENSE_BLOCK),
        in_specs=[
            ragged, narrow, ragged,
            columns((width, width), 3), columns((width, hidden), 4 * width // hidden),
            resident(w_down.shape),
            resident(vectors.shape), resident(up_row.shape),
        ],
        out_specs=(
            ragged, narrow, turned(width + hidden), wide, narrow, narrow, narrow,
            pl.BlockSpec((8, width), lambda d, i: (0, 0)),
            pl.BlockSpec((1, hidden), lambda d, i: (0, 0)),
        ),
        scratch_shapes=[pltpu.VMEM((DENSE_BLOCK, hidden), F32)],
        compiler_params=params(2),
        name="dense",
    )(layer_input, attended, cotangent, w_mixed, w_mixed, w_down, vectors, up_row)


def attend_back_kernel(
    rows, q_ref, k_ref, v_ref, probs_ref, do_ref, pos_ref, box_ref, dm_ref, bins_ref, line_ref,
    dk_ref, dv_ref, ds_ref, acc_ref, picks_ref,
):
    block, width = pl.program_id(1), q_ref.shape[2]
    padded = k_ref.shape[1]
    lane = lax.broadcasted_iota(jnp.int32, (1, LANES), 1)

    @pl.when((pl.program_id(0) == 0) & (block == 0))
    def _():
        acc_ref[...] = jnp.zeros_like(acc_ref)
        line_ref[...] = jnp.zeros_like(line_ref)
        ds_ref[...] = jnp.zeros_like(ds_ref)

    @pl.when(block == 0)
    def _():
        dk_ref[...] = jnp.zeros_like(dk_ref)
        dv_ref[...] = jnp.zeros_like(dv_ref)

    own = pl.ds(pl.multiple_of(block * BLOCK, BLOCK), BLOCK)
    for pair in range(width // LANES):
        cols = slice(pair * LANES, (pair + 1) * LANES)
        queries, key_rows, values = q_ref[0, :, cols], k_ref[0, :, cols], v_ref[0, :, cols]
        grads = do_ref[0, :, cols]
        turned_q, turned_g = queries.T, grads.T
        total = None
        for half in range(2):
            head = 2 * pair + half
            keep = (lane < HEAD_DIM) if half == 0 else (lane >= HEAD_DIM)
            part = slice(half * HEAD_DIM, (half + 1) * HEAD_DIM)
            lines = slice(head * HEAD_DIM, (head + 1) * HEAD_DIM)
            low = probs_ref[0, head]
            probs = low.astype(F32)
            dprobs = dot_nt(jnp.where(keep, grads, BF16(0)), values)
            delta = jnp.sum(probs * dprobs, axis=-1, keepdims=True)
            dscore = probs * (dprobs - delta)
            for chunk in range(padded // LANES):
                ds_ref[chunk, pl.ds(head, BLOCK, stride=16), :] = dscore[
                    :, chunk * LANES : (chunk + 1) * LANES
                ]
            dlow = dscore.astype(BF16)
            piece = dot(dlow, jnp.where(keep, key_rows, BF16(0)))
            total = piece if half == 0 else total + piece
            dk_ref[lines, :] += dot(turned_q[part, :], dlow)
            dv_ref[lines, :] += dot(turned_g[part, :], low)
        dm_ref[0, own, cols] = (total * SCALE).astype(BF16)

    group = 64
    low_bins = lax.broadcasted_iota(jnp.int32, (HALF, LANES), 0).astype(BF16)

    def hits(picks, bins):
        low = picks.astype(BF16)
        return jnp.concatenate(
            [
                jnp.where(low_bins[first : first + 16] == low, BF16(1), BF16(0))
                for first in range(0, bins, 16)
            ],
            axis=0,
        )

    for place, (picks, bits) in enumerate(
        (
            (box_ref[0, 0, 0], BOX_BINS),
            (box_ref[0, 0, 1], BOX_BINS),
            (pos_ref[0, 0], POS_BINS),
        )
    ):
        half = bits // 2
        for chunk in range(padded // LANES):
            part = picks[:, chunk * LANES : (chunk + 1) * LANES] & (bits - 1)
            picks_ref[2 * place, chunk] = (part & (half - 1)).astype(F32)
            picks_ref[2 * place + 1, chunk] = (part >> (half.bit_length() - 1)).astype(F32)

    def count(step, carry):
        total = None
        for line in range(0, group, LINES):
            left, right = [], []
            for own in range(LINES):
                row = step * group + line + own
                here = pl.ds(pl.multiple_of(row * 16, 16), 16)
                again = pl.ds(row, 16, stride=0)
                for chunk in range(padded // LANES):
                    base = ds_ref[chunk, here, :]
                    left.append(
                        jnp.concatenate(
                            [base.astype(BF16)]
                            + [
                                (base * picks_ref[2 * place + 1, chunk, again, :]).astype(BF16)
                                for place in range(3)
                            ],
                            axis=0,
                        )
                    )
                    right.append(
                        jnp.concatenate(
                            [
                                hits(picks_ref[2 * place, chunk, again, :], bins)
                                for place, bins in enumerate((HALF, HALF, HALF // 2))
                            ],
                            axis=0,
                        )
                    )
            part = dot_nt(jnp.concatenate(left, axis=1), jnp.concatenate(right, axis=1))
            total = part if total is None else total + part
        acc_ref[0, :, : total.shape[1]] += total
        return carry

    live = jnp.minimum(BLOCK, (rows + group - 1) // group * group - block * BLOCK)
    lax.fori_loop(0, live // group, count, 0)

    @pl.when(block == pl.num_programs(1) - 1)
    def _():
        dm_ref[0, :, width : 2 * width] = dk_ref[...].astype(BF16).T
        dm_ref[0, :, 2 * width :] = dv_ref[...].astype(BF16).T
        bins_ref[...] = jnp.sum(acc_ref[...], axis=0)
        line_ref[...] += dot(jnp.ones((16, padded), BF16), dm_ref[0])[0:8]


def attend_back(qkv, probs, d_attended, pos_buckets, box_buckets):
    docs, padded, width = qkv.shape[0], qkv.shape[1], qkv.shape[2] // 3
    heads, rows = probs.shape[1], pos_buckets.shape[2]
    return pl.pallas_call(
        partial(attend_back_kernel, rows),
        out_shape=(
            jax.ShapeDtypeStruct((docs, padded, 3 * width), BF16),
            jax.ShapeDtypeStruct((64, LANES), F32),
            jax.ShapeDtypeStruct((8, 3 * width), F32),
        ),
        grid=(docs, padded // BLOCK),
        in_specs=[
            pl.BlockSpec((1, BLOCK, width), lambda d, i: (d, i, 0)),
            pl.BlockSpec((1, padded, width), lambda d, i: (d, 0, 1)),
            pl.BlockSpec((1, padded, width), lambda d, i: (d, 0, 2)),
            pl.BlockSpec((1, heads, BLOCK, padded), lambda d, i: (d, 0, i, 0)),
            pl.BlockSpec((1, BLOCK, width), lambda d, i: (d, i, 0)),
            pl.BlockSpec((1, 1, BLOCK, padded), lambda d, i: (d, 0, i, 0)),
            pl.BlockSpec((1, 1, 2, BLOCK, padded), lambda d, i: (d, 0, 0, i, 0)),
        ],
        out_specs=(
            pl.BlockSpec((1, padded, 3 * width), lambda d, i: (d, 0, 0)),
            pl.BlockSpec((64, LANES), lambda d, i: (0, 0)),
            pl.BlockSpec((8, 3 * width), lambda d, i: (0, 0)),
        ),
        scratch_shapes=[
            pltpu.VMEM((width, padded), F32),
            pltpu.VMEM((width, padded), F32),
            pltpu.VMEM((padded // LANES, BLOCK * 16, LANES), F32),
            pltpu.VMEM((SPLIT, 64, LANES), F32),
            pltpu.VMEM((6, padded // LANES, BLOCK, LANES), F32),
        ],
        compiler_params=params(2),
        name="attend_back",
    )(qkv, qkv, qkv, probs, d_attended, pos_buckets, box_buckets)


def table_entries(table):
    heads = table.shape[1]
    lines = table.astype(F32).T * SCALE
    boxes = lines[:, POS_BINS:]
    spots = jnp.pad(lines[:, :POS_BINS], ((0, 0), (0, LANES - POS_BINS)))
    return jnp.concatenate([boxes, spots], axis=0).reshape(2 * heads, LANES)


def table_grad(bins, heads):
    base, upper = bins[:heads], (bins[16 : 16 + heads], bins[32 : 32 + heads], bins[48 : 48 + heads])
    pieces = []
    for which, (first, size) in enumerate(((0, HALF), (HALF, HALF), (2 * HALF, HALF // 2))):
        high = upper[which][:, first : first + size]
        pieces.append(jnp.concatenate([base[:, first : first + size] - high, high], axis=1))
    return jnp.concatenate([pieces[2], pieces[0], pieces[1]], axis=1).T * SCALE


def weight_grads(attended, d_branch, left, d_upper, d_ffn, devices):
    width, rows = attended.shape
    own, fold = width // devices, d_upper.shape[1] // width
    share = devices // fold
    steps = 1 + 2 * fold

    def kernel(
        l_ref, u_ref, a_ref, b_ref, f_ref, out_ref,
        attended_ref, branch_ref, ffn_ref, stage_ref, sems, load_sems,
    ):
        step = pl.program_id(0)
        slot = step % 2
        loads = [
            pltpu.make_async_copy(source, target, load_sems.at[place])
            for place, (source, target) in enumerate(
                ((f_ref, ffn_ref), (a_ref, attended_ref), (b_ref, branch_ref))
            )
        ]

        def flat_copy(part, spot):
            cols = pl.ds(pl.multiple_of(part * width, width), width)
            return pltpu.make_async_copy(
                stage_ref.at[spot], out_ref.at[:, :, cols], sems.at[spot, 0]
            )

        def fold_copy(where, spot, part):
            block = where - fold
            cols = pl.ds((1 + fold + part) * width, width)
            return pltpu.make_async_copy(
                stage_ref.at[spot].reshape(share, fold, own, width).at[:, part],
                out_ref.at[pl.ds(block * share, share), :, cols],
                sems.at[spot, part],
            )

        def wait_for(where, spot):
            @pl.when(where < fold)
            def _():
                flat_copy(where + 1, spot).wait()

            @pl.when((where >= fold) & (where < 2 * fold))
            def _():
                for part in range(fold):
                    fold_copy(where, spot, part).wait()

        @pl.when(step == 0)
        def _():
            for load in loads:
                load.start()

        @pl.when(step >= 2)
        def _():
            wait_for(step - 2, slot)

        def put(value):
            stage_ref[slot] = value.reshape(devices, own, width).astype(BF16)

        @pl.when(step < fold)
        def _():
            put(dot(l_ref[...], u_ref[...]))
            flat_copy(step + 1, slot).start()

        @pl.when(step == fold)
        def _():
            loads[0].wait()

        @pl.when((step >= fold) & (step < 2 * fold))
        def _():
            put(dot(l_ref[...], ffn_ref[...]))
            for part in range(fold):
                fold_copy(step, slot, part).start()

        @pl.when(step == 2 * fold)
        def _():
            loads[1].wait()
            loads[2].wait()
            put(dot(attended_ref[...], branch_ref[...]))
            flat_copy(0, slot).start()
            wait_for(step - 1, 1 - slot)
            flat_copy(0, slot).wait()

    away = pl.BlockSpec(memory_space=pl.ANY)
    return pl.pallas_call(
        kernel,
        out_shape=jax.ShapeDtypeStruct((devices, own, (1 + 2 * fold) * width), BF16),
        grid=(steps,),
        in_specs=[
            pl.BlockSpec((width, rows), lambda p: (jnp.clip(p - fold + 1, 0, fold), 0)),
            pl.BlockSpec((rows, width), lambda p: (0, jnp.minimum(p, fold - 1))),
            away,
            away,
            away,
        ],
        out_specs=away,
        scratch_shapes=[
            pltpu.VMEM((width, rows), BF16),
            pltpu.VMEM((rows, width), BF16),
            pltpu.VMEM((rows, width), BF16),
            pltpu.VMEM((2, devices, own, width), BF16),
            pltpu.SemaphoreType.DMA((2, fold)),
            pltpu.SemaphoreType.DMA((3,)),
        ],
        compiler_params=params(1),
        cost_estimate=pl.CostEstimate(
            flops=2 * rows * width * width * steps, transcendentals=0,
            bytes_accessed=2 * rows * width * (steps + 3),
        ),
        name="weight_grads",
    )(left, d_upper, attended, d_branch, d_ffn)


ORDERS = ((3, 1, 2, 0), (3, 2, 1, 0)) * 3
MATRICES = 3
TABLE_LINES = 64
MESH = pl.DeviceIdType.MESH


def remaining(part, level):
    return [axis for axis in range(4) if axis not in ORDERS[part][:level]]


def tail_kernel(
    dims, w_ref, tok_ref, mixed_ref, one_ref, small_ref, grad_ref, sums_ref, input_ref, *scratch
):
    parts, width = len(ORDERS), tok_ref.shape[0]
    cut = MATRICES * width // parts
    holders = [scratch[8 * part : 8 * part + 4] for part in range(parts)]
    inboxes = [scratch[8 * part + 4 : 8 * part + 8] for part in range(parts)]
    (
        turned, mixed, weights, kept, stage, own_sums, got_sums,
        send_sems, recv_sems, load_sems, keep_sems, store_sems,
    ) = scratch[8 * parts :]
    deep, across, along, cores = dims
    dp, fsdp = lax.axis_index("dp"), lax.axis_index("fsdp")
    mine = (dp // across, dp % across, fsdp // cores, fsdp % cores)
    docs, padded = one_ref.shape[0], one_ref.shape[1]
    rows, block = input_ref.shape[1], kept.shape[1]
    own_lines = sums_ref.shape[0] - TABLE_LINES

    def peer(axis, step):
        place = list(mine)
        place[axis] = (place[axis] + step) % dims[axis]
        return place[axis], (place[0] * across + place[1], place[2] * cores + place[3])

    loads = [pltpu.make_async_copy(tok_ref, turned, load_sems.at[0])]
    for part in range(MATRICES):
        loads.append(
            pltpu.make_async_copy(
                mixed_ref.at[:, pl.ds(part * width, width)], mixed.at[part], load_sems.at[1 + part]
            )
        )
    loads.append(
        pltpu.make_async_copy(
            w_ref.at[:, pl.ds(0, MATRICES * width)], weights, load_sems.at[1 + MATRICES]
        )
    )
    for load in loads:
        load.start()

    barrier = pltpu.get_barrier_semaphore()
    partners = 0
    for axis in range(4):
        for step in range(1, dims[axis]):
            pl.semaphore_signal(barrier, inc=1, device_id=peer(axis, step)[1], device_id_type=MESH)
            partners += 1
    pl.semaphore_wait(barrier, partners)

    flying = {}

    def launch(lane, axis, source, target):
        copies = []
        for step in range(1, dims[axis]):
            place, device = peer(axis, step)
            copies.append(
                pltpu.make_async_remote_copy(
                    src_ref=source(place),
                    dst_ref=target(step - 1),
                    send_sem=send_sems.at[lane, step - 1],
                    recv_sem=recv_sems.at[lane, step - 1],
                    device_id=device,
                    device_id_type=MESH,
                )
            )
        for copy in copies:
            copy.start()
        flying[lane] = copies

    def land(lane):
        for copy in flying.pop(lane):
            copy.wait()

    def joined(own, others):
        total = own.astype(F32)
        for other in others:
            total = total + other.astype(F32)
        return total

    def send(part, level):
        axis, axes = ORDERS[part][level], remaining(part, level)

        def source(place):
            return holders[part][level].at[
                tuple(place if item == axis else slice(None) for item in axes)
            ]

        launch(4 * part + level, axis, source, lambda slot: inboxes[part][level].at[slot])

    def join(part, level):
        land(4 * part + level)
        axis, axes = ORDERS[part][level], remaining(part, level)
        source, box = holders[part][level], inboxes[part][level]
        left = [item for item in axes if item != axis]
        count = dims[axis] - 1
        if not left:
            grad_ref[:, part * cut : (part + 1) * cut] = joined(
                source[mine[axis]], [box[slot] for slot in range(count)]
            )
            return
        spots = [()]
        for item in left[1:]:
            spots = [spot + (place,) for spot in spots for place in range(dims[item])]

        def add(k, carry):
            for spot in spots:
                there = (k,) + spot
                where = dict(zip(left, there))
                where[axis] = mine[axis]
                own = tuple(where[item] for item in axes)
                holders[part][level + 1][there] = joined(
                    source[own], [box[(slot,) + there] for slot in range(count)]
                ).astype(BF16)
            return carry

        lax.fori_loop(0, dims[left[0]], add, 0)
        send(part, level + 1)

    small_order = (3, 1, 2, 0)
    own_bins = deep * own_lines

    def small_send(level):
        axis, lane = small_order[level], 4 * parts + level
        if level < 3:
            launch(lane, axis, lambda place: own_sums.at[level], lambda slot: got_sums.at[level, slot])
            return
        launch(
            lane, axis,
            lambda place: own_sums.at[3, pl.ds(pl.multiple_of(place * own_lines, 8), own_lines)],
            lambda slot: got_sums.at[3, slot, pl.ds(0, own_lines)],
        )
        launch(
            lane + 1, axis,
            lambda place: own_sums.at[3, pl.ds(own_bins, TABLE_LINES)],
            lambda slot: got_sums.at[3, slot, pl.ds(own_bins, TABLE_LINES)],
        )

    def small_join(level):
        axis, lane = small_order[level], 4 * parts + level
        land(lane)
        slots = range(dims[axis] - 1)
        if level < 3:
            own_sums[level + 1] = joined(own_sums[level], [got_sums[level, slot] for slot in slots])
            small_send(level + 1)
            return
        land(lane + 1)
        here = pl.ds(pl.multiple_of(mine[0] * own_lines, 8), own_lines)
        sums_ref[0:own_lines] = joined(
            own_sums[3, here], [got_sums[3, slot, 0:own_lines] for slot in slots]
        )
        last = slice(own_bins, own_bins + TABLE_LINES)
        sums_ref[own_lines:] = joined(own_sums[3, last], [got_sums[3, slot, last] for slot in slots])

    spans = [(doc, first) for doc in range(docs) for first in range(0, padded, block)]

    def keep(step):
        doc, first = spans[step]
        return pltpu.make_async_copy(
            one_ref.at[doc, pl.ds(first, block), :], kept.at[step % 2], keep_sems.at[step % 2]
        )

    def store(step):
        doc, first = spans[step]
        count = min(block, rows - first)
        return pltpu.make_async_copy(
            stage.at[step % 2, pl.ds(0, count)],
            input_ref.at[doc, pl.ds(first, count)],
            store_sems.at[step % 2],
        )

    def input_step(step):
        doc, first = spans[step]
        if step == 0:
            loads[1 + MATRICES].wait()
            keep(0).start()
        if step + 1 < len(spans):
            keep(step + 1).start()
        keep(step).wait()
        if step >= 2:
            store(step - 2).wait()
        at = pl.ds(doc * padded + first, block)
        total = kept[step % 2]
        for part in range(MATRICES):
            total = total + dot_nt(
                mixed[part, at, :], weights[:, part * width : (part + 1) * width]
            )
        stage[step % 2, :, 0, :] = total
        store(step).start()

    loads[0].wait()
    own_sums[0] = small_ref[...]
    small_send(0)

    def multiply(matrix):
        loads[1 + matrix].wait()
        for part in range(matrix * parts // MATRICES, (matrix + 1) * parts // MATRICES):
            first = part * cut - matrix * width
            block_rows = dot(turned[...], mixed[matrix, :, first : first + cut])
            holders[part][0][...] = block_rows.reshape(holders[part][0].shape).astype(BF16)
            send(part, 0)

    multiply(0)
    small_join(0)
    multiply(1)
    join(0, 0)
    join(1, 0)
    multiply(2)
    small_join(1)
    join(2, 0)
    join(3, 0)
    join(0, 1)
    join(1, 1)
    join(4, 0)
    join(5, 0)
    small_join(2)
    input_step(0)
    join(2, 1)
    join(3, 1)
    join(0, 2)
    join(1, 2)
    input_step(1)
    join(4, 1)
    join(5, 1)
    join(2, 2)
    join(3, 2)
    input_step(2)
    small_join(3)
    join(4, 2)
    join(5, 2)
    input_step(3)
    for part in range(parts):
        join(part, 3)
    for step in range(max(len(spans) - 2, 0), len(spans)):
        store(step).wait()


def split_mesh(dp, fsdp):
    across = 1 << ((dp.bit_length() - 1) // 2)
    across = across if dp % across == 0 else 1
    cores = 2 if fsdp % 2 == 0 else 1
    return dp // across, across, fsdp // cores, cores


def tail(w_mixed, tok, d_mixed, d_one, small, rows, dims):
    docs, padded, width = d_one.shape
    parts = len(ORDERS)
    cut = MATRICES * width // parts
    devices = dims[0] * dims[1] * dims[2] * dims[3]
    own = width // devices
    lines = (small.shape[0] - TABLE_LINES) // dims[0] + TABLE_LINES
    any_space = pl.BlockSpec(memory_space=pl.ANY)
    vmem = pl.BlockSpec(memory_space=pltpu.VMEM)
    scratch = []
    for part in range(parts):
        boxes = []
        for level in range(4):
            axes = remaining(part, level)
            axis = ORDERS[part][level]
            scratch.append(pltpu.VMEM(tuple(dims[item] for item in axes) + (own, cut), BF16))
            boxes.append(
                pltpu.VMEM(
                    (max(dims[axis] - 1, 1),)
                    + tuple(dims[item] for item in axes if item != axis)
                    + (own, cut),
                    BF16,
                )
            )
        scratch += boxes
    most = max(max(dims) - 1, 1)
    flat = docs * padded
    scratch += [
        pltpu.VMEM((width, flat), BF16),
        pltpu.VMEM((MATRICES, flat, width), BF16),
        pltpu.VMEM((width, MATRICES * width), BF16),
        pltpu.VMEM((2, DENSE_BLOCK, width), F32),
        pltpu.VMEM((2, DENSE_BLOCK, 1, width), F32),
        pltpu.VMEM((4,) + small.shape, F32),
        pltpu.VMEM((4, most) + small.shape, F32),
        pltpu.SemaphoreType.DMA((4 * parts + 5, most)),
        pltpu.SemaphoreType.DMA((4 * parts + 5, most)),
        pltpu.SemaphoreType.DMA((MATRICES + 2,)),
        pltpu.SemaphoreType.DMA((2,)),
        pltpu.SemaphoreType.DMA((2,)),
    ]
    return pl.pallas_call(
        partial(tail_kernel, dims),
        out_shape=(
            jax.ShapeDtypeStruct((own, MATRICES * width), F32),
            jax.ShapeDtypeStruct((lines, LANES), F32),
            jax.ShapeDtypeStruct((docs, rows, 1, width), F32),
        ),
        in_specs=[any_space, any_space, any_space, any_space, vmem],
        out_specs=(vmem, vmem, any_space),
        scratch_shapes=scratch,
        compiler_params=pltpu.CompilerParams(
            collective_id=0, has_side_effects=True, vmem_limit_bytes=VMEM_LIMIT
        ),
        name="tail",
    )(w_mixed, tok, d_mixed, d_one, small)


def handed_on(rows_out):
    docs, pieces = rows_out.shape[0], 4

    def kernel(in_ref, out_ref, sems):
        copies = []
        for doc in range(docs):
            count = rows_out.shape[1]
            edges = [count * piece // pieces for piece in range(pieces + 1)]
            for piece in range(pieces):
                at = pl.ds(edges[piece], edges[piece + 1] - edges[piece])
                copies.append(
                    pltpu.make_async_copy(
                        in_ref.at[doc, at], out_ref.at[doc, at], sems.at[doc, piece]
                    )
                )
        for copy in copies:
            copy.start()
        for copy in copies:
            copy.wait()

    return pl.pallas_call(
        kernel,
        out_shape=jax.ShapeDtypeStruct(rows_out.shape, rows_out.dtype),
        in_specs=[pl.BlockSpec(memory_space=pl.ANY)],
        out_specs=pl.BlockSpec(memory_space=pl.ANY),
        scratch_shapes=[pltpu.SemaphoreType.DMA((docs, pieces))],
        name="handed_on",
    )(rows_out)


def packed_sums(sums, up_sum, bins, deep):
    width, hidden = sums.shape[1], up_sum.shape[1]
    sums = jnp.transpose(sums.reshape(8, deep, width // deep), (1, 0, 2)).reshape(deep, -1)
    lines = jnp.concatenate([sums, up_sum.reshape(deep, hidden // deep)], axis=1)
    share = pl.cdiv(lines.shape[1], 8 * LANES) * 8 * LANES
    lines = jnp.pad(lines, ((0, 0), (0, share - lines.shape[1])))
    return jnp.concatenate([lines.reshape(-1, LANES), bins], axis=0)


def small_results(packed, width, hidden, heads, deep, own, rank):
    flat = packed[:-TABLE_LINES].reshape(-1)
    count, more = 8 * width // deep, hidden // deep
    sums = lax.dynamic_slice_in_dim(flat[:count].reshape(8, -1), rank * own, own, 1)
    fold = hidden // width * own
    up_sum = lax.dynamic_slice_in_dim(flat[count : count + more], rank * fold, fold, 0)
    return sums, up_sum, table_grad(packed[-TABLE_LINES:], heads)


def local_step(dims, lengths, pos_buckets, box_buckets, layer_input, cotangent, w_mixed, w_down, vectors, up_row, table):
    heads, width = table.shape[1], layer_input.shape[3]
    docs, rows = layer_input.shape[0], layer_input.shape[2]
    bias = bias_rows(lengths, table_entries(table), pos_buckets, box_buckets, heads)
    qkv, tok = project(layer_input, w_mixed, vectors)
    probs, attended, turned = attend(qkv, bias)
    result, d_one, left, d_upper, d_ffn, d_branch, d_attended, sums, up_sum = dense(
        layer_input, attended, cotangent, w_mixed, w_down, vectors, up_row
    )

    def flat(item):
        return item.reshape(-1, item.shape[-1])

    d_weights = weight_grads(
        turned, flat(d_branch), left, flat(d_upper), flat(d_ffn), dims[0] * dims[1] * dims[2] * dims[3]
    )
    d_mixed, bins, line = attend_back(qkv, probs, d_attended, pos_buckets, box_buckets)
    sums = jnp.concatenate(
        [sums[:4], line[:1, :width], line[:1, 2 * width :], sums[6:]], axis=0
    )
    packed = packed_sums(sums, up_sum, bins, dims[0])
    return result, d_weights, (w_mixed, tok, flat(d_mixed), d_one, packed, rows, dims)


def body(
    layer_input, text_lengths, pos_buckets, box_buckets, w_qkv, w_out, w_up, w_down,
    norm_gains, norm_shifts, proj_biases, up_bias, rel_tables, cotangent,
):
    axes = ("dp", "fsdp")
    width, hidden = layer_input.shape[3], w_up.shape[1]
    own = norm_gains.shape[1]
    table = lax.all_gather(rel_tables, "fsdp", axis=0, tiled=True)
    heads = table.shape[1]
    small = jnp.concatenate(
        [norm_gains.T, norm_shifts.T, proj_biases.T, up_bias.reshape(own, hidden // width)], axis=1
    )
    small = jnp.pad(small, ((0, 0), (0, LANES - small.shape[1])))
    w_mixed = lax.all_gather(
        jnp.concatenate([w_qkv, w_out, w_up, small], axis=1), axes, axis=0, tiled=True
    )
    w_down = lax.all_gather(w_down, axes, axis=0, tiled=True)
    small = w_mixed[:, 4 * width + hidden :].astype(F32)
    vectors = small[:, :8].T
    up_row = small[:, 8 : 8 + hidden // width].reshape(1, hidden)
    dims = split_mesh(lax.axis_size("dp"), lax.axis_size("fsdp"))
    result, d_weights, rest = local_step(
        dims, text_lengths[:, 0], pos_buckets, box_buckets, layer_input, cotangent, w_mixed, w_down,
        vectors, up_row, table,
    )
    d_weights = lax.psum_scatter(
        d_weights.reshape(width, -1), axes, scatter_dimension=0, tiled=True
    ).astype(F32)
    d_down = [d_weights[:, first : first + width] for first in range(width + hidden, width + 2 * hidden, width)]
    d_down = jnp.concatenate(d_down, axis=0)
    d_qkv, packed, input_grad = tail(*rest)
    rank = lax.axis_index(axes) % (width // own // dims[0])
    sums, up_sum, d_table = small_results(packed, width, hidden, heads, dims[0], own, rank)
    table_rows = rel_tables.shape[0]
    d_table = lax.dynamic_slice_in_dim(d_table, lax.axis_index("fsdp") * table_rows, table_rows, 0)
    return (
        result, jnp.transpose(handed_on(input_grad), (0, 2, 1, 3)), d_qkv, d_weights[:, :width], d_weights[:, width : width + hidden], d_down,
        sums[0:2], sums[2:4], sums[4:8], up_sum, d_table,
    )


def solution(mesh):
    both = ("dp", "fsdp")
    docs = P(None, both, None, None)
    return jax.shard_map(
        body,
        mesh=mesh,
        in_specs=(
            docs, P(None, both), docs, P(None, both, None, None, None),
            P(both, None), P(both, None), P(both, None), P(both, None),
            P(None, both), P(None, both), P(None, both), P(both), P("fsdp", None), docs,
        ),
        out_specs=(
            docs, docs, P(both, None), P(both, None), P(both, None), P(both, None),
            P(None, both), P(None, both), P(None, both), P(both), P("fsdp", None),
        ),
        check_vma=False,
    )
```

```python
from functools import partial

import jax
import jax.numpy as jnp
from jax import lax
from jax.experimental import pallas as pl
from jax.experimental.pallas import tpu as pltpu
from jax.sharding import PartitionSpec as P

HEAD_DIM = 64
POS_BINS = 32
BOX_BINS = 64
TEXT_SLOTS = 512
NEG_FILL = -1000000000.0
NORM_EPS = 1e-05
BLOCK = 256
DENSE_BLOCK = 384
LANES = 128
HALF = 32
SPLIT = 1
LINES = 1
SCALE = 0.125
F32 = jnp.float32
BF16 = jnp.bfloat16
VMEM_LIMIT = 58 << 20


def dot(left, right):
    return jnp.dot(left, right, preferred_element_type=F32)


def dot_nt(left, right):
    return lax.dot_general(left, right, (((1,), (1,)), ((), ())), preferred_element_type=F32)


def params(count):
    return pltpu.CompilerParams(
        dimension_semantics=("arbitrary",) * count, vmem_limit_bytes=VMEM_LIMIT
    )


def resident(shape):
    zeros = (0,) * len(shape)
    return pl.BlockSpec(shape, lambda *_: zeros, pipeline_mode=pl.Buffered(1))


def columns(shape, place):
    return pl.BlockSpec(shape, lambda *_: (0, place), pipeline_mode=pl.Buffered(1))


def live_rows(values, rows, first):
    row = first + lax.broadcasted_iota(jnp.int32, (values.shape[0], 1), 0)
    return jnp.where(row < rows, values, jnp.zeros_like(values))


def bias_kernel(rows, len_ref, tab_ref, pos_ref, box_ref, out_ref):
    heads, chunks = out_ref.shape[1], out_ref.shape[3] // LANES
    block = pl.program_id(1)
    length = len_ref[pl.program_id(0)]
    steps = jnp.minimum(BLOCK, (rows + 7) // 8 * 8 - block * BLOCK) // 8

    def fill(step, carry):
        at = pl.ds(pl.multiple_of(step * 8, 8), 8)
        for chunk in range(chunks):
            cols = slice(chunk * LANES, (chunk + 1) * LANES)
            picks = (
                box_ref[0, 0, 0, at, cols] & (BOX_BINS - 1),
                (box_ref[0, 0, 1, at, cols] & (BOX_BINS - 1)) | BOX_BINS,
                pos_ref[0, 0, at, cols] & (POS_BINS - 1),
            )
            slot = chunk * LANES + lax.broadcasted_iota(jnp.int32, (8, LANES), 1)
            valid = ((slot >= TEXT_SLOTS) & (slot < rows)) | (slot < length)
            totals = [None] * heads
            for which, pick in enumerate(picks):
                for head in range(heads):
                    line = head + (heads if which == 2 else 0)
                    entries = jnp.broadcast_to(tab_ref[line : line + 1, :], (8, LANES))
                    term = jnp.take_along_axis(entries, pick, axis=1)
                    totals[head] = term if which == 0 else totals[head] + term
            for head in range(heads):
                out_ref[0, head, at, cols] = jnp.where(valid, totals[head], NEG_FILL)
        return carry

    def blank(step, carry):
        at = pl.ds(pl.multiple_of(step * 8, 8), 8)
        for head in range(heads):
            out_ref[0, head, at, :] = jnp.zeros((8, chunks * LANES), F32)
        return carry

    lax.fori_loop(0, steps, fill, 0)
    lax.fori_loop(steps, BLOCK // 8, blank, 0)


def bias_rows(lengths, entries, pos_buckets, box_buckets, heads):
    docs, rows = pos_buckets.shape[0], pos_buckets.shape[2]
    padded = pl.cdiv(rows, BLOCK) * BLOCK
    return pl.pallas_call(
        partial(bias_kernel, rows),
        out_shape=jax.ShapeDtypeStruct((docs, heads, padded, padded), F32),
        grid=(docs, padded // BLOCK),
        in_specs=[
            pl.BlockSpec(memory_space=pltpu.SMEM),
            resident(entries.shape),
            pl.BlockSpec((1, 1, BLOCK, padded), lambda d, i: (d, 0, i, 0)),
            pl.BlockSpec((1, 1, 2, BLOCK, padded), lambda d, i: (d, 0, 0, i, 0)),
        ],
        out_specs=pl.BlockSpec((1, heads, BLOCK, padded), lambda d, i: (d, 0, i, 0)),
        compiler_params=params(2),
        cost_estimate=pl.CostEstimate(
            flops=3 * docs * heads * rows * rows,
            transcendentals=0,
            bytes_accessed=docs * padded * padded * (4 * heads + 12),
        ),
        name="bias_rows",
    )(lengths, entries, pos_buckets, box_buckets)


def project_kernel(rows, x_ref, w_ref, vec_ref, out_ref, tok_ref):
    width = x_ref.shape[3]
    block = live_rows(x_ref[0, 0], rows, pl.program_id(1) * x_ref.shape[2])
    tok_ref[...] = block.T
    queries = dot(block, w_ref[:, :width]) + vec_ref[4:5, :]
    out_ref[0, :, :width] = queries.astype(BF16) * BF16(SCALE)
    out_ref[0, :, width : 2 * width] = dot(block, w_ref[:, width : 2 * width]).astype(BF16)
    values = dot(block, w_ref[:, 2 * width :]) + vec_ref[5:6, :]
    out_ref[0, :, 2 * width :] = values.astype(BF16)


def project(layer_input, w_mixed, vectors):
    docs, unused, rows, width = layer_input.shape
    padded = pl.cdiv(rows, BLOCK) * BLOCK
    return pl.pallas_call(
        partial(project_kernel, rows),
        out_shape=(
            jax.ShapeDtypeStruct((docs, padded, 3 * width), BF16),
            jax.ShapeDtypeStruct((width, docs * padded), BF16),
        ),
        grid=(docs, padded // DENSE_BLOCK),
        in_specs=[
            pl.BlockSpec((1, 1, DENSE_BLOCK, width), lambda d, i: (d, 0, i, 0)),
            columns((width, 3 * width), 0),
            resident(vectors.shape),
        ],
        out_specs=(
            pl.BlockSpec((1, DENSE_BLOCK, 3 * width), lambda d, i: (d, i, 0)),
            pl.BlockSpec((width, DENSE_BLOCK), lambda d, i: (0, d * (padded // DENSE_BLOCK) + i)),
        ),
        compiler_params=params(2),
        name="project",
    )(layer_input, w_mixed, vectors)


def attend_kernel(q_ref, k_ref, v_ref, bias_ref, probs_ref, out_ref, turned_ref):
    lane = lax.broadcasted_iota(jnp.int32, (1, LANES), 1)
    for pair in range(q_ref.shape[2] // LANES):
        cols = slice(pair * LANES, (pair + 1) * LANES)
        queries, key_rows, values = q_ref[0, :, cols], k_ref[0, :, cols], v_ref[0, :, cols]
        total = None
        for half in range(2):
            head = 2 * pair + half
            keep = (lane < HEAD_DIM) if half == 0 else (lane >= HEAD_DIM)
            scores = dot_nt(jnp.where(keep, queries, BF16(0)), key_rows) + bias_ref[0, head]
            top = jnp.max(scores, axis=-1, keepdims=True)
            powers = jnp.exp(scores - top)
            share = 1.0 / jnp.sum(powers, axis=-1, keepdims=True)
            probs = (powers * share).astype(BF16)
            probs_ref[0, head] = probs
            part = dot(probs, jnp.where(keep, values, BF16(0)))
            total = part if half == 0 else total + part
        low = total.astype(BF16)
        out_ref[0, :, cols] = low
        turned_ref[cols, :] = low.T


def attend(qkv, bias):
    docs, padded, width = qkv.shape[0], qkv.shape[1], qkv.shape[2] // 3
    heads = bias.shape[1]
    return pl.pallas_call(
        attend_kernel,
        out_shape=(
            jax.ShapeDtypeStruct((docs, heads, padded, padded), BF16),
            jax.ShapeDtypeStruct((docs, padded, width), BF16),
            jax.ShapeDtypeStruct((width, docs * padded), BF16),
        ),
        grid=(docs, padded // BLOCK),
        in_specs=[
            pl.BlockSpec((1, BLOCK, width), lambda d, i: (d, i, 0)),
            pl.BlockSpec((1, padded, width), lambda d, i: (d, 0, 1)),
            pl.BlockSpec((1, padded, width), lambda d, i: (d, 0, 2)),
            pl.BlockSpec((1, heads, BLOCK, padded), lambda d, i: (d, 0, i, 0)),
        ],
        out_specs=(
            pl.BlockSpec((1, heads, BLOCK, padded), lambda d, i: (d, 0, i, 0)),
            pl.BlockSpec((1, BLOCK, width), lambda d, i: (d, i, 0)),
            pl.BlockSpec((width, BLOCK), lambda d, i: (0, d * (padded // BLOCK) + i)),
        ),
        compiler_params=params(2),
        name="attend",
    )(qkv, qkv, qkv, bias)


def norm(rows_in):
    centre = rows_in - jnp.mean(rows_in, axis=-1, keepdims=True)
    inv_std = lax.rsqrt(jnp.mean(centre * centre, axis=-1, keepdims=True) + NORM_EPS)
    return centre * inv_std, inv_std


def norm_back(grad_in, normed, inv_std, gain_row):
    scaled = grad_in * gain_row
    return inv_std * (
        scaled
        - jnp.mean(scaled, axis=-1, keepdims=True)
        - normed * jnp.mean(scaled * normed, axis=-1, keepdims=True)
    )


def dense_kernel(
    rows, x_ref, o_ref, cot_ref, wo_ref, wu_ref, wd_ref, vec_ref, upb_ref,
    y_ref, dr_ref, left_ref, du_ref, df_ref, db_ref, do_ref, sums_ref, upsum_ref,
    slope_ref,
):
    width, hidden = wu_ref.shape
    first = pl.program_id(1) * x_ref.shape[2]
    vec = vec_ref[...]

    @pl.when((pl.program_id(0) == 0) & (pl.program_id(1) == 0))
    def _():
        sums_ref[...] = jnp.zeros_like(sums_ref)
        upsum_ref[...] = jnp.zeros_like(upsum_ref)

    tok = live_rows(x_ref[0, 0], rows, first).astype(F32)
    normed_one, inv_one = norm(tok + dot(o_ref[0], wo_ref[...]) + vec[6:7])
    state = normed_one * vec[0:1] + vec[2:3]
    low = state.astype(BF16)
    left_ref[0:width, :] = low.T
    second = state + vec[7:8]
    for part in range(hidden // width):
        cols = slice(part * width, (part + 1) * width)
        upper = dot(low, wu_ref[:, cols]) + upb_ref[:, cols]
        cdf = 0.5 * (1.0 + lax.erf(upper * (0.5**0.5)))
        slope_ref[:, cols] = cdf + upper * (jnp.exp(-0.5 * upper * upper) * 0.3989422804014327)
        active = (upper * cdf).astype(BF16)
        left_ref[(part + 1) * width : (part + 2) * width, :] = active.T
        second = second + dot(active, wd_ref[cols, :])
    normed_two, inv_two = norm(second)
    y_ref[0, 0] = (normed_two * vec[1:2] + vec[3:4]).astype(BF16)
    grad = live_rows(cot_ref[0, 0], rows, first).astype(F32)
    sums_ref[1:2, :] += jnp.sum(grad * normed_two, axis=0, keepdims=True)
    sums_ref[3:4, :] += jnp.sum(grad, axis=0, keepdims=True)
    d_two = norm_back(grad, normed_two, inv_two, vec[1:2])
    d_ffn = d_two.astype(BF16)
    df_ref[0] = d_ffn
    sums_ref[7:8, :] += jnp.sum(d_ffn.astype(F32), axis=0, keepdims=True)
    back = d_two
    for part in range(hidden // width):
        cols = slice(part * width, (part + 1) * width)
        d_upper = (dot_nt(d_ffn, wd_ref[cols, :]) * slope_ref[:, cols]).astype(BF16)
        du_ref[0, :, cols] = d_upper
        upsum_ref[:, cols] += jnp.sum(d_upper.astype(F32), axis=0, keepdims=True)
        back = back + dot_nt(d_upper, wu_ref[:, cols])
    sums_ref[0:1, :] += jnp.sum(back * normed_one, axis=0, keepdims=True)
    sums_ref[2:3, :] += jnp.sum(back, axis=0, keepdims=True)
    d_one = norm_back(back, normed_one, inv_one, vec[0:1])
    dr_ref[0] = d_one
    d_branch = d_one.astype(BF16)
    db_ref[0] = d_branch
    sums_ref[6:7, :] += jnp.sum(d_branch.astype(F32), axis=0, keepdims=True)
    do_ref[0] = dot_nt(d_branch, wo_ref[...]).astype(BF16)


def dense(layer_input, attended, cotangent, w_mixed, w_down, vectors, up_row):
    docs, unused, rows, width = layer_input.shape
    padded, hidden = attended.shape[1], w_down.shape[0]
    ragged = pl.BlockSpec((1, 1, DENSE_BLOCK, width), lambda d, i: (d, 0, i, 0))
    narrow = pl.BlockSpec((1, DENSE_BLOCK, width), lambda d, i: (d, i, 0))
    wide = pl.BlockSpec((1, DENSE_BLOCK, hidden), lambda d, i: (d, i, 0))

    def turned(lines):
        return pl.BlockSpec(
            (lines, DENSE_BLOCK), lambda d, i: (0, d * (padded // DENSE_BLOCK) + i)
        )

    def rows_of(columns, dtype):
        return jax.ShapeDtypeStruct((docs, padded, columns), dtype)

    return pl.pallas_call(
        partial(dense_kernel, rows),
        out_shape=(
            jax.ShapeDtypeStruct(layer_input.shape, BF16),
            rows_of(width, F32),
            jax.ShapeDtypeStruct((width + hidden, docs * padded), BF16),
            rows_of(hidden, BF16),
            rows_of(width, BF16),
            rows_of(width, BF16),
            rows_of(width, BF16),
            jax.ShapeDtypeStruct((8, width), F32),
            jax.ShapeDtypeStruct((1, hidden), F32),
        ),
        grid=(docs, padded // DENSE_BLOCK),
        in_specs=[
            ragged, narrow, ragged,
            columns((width, width), 3), columns((width, hidden), 4 * width // hidden),
            resident(w_down.shape),
            resident(vectors.shape), resident(up_row.shape),
        ],
        out_specs=(
            ragged, narrow, turned(width + hidden), wide, narrow, narrow, narrow,
            pl.BlockSpec((8, width), lambda d, i: (0, 0)),
            pl.BlockSpec((1, hidden), lambda d, i: (0, 0)),
        ),
        scratch_shapes=[pltpu.VMEM((DENSE_BLOCK, hidden), F32)],
        compiler_params=params(2),
        name="dense",
    )(layer_input, attended, cotangent, w_mixed, w_mixed, w_down, vectors, up_row)


def attend_back_kernel(
    rows, q_ref, k_ref, v_ref, probs_ref, do_ref, pos_ref, box_ref, dm_ref, bins_ref, line_ref,
    dk_ref, dv_ref, ds_ref, acc_ref, picks_ref,
):
    block, width = pl.program_id(1), q_ref.shape[2]
    padded = k_ref.shape[1]
    lane = lax.broadcasted_iota(jnp.int32, (1, LANES), 1)

    @pl.when((pl.program_id(0) == 0) & (block == 0))
    def _():
        acc_ref[...] = jnp.zeros_like(acc_ref)
        line_ref[...] = jnp.zeros_like(line_ref)
        ds_ref[...] = jnp.zeros_like(ds_ref)

    @pl.when(block == 0)
    def _():
        dk_ref[...] = jnp.zeros_like(dk_ref)
        dv_ref[...] = jnp.zeros_like(dv_ref)

    own = pl.ds(pl.multiple_of(block * BLOCK, BLOCK), BLOCK)
    for pair in range(width // LANES):
        cols = slice(pair * LANES, (pair + 1) * LANES)
        queries, key_rows, values = q_ref[0, :, cols], k_ref[0, :, cols], v_ref[0, :, cols]
        grads = do_ref[0, :, cols]
        turned_q, turned_g = queries.T, grads.T
        total = None
        for half in range(2):
            head = 2 * pair + half
            keep = (lane < HEAD_DIM) if half == 0 else (lane >= HEAD_DIM)
            part = slice(half * HEAD_DIM, (half + 1) * HEAD_DIM)
            lines = slice(head * HEAD_DIM, (head + 1) * HEAD_DIM)
            low = probs_ref[0, head]
            probs = low.astype(F32)
            dprobs = dot_nt(jnp.where(keep, grads, BF16(0)), values)
            delta = jnp.sum(probs * dprobs, axis=-1, keepdims=True)
            dscore = probs * (dprobs - delta)
            for chunk in range(padded // LANES):
                ds_ref[chunk, pl.ds(head, BLOCK, stride=16), :] = dscore[
                    :, chunk * LANES : (chunk + 1) * LANES
                ]
            dlow = dscore.astype(BF16)
            piece = dot(dlow, jnp.where(keep, key_rows, BF16(0)))
            total = piece if half == 0 else total + piece
            dk_ref[lines, :] += dot(turned_q[part, :], dlow)
            dv_ref[lines, :] += dot(turned_g[part, :], low)
        dm_ref[0, own, cols] = (total * SCALE).astype(BF16)

    group = 32
    low_bins = lax.broadcasted_iota(jnp.int32, (HALF, LANES), 0).astype(BF16)

    def hits(picks, bins):
        low = picks.astype(BF16)
        return jnp.concatenate(
            [
                jnp.where(low_bins[first : first + 16] == low, BF16(1), BF16(0))
                for first in range(0, bins, 16)
            ],
            axis=0,
        )

    for place, (picks, bits) in enumerate(
        (
            (box_ref[0, 0, 0], BOX_BINS),
            (box_ref[0, 0, 1], BOX_BINS),
            (pos_ref[0, 0], POS_BINS),
        )
    ):
        half = bits // 2
        for chunk in range(padded // LANES):
            part = picks[:, chunk * LANES : (chunk + 1) * LANES] & (bits - 1)
            picks_ref[2 * place, chunk] = (part & (half - 1)).astype(F32)
            picks_ref[2 * place + 1, chunk] = (part >> (half.bit_length() - 1)).astype(F32)

    def count(step, carry):
        total = None
        for line in range(0, group, LINES):
            left, right = [], []
            for own in range(LINES):
                row = step * group + line + own
                here = pl.ds(pl.multiple_of(row * 16, 16), 16)
                again = pl.ds(row, 16, stride=0)
                for chunk in range(padded // LANES):
                    base = ds_ref[chunk, here, :]
                    left.append(
                        jnp.concatenate(
                            [base.astype(BF16)]
                            + [
                                (base * picks_ref[2 * place + 1, chunk, again, :]).astype(BF16)
                                for place in range(3)
                            ],
                            axis=0,
                        )
                    )
                    right.append(
                        jnp.concatenate(
                            [
                                hits(picks_ref[2 * place, chunk, again, :], bins)
                                for place, bins in enumerate((HALF, HALF, HALF // 2))
                            ],
                            axis=0,
                        )
                    )
            part = dot_nt(jnp.concatenate(left, axis=1), jnp.concatenate(right, axis=1))
            total = part if total is None else total + part
        acc_ref[0, :, : total.shape[1]] += total
        return carry

    live = jnp.minimum(BLOCK, (rows + group - 1) // group * group - block * BLOCK)
    lax.fori_loop(0, live // group, count, 0)

    @pl.when(block == pl.num_programs(1) - 1)
    def _():
        dm_ref[0, :, width : 2 * width] = dk_ref[...].astype(BF16).T
        dm_ref[0, :, 2 * width :] = dv_ref[...].astype(BF16).T
        bins_ref[...] = jnp.sum(acc_ref[...], axis=0)
        line_ref[...] += dot(jnp.ones((16, padded), BF16), dm_ref[0])[0:8]


def attend_back(qkv, probs, d_attended, pos_buckets, box_buckets):
    docs, padded, width = qkv.shape[0], qkv.shape[1], qkv.shape[2] // 3
    heads, rows = probs.shape[1], pos_buckets.shape[2]
    return pl.pallas_call(
        partial(attend_back_kernel, rows),
        out_shape=(
            jax.ShapeDtypeStruct((docs, padded, 3 * width), BF16),
            jax.ShapeDtypeStruct((64, LANES), F32),
            jax.ShapeDtypeStruct((8, 3 * width), F32),
        ),
        grid=(docs, padded // BLOCK),
        in_specs=[
            pl.BlockSpec((1, BLOCK, width), lambda d, i: (d, i, 0)),
            pl.BlockSpec((1, padded, width), lambda d, i: (d, 0, 1)),
            pl.BlockSpec((1, padded, width), lambda d, i: (d, 0, 2)),
            pl.BlockSpec((1, heads, BLOCK, padded), lambda d, i: (d, 0, i, 0)),
            pl.BlockSpec((1, BLOCK, width), lambda d, i: (d, i, 0)),
            pl.BlockSpec((1, 1, BLOCK, padded), lambda d, i: (d, 0, i, 0)),
            pl.BlockSpec((1, 1, 2, BLOCK, padded), lambda d, i: (d, 0, 0, i, 0)),
        ],
        out_specs=(
            pl.BlockSpec((1, padded, 3 * width), lambda d, i: (d, 0, 0)),
            pl.BlockSpec((64, LANES), lambda d, i: (0, 0)),
            pl.BlockSpec((8, 3 * width), lambda d, i: (0, 0)),
        ),
        scratch_shapes=[
            pltpu.VMEM((width, padded), F32),
            pltpu.VMEM((width, padded), F32),
            pltpu.VMEM((padded // LANES, BLOCK * 16, LANES), F32),
            pltpu.VMEM((SPLIT, 64, LANES), F32),
            pltpu.VMEM((6, padded // LANES, BLOCK, LANES), F32),
        ],
        compiler_params=params(2),
        name="attend_back",
    )(qkv, qkv, qkv, probs, d_attended, pos_buckets, box_buckets)


def table_entries(table):
    heads = table.shape[1]
    lines = table.astype(F32).T * SCALE
    boxes = lines[:, POS_BINS:]
    spots = jnp.pad(lines[:, :POS_BINS], ((0, 0), (0, LANES - POS_BINS)))
    return jnp.concatenate([boxes, spots], axis=0).reshape(2 * heads, LANES)


def table_grad(bins, heads):
    base, upper = bins[:heads], (bins[16 : 16 + heads], bins[32 : 32 + heads], bins[48 : 48 + heads])
    pieces = []
    for which, (first, size) in enumerate(((0, HALF), (HALF, HALF), (2 * HALF, HALF // 2))):
        high = upper[which][:, first : first + size]
        pieces.append(jnp.concatenate([base[:, first : first + size] - high, high], axis=1))
    return jnp.concatenate([pieces[2], pieces[0], pieces[1]], axis=1).T * SCALE


def weight_grads(attended, d_branch, left, d_upper, d_ffn, devices):
    width, rows = attended.shape
    own, fold = width // devices, d_upper.shape[1] // width
    share = devices // fold
    steps = 1 + 2 * fold

    def kernel(
        l_ref, u_ref, a_ref, b_ref, f_ref, out_ref,
        attended_ref, branch_ref, ffn_ref, stage_ref, sems, load_sems,
    ):
        step = pl.program_id(0)
        slot = step % 2
        loads = [
            pltpu.make_async_copy(source, target, load_sems.at[place])
            for place, (source, target) in enumerate(
                ((f_ref, ffn_ref), (a_ref, attended_ref), (b_ref, branch_ref))
            )
        ]

        def flat_copy(part, spot):
            cols = pl.ds(pl.multiple_of(part * width, width), width)
            return pltpu.make_async_copy(
                stage_ref.at[spot], out_ref.at[:, :, cols], sems.at[spot, 0]
            )

        def fold_copy(where, spot, part):
            block = where - fold
            cols = pl.ds((1 + fold + part) * width, width)
            return pltpu.make_async_copy(
                stage_ref.at[spot].reshape(share, fold, own, width).at[:, part],
                out_ref.at[pl.ds(block * share, share), :, cols],
                sems.at[spot, part],
            )

        def wait_for(where, spot):
            @pl.when(where < fold)
            def _():
                flat_copy(where + 1, spot).wait()

            @pl.when((where >= fold) & (where < 2 * fold))
            def _():
                for part in range(fold):
                    fold_copy(where, spot, part).wait()

        @pl.when(step == 0)
        def _():
            for load in loads:
                load.start()

        @pl.when(step >= 2)
        def _():
            wait_for(step - 2, slot)

        def put(value):
            stage_ref[slot] = value.reshape(devices, own, width).astype(BF16)

        @pl.when(step < fold)
        def _():
            put(dot(l_ref[...], u_ref[...]))
            flat_copy(step + 1, slot).start()

        @pl.when(step == fold)
        def _():
            loads[0].wait()

        @pl.when((step >= fold) & (step < 2 * fold))
        def _():
            put(dot(l_ref[...], ffn_ref[...]))
            for part in range(fold):
                fold_copy(step, slot, part).start()

        @pl.when(step == 2 * fold)
        def _():
            loads[1].wait()
            loads[2].wait()
            put(dot(attended_ref[...], branch_ref[...]))
            flat_copy(0, slot).start()
            wait_for(step - 1, 1 - slot)
            flat_copy(0, slot).wait()

    away = pl.BlockSpec(memory_space=pl.ANY)
    return pl.pallas_call(
        kernel,
        out_shape=jax.ShapeDtypeStruct((devices, own, (1 + 2 * fold) * width), BF16),
        grid=(steps,),
        in_specs=[
            pl.BlockSpec((width, rows), lambda p: (jnp.clip(p - fold + 1, 0, fold), 0)),
            pl.BlockSpec((rows, width), lambda p: (0, jnp.minimum(p, fold - 1))),
            away,
            away,
            away,
        ],
        out_specs=away,
        scratch_shapes=[
            pltpu.VMEM((width, rows), BF16),
            pltpu.VMEM((rows, width), BF16),
            pltpu.VMEM((rows, width), BF16),
            pltpu.VMEM((2, devices, own, width), BF16),
            pltpu.SemaphoreType.DMA((2, fold)),
            pltpu.SemaphoreType.DMA((3,)),
        ],
        compiler_params=params(1),
        cost_estimate=pl.CostEstimate(
            flops=2 * rows * width * width * steps, transcendentals=0,
            bytes_accessed=2 * rows * width * (steps + 3),
        ),
        name="weight_grads",
    )(left, d_upper, attended, d_branch, d_ffn)


ORDERS = ((3, 1, 2, 0), (3, 2, 1, 0)) * 3
MATRICES = 3
TABLE_LINES = 64
MESH = pl.DeviceIdType.MESH


def remaining(part, level):
    return [axis for axis in range(4) if axis not in ORDERS[part][:level]]


def tail_kernel(
    dims, w_ref, tok_ref, mixed_ref, one_ref, small_ref, grad_ref, sums_ref, input_ref, *scratch
):
    parts, width = len(ORDERS), tok_ref.shape[0]
    cut = MATRICES * width // parts
    holders = [scratch[8 * part : 8 * part + 4] for part in range(parts)]
    inboxes = [scratch[8 * part + 4 : 8 * part + 8] for part in range(parts)]
    (
        turned, mixed, weights, kept, stage, own_sums, got_sums,
        send_sems, recv_sems, load_sems, keep_sems, store_sems,
    ) = scratch[8 * parts :]
    deep, across, along, cores = dims
    dp, fsdp = lax.axis_index("dp"), lax.axis_index("fsdp")
    mine = (dp // across, dp % across, fsdp // cores, fsdp % cores)
    docs, padded = one_ref.shape[0], one_ref.shape[1]
    rows, block = input_ref.shape[1], kept.shape[1]
    own_lines = sums_ref.shape[0] - TABLE_LINES

    def peer(axis, step):
        place = list(mine)
        place[axis] = (place[axis] + step) % dims[axis]
        return place[axis], (place[0] * across + place[1], place[2] * cores + place[3])

    loads = [pltpu.make_async_copy(tok_ref, turned, load_sems.at[0])]
    for part in range(MATRICES):
        loads.append(
            pltpu.make_async_copy(
                mixed_ref.at[:, pl.ds(part * width, width)], mixed.at[part], load_sems.at[1 + part]
            )
        )
    loads.append(
        pltpu.make_async_copy(
            w_ref.at[:, pl.ds(0, MATRICES * width)], weights, load_sems.at[1 + MATRICES]
        )
    )
    for load in loads:
        load.start()

    barrier = pltpu.get_barrier_semaphore()
    partners = 0
    for axis in range(4):
        for step in range(1, dims[axis]):
            pl.semaphore_signal(barrier, inc=1, device_id=peer(axis, step)[1], device_id_type=MESH)
            partners += 1
    pl.semaphore_wait(barrier, partners)

    flying = {}

    def launch(lane, axis, source, target):
        copies = []
        for step in range(1, dims[axis]):
            place, device = peer(axis, step)
            copies.append(
                pltpu.make_async_remote_copy(
                    src_ref=source(place),
                    dst_ref=target(step - 1),
                    send_sem=send_sems.at[lane, step - 1],
                    recv_sem=recv_sems.at[lane, step - 1],
                    device_id=device,
                    device_id_type=MESH,
                )
            )
        for copy in copies:
            copy.start()
        flying[lane] = copies

    def land(lane):
        for copy in flying.pop(lane):
            copy.wait()

    def joined(own, others):
        total = own.astype(F32)
        for other in others:
            total = total + other.astype(F32)
        return total

    def send(part, level):
        axis, axes = ORDERS[part][level], remaining(part, level)

        def source(place):
            return holders[part][level].at[
                tuple(place if item == axis else slice(None) for item in axes)
            ]

        launch(4 * part + level, axis, source, lambda slot: inboxes[part][level].at[slot])

    def join(part, level):
        land(4 * part + level)
        axis, axes = ORDERS[part][level], remaining(part, level)
        source, box = holders[part][level], inboxes[part][level]
        left = [item for item in axes if item != axis]
        count = dims[axis] - 1
        if not left:
            grad_ref[:, part * cut : (part + 1) * cut] = joined(
                source[mine[axis]], [box[slot] for slot in range(count)]
            )
            return
        spots = [()]
        for item in left[1:]:
            spots = [spot + (place,) for spot in spots for place in range(dims[item])]

        def add(k, carry):
            for spot in spots:
                there = (k,) + spot
                where = dict(zip(left, there))
                where[axis] = mine[axis]
                own = tuple(where[item] for item in axes)
                holders[part][level + 1][there] = joined(
                    source[own], [box[(slot,) + there] for slot in range(count)]
                ).astype(BF16)
            return carry

        lax.fori_loop(0, dims[left[0]], add, 0)
        send(part, level + 1)

    small_order = (3, 1, 2, 0)
    own_bins = deep * own_lines

    def small_send(level):
        axis, lane = small_order[level], 4 * parts + level
        if level < 3:
            launch(lane, axis, lambda place: own_sums.at[level], lambda slot: got_sums.at[level, slot])
            return
        launch(
            lane, axis,
            lambda place: own_sums.at[3, pl.ds(pl.multiple_of(place * own_lines, 8), own_lines)],
            lambda slot: got_sums.at[3, slot, pl.ds(0, own_lines)],
        )
        launch(
            lane + 1, axis,
            lambda place: own_sums.at[3, pl.ds(own_bins, TABLE_LINES)],
            lambda slot: got_sums.at[3, slot, pl.ds(own_bins, TABLE_LINES)],
        )

    def small_join(level):
        axis, lane = small_order[level], 4 * parts + level
        land(lane)
        slots = range(dims[axis] - 1)
        if level < 3:
            own_sums[level + 1] = joined(own_sums[level], [got_sums[level, slot] for slot in slots])
            small_send(level + 1)
            return
        land(lane + 1)
        here = pl.ds(pl.multiple_of(mine[0] * own_lines, 8), own_lines)
        sums_ref[0:own_lines] = joined(
            own_sums[3, here], [got_sums[3, slot, 0:own_lines] for slot in slots]
        )
        last = slice(own_bins, own_bins + TABLE_LINES)
        sums_ref[own_lines:] = joined(own_sums[3, last], [got_sums[3, slot, last] for slot in slots])

    spans = [(doc, first) for doc in range(docs) for first in range(0, padded, block)]

    def keep(step):
        doc, first = spans[step]
        return pltpu.make_async_copy(
            one_ref.at[doc, pl.ds(first, block), :], kept.at[step % 2], keep_sems.at[step % 2]
        )

    def store(step):
        doc, first = spans[step]
        count = min(block, rows - first)
        return pltpu.make_async_copy(
            stage.at[step % 2, pl.ds(0, count)],
            input_ref.at[doc, pl.ds(first, count)],
            store_sems.at[step % 2],
        )

    def input_step(step):
        doc, first = spans[step]
        if step == 0:
            loads[1 + MATRICES].wait()
            keep(0).start()
        if step + 1 < len(spans):
            keep(step + 1).start()
        keep(step).wait()
        if step >= 2:
            store(step - 2).wait()
        at = pl.ds(doc * padded + first, block)
        total = kept[step % 2]
        for part in range(MATRICES):
            total = total + dot_nt(
                mixed[part, at, :], weights[:, part * width : (part + 1) * width]
            )
        stage[step % 2, :, 0, :] = total
        store(step).start()

    loads[0].wait()
    own_sums[0] = small_ref[...]
    small_send(0)

    def multiply(matrix):
        loads[1 + matrix].wait()
        for part in range(matrix * parts // MATRICES, (matrix + 1) * parts // MATRICES):
            first = part * cut - matrix * width
            block_rows = dot(turned[...], mixed[matrix, :, first : first + cut])
            holders[part][0][...] = block_rows.reshape(holders[part][0].shape).astype(BF16)
            send(part, 0)

    multiply(0)
    small_join(0)
    multiply(1)
    join(0, 0)
    join(1, 0)
    multiply(2)
    small_join(1)
    join(2, 0)
    join(3, 0)
    join(0, 1)
    join(1, 1)
    join(4, 0)
    join(5, 0)
    small_join(2)
    input_step(0)
    join(2, 1)
    join(3, 1)
    join(0, 2)
    join(1, 2)
    input_step(1)
    join(4, 1)
    join(5, 1)
    join(2, 2)
    join(3, 2)
    input_step(2)
    small_join(3)
    join(4, 2)
    join(5, 2)
    input_step(3)
    for part in range(parts):
        join(part, 3)
    for step in range(max(len(spans) - 2, 0), len(spans)):
        store(step).wait()


def split_mesh(dp, fsdp):
    across = 1 << ((dp.bit_length() - 1) // 2)
    across = across if dp % across == 0 else 1
    cores = 2 if fsdp % 2 == 0 else 1
    return dp // across, across, fsdp // cores, cores


def tail(w_mixed, tok, d_mixed, d_one, small, rows, dims):
    docs, padded, width = d_one.shape
    parts = len(ORDERS)
    cut = MATRICES * width // parts
    devices = dims[0] * dims[1] * dims[2] * dims[3]
    own = width // devices
    lines = (small.shape[0] - TABLE_LINES) // dims[0] + TABLE_LINES
    any_space = pl.BlockSpec(memory_space=pl.ANY)
    vmem = pl.BlockSpec(memory_space=pltpu.VMEM)
    scratch = []
    for part in range(parts):
        boxes = []
        for level in range(4):
            axes = remaining(part, level)
            axis = ORDERS[part][level]
            scratch.append(pltpu.VMEM(tuple(dims[item] for item in axes) + (own, cut), BF16))
            boxes.append(
                pltpu.VMEM(
                    (max(dims[axis] - 1, 1),)
                    + tuple(dims[item] for item in axes if item != axis)
                    + (own, cut),
                    BF16,
                )
            )
        scratch += boxes
    most = max(max(dims) - 1, 1)
    flat = docs * padded
    scratch += [
        pltpu.VMEM((width, flat), BF16),
        pltpu.VMEM((MATRICES, flat, width), BF16),
        pltpu.VMEM((width, MATRICES * width), BF16),
        pltpu.VMEM((2, DENSE_BLOCK, width), F32),
        pltpu.VMEM((2, DENSE_BLOCK, 1, width), F32),
        pltpu.VMEM((4,) + small.shape, F32),
        pltpu.VMEM((4, most) + small.shape, F32),
        pltpu.SemaphoreType.DMA((4 * parts + 5, most)),
        pltpu.SemaphoreType.DMA((4 * parts + 5, most)),
        pltpu.SemaphoreType.DMA((MATRICES + 2,)),
        pltpu.SemaphoreType.DMA((2,)),
        pltpu.SemaphoreType.DMA((2,)),
    ]
    return pl.pallas_call(
        partial(tail_kernel, dims),
        out_shape=(
            jax.ShapeDtypeStruct((own, MATRICES * width), F32),
            jax.ShapeDtypeStruct((lines, LANES), F32),
            jax.ShapeDtypeStruct((docs, rows, 1, width), F32),
        ),
        in_specs=[any_space, any_space, any_space, any_space, vmem],
        out_specs=(vmem, vmem, any_space),
        scratch_shapes=scratch,
        compiler_params=pltpu.CompilerParams(
            collective_id=0, has_side_effects=True, vmem_limit_bytes=VMEM_LIMIT
        ),
        name="tail",
    )(w_mixed, tok, d_mixed, d_one, small)


def handed_on(rows_out):
    docs, count, unused, width = rows_out.shape
    pieces = 4
    edges = [count * piece // pieces for piece in range(pieces + 1)]

    def kernel(in_ref, out_ref, held_ref, in_sems, out_sems):
        arrivals, departures = [], []
        for doc in range(docs):
            for piece in range(pieces):
                at = pl.ds(edges[piece], edges[piece + 1] - edges[piece])
                held = held_ref.at[doc, at]
                arrivals.append(
                    pltpu.make_async_copy(in_ref.at[doc, at], held, in_sems.at[doc, piece])
                )
                departures.append(
                    pltpu.make_async_copy(held, out_ref.at[doc, at], out_sems.at[doc, piece])
                )
        for copy in arrivals:
            copy.start()
        for arrival, departure in zip(arrivals, departures):
            arrival.wait()
            departure.start()
        for copy in departures:
            copy.wait()

    return pl.pallas_call(
        kernel,
        out_shape=jax.ShapeDtypeStruct(rows_out.shape, rows_out.dtype),
        in_specs=[pl.BlockSpec(memory_space=pl.ANY)],
        out_specs=pl.BlockSpec(memory_space=pl.ANY),
        scratch_shapes=[
            pltpu.VMEM(rows_out.shape, rows_out.dtype),
            pltpu.SemaphoreType.DMA((docs, pieces)),
            pltpu.SemaphoreType.DMA((docs, pieces)),
        ],
        compiler_params=pltpu.CompilerParams(vmem_limit_bytes=VMEM_LIMIT),
        name="handed_on",
    )(rows_out)


def packed_sums(sums, up_sum, bins, deep):
    width, hidden = sums.shape[1], up_sum.shape[1]
    sums = jnp.transpose(sums.reshape(8, deep, width // deep), (1, 0, 2)).reshape(deep, -1)
    lines = jnp.concatenate([sums, up_sum.reshape(deep, hidden // deep)], axis=1)
    share = pl.cdiv(lines.shape[1], 8 * LANES) * 8 * LANES
    lines = jnp.pad(lines, ((0, 0), (0, share - lines.shape[1])))
    return jnp.concatenate([lines.reshape(-1, LANES), bins], axis=0)


def small_results(packed, width, hidden, heads, deep, own, rank):
    flat = packed[:-TABLE_LINES].reshape(-1)
    count, more = 8 * width // deep, hidden // deep
    sums = lax.dynamic_slice_in_dim(flat[:count].reshape(8, -1), rank * own, own, 1)
    fold = hidden // width * own
    up_sum = lax.dynamic_slice_in_dim(flat[count : count + more], rank * fold, fold, 0)
    return sums, up_sum, table_grad(packed[-TABLE_LINES:], heads)


def local_step(dims, lengths, pos_buckets, box_buckets, layer_input, cotangent, w_mixed, w_down, vectors, up_row, table):
    heads, width = table.shape[1], layer_input.shape[3]
    docs, rows = layer_input.shape[0], layer_input.shape[2]
    bias = bias_rows(lengths, table_entries(table), pos_buckets, box_buckets, heads)
    qkv, tok = project(layer_input, w_mixed, vectors)
    probs, attended, turned = attend(qkv, bias)
    result, d_one, left, d_upper, d_ffn, d_branch, d_attended, sums, up_sum = dense(
        layer_input, attended, cotangent, w_mixed, w_down, vectors, up_row
    )

    def flat(item):
        return item.reshape(-1, item.shape[-1])

    d_weights = weight_grads(
        turned, flat(d_branch), left, flat(d_upper), flat(d_ffn), dims[0] * dims[1] * dims[2] * dims[3]
    )
    d_mixed, bins, line = attend_back(qkv, probs, d_attended, pos_buckets, box_buckets)
    sums = jnp.concatenate(
        [sums[:4], line[:1, :width], line[:1, 2 * width :], sums[6:]], axis=0
    )
    packed = packed_sums(sums, up_sum, bins, dims[0])
    return result, d_weights, (w_mixed, tok, flat(d_mixed), d_one, packed, rows, dims)


def body(
    layer_input, text_lengths, pos_buckets, box_buckets, w_qkv, w_out, w_up, w_down,
    norm_gains, norm_shifts, proj_biases, up_bias, rel_tables, cotangent,
):
    axes = ("dp", "fsdp")
    width, hidden = layer_input.shape[3], w_up.shape[1]
    own = norm_gains.shape[1]
    table = lax.all_gather(rel_tables, "fsdp", axis=0, tiled=True)
    heads = table.shape[1]
    small = jnp.concatenate(
        [norm_gains.T, norm_shifts.T, proj_biases.T, up_bias.reshape(own, hidden // width)], axis=1
    )
    small = jnp.pad(small, ((0, 0), (0, LANES - small.shape[1])))
    w_mixed = lax.all_gather(
        jnp.concatenate([w_qkv, w_out, w_up, small], axis=1), axes, axis=0, tiled=True
    )
    w_down = lax.all_gather(w_down, axes, axis=0, tiled=True)
    small = w_mixed[:, 4 * width + hidden :].astype(F32)
    vectors = small[:, :8].T
    up_row = small[:, 8 : 8 + hidden // width].reshape(1, hidden)
    dims = split_mesh(lax.axis_size("dp"), lax.axis_size("fsdp"))
    result, d_weights, rest = local_step(
        dims, text_lengths[:, 0], pos_buckets, box_buckets, layer_input, cotangent, w_mixed, w_down,
        vectors, up_row, table,
    )
    d_weights = lax.psum_scatter(
        d_weights.reshape(width, -1), axes, scatter_dimension=0, tiled=True
    ).astype(F32)
    d_down = [d_weights[:, first : first + width] for first in range(width + hidden, width + 2 * hidden, width)]
    d_down = jnp.concatenate(d_down, axis=0)
    d_qkv, packed, input_grad = tail(*rest)
    rank = lax.axis_index(axes) % (width // own // dims[0])
    sums, up_sum, d_table = small_results(packed, width, hidden, heads, dims[0], own, rank)
    table_rows = rel_tables.shape[0]
    d_table = lax.dynamic_slice_in_dim(d_table, lax.axis_index("fsdp") * table_rows, table_rows, 0)
    return (
        result, jnp.transpose(handed_on(input_grad), (0, 2, 1, 3)), d_qkv, d_weights[:, :width], d_weights[:, width : width + hidden], d_down,
        sums[0:2], sums[2:4], sums[4:8], up_sum, d_table,
    )


def solution(mesh):
    both = ("dp", "fsdp")
    docs = P(None, both, None, None)
    return jax.shard_map(
        body,
        mesh=mesh,
        in_specs=(
            docs, P(None, both), docs, P(None, both, None, None, None),
            P(both, None), P(both, None), P(both, None), P(both, None),
            P(None, both), P(None, both), P(None, both), P(both), P("fsdp", None), docs,
        ),
        out_specs=(
            docs, docs, P(both, None), P(both, None), P(both, None), P(both, None),
            P(None, both), P(None, both), P(None, both), P(both), P("fsdp", None),
        ),
        check_vma=False,
    )
```

```python
from functools import partial

import jax
import jax.numpy as jnp
from jax import lax
from jax.experimental import pallas as pl
from jax.experimental.pallas import tpu as pltpu
from jax.sharding import PartitionSpec as P

HEAD_DIM = 64
POS_BINS = 32
BOX_BINS = 64
TEXT_SLOTS = 512
NEG_FILL = -1000000000.0
NORM_EPS = 1e-05
BLOCK = 256
DENSE_BLOCK = 384
LANES = 128
HALF = 32
SPLIT = 1
LINES = 1
SCALE = 0.125
F32 = jnp.float32
BF16 = jnp.bfloat16
VMEM_LIMIT = 58 << 20


def dot(left, right):
    return jnp.dot(left, right, preferred_element_type=F32)


def dot_nt(left, right):
    return lax.dot_general(left, right, (((1,), (1,)), ((), ())), preferred_element_type=F32)


def params(count):
    return pltpu.CompilerParams(
        dimension_semantics=("arbitrary",) * count, vmem_limit_bytes=VMEM_LIMIT
    )


def resident(shape):
    zeros = (0,) * len(shape)
    return pl.BlockSpec(shape, lambda *_: zeros, pipeline_mode=pl.Buffered(1))


def columns(shape, place):
    return pl.BlockSpec(shape, lambda *_: (0, place), pipeline_mode=pl.Buffered(1))


def live_rows(values, rows, first):
    row = first + lax.broadcasted_iota(jnp.int32, (values.shape[0], 1), 0)
    return jnp.where(row < rows, values, jnp.zeros_like(values))


def bias_kernel(rows, len_ref, tab_ref, pos_ref, box_ref, out_ref):
    heads, chunks = out_ref.shape[1], out_ref.shape[3] // LANES
    block = pl.program_id(1)
    length = len_ref[pl.program_id(0)]
    steps = jnp.minimum(BLOCK, (rows + 7) // 8 * 8 - block * BLOCK) // 8

    def fill(step, carry):
        at = pl.ds(pl.multiple_of(step * 8, 8), 8)
        for chunk in range(chunks):
            cols = slice(chunk * LANES, (chunk + 1) * LANES)
            picks = (
                box_ref[0, 0, 0, at, cols] & (BOX_BINS - 1),
                (box_ref[0, 0, 1, at, cols] & (BOX_BINS - 1)) | BOX_BINS,
                pos_ref[0, 0, at, cols] & (POS_BINS - 1),
            )
            slot = chunk * LANES + lax.broadcasted_iota(jnp.int32, (8, LANES), 1)
            valid = ((slot >= TEXT_SLOTS) & (slot < rows)) | (slot < length)
            totals = [None] * heads
            for which, pick in enumerate(picks):
                for head in range(heads):
                    line = head + (heads if which == 2 else 0)
                    entries = jnp.broadcast_to(tab_ref[line : line + 1, :], (8, LANES))
                    term = jnp.take_along_axis(entries, pick, axis=1)
                    totals[head] = term if which == 0 else totals[head] + term
            for head in range(heads):
                out_ref[0, head, at, cols] = jnp.where(valid, totals[head], NEG_FILL)
        return carry

    def blank(step, carry):
        at = pl.ds(pl.multiple_of(step * 8, 8), 8)
        for head in range(heads):
            out_ref[0, head, at, :] = jnp.zeros((8, chunks * LANES), F32)
        return carry

    lax.fori_loop(0, steps, fill, 0)
    lax.fori_loop(steps, BLOCK // 8, blank, 0)


def bias_rows(lengths, entries, pos_buckets, box_buckets, heads):
    docs, rows = pos_buckets.shape[0], pos_buckets.shape[2]
    padded = pl.cdiv(rows, BLOCK) * BLOCK
    return pl.pallas_call(
        partial(bias_kernel, rows),
        out_shape=jax.ShapeDtypeStruct((docs, heads, padded, padded), F32),
        grid=(docs, padded // BLOCK),
        in_specs=[
            pl.BlockSpec(memory_space=pltpu.SMEM),
            resident(entries.shape),
            pl.BlockSpec((1, 1, BLOCK, padded), lambda d, i: (d, 0, i, 0)),
            pl.BlockSpec((1, 1, 2, BLOCK, padded), lambda d, i: (d, 0, 0, i, 0)),
        ],
        out_specs=pl.BlockSpec((1, heads, BLOCK, padded), lambda d, i: (d, 0, i, 0)),
        compiler_params=params(2),
        cost_estimate=pl.CostEstimate(
            flops=3 * docs * heads * rows * rows,
            transcendentals=0,
            bytes_accessed=docs * padded * padded * (4 * heads + 12),
        ),
        name="bias_rows",
    )(lengths, entries, pos_buckets, box_buckets)


def project_kernel(rows, x_ref, w_ref, vec_ref, out_ref, tok_ref):
    width = x_ref.shape[3]
    block = live_rows(x_ref[0, 0], rows, pl.program_id(1) * x_ref.shape[2])
    tok_ref[...] = block.T
    queries = dot(block, w_ref[:, :width]) + vec_ref[4:5, :]
    out_ref[0, :, :width] = queries.astype(BF16) * BF16(SCALE)
    out_ref[0, :, width : 2 * width] = dot(block, w_ref[:, width : 2 * width]).astype(BF16)
    values = dot(block, w_ref[:, 2 * width :]) + vec_ref[5:6, :]
    out_ref[0, :, 2 * width :] = values.astype(BF16)


def project(layer_input, w_mixed, vectors):
    docs, unused, rows, width = layer_input.shape
    padded = pl.cdiv(rows, BLOCK) * BLOCK
    return pl.pallas_call(
        partial(project_kernel, rows),
        out_shape=(
            jax.ShapeDtypeStruct((docs, padded, 3 * width), BF16),
            jax.ShapeDtypeStruct((width, docs * padded), BF16),
        ),
        grid=(docs, padded // DENSE_BLOCK),
        in_specs=[
            pl.BlockSpec((1, 1, DENSE_BLOCK, width), lambda d, i: (d, 0, i, 0)),
            columns((width, 3 * width), 0),
            resident(vectors.shape),
        ],
        out_specs=(
            pl.BlockSpec((1, DENSE_BLOCK, 3 * width), lambda d, i: (d, i, 0)),
            pl.BlockSpec((width, DENSE_BLOCK), lambda d, i: (0, d * (padded // DENSE_BLOCK) + i)),
        ),
        compiler_params=params(2),
        name="project",
    )(layer_input, w_mixed, vectors)


def attend_kernel(q_ref, k_ref, v_ref, bias_ref, probs_ref, out_ref, turned_ref):
    lane = lax.broadcasted_iota(jnp.int32, (1, LANES), 1)
    for pair in range(q_ref.shape[2] // LANES):
        cols = slice(pair * LANES, (pair + 1) * LANES)
        queries, key_rows, values = q_ref[0, :, cols], k_ref[0, :, cols], v_ref[0, :, cols]
        total = None
        for half in range(2):
            head = 2 * pair + half
            keep = (lane < HEAD_DIM) if half == 0 else (lane >= HEAD_DIM)
            scores = dot_nt(jnp.where(keep, queries, BF16(0)), key_rows) + bias_ref[0, head]
            top = jnp.max(scores, axis=-1, keepdims=True)
            powers = jnp.exp(scores - top)
            share = 1.0 / jnp.sum(powers, axis=-1, keepdims=True)
            probs = (powers * share).astype(BF16)
            probs_ref[0, head] = probs
            part = dot(probs, jnp.where(keep, values, BF16(0)))
            total = part if half == 0 else total + part
        low = total.astype(BF16)
        out_ref[0, :, cols] = low
        turned_ref[cols, :] = low.T


def attend(qkv, bias):
    docs, padded, width = qkv.shape[0], qkv.shape[1], qkv.shape[2] // 3
    heads = bias.shape[1]
    return pl.pallas_call(
        attend_kernel,
        out_shape=(
            jax.ShapeDtypeStruct((docs, heads, padded, padded), BF16),
            jax.ShapeDtypeStruct((docs, padded, width), BF16),
            jax.ShapeDtypeStruct((width, docs * padded), BF16),
        ),
        grid=(docs, padded // BLOCK),
        in_specs=[
            pl.BlockSpec((1, BLOCK, width), lambda d, i: (d, i, 0)),
            pl.BlockSpec((1, padded, width), lambda d, i: (d, 0, 1)),
            pl.BlockSpec((1, padded, width), lambda d, i: (d, 0, 2)),
            pl.BlockSpec((1, heads, BLOCK, padded), lambda d, i: (d, 0, i, 0)),
        ],
        out_specs=(
            pl.BlockSpec((1, heads, BLOCK, padded), lambda d, i: (d, 0, i, 0)),
            pl.BlockSpec((1, BLOCK, width), lambda d, i: (d, i, 0)),
            pl.BlockSpec((width, BLOCK), lambda d, i: (0, d * (padded // BLOCK) + i)),
        ),
        compiler_params=params(2),
        name="attend",
    )(qkv, qkv, qkv, bias)


def norm(rows_in):
    centre = rows_in - jnp.mean(rows_in, axis=-1, keepdims=True)
    inv_std = lax.rsqrt(jnp.mean(centre * centre, axis=-1, keepdims=True) + NORM_EPS)
    return centre * inv_std, inv_std


def norm_back(grad_in, normed, inv_std, gain_row):
    scaled = grad_in * gain_row
    return inv_std * (
        scaled
        - jnp.mean(scaled, axis=-1, keepdims=True)
        - normed * jnp.mean(scaled * normed, axis=-1, keepdims=True)
    )


def dense_kernel(
    rows, x_ref, o_ref, cot_ref, wo_ref, wu_ref, wd_ref, vec_ref, upb_ref,
    y_ref, dr_ref, left_ref, du_ref, df_ref, db_ref, do_ref, sums_ref, upsum_ref,
    slope_ref,
):
    width, hidden = wu_ref.shape
    first = pl.program_id(1) * x_ref.shape[2]
    vec = vec_ref[...]

    @pl.when((pl.program_id(0) == 0) & (pl.program_id(1) == 0))
    def _():
        sums_ref[...] = jnp.zeros_like(sums_ref)
        upsum_ref[...] = jnp.zeros_like(upsum_ref)

    tok = live_rows(x_ref[0, 0], rows, first).astype(F32)
    normed_one, inv_one = norm(tok + dot(o_ref[0], wo_ref[...]) + vec[6:7])
    state = normed_one * vec[0:1] + vec[2:3]
    low = state.astype(BF16)
    left_ref[0:width, :] = low.T
    second = state + vec[7:8]
    for part in range(hidden // width):
        cols = slice(part * width, (part + 1) * width)
        upper = dot(low, wu_ref[:, cols]) + upb_ref[:, cols]
        cdf = 0.5 * (1.0 + lax.erf(upper * (0.5**0.5)))
        slope_ref[:, cols] = cdf + upper * (jnp.exp(-0.5 * upper * upper) * 0.3989422804014327)
        active = (upper * cdf).astype(BF16)
        left_ref[(part + 1) * width : (part + 2) * width, :] = active.T
        second = second + dot(active, wd_ref[cols, :])
    normed_two, inv_two = norm(second)
    y_ref[0, 0] = (normed_two * vec[1:2] + vec[3:4]).astype(BF16)
    grad = live_rows(cot_ref[0, 0], rows, first).astype(F32)
    sums_ref[1:2, :] += jnp.sum(grad * normed_two, axis=0, keepdims=True)
    sums_ref[3:4, :] += jnp.sum(grad, axis=0, keepdims=True)
    d_two = norm_back(grad, normed_two, inv_two, vec[1:2])
    d_ffn = d_two.astype(BF16)
    df_ref[0] = d_ffn
    sums_ref[7:8, :] += jnp.sum(d_ffn.astype(F32), axis=0, keepdims=True)
    back = d_two
    for part in range(hidden // width):
        cols = slice(part * width, (part + 1) * width)
        d_upper = (dot_nt(d_ffn, wd_ref[cols, :]) * slope_ref[:, cols]).astype(BF16)
        du_ref[0, :, cols] = d_upper
        upsum_ref[:, cols] += jnp.sum(d_upper.astype(F32), axis=0, keepdims=True)
        back = back + dot_nt(d_upper, wu_ref[:, cols])
    sums_ref[0:1, :] += jnp.sum(back * normed_one, axis=0, keepdims=True)
    sums_ref[2:3, :] += jnp.sum(back, axis=0, keepdims=True)
    d_one = norm_back(back, normed_one, inv_one, vec[0:1])
    dr_ref[0] = d_one
    d_branch = d_one.astype(BF16)
    db_ref[0] = d_branch
    sums_ref[6:7, :] += jnp.sum(d_branch.astype(F32), axis=0, keepdims=True)
    do_ref[0] = dot_nt(d_branch, wo_ref[...]).astype(BF16)


def dense(layer_input, attended, cotangent, w_mixed, w_down, vectors, up_row):
    docs, unused, rows, width = layer_input.shape
    padded, hidden = attended.shape[1], w_down.shape[0]
    ragged = pl.BlockSpec((1, 1, DENSE_BLOCK, width), lambda d, i: (d, 0, i, 0))
    narrow = pl.BlockSpec((1, DENSE_BLOCK, width), lambda d, i: (d, i, 0))
    wide = pl.BlockSpec((1, DENSE_BLOCK, hidden), lambda d, i: (d, i, 0))

    def turned(lines):
        return pl.BlockSpec(
            (lines, DENSE_BLOCK), lambda d, i: (0, d * (padded // DENSE_BLOCK) + i)
        )

    def rows_of(columns, dtype):
        return jax.ShapeDtypeStruct((docs, padded, columns), dtype)

    return pl.pallas_call(
        partial(dense_kernel, rows),
        out_shape=(
            jax.ShapeDtypeStruct(layer_input.shape, BF16),
            rows_of(width, F32),
            jax.ShapeDtypeStruct((width + hidden, docs * padded), BF16),
            rows_of(hidden, BF16),
            rows_of(width, BF16),
            rows_of(width, BF16),
            rows_of(width, BF16),
            jax.ShapeDtypeStruct((8, width), F32),
            jax.ShapeDtypeStruct((1, hidden), F32),
        ),
        grid=(docs, padded // DENSE_BLOCK),
        in_specs=[
            ragged, narrow, ragged,
            columns((width, width), 3), columns((width, hidden), 4 * width // hidden),
            resident(w_down.shape),
            resident(vectors.shape), resident(up_row.shape),
        ],
        out_specs=(
            ragged, narrow, turned(width + hidden), wide, narrow, narrow, narrow,
            pl.BlockSpec((8, width), lambda d, i: (0, 0)),
            pl.BlockSpec((1, hidden), lambda d, i: (0, 0)),
        ),
        scratch_shapes=[pltpu.VMEM((DENSE_BLOCK, hidden), F32)],
        compiler_params=params(2),
        name="dense",
    )(layer_input, attended, cotangent, w_mixed, w_mixed, w_down, vectors, up_row)


def attend_back_kernel(
    rows, q_ref, k_ref, v_ref, probs_ref, do_ref, o_ref, pos_ref, box_ref, dm_ref, bins_ref, line_ref,
    dk_ref, dv_ref, ds_ref, acc_ref, picks_ref,
):
    block, width = pl.program_id(1), q_ref.shape[2]
    padded = k_ref.shape[1]
    lane = lax.broadcasted_iota(jnp.int32, (1, LANES), 1)

    @pl.when((pl.program_id(0) == 0) & (block == 0))
    def _():
        acc_ref[...] = jnp.zeros_like(acc_ref)
        line_ref[...] = jnp.zeros_like(line_ref)
        ds_ref[...] = jnp.zeros_like(ds_ref)

    @pl.when(block == 0)
    def _():
        dk_ref[...] = jnp.zeros_like(dk_ref)
        dv_ref[...] = jnp.zeros_like(dv_ref)

    own = pl.ds(pl.multiple_of(block * BLOCK, BLOCK), BLOCK)
    for pair in range(width // LANES):
        cols = slice(pair * LANES, (pair + 1) * LANES)
        queries, key_rows, values = q_ref[0, :, cols], k_ref[0, :, cols], v_ref[0, :, cols]
        grads = do_ref[0, :, cols]
        turned_q, turned_g = queries.T, grads.T
        shared = grads.astype(F32) * o_ref[0, :, cols].astype(F32)
        total = None
        for half in range(2):
            head = 2 * pair + half
            keep = (lane < HEAD_DIM) if half == 0 else (lane >= HEAD_DIM)
            part = slice(half * HEAD_DIM, (half + 1) * HEAD_DIM)
            lines = slice(head * HEAD_DIM, (head + 1) * HEAD_DIM)
            low = probs_ref[0, head]
            probs = low.astype(F32)
            dprobs = dot_nt(jnp.where(keep, grads, BF16(0)), values)
            delta = jnp.sum(jnp.where(keep, shared, 0.0), axis=-1, keepdims=True)
            dscore = probs * (dprobs - delta)
            for chunk in range(padded // LANES):
                ds_ref[chunk, pl.ds(head, BLOCK, stride=16), :] = dscore[
                    :, chunk * LANES : (chunk + 1) * LANES
                ]
            dlow = dscore.astype(BF16)
            piece = dot(dlow, jnp.where(keep, key_rows, BF16(0)))
            total = piece if half == 0 else total + piece
            dk_ref[lines, :] += dot(turned_q[part, :], dlow)
            dv_ref[lines, :] += dot(turned_g[part, :], low)
        dm_ref[0, own, cols] = (total * SCALE).astype(BF16)

    group = 32
    low_bins = lax.broadcasted_iota(jnp.int32, (HALF, LANES), 0).astype(BF16)

    def hits(picks, bins):
        low = picks.astype(BF16)
        return jnp.concatenate(
            [
                jnp.where(low_bins[first : first + 16] == low, BF16(1), BF16(0))
                for first in range(0, bins, 16)
            ],
            axis=0,
        )

    for place, (picks, bits) in enumerate(
        (
            (box_ref[0, 0, 0], BOX_BINS),
            (box_ref[0, 0, 1], BOX_BINS),
            (pos_ref[0, 0], POS_BINS),
        )
    ):
        half = bits // 2
        for chunk in range(padded // LANES):
            part = picks[:, chunk * LANES : (chunk + 1) * LANES] & (bits - 1)
            picks_ref[2 * place, chunk] = (part & (half - 1)).astype(F32)
            picks_ref[2 * place + 1, chunk] = (part >> (half.bit_length() - 1)).astype(F32)

    def count(step, carry):
        total = None
        for line in range(0, group, LINES):
            left, right = [], []
            for own in range(LINES):
                row = step * group + line + own
                here = pl.ds(pl.multiple_of(row * 16, 16), 16)
                again = pl.ds(row, 16, stride=0)
                for chunk in range(padded // LANES):
                    base = ds_ref[chunk, here, :]
                    left.append(
                        jnp.concatenate(
                            [base.astype(BF16)]
                            + [
                                (base * picks_ref[2 * place + 1, chunk, again, :]).astype(BF16)
                                for place in range(3)
                            ],
                            axis=0,
                        )
                    )
                    right.append(
                        jnp.concatenate(
                            [
                                hits(picks_ref[2 * place, chunk, again, :], bins)
                                for place, bins in enumerate((HALF, HALF, HALF // 2))
                            ],
                            axis=0,
                        )
                    )
            part = dot_nt(jnp.concatenate(left, axis=1), jnp.concatenate(right, axis=1))
            total = part if total is None else total + part
        acc_ref[0, :, : total.shape[1]] += total
        return carry

    live = jnp.minimum(BLOCK, (rows + group - 1) // group * group - block * BLOCK)
    lax.fori_loop(0, live // group, count, 0)

    @pl.when(block == pl.num_programs(1) - 1)
    def _():
        dm_ref[0, :, width : 2 * width] = dk_ref[...].astype(BF16).T
        dm_ref[0, :, 2 * width :] = dv_ref[...].astype(BF16).T
        bins_ref[...] = jnp.sum(acc_ref[...], axis=0)
        line_ref[...] += dot(jnp.ones((16, padded), BF16), dm_ref[0])[0:8]


def attend_back(qkv, probs, d_attended, attended, pos_buckets, box_buckets):
    docs, padded, width = qkv.shape[0], qkv.shape[1], qkv.shape[2] // 3
    heads, rows = probs.shape[1], pos_buckets.shape[2]
    return pl.pallas_call(
        partial(attend_back_kernel, rows),
        out_shape=(
            jax.ShapeDtypeStruct((docs, padded, 3 * width), BF16),
            jax.ShapeDtypeStruct((64, LANES), F32),
            jax.ShapeDtypeStruct((8, 3 * width), F32),
        ),
        grid=(docs, padded // BLOCK),
        in_specs=[
            pl.BlockSpec((1, BLOCK, width), lambda d, i: (d, i, 0)),
            pl.BlockSpec((1, padded, width), lambda d, i: (d, 0, 1)),
            pl.BlockSpec((1, padded, width), lambda d, i: (d, 0, 2)),
            pl.BlockSpec((1, heads, BLOCK, padded), lambda d, i: (d, 0, i, 0)),
            pl.BlockSpec((1, BLOCK, width), lambda d, i: (d, i, 0)),
            pl.BlockSpec((1, BLOCK, width), lambda d, i: (d, i, 0)),
            pl.BlockSpec((1, 1, BLOCK, padded), lambda d, i: (d, 0, i, 0)),
            pl.BlockSpec((1, 1, 2, BLOCK, padded), lambda d, i: (d, 0, 0, i, 0)),
        ],
        out_specs=(
            pl.BlockSpec((1, padded, 3 * width), lambda d, i: (d, 0, 0)),
            pl.BlockSpec((64, LANES), lambda d, i: (0, 0)),
            pl.BlockSpec((8, 3 * width), lambda d, i: (0, 0)),
        ),
        scratch_shapes=[
            pltpu.VMEM((width, padded), F32),
            pltpu.VMEM((width, padded), F32),
            pltpu.VMEM((padded // LANES, BLOCK * 16, LANES), F32),
            pltpu.VMEM((SPLIT, 64, LANES), F32),
            pltpu.VMEM((6, padded // LANES, BLOCK, LANES), F32),
        ],
        compiler_params=params(2),
        name="attend_back",
    )(qkv, qkv, qkv, probs, d_attended, attended, pos_buckets, box_buckets)


def table_entries(table):
    heads = table.shape[1]
    lines = table.astype(F32).T * SCALE
    boxes = lines[:, POS_BINS:]
    spots = jnp.pad(lines[:, :POS_BINS], ((0, 0), (0, LANES - POS_BINS)))
    return jnp.concatenate([boxes, spots], axis=0).reshape(2 * heads, LANES)


def table_grad(bins, heads):
    base, upper = bins[:heads], (bins[16 : 16 + heads], bins[32 : 32 + heads], bins[48 : 48 + heads])
    pieces = []
    for which, (first, size) in enumerate(((0, HALF), (HALF, HALF), (2 * HALF, HALF // 2))):
        high = upper[which][:, first : first + size]
        pieces.append(jnp.concatenate([base[:, first : first + size] - high, high], axis=1))
    return jnp.concatenate([pieces[2], pieces[0], pieces[1]], axis=1).T * SCALE


def weight_grads(attended, d_branch, left, d_upper, d_ffn, devices):
    width, rows = attended.shape
    own, fold = width // devices, d_upper.shape[1] // width
    share = devices // fold
    steps = 1 + 2 * fold

    def kernel(
        l_ref, u_ref, a_ref, b_ref, f_ref, out_ref,
        attended_ref, branch_ref, ffn_ref, stage_ref, sems, load_sems,
    ):
        step = pl.program_id(0)
        slot = step % 2
        loads = [
            pltpu.make_async_copy(source, target, load_sems.at[place])
            for place, (source, target) in enumerate(
                ((f_ref, ffn_ref), (a_ref, attended_ref), (b_ref, branch_ref))
            )
        ]

        def flat_copy(part, spot):
            cols = pl.ds(pl.multiple_of(part * width, width), width)
            return pltpu.make_async_copy(
                stage_ref.at[spot], out_ref.at[:, :, cols], sems.at[spot, 0]
            )

        def fold_copy(where, spot, part):
            block = where - fold
            cols = pl.ds((1 + fold + part) * width, width)
            return pltpu.make_async_copy(
                stage_ref.at[spot].reshape(share, fold, own, width).at[:, part],
                out_ref.at[pl.ds(block * share, share), :, cols],
                sems.at[spot, part],
            )

        def wait_for(where, spot):
            @pl.when(where < fold)
            def _():
                flat_copy(where + 1, spot).wait()

            @pl.when((where >= fold) & (where < 2 * fold))
            def _():
                for part in range(fold):
                    fold_copy(where, spot, part).wait()

        @pl.when(step == 0)
        def _():
            for load in loads:
                load.start()

        @pl.when(step >= 2)
        def _():
            wait_for(step - 2, slot)

        def put(value):
            stage_ref[slot] = value.reshape(devices, own, width).astype(BF16)

        @pl.when(step < fold)
        def _():
            put(dot(l_ref[...], u_ref[...]))
            flat_copy(step + 1, slot).start()

        @pl.when(step == fold)
        def _():
            loads[0].wait()

        @pl.when((step >= fold) & (step < 2 * fold))
        def _():
            put(dot(l_ref[...], ffn_ref[...]))
            for part in range(fold):
                fold_copy(step, slot, part).start()

        @pl.when(step == 2 * fold)
        def _():
            loads[1].wait()
            loads[2].wait()
            put(dot(attended_ref[...], branch_ref[...]))
            flat_copy(0, slot).start()
            wait_for(step - 1, 1 - slot)
            flat_copy(0, slot).wait()

    away = pl.BlockSpec(memory_space=pl.ANY)
    return pl.pallas_call(
        kernel,
        out_shape=jax.ShapeDtypeStruct((devices, own, (1 + 2 * fold) * width), BF16),
        grid=(steps,),
        in_specs=[
            pl.BlockSpec((width, rows), lambda p: (jnp.clip(p - fold + 1, 0, fold), 0)),
            pl.BlockSpec((rows, width), lambda p: (0, jnp.minimum(p, fold - 1))),
            away,
            away,
            away,
        ],
        out_specs=away,
        scratch_shapes=[
            pltpu.VMEM((width, rows), BF16),
            pltpu.VMEM((rows, width), BF16),
            pltpu.VMEM((rows, width), BF16),
            pltpu.VMEM((2, devices, own, width), BF16),
            pltpu.SemaphoreType.DMA((2, fold)),
            pltpu.SemaphoreType.DMA((3,)),
        ],
        compiler_params=params(1),
        cost_estimate=pl.CostEstimate(
            flops=2 * rows * width * width * steps, transcendentals=0,
            bytes_accessed=2 * rows * width * (steps + 3),
        ),
        name="weight_grads",
    )(left, d_upper, attended, d_branch, d_ffn)


ORDERS = ((3, 1, 2, 0), (3, 2, 1, 0)) * 3
MATRICES = 3
TABLE_LINES = 64
MESH = pl.DeviceIdType.MESH


def remaining(part, level):
    return [axis for axis in range(4) if axis not in ORDERS[part][:level]]


def tail_kernel(
    dims, w_ref, tok_ref, mixed_ref, one_ref, small_ref, grad_ref, sums_ref, input_ref, *scratch
):
    parts, width = len(ORDERS), tok_ref.shape[0]
    cut = MATRICES * width // parts
    holders = [scratch[8 * part : 8 * part + 4] for part in range(parts)]
    inboxes = [scratch[8 * part + 4 : 8 * part + 8] for part in range(parts)]
    (
        turned, mixed, weights, kept, stage, own_sums, got_sums,
        send_sems, recv_sems, load_sems, keep_sems, store_sems,
    ) = scratch[8 * parts :]
    deep, across, along, cores = dims
    dp, fsdp = lax.axis_index("dp"), lax.axis_index("fsdp")
    mine = (dp // across, dp % across, fsdp // cores, fsdp % cores)
    docs, padded = one_ref.shape[0], one_ref.shape[1]
    rows, block = input_ref.shape[1], kept.shape[1]
    own_lines = sums_ref.shape[0] - TABLE_LINES

    def peer(axis, step):
        place = list(mine)
        place[axis] = (place[axis] + step) % dims[axis]
        return place[axis], (place[0] * across + place[1], place[2] * cores + place[3])

    loads = [pltpu.make_async_copy(tok_ref, turned, load_sems.at[0])]
    for part in range(MATRICES):
        loads.append(
            pltpu.make_async_copy(
                mixed_ref.at[:, pl.ds(part * width, width)], mixed.at[part], load_sems.at[1 + part]
            )
        )
    loads.append(
        pltpu.make_async_copy(
            w_ref.at[:, pl.ds(0, MATRICES * width)], weights, load_sems.at[1 + MATRICES]
        )
    )
    for load in loads:
        load.start()

    barrier = pltpu.get_barrier_semaphore()
    partners = 0
    for axis in range(4):
        for step in range(1, dims[axis]):
            pl.semaphore_signal(barrier, inc=1, device_id=peer(axis, step)[1], device_id_type=MESH)
            partners += 1
    pl.semaphore_wait(barrier, partners)

    flying = {}

    def launch(lane, axis, source, target):
        copies = []
        for step in range(1, dims[axis]):
            place, device = peer(axis, step)
            copies.append(
                pltpu.make_async_remote_copy(
                    src_ref=source(place),
                    dst_ref=target(step - 1),
                    send_sem=send_sems.at[lane, step - 1],
                    recv_sem=recv_sems.at[lane, step - 1],
                    device_id=device,
                    device_id_type=MESH,
                )
            )
        for copy in copies:
            copy.start()
        flying[lane] = copies

    def land(lane):
        for copy in flying.pop(lane):
            copy.wait()

    def joined(own, others):
        total = own.astype(F32)
        for other in others:
            total = total + other.astype(F32)
        return total

    def send(part, level):
        axis, axes = ORDERS[part][level], remaining(part, level)

        def source(place):
            return holders[part][level].at[
                tuple(place if item == axis else slice(None) for item in axes)
            ]

        launch(4 * part + level, axis, source, lambda slot: inboxes[part][level].at[slot])

    def join(part, level):
        land(4 * part + level)
        axis, axes = ORDERS[part][level], remaining(part, level)
        source, box = holders[part][level], inboxes[part][level]
        left = [item for item in axes if item != axis]
        count = dims[axis] - 1
        if not left:
            grad_ref[:, part * cut : (part + 1) * cut] = joined(
                source[mine[axis]], [box[slot] for slot in range(count)]
            )
            return
        spots = [()]
        for item in left[1:]:
            spots = [spot + (place,) for spot in spots for place in range(dims[item])]

        def add(k, carry):
            for spot in spots:
                there = (k,) + spot
                where = dict(zip(left, there))
                where[axis] = mine[axis]
                own = tuple(where[item] for item in axes)
                holders[part][level + 1][there] = joined(
                    source[own], [box[(slot,) + there] for slot in range(count)]
                ).astype(BF16)
            return carry

        lax.fori_loop(0, dims[left[0]], add, 0)
        send(part, level + 1)

    small_order = (3, 1, 2, 0)
    own_bins = deep * own_lines

    def small_send(level):
        axis, lane = small_order[level], 4 * parts + level
        if level < 3:
            launch(lane, axis, lambda place: own_sums.at[level], lambda slot: got_sums.at[level, slot])
            return
        launch(
            lane, axis,
            lambda place: own_sums.at[3, pl.ds(pl.multiple_of(place * own_lines, 8), own_lines)],
            lambda slot: got_sums.at[3, slot, pl.ds(0, own_lines)],
        )
        launch(
            lane + 1, axis,
            lambda place: own_sums.at[3, pl.ds(own_bins, TABLE_LINES)],
            lambda slot: got_sums.at[3, slot, pl.ds(own_bins, TABLE_LINES)],
        )

    def small_join(level):
        axis, lane = small_order[level], 4 * parts + level
        land(lane)
        slots = range(dims[axis] - 1)
        if level < 3:
            own_sums[level + 1] = joined(own_sums[level], [got_sums[level, slot] for slot in slots])
            small_send(level + 1)
            return
        land(lane + 1)
        here = pl.ds(pl.multiple_of(mine[0] * own_lines, 8), own_lines)
        sums_ref[0:own_lines] = joined(
            own_sums[3, here], [got_sums[3, slot, 0:own_lines] for slot in slots]
        )
        last = slice(own_bins, own_bins + TABLE_LINES)
        sums_ref[own_lines:] = joined(own_sums[3, last], [got_sums[3, slot, last] for slot in slots])

    spans = [(doc, first) for doc in range(docs) for first in range(0, padded, block)]

    def keep(step):
        doc, first = spans[step]
        return pltpu.make_async_copy(
            one_ref.at[doc, pl.ds(first, block), :], kept.at[step % 2], keep_sems.at[step % 2]
        )

    def store(step):
        doc, first = spans[step]
        count = min(block, rows - first)
        return pltpu.make_async_copy(
            stage.at[step % 2, pl.ds(0, count)],
            input_ref.at[doc, pl.ds(first, count)],
            store_sems.at[step % 2],
        )

    def input_step(step):
        doc, first = spans[step]
        if step == 0:
            loads[1 + MATRICES].wait()
            keep(0).start()
        if step + 1 < len(spans):
            keep(step + 1).start()
        keep(step).wait()
        if step >= 2:
            store(step - 2).wait()
        at = pl.ds(doc * padded + first, block)
        total = kept[step % 2]
        for part in range(MATRICES):
            total = total + dot_nt(
                mixed[part, at, :], weights[:, part * width : (part + 1) * width]
            )
        stage[step % 2, :, 0, :] = total
        store(step).start()

    loads[0].wait()
    own_sums[0] = small_ref[...]
    small_send(0)

    def multiply(matrix):
        loads[1 + matrix].wait()
        for part in range(matrix * parts // MATRICES, (matrix + 1) * parts // MATRICES):
            first = part * cut - matrix * width
            block_rows = dot(turned[...], mixed[matrix, :, first : first + cut])
            holders[part][0][...] = block_rows.reshape(holders[part][0].shape).astype(BF16)
            send(part, 0)

    multiply(0)
    small_join(0)
    multiply(1)
    join(0, 0)
    join(1, 0)
    multiply(2)
    small_join(1)
    join(2, 0)
    join(3, 0)
    join(0, 1)
    join(1, 1)
    join(4, 0)
    join(5, 0)
    small_join(2)
    input_step(0)
    join(2, 1)
    join(3, 1)
    join(0, 2)
    join(1, 2)
    input_step(1)
    join(4, 1)
    join(5, 1)
    join(2, 2)
    join(3, 2)
    input_step(2)
    small_join(3)
    join(4, 2)
    join(5, 2)
    input_step(3)
    for part in range(parts):
        join(part, 3)
    for step in range(max(len(spans) - 2, 0), len(spans)):
        store(step).wait()


def split_mesh(dp, fsdp):
    across = 1 << ((dp.bit_length() - 1) // 2)
    across = across if dp % across == 0 else 1
    cores = 2 if fsdp % 2 == 0 else 1
    return dp // across, across, fsdp // cores, cores


def tail(w_mixed, tok, d_mixed, d_one, small, rows, dims):
    docs, padded, width = d_one.shape
    parts = len(ORDERS)
    cut = MATRICES * width // parts
    devices = dims[0] * dims[1] * dims[2] * dims[3]
    own = width // devices
    lines = (small.shape[0] - TABLE_LINES) // dims[0] + TABLE_LINES
    any_space = pl.BlockSpec(memory_space=pl.ANY)
    vmem = pl.BlockSpec(memory_space=pltpu.VMEM)
    scratch = []
    for part in range(parts):
        boxes = []
        for level in range(4):
            axes = remaining(part, level)
            axis = ORDERS[part][level]
            scratch.append(pltpu.VMEM(tuple(dims[item] for item in axes) + (own, cut), BF16))
            boxes.append(
                pltpu.VMEM(
                    (max(dims[axis] - 1, 1),)
                    + tuple(dims[item] for item in axes if item != axis)
                    + (own, cut),
                    BF16,
                )
            )
        scratch += boxes
    most = max(max(dims) - 1, 1)
    flat = docs * padded
    scratch += [
        pltpu.VMEM((width, flat), BF16),
        pltpu.VMEM((MATRICES, flat, width), BF16),
        pltpu.VMEM((width, MATRICES * width), BF16),
        pltpu.VMEM((2, DENSE_BLOCK, width), F32),
        pltpu.VMEM((2, DENSE_BLOCK, 1, width), F32),
        pltpu.VMEM((4,) + small.shape, F32),
        pltpu.VMEM((4, most) + small.shape, F32),
        pltpu.SemaphoreType.DMA((4 * parts + 5, most)),
        pltpu.SemaphoreType.DMA((4 * parts + 5, most)),
        pltpu.SemaphoreType.DMA((MATRICES + 2,)),
        pltpu.SemaphoreType.DMA((2,)),
        pltpu.SemaphoreType.DMA((2,)),
    ]
    return pl.pallas_call(
        partial(tail_kernel, dims),
        out_shape=(
            jax.ShapeDtypeStruct((own, MATRICES * width), F32),
            jax.ShapeDtypeStruct((lines, LANES), F32),
            jax.ShapeDtypeStruct((docs, rows, 1, width), F32),
        ),
        in_specs=[any_space, any_space, any_space, any_space, vmem],
        out_specs=(vmem, vmem, any_space),
        scratch_shapes=scratch,
        compiler_params=pltpu.CompilerParams(
            collective_id=0, has_side_effects=True, vmem_limit_bytes=VMEM_LIMIT
        ),
        name="tail",
    )(w_mixed, tok, d_mixed, d_one, small)


def handed_on(rows_out):
    docs, count, unused, width = rows_out.shape
    pieces = 4
    edges = [count * piece // pieces for piece in range(pieces + 1)]

    def kernel(in_ref, out_ref, held_ref, in_sems, out_sems):
        arrivals, departures = [], []
        for doc in range(docs):
            for piece in range(pieces):
                at = pl.ds(edges[piece], edges[piece + 1] - edges[piece])
                held = held_ref.at[doc, at]
                arrivals.append(
                    pltpu.make_async_copy(in_ref.at[doc, at], held, in_sems.at[doc, piece])
                )
                departures.append(
                    pltpu.make_async_copy(held, out_ref.at[doc, at], out_sems.at[doc, piece])
                )
        for copy in arrivals:
            copy.start()
        for arrival, departure in zip(arrivals, departures):
            arrival.wait()
            departure.start()
        for copy in departures:
            copy.wait()

    return pl.pallas_call(
        kernel,
        out_shape=jax.ShapeDtypeStruct(rows_out.shape, rows_out.dtype),
        in_specs=[pl.BlockSpec(memory_space=pl.ANY)],
        out_specs=pl.BlockSpec(memory_space=pl.ANY),
        scratch_shapes=[
            pltpu.VMEM(rows_out.shape, rows_out.dtype),
            pltpu.SemaphoreType.DMA((docs, pieces)),
            pltpu.SemaphoreType.DMA((docs, pieces)),
        ],
        compiler_params=pltpu.CompilerParams(vmem_limit_bytes=VMEM_LIMIT),
        name="handed_on",
    )(rows_out)


def packed_sums(sums, up_sum, bins, deep):
    width, hidden = sums.shape[1], up_sum.shape[1]
    sums = jnp.transpose(sums.reshape(8, deep, width // deep), (1, 0, 2)).reshape(deep, -1)
    lines = jnp.concatenate([sums, up_sum.reshape(deep, hidden // deep)], axis=1)
    share = pl.cdiv(lines.shape[1], 8 * LANES) * 8 * LANES
    lines = jnp.pad(lines, ((0, 0), (0, share - lines.shape[1])))
    return jnp.concatenate([lines.reshape(-1, LANES), bins], axis=0)


def small_results(packed, width, hidden, heads, deep, own, rank):
    flat = packed[:-TABLE_LINES].reshape(-1)
    count, more = 8 * width // deep, hidden // deep
    sums = lax.dynamic_slice_in_dim(flat[:count].reshape(8, -1), rank * own, own, 1)
    fold = hidden // width * own
    up_sum = lax.dynamic_slice_in_dim(flat[count : count + more], rank * fold, fold, 0)
    return sums, up_sum, table_grad(packed[-TABLE_LINES:], heads)


def local_step(dims, lengths, pos_buckets, box_buckets, layer_input, cotangent, w_mixed, w_down, vectors, up_row, table):
    heads, width = table.shape[1], layer_input.shape[3]
    docs, rows = layer_input.shape[0], layer_input.shape[2]
    bias = bias_rows(lengths, table_entries(table), pos_buckets, box_buckets, heads)
    qkv, tok = project(layer_input, w_mixed, vectors)
    probs, attended, turned = attend(qkv, bias)
    result, d_one, left, d_upper, d_ffn, d_branch, d_attended, sums, up_sum = dense(
        layer_input, attended, cotangent, w_mixed, w_down, vectors, up_row
    )

    def flat(item):
        return item.reshape(-1, item.shape[-1])

    d_weights = weight_grads(
        turned, flat(d_branch), left, flat(d_upper), flat(d_ffn), dims[0] * dims[1] * dims[2] * dims[3]
    )
    d_mixed, bins, line = attend_back(qkv, probs, d_attended, attended, pos_buckets, box_buckets)
    sums = jnp.concatenate(
        [sums[:4], line[:1, :width], line[:1, 2 * width :], sums[6:]], axis=0
    )
    packed = packed_sums(sums, up_sum, bins, dims[0])
    return result, d_weights, (w_mixed, tok, flat(d_mixed), d_one, packed, rows, dims)


def body(
    layer_input, text_lengths, pos_buckets, box_buckets, w_qkv, w_out, w_up, w_down,
    norm_gains, norm_shifts, proj_biases, up_bias, rel_tables, cotangent,
):
    axes = ("dp", "fsdp")
    width, hidden = layer_input.shape[3], w_up.shape[1]
    own = norm_gains.shape[1]
    table = lax.all_gather(rel_tables, "fsdp", axis=0, tiled=True)
    heads = table.shape[1]
    small = jnp.concatenate(
        [
            jnp.concatenate([norm_gains, norm_shifts, proj_biases], axis=0).T,
            up_bias.reshape(own, hidden // width),
        ],
        axis=1,
    )
    small = jnp.pad(small, ((0, 0), (0, LANES - small.shape[1])))
    w_mixed = lax.all_gather(
        jnp.concatenate([w_qkv, w_out, w_up, small], axis=1), axes, axis=0, tiled=True
    )
    w_down = lax.all_gather(w_down, axes, axis=0, tiled=True)
    small = w_mixed[:, 4 * width + hidden :].astype(F32)
    vectors = small[:, :8].T
    up_row = small[:, 8 : 8 + hidden // width].reshape(1, hidden)
    dims = split_mesh(lax.axis_size("dp"), lax.axis_size("fsdp"))
    result, d_weights, rest = local_step(
        dims, text_lengths[:, 0], pos_buckets, box_buckets, layer_input, cotangent, w_mixed, w_down,
        vectors, up_row, table,
    )
    d_weights = lax.psum_scatter(
        d_weights.reshape(width, -1), axes, scatter_dimension=0, tiled=True
    ).astype(F32)
    d_down = [d_weights[:, first : first + width] for first in range(width + hidden, width + 2 * hidden, width)]
    d_down = jnp.concatenate(d_down, axis=0)
    d_qkv, packed, input_grad = tail(*rest)
    rank = lax.axis_index(axes) % (width // own // dims[0])
    sums, up_sum, d_table = small_results(packed, width, hidden, heads, dims[0], own, rank)
    table_rows = rel_tables.shape[0]
    d_table = lax.dynamic_slice_in_dim(d_table, lax.axis_index("fsdp") * table_rows, table_rows, 0)
    return (
        result, jnp.transpose(handed_on(input_grad), (0, 2, 1, 3)), d_qkv, d_weights[:, :width], d_weights[:, width : width + hidden], d_down,
        sums[0:2], sums[2:4], sums[4:8], up_sum, d_table,
    )


def solution(mesh):
    both = ("dp", "fsdp")
    docs = P(None, both, None, None)
    return jax.shard_map(
        body,
        mesh=mesh,
        in_specs=(
            docs, P(None, both), docs, P(None, both, None, None, None),
            P(both, None), P(both, None), P(both, None), P(both, None),
            P(None, both), P(None, both), P(None, both), P(both), P("fsdp", None), docs,
        ),
        out_specs=(
            docs, docs, P(both, None), P(both, None), P(both, None), P(both, None),
            P(None, both), P(None, both), P(None, both), P(both), P("fsdp", None),
        ),
        check_vma=False,
    )
```

```python
from functools import partial

import jax
import jax.numpy as jnp
from jax import lax
from jax.experimental import pallas as pl
from jax.experimental.pallas import tpu as pltpu
from jax.sharding import PartitionSpec as P

HEAD_DIM = 64
POS_BINS = 32
BOX_BINS = 64
TEXT_SLOTS = 512
NEG_FILL = -1000000000.0
NORM_EPS = 1e-05
BLOCK = 256
DENSE_BLOCK = 384
LANES = 128
HALF = 32
SPLIT = 1
LINES = 1
SCALE = 0.125
F32 = jnp.float32
BF16 = jnp.bfloat16
VMEM_LIMIT = 58 << 20


def dot(left, right):
    return jnp.dot(left, right, preferred_element_type=F32)


def dot_nt(left, right):
    return lax.dot_general(left, right, (((1,), (1,)), ((), ())), preferred_element_type=F32)


def params(count):
    return pltpu.CompilerParams(
        dimension_semantics=("arbitrary",) * count, vmem_limit_bytes=VMEM_LIMIT
    )


def resident(shape):
    zeros = (0,) * len(shape)
    return pl.BlockSpec(shape, lambda *_: zeros, pipeline_mode=pl.Buffered(1))


def columns(shape, place):
    return pl.BlockSpec(shape, lambda *_: (0, place), pipeline_mode=pl.Buffered(1))


def live_rows(values, rows, first):
    row = first + lax.broadcasted_iota(jnp.int32, (values.shape[0], 1), 0)
    return jnp.where(row < rows, values, jnp.zeros_like(values))


def bias_kernel(rows, len_ref, tab_ref, pos_ref, box_ref, out_ref):
    heads, chunks = out_ref.shape[1], out_ref.shape[3] // LANES
    block = pl.program_id(1)
    length = len_ref[pl.program_id(0)]
    steps = jnp.minimum(BLOCK, (rows + 7) // 8 * 8 - block * BLOCK) // 8

    def fill(step, carry):
        at = pl.ds(pl.multiple_of(step * 8, 8), 8)
        for chunk in range(chunks):
            cols = slice(chunk * LANES, (chunk + 1) * LANES)
            picks = (
                box_ref[0, 0, 0, at, cols] & (BOX_BINS - 1),
                (box_ref[0, 0, 1, at, cols] & (BOX_BINS - 1)) | BOX_BINS,
                pos_ref[0, 0, at, cols] & (POS_BINS - 1),
            )
            slot = chunk * LANES + lax.broadcasted_iota(jnp.int32, (8, LANES), 1)
            valid = ((slot >= TEXT_SLOTS) & (slot < rows)) | (slot < length)
            totals = [None] * heads
            for which, pick in enumerate(picks):
                for head in range(heads):
                    line = head + (heads if which == 2 else 0)
                    entries = jnp.broadcast_to(tab_ref[line : line + 1, :], (8, LANES))
                    term = jnp.take_along_axis(entries, pick, axis=1)
                    totals[head] = term if which == 0 else totals[head] + term
            for head in range(heads):
                out_ref[0, head, at, cols] = jnp.where(valid, totals[head], NEG_FILL)
        return carry

    def blank(step, carry):
        at = pl.ds(pl.multiple_of(step * 8, 8), 8)
        for head in range(heads):
            out_ref[0, head, at, :] = jnp.zeros((8, chunks * LANES), F32)
        return carry

    lax.fori_loop(0, steps, fill, 0)
    lax.fori_loop(steps, BLOCK // 8, blank, 0)


def bias_rows(lengths, entries, pos_buckets, box_buckets, heads):
    docs, rows = pos_buckets.shape[0], pos_buckets.shape[2]
    padded = pl.cdiv(rows, BLOCK) * BLOCK
    return pl.pallas_call(
        partial(bias_kernel, rows),
        out_shape=jax.ShapeDtypeStruct((docs, heads, padded, padded), F32),
        grid=(docs, padded // BLOCK),
        in_specs=[
            pl.BlockSpec(memory_space=pltpu.SMEM),
            resident(entries.shape),
            pl.BlockSpec((1, 1, BLOCK, padded), lambda d, i: (d, 0, i, 0)),
            pl.BlockSpec((1, 1, 2, BLOCK, padded), lambda d, i: (d, 0, 0, i, 0)),
        ],
        out_specs=pl.BlockSpec((1, heads, BLOCK, padded), lambda d, i: (d, 0, i, 0)),
        compiler_params=params(2),
        cost_estimate=pl.CostEstimate(
            flops=3 * docs * heads * rows * rows,
            transcendentals=0,
            bytes_accessed=docs * padded * padded * (4 * heads + 12),
        ),
        name="bias_rows",
    )(lengths, entries, pos_buckets, box_buckets)


def project_kernel(rows, x_ref, w_ref, vec_ref, out_ref, tok_ref):
    width = x_ref.shape[3]
    block = live_rows(x_ref[0, 0], rows, pl.program_id(1) * x_ref.shape[2])
    tok_ref[...] = block.T
    queries = dot(block, w_ref[:, :width]) + vec_ref[4:5, :]
    out_ref[0, :, :width] = queries.astype(BF16) * BF16(SCALE)
    out_ref[0, :, width : 2 * width] = dot(block, w_ref[:, width : 2 * width]).astype(BF16)
    values = dot(block, w_ref[:, 2 * width :]) + vec_ref[5:6, :]
    out_ref[0, :, 2 * width :] = values.astype(BF16)


def project(layer_input, w_mixed, vectors):
    docs, unused, rows, width = layer_input.shape
    padded = pl.cdiv(rows, BLOCK) * BLOCK
    return pl.pallas_call(
        partial(project_kernel, rows),
        out_shape=(
            jax.ShapeDtypeStruct((docs, padded, 3 * width), BF16),
            jax.ShapeDtypeStruct((width, docs * padded), BF16),
        ),
        grid=(docs, padded // DENSE_BLOCK),
        in_specs=[
            pl.BlockSpec((1, 1, DENSE_BLOCK, width), lambda d, i: (d, 0, i, 0)),
            columns((width, 3 * width), 0),
            resident(vectors.shape),
        ],
        out_specs=(
            pl.BlockSpec((1, DENSE_BLOCK, 3 * width), lambda d, i: (d, i, 0)),
            pl.BlockSpec((width, DENSE_BLOCK), lambda d, i: (0, d * (padded // DENSE_BLOCK) + i)),
        ),
        compiler_params=params(2),
        name="project",
    )(layer_input, w_mixed, vectors)


def attend_kernel(q_ref, k_ref, v_ref, bias_ref, probs_ref, out_ref, turned_ref):
    lane = lax.broadcasted_iota(jnp.int32, (1, LANES), 1)
    for pair in range(q_ref.shape[2] // LANES):
        cols = slice(pair * LANES, (pair + 1) * LANES)
        queries, key_rows, values = q_ref[0, :, cols], k_ref[0, :, cols], v_ref[0, :, cols]
        total = None
        for half in range(2):
            head = 2 * pair + half
            keep = (lane < HEAD_DIM) if half == 0 else (lane >= HEAD_DIM)
            scores = dot_nt(jnp.where(keep, queries, BF16(0)), key_rows) + bias_ref[0, head]
            top = jnp.max(scores, axis=-1, keepdims=True)
            powers = jnp.exp(scores - top)
            share = 1.0 / jnp.sum(powers, axis=-1, keepdims=True)
            probs = (powers * share).astype(BF16)
            probs_ref[0, head] = probs
            part = dot(probs, jnp.where(keep, values, BF16(0)))
            total = part if half == 0 else total + part
        low = total.astype(BF16)
        out_ref[0, :, cols] = low
        turned_ref[cols, :] = low.T


def attend(qkv, bias):
    docs, padded, width = qkv.shape[0], qkv.shape[1], qkv.shape[2] // 3
    heads = bias.shape[1]
    return pl.pallas_call(
        attend_kernel,
        out_shape=(
            jax.ShapeDtypeStruct((docs, heads, padded, padded), BF16),
            jax.ShapeDtypeStruct((docs, padded, width), BF16),
            jax.ShapeDtypeStruct((width, docs * padded), BF16),
        ),
        grid=(docs, padded // BLOCK),
        in_specs=[
            pl.BlockSpec((1, BLOCK, width), lambda d, i: (d, i, 0)),
            pl.BlockSpec((1, padded, width), lambda d, i: (d, 0, 1)),
            pl.BlockSpec((1, padded, width), lambda d, i: (d, 0, 2)),
            pl.BlockSpec((1, heads, BLOCK, padded), lambda d, i: (d, 0, i, 0)),
        ],
        out_specs=(
            pl.BlockSpec((1, heads, BLOCK, padded), lambda d, i: (d, 0, i, 0)),
            pl.BlockSpec((1, BLOCK, width), lambda d, i: (d, i, 0)),
            pl.BlockSpec((width, BLOCK), lambda d, i: (0, d * (padded // BLOCK) + i)),
        ),
        compiler_params=params(2),
        name="attend",
    )(qkv, qkv, qkv, bias)


def norm(rows_in):
    centre = rows_in - jnp.mean(rows_in, axis=-1, keepdims=True)
    inv_std = lax.rsqrt(jnp.mean(centre * centre, axis=-1, keepdims=True) + NORM_EPS)
    return centre * inv_std, inv_std


def norm_back(grad_in, normed, inv_std, gain_row):
    scaled = grad_in * gain_row
    return inv_std * (
        scaled
        - jnp.mean(scaled, axis=-1, keepdims=True)
        - normed * jnp.mean(scaled * normed, axis=-1, keepdims=True)
    )


def dense_kernel(
    rows, x_ref, o_ref, cot_ref, wo_ref, wu_ref, wd_ref, vec_ref, upb_ref,
    y_ref, dr_ref, left_ref, du_ref, df_ref, db_ref, do_ref, sums_ref, upsum_ref,
    slope_ref,
):
    width, hidden = wu_ref.shape
    first = pl.program_id(1) * x_ref.shape[2]
    vec = vec_ref[...]

    @pl.when((pl.program_id(0) == 0) & (pl.program_id(1) == 0))
    def _():
        sums_ref[...] = jnp.zeros_like(sums_ref)
        upsum_ref[...] = jnp.zeros_like(upsum_ref)

    tok = live_rows(x_ref[0, 0], rows, first).astype(F32)
    normed_one, inv_one = norm(tok + dot(o_ref[0], wo_ref[...]) + vec[6:7])
    state = normed_one * vec[0:1] + vec[2:3]
    low = state.astype(BF16)
    left_ref[0:width, :] = low.T
    second = state + vec[7:8]
    for part in range(hidden // width):
        cols = slice(part * width, (part + 1) * width)
        upper = dot(low, wu_ref[:, cols]) + upb_ref[:, cols]
        cdf = 0.5 * (1.0 + lax.erf(upper * (0.5**0.5)))
        slope_ref[:, cols] = cdf + upper * (jnp.exp(-0.5 * upper * upper) * 0.3989422804014327)
        active = (upper * cdf).astype(BF16)
        left_ref[(part + 1) * width : (part + 2) * width, :] = active.T
        second = second + dot(active, wd_ref[cols, :])
    normed_two, inv_two = norm(second)
    y_ref[0, 0] = (normed_two * vec[1:2] + vec[3:4]).astype(BF16)
    grad = live_rows(cot_ref[0, 0], rows, first).astype(F32)
    sums_ref[1:2, :] += jnp.sum(grad * normed_two, axis=0, keepdims=True)
    sums_ref[3:4, :] += jnp.sum(grad, axis=0, keepdims=True)
    d_two = norm_back(grad, normed_two, inv_two, vec[1:2])
    d_ffn = d_two.astype(BF16)
    df_ref[0] = d_ffn
    sums_ref[7:8, :] += jnp.sum(d_ffn.astype(F32), axis=0, keepdims=True)
    back = d_two
    for part in range(hidden // width):
        cols = slice(part * width, (part + 1) * width)
        d_upper = (dot_nt(d_ffn, wd_ref[cols, :]) * slope_ref[:, cols]).astype(BF16)
        du_ref[0, :, cols] = d_upper
        upsum_ref[:, cols] += jnp.sum(d_upper.astype(F32), axis=0, keepdims=True)
        back = back + dot_nt(d_upper, wu_ref[:, cols])
    sums_ref[0:1, :] += jnp.sum(back * normed_one, axis=0, keepdims=True)
    sums_ref[2:3, :] += jnp.sum(back, axis=0, keepdims=True)
    d_one = norm_back(back, normed_one, inv_one, vec[0:1])
    dr_ref[0] = d_one
    d_branch = d_one.astype(BF16)
    db_ref[0] = d_branch
    sums_ref[6:7, :] += jnp.sum(d_branch.astype(F32), axis=0, keepdims=True)
    do_ref[0] = dot_nt(d_branch, wo_ref[...]).astype(BF16)


def dense(layer_input, attended, cotangent, w_mixed, w_down, vectors, up_row):
    docs, unused, rows, width = layer_input.shape
    padded, hidden = attended.shape[1], w_down.shape[0]
    ragged = pl.BlockSpec((1, 1, DENSE_BLOCK, width), lambda d, i: (d, 0, i, 0))
    narrow = pl.BlockSpec((1, DENSE_BLOCK, width), lambda d, i: (d, i, 0))
    wide = pl.BlockSpec((1, DENSE_BLOCK, hidden), lambda d, i: (d, i, 0))

    def turned(lines):
        return pl.BlockSpec(
            (lines, DENSE_BLOCK), lambda d, i: (0, d * (padded // DENSE_BLOCK) + i)
        )

    def rows_of(columns, dtype):
        return jax.ShapeDtypeStruct((docs, padded, columns), dtype)

    return pl.pallas_call(
        partial(dense_kernel, rows),
        out_shape=(
            jax.ShapeDtypeStruct(layer_input.shape, BF16),
            rows_of(width, F32),
            jax.ShapeDtypeStruct((width + hidden, docs * padded), BF16),
            rows_of(hidden, BF16),
            rows_of(width, BF16),
            rows_of(width, BF16),
            rows_of(width, BF16),
            jax.ShapeDtypeStruct((8, width), F32),
            jax.ShapeDtypeStruct((1, hidden), F32),
        ),
        grid=(docs, padded // DENSE_BLOCK),
        in_specs=[
            ragged, narrow, ragged,
            columns((width, width), 3), columns((width, hidden), 4 * width // hidden),
            resident(w_down.shape),
            resident(vectors.shape), resident(up_row.shape),
        ],
        out_specs=(
            ragged, narrow, turned(width + hidden), wide, narrow, narrow, narrow,
            pl.BlockSpec((8, width), lambda d, i: (0, 0)),
            pl.BlockSpec((1, hidden), lambda d, i: (0, 0)),
        ),
        scratch_shapes=[pltpu.VMEM((DENSE_BLOCK, hidden), F32)],
        compiler_params=params(2),
        name="dense",
    )(layer_input, attended, cotangent, w_mixed, w_mixed, w_down, vectors, up_row)


def attend_back_kernel(
    rows, q_ref, k_ref, v_ref, probs_ref, do_ref, o_ref, pos_ref, box_ref, dm_ref, bins_ref, line_ref,
    dk_ref, dv_ref, ds_ref, acc_ref, picks_ref,
):
    block, width = pl.program_id(1), q_ref.shape[2]
    padded = k_ref.shape[1]
    lane = lax.broadcasted_iota(jnp.int32, (1, LANES), 1)

    @pl.when((pl.program_id(0) == 0) & (block == 0))
    def _():
        acc_ref[...] = jnp.zeros_like(acc_ref)
        line_ref[...] = jnp.zeros_like(line_ref)
        ds_ref[...] = jnp.zeros_like(ds_ref)

    @pl.when(block == 0)
    def _():
        dk_ref[...] = jnp.zeros_like(dk_ref)
        dv_ref[...] = jnp.zeros_like(dv_ref)

    own = pl.ds(pl.multiple_of(block * BLOCK, BLOCK), BLOCK)
    for pair in range(width // LANES):
        cols = slice(pair * LANES, (pair + 1) * LANES)
        queries, key_rows, values = q_ref[0, :, cols], k_ref[0, :, cols], v_ref[0, :, cols]
        grads = do_ref[0, :, cols]
        turned_q, turned_g = queries.T, grads.T
        shared = grads.astype(F32) * o_ref[0, :, cols].astype(F32)
        total = None
        for half in range(2):
            head = 2 * pair + half
            keep = (lane < HEAD_DIM) if half == 0 else (lane >= HEAD_DIM)
            part = slice(half * HEAD_DIM, (half + 1) * HEAD_DIM)
            lines = slice(head * HEAD_DIM, (head + 1) * HEAD_DIM)
            low = probs_ref[0, head]
            probs = low.astype(F32)
            dprobs = dot_nt(jnp.where(keep, grads, BF16(0)), values)
            delta = jnp.sum(jnp.where(keep, shared, 0.0), axis=-1, keepdims=True)
            dscore = probs * (dprobs - delta)
            for chunk in range(padded // LANES):
                ds_ref[chunk, pl.ds(head, BLOCK, stride=16), :] = dscore[
                    :, chunk * LANES : (chunk + 1) * LANES
                ]
            dlow = dscore.astype(BF16)
            piece = dot(dlow, jnp.where(keep, key_rows, BF16(0)))
            total = piece if half == 0 else total + piece
            dk_ref[lines, :] += dot(turned_q[part, :], dlow)
            dv_ref[lines, :] += dot(turned_g[part, :], low)
        dm_ref[0, own, cols] = (total * SCALE).astype(BF16)

    group = 32
    low_bins = lax.broadcasted_iota(jnp.int32, (HALF, LANES), 0).astype(BF16)

    def hits(picks, bins):
        low = picks.astype(BF16)
        return jnp.concatenate(
            [
                jnp.where(low_bins[first : first + 16] == low, BF16(1), BF16(0))
                for first in range(0, bins, 16)
            ],
            axis=0,
        )

    for place, (picks, bits) in enumerate(
        (
            (box_ref[0, 0, 0], BOX_BINS),
            (box_ref[0, 0, 1], BOX_BINS),
            (pos_ref[0, 0], POS_BINS),
        )
    ):
        half = bits // 2
        for chunk in range(padded // LANES):
            part = picks[:, chunk * LANES : (chunk + 1) * LANES] & (bits - 1)
            picks_ref[2 * place, chunk] = (part & (half - 1)).astype(F32)
            picks_ref[2 * place + 1, chunk] = (part >> (half.bit_length() - 1)).astype(F32)

    def count(step, carry):
        total = None
        for line in range(0, group, LINES):
            left, right = [], []
            for own in range(LINES):
                row = step * group + line + own
                here = pl.ds(pl.multiple_of(row * 16, 16), 16)
                again = pl.ds(row, 16, stride=0)
                for chunk in range(padded // LANES):
                    base = ds_ref[chunk, here, :]
                    left.append(
                        jnp.concatenate(
                            [base.astype(BF16)]
                            + [
                                (base * picks_ref[2 * place + 1, chunk, again, :]).astype(BF16)
                                for place in range(3)
                            ],
                            axis=0,
                        )
                    )
                    right.append(
                        jnp.concatenate(
                            [
                                hits(picks_ref[2 * place, chunk, again, :], bins)
                                for place, bins in enumerate((HALF, HALF, HALF // 2))
                            ],
                            axis=0,
                        )
                    )
            part = dot_nt(jnp.concatenate(left, axis=1), jnp.concatenate(right, axis=1))
            total = part if total is None else total + part
        acc_ref[0, :, : total.shape[1]] += total
        return carry

    live = jnp.minimum(BLOCK, (rows + group - 1) // group * group - block * BLOCK)
    lax.fori_loop(0, live // group, count, 0)

    @pl.when(block == pl.num_programs(1) - 1)
    def _():
        dm_ref[0, :, width : 2 * width] = dk_ref[...].astype(BF16).T
        dm_ref[0, :, 2 * width :] = dv_ref[...].astype(BF16).T
        bins_ref[...] = jnp.sum(acc_ref[...], axis=0)
        line_ref[...] += dot(jnp.ones((16, padded), BF16), dm_ref[0])[0:8]


def attend_back(qkv, probs, d_attended, attended, pos_buckets, box_buckets):
    docs, padded, width = qkv.shape[0], qkv.shape[1], qkv.shape[2] // 3
    heads, rows = probs.shape[1], pos_buckets.shape[2]
    return pl.pallas_call(
        partial(attend_back_kernel, rows),
        out_shape=(
            jax.ShapeDtypeStruct((docs, padded, 3 * width), BF16),
            jax.ShapeDtypeStruct((64, LANES), F32),
            jax.ShapeDtypeStruct((8, 3 * width), F32),
        ),
        grid=(docs, padded // BLOCK),
        in_specs=[
            pl.BlockSpec((1, BLOCK, width), lambda d, i: (d, i, 0)),
            pl.BlockSpec((1, padded, width), lambda d, i: (d, 0, 1)),
            pl.BlockSpec((1, padded, width), lambda d, i: (d, 0, 2)),
            pl.BlockSpec((1, heads, BLOCK, padded), lambda d, i: (d, 0, i, 0)),
            pl.BlockSpec((1, BLOCK, width), lambda d, i: (d, i, 0)),
            pl.BlockSpec((1, BLOCK, width), lambda d, i: (d, i, 0)),
            pl.BlockSpec((1, 1, BLOCK, padded), lambda d, i: (d, 0, i, 0)),
            pl.BlockSpec((1, 1, 2, BLOCK, padded), lambda d, i: (d, 0, 0, i, 0)),
        ],
        out_specs=(
            pl.BlockSpec((1, padded, 3 * width), lambda d, i: (d, 0, 0)),
            pl.BlockSpec((64, LANES), lambda d, i: (0, 0)),
            pl.BlockSpec((8, 3 * width), lambda d, i: (0, 0)),
        ),
        scratch_shapes=[
            pltpu.VMEM((width, padded), F32),
            pltpu.VMEM((width, padded), F32),
            pltpu.VMEM((padded // LANES, BLOCK * 16, LANES), F32),
            pltpu.VMEM((SPLIT, 64, LANES), F32),
            pltpu.VMEM((6, padded // LANES, BLOCK, LANES), F32),
        ],
        compiler_params=params(2),
        name="attend_back",
    )(qkv, qkv, qkv, probs, d_attended, attended, pos_buckets, box_buckets)


def table_entries(table):
    heads = table.shape[1]
    lines = table.astype(F32).T * SCALE
    boxes = lines[:, POS_BINS:]
    spots = jnp.pad(lines[:, :POS_BINS], ((0, 0), (0, LANES - POS_BINS)))
    return jnp.concatenate([boxes, spots], axis=0).reshape(2 * heads, LANES)


def table_grad(bins, heads):
    base, upper = bins[:heads], (bins[16 : 16 + heads], bins[32 : 32 + heads], bins[48 : 48 + heads])
    pieces = []
    for which, (first, size) in enumerate(((0, HALF), (HALF, HALF), (2 * HALF, HALF // 2))):
        high = upper[which][:, first : first + size]
        pieces.append(jnp.concatenate([base[:, first : first + size] - high, high], axis=1))
    return jnp.concatenate([pieces[2], pieces[0], pieces[1]], axis=1).T * SCALE


def weight_grads(attended, d_branch, left, d_upper, d_ffn, devices):
    width, rows = attended.shape
    own, fold = width // devices, d_upper.shape[1] // width
    share = devices // fold
    steps = 1 + 2 * fold

    def kernel(
        l_ref, u_ref, a_ref, b_ref, f_ref, out_ref,
        attended_ref, branch_ref, ffn_ref, stage_ref, sems, load_sems,
    ):
        step = pl.program_id(0)
        slot = step % 2
        loads = [
            pltpu.make_async_copy(source, target, load_sems.at[place])
            for place, (source, target) in enumerate(
                ((f_ref, ffn_ref), (a_ref, attended_ref), (b_ref, branch_ref))
            )
        ]

        def flat_copy(part, spot):
            cols = pl.ds(pl.multiple_of(part * width, width), width)
            return pltpu.make_async_copy(
                stage_ref.at[spot], out_ref.at[:, :, cols], sems.at[spot, 0]
            )

        def fold_copy(where, spot, part):
            block = where - fold
            cols = pl.ds((1 + fold + part) * width, width)
            return pltpu.make_async_copy(
                stage_ref.at[spot].reshape(share, fold, own, width).at[:, part],
                out_ref.at[pl.ds(block * share, share), :, cols],
                sems.at[spot, part],
            )

        def wait_for(where, spot):
            @pl.when(where < fold)
            def _():
                flat_copy(where + 1, spot).wait()

            @pl.when((where >= fold) & (where < 2 * fold))
            def _():
                for part in range(fold):
                    fold_copy(where, spot, part).wait()

        @pl.when(step == 0)
        def _():
            for load in loads:
                load.start()

        @pl.when(step >= 2)
        def _():
            wait_for(step - 2, slot)

        def put(value):
            stage_ref[slot] = value.reshape(devices, own, width).astype(BF16)

        @pl.when(step < fold)
        def _():
            put(dot(l_ref[...], u_ref[...]))
            flat_copy(step + 1, slot).start()

        @pl.when(step == fold)
        def _():
            loads[0].wait()

        @pl.when((step >= fold) & (step < 2 * fold))
        def _():
            put(dot(l_ref[...], ffn_ref[...]))
            for part in range(fold):
                fold_copy(step, slot, part).start()

        @pl.when(step == 2 * fold)
        def _():
            loads[1].wait()
            loads[2].wait()
            put(dot(attended_ref[...], branch_ref[...]))
            flat_copy(0, slot).start()
            wait_for(step - 1, 1 - slot)
            flat_copy(0, slot).wait()

    away = pl.BlockSpec(memory_space=pl.ANY)
    return pl.pallas_call(
        kernel,
        out_shape=jax.ShapeDtypeStruct((devices, own, (1 + 2 * fold) * width), BF16),
        grid=(steps,),
        in_specs=[
            pl.BlockSpec((width, rows), lambda p: (jnp.clip(p - fold + 1, 0, fold), 0)),
            pl.BlockSpec((rows, width), lambda p: (0, jnp.minimum(p, fold - 1))),
            away,
            away,
            away,
        ],
        out_specs=away,
        scratch_shapes=[
            pltpu.VMEM((width, rows), BF16),
            pltpu.VMEM((rows, width), BF16),
            pltpu.VMEM((rows, width), BF16),
            pltpu.VMEM((2, devices, own, width), BF16),
            pltpu.SemaphoreType.DMA((2, fold)),
            pltpu.SemaphoreType.DMA((3,)),
        ],
        compiler_params=params(1),
        cost_estimate=pl.CostEstimate(
            flops=2 * rows * width * width * steps, transcendentals=0,
            bytes_accessed=2 * rows * width * (steps + 3),
        ),
        name="weight_grads",
    )(left, d_upper, attended, d_branch, d_ffn)


ORDERS = ((3, 1, 2, 0), (3, 2, 1, 0)) * 3
MATRICES = 3
MESH = pl.DeviceIdType.MESH


def remaining(part, level):
    return [axis for axis in range(4) if axis not in ORDERS[part][:level]]


def tail_kernel(
    dims, w_ref, tok_ref, mixed_ref, one_ref, dense_ref, up_ref, line_ref, bins_ref,
    grad_ref, sums_ref, input_ref, *scratch
):
    parts, width = len(ORDERS), tok_ref.shape[0]
    cut = MATRICES * width // parts
    holders = [scratch[8 * part : 8 * part + 4] for part in range(parts)]
    inboxes = [scratch[8 * part + 4 : 8 * part + 8] for part in range(parts)]
    (
        turned, mixed, weights, kept, stage, own_sums, got_sums,
        send_sems, recv_sems, load_sems, keep_sems, store_sems,
    ) = scratch[8 * parts :]
    deep, across, along, cores = dims
    dp, fsdp = lax.axis_index("dp"), lax.axis_index("fsdp")
    mine = (dp // across, dp % across, fsdp // cores, fsdp % cores)
    docs, padded = one_ref.shape[0], one_ref.shape[1]
    rows, block = input_ref.shape[1], kept.shape[1]

    def peer(axis, step):
        place = list(mine)
        place[axis] = (place[axis] + step) % dims[axis]
        return place[axis], (place[0] * across + place[1], place[2] * cores + place[3])

    loads = [pltpu.make_async_copy(tok_ref, turned, load_sems.at[0])]
    for part in range(MATRICES):
        loads.append(
            pltpu.make_async_copy(
                mixed_ref.at[:, pl.ds(part * width, width)], mixed.at[part], load_sems.at[1 + part]
            )
        )
    loads.append(
        pltpu.make_async_copy(
            w_ref.at[:, pl.ds(0, MATRICES * width)], weights, load_sems.at[1 + MATRICES]
        )
    )
    for load in loads:
        load.start()

    barrier = pltpu.get_barrier_semaphore()
    partners = 0
    for axis in range(4):
        for step in range(1, dims[axis]):
            pl.semaphore_signal(barrier, inc=1, device_id=peer(axis, step)[1], device_id_type=MESH)
            partners += 1
    pl.semaphore_wait(barrier, partners)

    flying = {}

    def launch(lane, axis, source, target):
        copies = []
        for step in range(1, dims[axis]):
            place, device = peer(axis, step)
            copies.append(
                pltpu.make_async_remote_copy(
                    src_ref=source(place),
                    dst_ref=target(step - 1),
                    send_sem=send_sems.at[lane, step - 1],
                    recv_sem=recv_sems.at[lane, step - 1],
                    device_id=device,
                    device_id_type=MESH,
                )
            )
        for copy in copies:
            copy.start()
        flying[lane] = copies

    def land(lane):
        for copy in flying.pop(lane):
            copy.wait()

    def joined(own, others):
        total = own.astype(F32)
        for other in others:
            total = total + other.astype(F32)
        return total

    def send(part, level):
        axis, axes = ORDERS[part][level], remaining(part, level)

        def source(place):
            return holders[part][level].at[
                tuple(place if item == axis else slice(None) for item in axes)
            ]

        launch(4 * part + level, axis, source, lambda slot: inboxes[part][level].at[slot])

    def join(part, level):
        land(4 * part + level)
        axis, axes = ORDERS[part][level], remaining(part, level)
        source, box = holders[part][level], inboxes[part][level]
        left = [item for item in axes if item != axis]
        count = dims[axis] - 1
        if not left:
            grad_ref[:, part * cut : (part + 1) * cut] = joined(
                source[mine[axis]], [box[slot] for slot in range(count)]
            )
            return
        spots = [()]
        for item in left[1:]:
            spots = [spot + (place,) for spot in spots for place in range(dims[item])]

        def add(k, carry):
            for spot in spots:
                there = (k,) + spot
                where = dict(zip(left, there))
                where[axis] = mine[axis]
                own = tuple(where[item] for item in axes)
                holders[part][level + 1][there] = joined(
                    source[own], [box[(slot,) + there] for slot in range(count)]
                ).astype(BF16)
            return carry

        lax.fori_loop(0, dims[left[0]], add, 0)
        send(part, level + 1)

    small_order = (3, 1, 2, 0)
    chunks = width // LANES
    span = 8 * min(2, chunks)
    rest = sums_ref.shape[0] - span

    def window(place):
        return pl.ds(pl.multiple_of(8 * window_start(place, width, deep), 8), span)

    tail_lines = pl.ds(8 * chunks, rest)

    def small_send(level):
        axis, lane = small_order[level], 4 * parts + level
        if level < 3:
            launch(lane, axis, lambda place: own_sums.at[level], lambda slot: got_sums.at[level, slot])
            return
        launch(
            lane, axis,
            lambda place: own_sums.at[3, window(place)],
            lambda slot: got_sums.at[3, slot, pl.ds(0, span)],
        )
        launch(
            lane + 1, axis,
            lambda place: own_sums.at[3, tail_lines],
            lambda slot: got_sums.at[3, slot, tail_lines],
        )

    def small_join(level):
        axis, lane = small_order[level], 4 * parts + level
        land(lane)
        slots = range(dims[axis] - 1)
        if level < 3:
            own_sums[level + 1] = joined(own_sums[level], [got_sums[level, slot] for slot in slots])
            small_send(level + 1)
            return
        land(lane + 1)
        sums_ref[0:span] = joined(
            own_sums[3, window(mine[0])], [got_sums[3, slot, 0:span] for slot in slots]
        )
        sums_ref[span:] = joined(
            own_sums[3, tail_lines], [got_sums[3, slot, tail_lines] for slot in slots]
        )

    spans = [(doc, first) for doc in range(docs) for first in range(0, padded, block)]

    def keep(step):
        doc, first = spans[step]
        return pltpu.make_async_copy(
            one_ref.at[doc, pl.ds(first, block), :], kept.at[step % 2], keep_sems.at[step % 2]
        )

    def store(step):
        doc, first = spans[step]
        count = min(block, rows - first)
        return pltpu.make_async_copy(
            stage.at[step % 2, pl.ds(0, count)],
            input_ref.at[doc, pl.ds(first, count)],
            store_sems.at[step % 2],
        )

    def input_step(step):
        doc, first = spans[step]
        if step == 0:
            loads[1 + MATRICES].wait()
            keep(0).start()
        if step + 1 < len(spans):
            keep(step + 1).start()
        keep(step).wait()
        if step >= 2:
            store(step - 2).wait()
        at = pl.ds(doc * padded + first, block)
        total = kept[step % 2]
        for part in range(MATRICES):
            total = total + dot_nt(
                mixed[part, at, :], weights[:, part * width : (part + 1) * width]
            )
        stage[step % 2, :, 0, :] = total
        store(step).start()

    loads[0].wait()
    place = lax.broadcasted_iota(jnp.int32, (8, width), 0)
    eight = jnp.where(
        place == 4, line_ref[:, :width],
        jnp.where(place == 5, line_ref[:, 2 * width :], dense_ref[...]),
    )
    for chunk in range(chunks):
        own_sums[0, 8 * chunk : 8 * chunk + 8] = eight[:, chunk * LANES : (chunk + 1) * LANES]
    ups = up_ref.shape[1] // LANES
    for chunk in range(ups):
        at = 8 * chunks + chunk
        own_sums[0, at : at + 1] = up_ref[:, chunk * LANES : (chunk + 1) * LANES]
    own_sums[0, 8 * chunks + ups :] = bins_ref[...]
    small_send(0)

    def multiply(matrix):
        loads[1 + matrix].wait()
        for part in range(matrix * parts // MATRICES, (matrix + 1) * parts // MATRICES):
            first = part * cut - matrix * width
            block_rows = dot(turned[...], mixed[matrix, :, first : first + cut])
            holders[part][0][...] = block_rows.reshape(holders[part][0].shape).astype(BF16)
            send(part, 0)

    multiply(0)
    small_join(0)
    multiply(1)
    join(0, 0)
    join(1, 0)
    multiply(2)
    small_join(1)
    join(2, 0)
    join(3, 0)
    join(0, 1)
    join(1, 1)
    join(4, 0)
    join(5, 0)
    small_join(2)
    input_step(0)
    join(2, 1)
    join(3, 1)
    join(0, 2)
    join(1, 2)
    input_step(1)
    join(4, 1)
    join(5, 1)
    join(2, 2)
    join(3, 2)
    input_step(2)
    small_join(3)
    join(4, 2)
    join(5, 2)
    input_step(3)
    for part in range(parts):
        join(part, 3)
    for step in range(max(len(spans) - 2, 0), len(spans)):
        store(step).wait()


def split_mesh(dp, fsdp):
    across = 1 << ((dp.bit_length() - 1) // 2)
    across = across if dp % across == 0 else 1
    cores = 2 if fsdp % 2 == 0 else 1
    return dp // across, across, fsdp // cores, cores


def window_start(place, width, deep):
    chunks = width // LANES
    return jnp.minimum(place * (width // deep) // LANES, max(chunks - 2, 0))


def tail(w_mixed, tok, d_mixed, d_one, sums, up_sum, line, bins, rows, dims):
    docs, padded, width = d_one.shape
    parts = len(ORDERS)
    cut = MATRICES * width // parts
    devices = dims[0] * dims[1] * dims[2] * dims[3]
    own = width // devices
    more = up_sum.shape[1] // LANES + bins.shape[0]
    small = (8 * width // LANES + more, LANES)
    lines = 8 * min(2, width // LANES) + more
    any_space = pl.BlockSpec(memory_space=pl.ANY)
    vmem = pl.BlockSpec(memory_space=pltpu.VMEM)
    scratch = []
    for part in range(parts):
        boxes = []
        for level in range(4):
            axes = remaining(part, level)
            axis = ORDERS[part][level]
            scratch.append(pltpu.VMEM(tuple(dims[item] for item in axes) + (own, cut), BF16))
            boxes.append(
                pltpu.VMEM(
                    (max(dims[axis] - 1, 1),)
                    + tuple(dims[item] for item in axes if item != axis)
                    + (own, cut),
                    BF16,
                )
            )
        scratch += boxes
    most = max(max(dims) - 1, 1)
    flat = docs * padded
    scratch += [
        pltpu.VMEM((width, flat), BF16),
        pltpu.VMEM((MATRICES, flat, width), BF16),
        pltpu.VMEM((width, MATRICES * width), BF16),
        pltpu.VMEM((2, DENSE_BLOCK, width), F32),
        pltpu.VMEM((2, DENSE_BLOCK, 1, width), F32),
        pltpu.VMEM((4,) + small, F32),
        pltpu.VMEM((4, most) + small, F32),
        pltpu.SemaphoreType.DMA((4 * parts + 5, most)),
        pltpu.SemaphoreType.DMA((4 * parts + 5, most)),
        pltpu.SemaphoreType.DMA((MATRICES + 2,)),
        pltpu.SemaphoreType.DMA((2,)),
        pltpu.SemaphoreType.DMA((2,)),
    ]
    return pl.pallas_call(
        partial(tail_kernel, dims),
        out_shape=(
            jax.ShapeDtypeStruct((own, MATRICES * width), F32),
            jax.ShapeDtypeStruct((lines, LANES), F32),
            jax.ShapeDtypeStruct((docs, rows, 1, width), F32),
        ),
        in_specs=[any_space] * 4 + [vmem] * 4,
        out_specs=(vmem, vmem, any_space),
        scratch_shapes=scratch,
        compiler_params=pltpu.CompilerParams(
            collective_id=0, has_side_effects=True, vmem_limit_bytes=VMEM_LIMIT
        ),
        name="tail",
    )(w_mixed, tok, d_mixed, d_one, sums, up_sum, line, bins)


def handed_on(rows_out):
    docs, count, unused, width = rows_out.shape
    pieces = 4
    edges = [count * piece // pieces for piece in range(pieces + 1)]

    def kernel(in_ref, out_ref, held_ref, in_sems, out_sems):
        arrivals, departures = [], []
        for doc in range(docs):
            for piece in range(pieces):
                at = pl.ds(edges[piece], edges[piece + 1] - edges[piece])
                held = held_ref.at[doc, at]
                arrivals.append(
                    pltpu.make_async_copy(in_ref.at[doc, at], held, in_sems.at[doc, piece])
                )
                departures.append(
                    pltpu.make_async_copy(held, out_ref.at[doc, at], out_sems.at[doc, piece])
                )
        for copy in arrivals:
            copy.start()
        for arrival, departure in zip(arrivals, departures):
            arrival.wait()
            departure.start()
        for copy in departures:
            copy.wait()

    return pl.pallas_call(
        kernel,
        out_shape=jax.ShapeDtypeStruct(rows_out.shape, rows_out.dtype),
        in_specs=[pl.BlockSpec(memory_space=pl.ANY)],
        out_specs=pl.BlockSpec(memory_space=pl.ANY),
        scratch_shapes=[
            pltpu.VMEM(rows_out.shape, rows_out.dtype),
            pltpu.SemaphoreType.DMA((docs, pieces)),
            pltpu.SemaphoreType.DMA((docs, pieces)),
        ],
        compiler_params=pltpu.CompilerParams(vmem_limit_bytes=VMEM_LIMIT),
        name="handed_on",
    )(rows_out)


def small_results(packed, width, hidden, heads, deep, own, place):
    span, more = 8 * min(2, width // LANES), hidden // LANES
    sums = jnp.transpose(packed[:span].reshape(-1, 8, LANES), (1, 0, 2)).reshape(8, -1)
    depth = place * own // (width // deep)
    first = place * own - LANES * window_start(depth, width, deep)
    sums = lax.dynamic_slice_in_dim(sums, first, own, 1)
    fold = hidden // width * own
    up_sum = packed[span : span + more].reshape(hidden)
    up_sum = lax.dynamic_slice_in_dim(up_sum, place * fold, fold, 0)
    return sums, up_sum, table_grad(packed[span + more :], heads)


def local_step(dims, lengths, pos_buckets, box_buckets, layer_input, cotangent, w_mixed, w_down, vectors, up_row, table):
    heads, width = table.shape[1], layer_input.shape[3]
    docs, rows = layer_input.shape[0], layer_input.shape[2]
    bias = bias_rows(lengths, table_entries(table), pos_buckets, box_buckets, heads)
    qkv, tok = project(layer_input, w_mixed, vectors)
    probs, attended, turned = attend(qkv, bias)
    result, d_one, left, d_upper, d_ffn, d_branch, d_attended, sums, up_sum = dense(
        layer_input, attended, cotangent, w_mixed, w_down, vectors, up_row
    )

    def flat(item):
        return item.reshape(-1, item.shape[-1])

    d_weights = weight_grads(
        turned, flat(d_branch), left, flat(d_upper), flat(d_ffn), dims[0] * dims[1] * dims[2] * dims[3]
    )
    d_mixed, bins, line = attend_back(qkv, probs, d_attended, attended, pos_buckets, box_buckets)
    return result, d_weights, (w_mixed, tok, flat(d_mixed), d_one, sums, up_sum, line, bins, rows, dims)


def body(
    layer_input, text_lengths, pos_buckets, box_buckets, w_qkv, w_out, w_up, w_down,
    norm_gains, norm_shifts, proj_biases, up_bias, rel_tables, cotangent,
):
    axes = ("dp", "fsdp")
    width, hidden = layer_input.shape[3], w_up.shape[1]
    own = norm_gains.shape[1]
    table = lax.all_gather(rel_tables, "fsdp", axis=0, tiled=True)
    heads = table.shape[1]
    small = jnp.concatenate(
        [
            jnp.concatenate([norm_gains, norm_shifts, proj_biases], axis=0).T,
            up_bias.reshape(own, hidden // width),
        ],
        axis=1,
    )
    small = jnp.pad(small, ((0, 0), (0, LANES - small.shape[1])))
    w_mixed = lax.all_gather(
        jnp.concatenate([w_qkv, w_out, w_up, small], axis=1), axes, axis=0, tiled=True
    )
    w_down = lax.all_gather(w_down, axes, axis=0, tiled=True)
    small = w_mixed[:, 4 * width + hidden :].astype(F32)
    vectors = small[:, :8].T
    up_row = small[:, 8 : 8 + hidden // width].reshape(1, hidden)
    dims = split_mesh(lax.axis_size("dp"), lax.axis_size("fsdp"))
    result, d_weights, rest = local_step(
        dims, text_lengths[:, 0], pos_buckets, box_buckets, layer_input, cotangent, w_mixed, w_down,
        vectors, up_row, table,
    )
    d_weights = lax.psum_scatter(
        d_weights.reshape(width, -1), axes, scatter_dimension=0, tiled=True
    ).astype(F32)
    d_down = [d_weights[:, first : first + width] for first in range(width + hidden, width + 2 * hidden, width)]
    d_down = jnp.concatenate(d_down, axis=0)
    d_qkv, packed, input_grad = tail(*rest)
    sums, up_sum, d_table = small_results(
        packed, width, hidden, heads, dims[0], own, lax.axis_index(axes)
    )
    table_rows = rel_tables.shape[0]
    d_table = lax.dynamic_slice_in_dim(d_table, lax.axis_index("fsdp") * table_rows, table_rows, 0)
    return (
        result, jnp.transpose(handed_on(input_grad), (0, 2, 1, 3)), d_qkv, d_weights[:, :width], d_weights[:, width : width + hidden], d_down,
        sums[0:2], sums[2:4], sums[4:8], up_sum, d_table,
    )


def solution(mesh):
    both = ("dp", "fsdp")
    docs = P(None, both, None, None)
    return jax.shard_map(
        body,
        mesh=mesh,
        in_specs=(
            docs, P(None, both), docs, P(None, both, None, None, None),
            P(both, None), P(both, None), P(both, None), P(both, None),
            P(None, both), P(None, both), P(None, both), P(both), P("fsdp", None), docs,
        ),
        out_specs=(
            docs, docs, P(both, None), P(both, None), P(both, None), P(both, None),
            P(None, both), P(None, both), P(None, both), P(both), P("fsdp", None),
        ),
        check_vma=False,
    )
```

```python
from functools import partial

import jax
import jax.numpy as jnp
from jax import lax
from jax.experimental import pallas as pl
from jax.experimental.pallas import tpu as pltpu
from jax.sharding import PartitionSpec as P

HEAD_DIM = 64
POS_BINS = 32
BOX_BINS = 64
TEXT_SLOTS = 512
NEG_FILL = -1000000000.0
NORM_EPS = 1e-05
BLOCK = 256
DENSE_BLOCK = 384
LANES = 128
HALF = 32
SPLIT = 1
LINES = 1
SCALE = 0.125
F32 = jnp.float32
BF16 = jnp.bfloat16
VMEM_LIMIT = 58 << 20


def dot(left, right):
    return jnp.dot(left, right, preferred_element_type=F32)


def dot_nt(left, right):
    return lax.dot_general(left, right, (((1,), (1,)), ((), ())), preferred_element_type=F32)


def params(count):
    return pltpu.CompilerParams(
        dimension_semantics=("arbitrary",) * count, vmem_limit_bytes=VMEM_LIMIT
    )


def resident(shape):
    zeros = (0,) * len(shape)
    return pl.BlockSpec(shape, lambda *_: zeros, pipeline_mode=pl.Buffered(1))


def columns(shape, place):
    return pl.BlockSpec(shape, lambda *_: (0, place), pipeline_mode=pl.Buffered(1))


def live_rows(values, rows, first):
    row = first + lax.broadcasted_iota(jnp.int32, (values.shape[0], 1), 0)
    return jnp.where(row < rows, values, jnp.zeros_like(values))


def bias_kernel(rows, len_ref, tab_ref, pos_ref, box_ref, out_ref):
    heads, chunks = out_ref.shape[1], out_ref.shape[3] // LANES
    block = pl.program_id(1)
    length = len_ref[pl.program_id(0)]
    steps = jnp.minimum(BLOCK, (rows + 7) // 8 * 8 - block * BLOCK) // 8

    def fill(step, carry):
        at = pl.ds(pl.multiple_of(step * 8, 8), 8)
        for chunk in range(chunks):
            cols = slice(chunk * LANES, (chunk + 1) * LANES)
            picks = (
                box_ref[0, 0, 0, at, cols] & (BOX_BINS - 1),
                (box_ref[0, 0, 1, at, cols] & (BOX_BINS - 1)) | BOX_BINS,
                pos_ref[0, 0, at, cols] & (POS_BINS - 1),
            )
            slot = chunk * LANES + lax.broadcasted_iota(jnp.int32, (8, LANES), 1)
            valid = ((slot >= TEXT_SLOTS) & (slot < rows)) | (slot < length)
            totals = [None] * heads
            for which, pick in enumerate(picks):
                for head in range(heads):
                    line = head + (heads if which == 2 else 0)
                    entries = jnp.broadcast_to(tab_ref[line : line + 1, :], (8, LANES))
                    term = jnp.take_along_axis(entries, pick, axis=1)
                    totals[head] = term if which == 0 else totals[head] + term
            for head in range(heads):
                out_ref[0, head, at, cols] = jnp.where(valid, totals[head], NEG_FILL)
        return carry

    def blank(step, carry):
        at = pl.ds(pl.multiple_of(step * 8, 8), 8)
        for head in range(heads):
            out_ref[0, head, at, :] = jnp.zeros((8, chunks * LANES), F32)
        return carry

    lax.fori_loop(0, steps, fill, 0)
    lax.fori_loop(steps, BLOCK // 8, blank, 0)


def bias_rows(lengths, entries, pos_buckets, box_buckets, heads):
    docs, rows = pos_buckets.shape[0], pos_buckets.shape[2]
    padded = pl.cdiv(rows, BLOCK) * BLOCK
    return pl.pallas_call(
        partial(bias_kernel, rows),
        out_shape=jax.ShapeDtypeStruct((docs, heads, padded, padded), F32),
        grid=(docs, padded // BLOCK),
        in_specs=[
            pl.BlockSpec(memory_space=pltpu.SMEM),
            resident(entries.shape),
            pl.BlockSpec((1, 1, BLOCK, padded), lambda d, i: (d, 0, i, 0)),
            pl.BlockSpec((1, 1, 2, BLOCK, padded), lambda d, i: (d, 0, 0, i, 0)),
        ],
        out_specs=pl.BlockSpec((1, heads, BLOCK, padded), lambda d, i: (d, 0, i, 0)),
        compiler_params=params(2),
        cost_estimate=pl.CostEstimate(
            flops=3 * docs * heads * rows * rows,
            transcendentals=0,
            bytes_accessed=docs * padded * padded * (4 * heads + 12),
        ),
        name="bias_rows",
    )(lengths, entries, pos_buckets, box_buckets)


def project_kernel(rows, x_ref, w_ref, vec_ref, out_ref, tok_ref):
    width = x_ref.shape[3]
    block = live_rows(x_ref[0, 0], rows, pl.program_id(1) * x_ref.shape[2])
    tok_ref[...] = block.T
    queries = dot(block, w_ref[:, :width]) + vec_ref[4:5, :]
    out_ref[0, :, :width] = queries.astype(BF16) * BF16(SCALE)
    out_ref[0, :, width : 2 * width] = dot(block, w_ref[:, width : 2 * width]).astype(BF16)
    values = dot(block, w_ref[:, 2 * width :]) + vec_ref[5:6, :]
    out_ref[0, :, 2 * width :] = values.astype(BF16)


def project(layer_input, w_mixed, vectors):
    docs, unused, rows, width = layer_input.shape
    padded = pl.cdiv(rows, BLOCK) * BLOCK
    return pl.pallas_call(
        partial(project_kernel, rows),
        out_shape=(
            jax.ShapeDtypeStruct((docs, padded, 3 * width), BF16),
            jax.ShapeDtypeStruct((width, docs * padded), BF16),
        ),
        grid=(docs, padded // DENSE_BLOCK),
        in_specs=[
            pl.BlockSpec((1, 1, DENSE_BLOCK, width), lambda d, i: (d, 0, i, 0)),
            columns((width, 3 * width), 0),
            resident(vectors.shape),
        ],
        out_specs=(
            pl.BlockSpec((1, DENSE_BLOCK, 3 * width), lambda d, i: (d, i, 0)),
            pl.BlockSpec((width, DENSE_BLOCK), lambda d, i: (0, d * (padded // DENSE_BLOCK) + i)),
        ),
        compiler_params=params(2),
        name="project",
    )(layer_input, w_mixed, vectors)


def attend_kernel(q_ref, k_ref, v_ref, bias_ref, probs_ref, out_ref, turned_ref):
    lane = lax.broadcasted_iota(jnp.int32, (1, LANES), 1)
    for pair in range(q_ref.shape[2] // LANES):
        cols = slice(pair * LANES, (pair + 1) * LANES)
        queries, key_rows, values = q_ref[0, :, cols], k_ref[0, :, cols], v_ref[0, :, cols]
        total = None
        for half in range(2):
            head = 2 * pair + half
            keep = (lane < HEAD_DIM) if half == 0 else (lane >= HEAD_DIM)
            scores = dot_nt(jnp.where(keep, queries, BF16(0)), key_rows) + bias_ref[0, head]
            top = jnp.max(scores, axis=-1, keepdims=True)
            powers = jnp.exp(scores - top)
            share = 1.0 / jnp.sum(powers, axis=-1, keepdims=True)
            probs = (powers * share).astype(BF16)
            probs_ref[0, head] = probs
            part = dot(probs, jnp.where(keep, values, BF16(0)))
            total = part if half == 0 else total + part
        low = total.astype(BF16)
        out_ref[0, :, cols] = low
        turned_ref[cols, :] = low.T


def attend(qkv, bias):
    docs, padded, width = qkv.shape[0], qkv.shape[1], qkv.shape[2] // 3
    heads = bias.shape[1]
    return pl.pallas_call(
        attend_kernel,
        out_shape=(
            jax.ShapeDtypeStruct((docs, heads, padded, padded), BF16),
            jax.ShapeDtypeStruct((docs, padded, width), BF16),
            jax.ShapeDtypeStruct((width, docs * padded), BF16),
        ),
        grid=(docs, padded // BLOCK),
        in_specs=[
            pl.BlockSpec((1, BLOCK, width), lambda d, i: (d, i, 0)),
            pl.BlockSpec((1, padded, width), lambda d, i: (d, 0, 1)),
            pl.BlockSpec((1, padded, width), lambda d, i: (d, 0, 2)),
            pl.BlockSpec((1, heads, BLOCK, padded), lambda d, i: (d, 0, i, 0)),
        ],
        out_specs=(
            pl.BlockSpec((1, heads, BLOCK, padded), lambda d, i: (d, 0, i, 0)),
            pl.BlockSpec((1, BLOCK, width), lambda d, i: (d, i, 0)),
            pl.BlockSpec((width, BLOCK), lambda d, i: (0, d * (padded // BLOCK) + i)),
        ),
        compiler_params=params(2),
        name="attend",
    )(qkv, qkv, qkv, bias)


def norm(rows_in):
    centre = rows_in - jnp.mean(rows_in, axis=-1, keepdims=True)
    inv_std = lax.rsqrt(jnp.mean(centre * centre, axis=-1, keepdims=True) + NORM_EPS)
    return centre * inv_std, inv_std


def norm_back(grad_in, normed, inv_std, gain_row):
    scaled = grad_in * gain_row
    return inv_std * (
        scaled
        - jnp.mean(scaled, axis=-1, keepdims=True)
        - normed * jnp.mean(scaled * normed, axis=-1, keepdims=True)
    )


def dense_kernel(
    rows, x_ref, o_ref, cot_ref, wo_ref, wu_ref, wd_ref, vec_ref, upb_ref,
    y_ref, dr_ref, left_ref, du_ref, df_ref, db_ref, do_ref, sums_ref, upsum_ref,
    slope_ref,
):
    width, hidden = wu_ref.shape
    first = pl.program_id(1) * x_ref.shape[2]
    vec = vec_ref[...]

    @pl.when((pl.program_id(0) == 0) & (pl.program_id(1) == 0))
    def _():
        sums_ref[...] = jnp.zeros_like(sums_ref)
        upsum_ref[...] = jnp.zeros_like(upsum_ref)

    tok = live_rows(x_ref[0, 0], rows, first).astype(F32)
    normed_one, inv_one = norm(tok + dot(o_ref[0], wo_ref[...]) + vec[6:7])
    state = normed_one * vec[0:1] + vec[2:3]
    low = state.astype(BF16)
    left_ref[0:width, :] = low.T
    second = state + vec[7:8]
    for part in range(hidden // width):
        cols = slice(part * width, (part + 1) * width)
        upper = dot(low, wu_ref[:, cols]) + upb_ref[:, cols]
        cdf = 0.5 * (1.0 + lax.erf(upper * (0.5**0.5)))
        slope_ref[:, cols] = cdf + upper * (jnp.exp(-0.5 * upper * upper) * 0.3989422804014327)
        active = (upper * cdf).astype(BF16)
        left_ref[(part + 1) * width : (part + 2) * width, :] = active.T
        second = second + dot(active, wd_ref[cols, :])
    normed_two, inv_two = norm(second)
    y_ref[0, 0] = (normed_two * vec[1:2] + vec[3:4]).astype(BF16)
    grad = live_rows(cot_ref[0, 0], rows, first).astype(F32)
    sums_ref[1:2, :] += jnp.sum(grad * normed_two, axis=0, keepdims=True)
    sums_ref[3:4, :] += jnp.sum(grad, axis=0, keepdims=True)
    d_two = norm_back(grad, normed_two, inv_two, vec[1:2])
    d_ffn = d_two.astype(BF16)
    df_ref[0] = d_ffn
    sums_ref[7:8, :] += jnp.sum(d_ffn.astype(F32), axis=0, keepdims=True)
    back = d_two
    for part in range(hidden // width):
        cols = slice(part * width, (part + 1) * width)
        d_upper = (dot_nt(d_ffn, wd_ref[cols, :]) * slope_ref[:, cols]).astype(BF16)
        du_ref[0, :, cols] = d_upper
        upsum_ref[:, cols] += jnp.sum(d_upper.astype(F32), axis=0, keepdims=True)
        back = back + dot_nt(d_upper, wu_ref[:, cols])
    sums_ref[0:1, :] += jnp.sum(back * normed_one, axis=0, keepdims=True)
    sums_ref[2:3, :] += jnp.sum(back, axis=0, keepdims=True)
    d_one = norm_back(back, normed_one, inv_one, vec[0:1])
    dr_ref[0] = d_one
    d_branch = d_one.astype(BF16)
    db_ref[0] = d_branch
    sums_ref[6:7, :] += jnp.sum(d_branch.astype(F32), axis=0, keepdims=True)
    do_ref[0] = dot_nt(d_branch, wo_ref[...]).astype(BF16)


def dense(layer_input, attended, cotangent, w_mixed, w_down, vectors, up_row):
    docs, unused, rows, width = layer_input.shape
    padded, hidden = attended.shape[1], w_down.shape[0]
    ragged = pl.BlockSpec((1, 1, DENSE_BLOCK, width), lambda d, i: (d, 0, i, 0))
    narrow = pl.BlockSpec((1, DENSE_BLOCK, width), lambda d, i: (d, i, 0))
    wide = pl.BlockSpec((1, DENSE_BLOCK, hidden), lambda d, i: (d, i, 0))

    def turned(lines):
        return pl.BlockSpec(
            (lines, DENSE_BLOCK), lambda d, i: (0, d * (padded // DENSE_BLOCK) + i)
        )

    def rows_of(columns, dtype):
        return jax.ShapeDtypeStruct((docs, padded, columns), dtype)

    return pl.pallas_call(
        partial(dense_kernel, rows),
        out_shape=(
            jax.ShapeDtypeStruct(layer_input.shape, BF16),
            rows_of(width, F32),
            jax.ShapeDtypeStruct((width + hidden, docs * padded), BF16),
            rows_of(hidden, BF16),
            rows_of(width, BF16),
            rows_of(width, BF16),
            rows_of(width, BF16),
            jax.ShapeDtypeStruct((8, width), F32),
            jax.ShapeDtypeStruct((1, hidden), F32),
        ),
        grid=(docs, padded // DENSE_BLOCK),
        in_specs=[
            ragged, narrow, ragged,
            columns((width, width), 3), columns((width, hidden), 4 * width // hidden),
            resident(w_down.shape),
            resident(vectors.shape), resident(up_row.shape),
        ],
        out_specs=(
            ragged, narrow, turned(width + hidden), wide, narrow, narrow, narrow,
            pl.BlockSpec((8, width), lambda d, i: (0, 0)),
            pl.BlockSpec((1, hidden), lambda d, i: (0, 0)),
        ),
        scratch_shapes=[pltpu.VMEM((DENSE_BLOCK, hidden), F32)],
        compiler_params=params(2),
        name="dense",
    )(layer_input, attended, cotangent, w_mixed, w_mixed, w_down, vectors, up_row)


def attend_back_kernel(
    rows, q_ref, k_ref, v_ref, probs_ref, do_ref, o_ref, pos_ref, box_ref, dm_ref, bins_ref, line_ref,
    dk_ref, dv_ref, ds_ref, acc_ref, picks_ref,
):
    block, width = pl.program_id(1), q_ref.shape[2]
    padded = k_ref.shape[1]
    lane = lax.broadcasted_iota(jnp.int32, (1, LANES), 1)

    @pl.when((pl.program_id(0) == 0) & (block == 0))
    def _():
        acc_ref[...] = jnp.zeros_like(acc_ref)
        line_ref[...] = jnp.zeros_like(line_ref)
        ds_ref[...] = jnp.zeros_like(ds_ref)

    @pl.when(block == 0)
    def _():
        dk_ref[...] = jnp.zeros_like(dk_ref)
        dv_ref[...] = jnp.zeros_like(dv_ref)

    own = pl.ds(pl.multiple_of(block * BLOCK, BLOCK), BLOCK)
    for pair in range(width // LANES):
        cols = slice(pair * LANES, (pair + 1) * LANES)
        queries, key_rows, values = q_ref[0, :, cols], k_ref[0, :, cols], v_ref[0, :, cols]
        grads = do_ref[0, :, cols]
        turned_q, turned_g = queries.T, grads.T
        shared = grads.astype(F32) * o_ref[0, :, cols].astype(F32)
        total = None
        for half in range(2):
            head = 2 * pair + half
            keep = (lane < HEAD_DIM) if half == 0 else (lane >= HEAD_DIM)
            part = slice(half * HEAD_DIM, (half + 1) * HEAD_DIM)
            lines = slice(head * HEAD_DIM, (head + 1) * HEAD_DIM)
            low = probs_ref[0, head]
            probs = low.astype(F32)
            dprobs = dot_nt(jnp.where(keep, grads, BF16(0)), values)
            delta = jnp.sum(jnp.where(keep, shared, 0.0), axis=-1, keepdims=True)
            dscore = probs * (dprobs - delta)
            for chunk in range(padded // LANES):
                ds_ref[chunk, pl.ds(head, BLOCK, stride=16), :] = dscore[
                    :, chunk * LANES : (chunk + 1) * LANES
                ]
            dlow = dscore.astype(BF16)
            piece = dot(dlow, jnp.where(keep, key_rows, BF16(0)))
            total = piece if half == 0 else total + piece
            dk_ref[lines, :] += dot(turned_q[part, :], dlow)
            dv_ref[lines, :] += dot(turned_g[part, :], low)
        dm_ref[0, own, cols] = (total * SCALE).astype(BF16)

    group = 32
    low_bins = lax.broadcasted_iota(jnp.int32, (HALF, LANES), 0).astype(BF16)

    def hits(picks, bins):
        low = picks.astype(BF16)
        return jnp.concatenate(
            [
                jnp.where(low_bins[first : first + 16] == low, BF16(1), BF16(0))
                for first in range(0, bins, 16)
            ],
            axis=0,
        )

    for place, (picks, bits) in enumerate(
        (
            (box_ref[0, 0, 0], BOX_BINS),
            (box_ref[0, 0, 1], BOX_BINS),
            (pos_ref[0, 0], POS_BINS),
        )
    ):
        half = bits // 2
        for chunk in range(padded // LANES):
            part = picks[:, chunk * LANES : (chunk + 1) * LANES] & (bits - 1)
            picks_ref[2 * place, chunk] = (part & (half - 1)).astype(F32)
            picks_ref[2 * place + 1, chunk] = (part >> (half.bit_length() - 1)).astype(F32)

    def count(step, carry):
        total = None
        for line in range(0, group, LINES):
            left, right = [], []
            for own in range(LINES):
                row = step * group + line + own
                here = pl.ds(pl.multiple_of(row * 16, 16), 16)
                again = pl.ds(row, 16, stride=0)
                for chunk in range(padded // LANES):
                    base = ds_ref[chunk, here, :]
                    left.append(
                        jnp.concatenate(
                            [base.astype(BF16)]
                            + [
                                (base * picks_ref[2 * place + 1, chunk, again, :]).astype(BF16)
                                for place in range(3)
                            ],
                            axis=0,
                        )
                    )
                    right.append(
                        jnp.concatenate(
                            [
                                hits(picks_ref[2 * place, chunk, again, :], bins)
                                for place, bins in enumerate((HALF, HALF, HALF // 2))
                            ],
                            axis=0,
                        )
                    )
            part = dot_nt(jnp.concatenate(left, axis=1), jnp.concatenate(right, axis=1))
            total = part if total is None else total + part
        acc_ref[0, :, : total.shape[1]] += total
        return carry

    live = jnp.minimum(BLOCK, (rows + group - 1) // group * group - block * BLOCK)
    lax.fori_loop(0, live // group, count, 0)

    @pl.when(block == pl.num_programs(1) - 1)
    def _():
        dm_ref[0, :, width : 2 * width] = dk_ref[...].astype(BF16).T
        dm_ref[0, :, 2 * width :] = dv_ref[...].astype(BF16).T
        bins_ref[...] = jnp.sum(acc_ref[...], axis=0)
        line_ref[...] += dot(jnp.ones((16, padded), BF16), dm_ref[0])[0:8]


def attend_back(qkv, probs, d_attended, attended, pos_buckets, box_buckets):
    docs, padded, width = qkv.shape[0], qkv.shape[1], qkv.shape[2] // 3
    heads, rows = probs.shape[1], pos_buckets.shape[2]
    return pl.pallas_call(
        partial(attend_back_kernel, rows),
        out_shape=(
            jax.ShapeDtypeStruct((docs, padded, 3 * width), BF16),
            jax.ShapeDtypeStruct((64, LANES), F32),
            jax.ShapeDtypeStruct((8, 3 * width), F32),
        ),
        grid=(docs, padded // BLOCK),
        in_specs=[
            pl.BlockSpec((1, BLOCK, width), lambda d, i: (d, i, 0)),
            pl.BlockSpec((1, padded, width), lambda d, i: (d, 0, 1)),
            pl.BlockSpec((1, padded, width), lambda d, i: (d, 0, 2)),
            pl.BlockSpec((1, heads, BLOCK, padded), lambda d, i: (d, 0, i, 0)),
            pl.BlockSpec((1, BLOCK, width), lambda d, i: (d, i, 0)),
            pl.BlockSpec((1, BLOCK, width), lambda d, i: (d, i, 0)),
            pl.BlockSpec((1, 1, BLOCK, padded), lambda d, i: (d, 0, i, 0)),
            pl.BlockSpec((1, 1, 2, BLOCK, padded), lambda d, i: (d, 0, 0, i, 0)),
        ],
        out_specs=(
            pl.BlockSpec((1, padded, 3 * width), lambda d, i: (d, 0, 0)),
            pl.BlockSpec((64, LANES), lambda d, i: (0, 0)),
            pl.BlockSpec((8, 3 * width), lambda d, i: (0, 0)),
        ),
        scratch_shapes=[
            pltpu.VMEM((width, padded), F32),
            pltpu.VMEM((width, padded), F32),
            pltpu.VMEM((padded // LANES, BLOCK * 16, LANES), F32),
            pltpu.VMEM((SPLIT, 64, LANES), F32),
            pltpu.VMEM((6, padded // LANES, BLOCK, LANES), F32),
        ],
        compiler_params=params(2),
        name="attend_back",
    )(qkv, qkv, qkv, probs, d_attended, attended, pos_buckets, box_buckets)


def table_entries(table):
    heads = table.shape[1]
    lines = table.astype(F32).T * SCALE
    boxes = lines[:, POS_BINS:]
    spots = jnp.pad(lines[:, :POS_BINS], ((0, 0), (0, LANES - POS_BINS)))
    return jnp.concatenate([boxes, spots], axis=0).reshape(2 * heads, LANES)


def table_grad(bins, heads):
    base, upper = bins[:heads], (bins[16 : 16 + heads], bins[32 : 32 + heads], bins[48 : 48 + heads])
    pieces = []
    for which, (first, size) in enumerate(((0, HALF), (HALF, HALF), (2 * HALF, HALF // 2))):
        high = upper[which][:, first : first + size]
        pieces.append(jnp.concatenate([base[:, first : first + size] - high, high], axis=1))
    return jnp.concatenate([pieces[2], pieces[0], pieces[1]], axis=1).T * SCALE


def weight_grads(attended, d_branch, left, d_upper, d_ffn, devices):
    width, rows = attended.shape
    own, fold = width // devices, d_upper.shape[1] // width
    share = devices // fold
    steps = 1 + 2 * fold

    def kernel(
        l_ref, u_ref, a_ref, b_ref, f_ref, out_ref,
        attended_ref, branch_ref, ffn_ref, stage_ref, sems, load_sems,
    ):
        step = pl.program_id(0)
        slot = step % 2
        loads = [
            pltpu.make_async_copy(source, target, load_sems.at[place])
            for place, (source, target) in enumerate(
                ((f_ref, ffn_ref), (a_ref, attended_ref), (b_ref, branch_ref))
            )
        ]

        def flat_copy(part, spot):
            cols = pl.ds(pl.multiple_of(part * width, width), width)
            return pltpu.make_async_copy(
                stage_ref.at[spot], out_ref.at[:, :, cols], sems.at[spot, 0]
            )

        def fold_copy(where, spot, part):
            block = where - fold
            cols = pl.ds((1 + fold + part) * width, width)
            return pltpu.make_async_copy(
                stage_ref.at[spot].reshape(share, fold, own, width).at[:, part],
                out_ref.at[pl.ds(block * share, share), :, cols],
                sems.at[spot, part],
            )

        def wait_for(where, spot):
            @pl.when(where < fold)
            def _():
                flat_copy(where + 1, spot).wait()

            @pl.when((where >= fold) & (where < 2 * fold))
            def _():
                for part in range(fold):
                    fold_copy(where, spot, part).wait()

        @pl.when(step == 0)
        def _():
            for load in loads:
                load.start()

        @pl.when(step >= 2)
        def _():
            wait_for(step - 2, slot)

        def put(value):
            stage_ref[slot] = value.reshape(devices, own, width).astype(BF16)

        @pl.when(step < fold)
        def _():
            put(dot(l_ref[...], u_ref[...]))
            flat_copy(step + 1, slot).start()

        @pl.when(step == fold)
        def _():
            loads[0].wait()

        @pl.when((step >= fold) & (step < 2 * fold))
        def _():
            put(dot(l_ref[...], ffn_ref[...]))
            for part in range(fold):
                fold_copy(step, slot, part).start()

        @pl.when(step == 2 * fold)
        def _():
            loads[1].wait()
            loads[2].wait()
            put(dot(attended_ref[...], branch_ref[...]))
            flat_copy(0, slot).start()
            wait_for(step - 1, 1 - slot)
            flat_copy(0, slot).wait()

    away = pl.BlockSpec(memory_space=pl.ANY)
    return pl.pallas_call(
        kernel,
        out_shape=jax.ShapeDtypeStruct((devices, own, (1 + 2 * fold) * width), BF16),
        grid=(steps,),
        in_specs=[
            pl.BlockSpec((width, rows), lambda p: (jnp.clip(p - fold + 1, 0, fold), 0)),
            pl.BlockSpec((rows, width), lambda p: (0, jnp.minimum(p, fold - 1))),
            away,
            away,
            away,
        ],
        out_specs=away,
        scratch_shapes=[
            pltpu.VMEM((width, rows), BF16),
            pltpu.VMEM((rows, width), BF16),
            pltpu.VMEM((rows, width), BF16),
            pltpu.VMEM((2, devices, own, width), BF16),
            pltpu.SemaphoreType.DMA((2, fold)),
            pltpu.SemaphoreType.DMA((3,)),
        ],
        compiler_params=params(1),
        cost_estimate=pl.CostEstimate(
            flops=2 * rows * width * width * steps, transcendentals=0,
            bytes_accessed=2 * rows * width * (steps + 3),
        ),
        name="weight_grads",
    )(left, d_upper, attended, d_branch, d_ffn)


ORDERS = ((3, 1, 2, 0), (3, 2, 1, 0)) * 3
MATRICES = 3
MESH = pl.DeviceIdType.MESH


def remaining(part, level):
    return [axis for axis in range(4) if axis not in ORDERS[part][:level]]


def tail_kernel(
    dims, w_ref, tok_ref, mixed_ref, one_ref, dense_ref, up_ref, line_ref, bins_ref,
    grad_ref, sums_ref, input_ref, *scratch
):
    parts, width = len(ORDERS), tok_ref.shape[0]
    cut = MATRICES * width // parts
    holders = [scratch[8 * part : 8 * part + 4] for part in range(parts)]
    inboxes = [scratch[8 * part + 4 : 8 * part + 8] for part in range(parts)]
    (
        turned, mixed, weights, kept, stage, own_sums, got_sums,
        send_sems, recv_sems, load_sems, keep_sems, store_sems,
    ) = scratch[8 * parts :]
    deep, across, along, cores = dims
    dp, fsdp = lax.axis_index("dp"), lax.axis_index("fsdp")
    mine = (dp // across, dp % across, fsdp // cores, fsdp % cores)
    docs, padded = one_ref.shape[0], one_ref.shape[1]
    rows, block = input_ref.shape[1], kept.shape[1]

    def peer(axis, step):
        place = list(mine)
        place[axis] = (place[axis] + step) % dims[axis]
        return place[axis], (place[0] * across + place[1], place[2] * cores + place[3])

    loads = [pltpu.make_async_copy(tok_ref, turned, load_sems.at[0])]
    for part in range(MATRICES):
        loads.append(
            pltpu.make_async_copy(
                mixed_ref.at[:, pl.ds(part * width, width)], mixed.at[part], load_sems.at[1 + part]
            )
        )
    loads.append(
        pltpu.make_async_copy(
            w_ref.at[:, pl.ds(0, MATRICES * width)], weights, load_sems.at[1 + MATRICES]
        )
    )
    for load in loads:
        load.start()

    barrier = pltpu.get_barrier_semaphore()
    partners = 0
    for axis in range(4):
        for step in range(1, dims[axis]):
            pl.semaphore_signal(barrier, inc=1, device_id=peer(axis, step)[1], device_id_type=MESH)
            partners += 1
    pl.semaphore_wait(barrier, partners)

    flying = {}

    def launch(lane, axis, source, target):
        copies = []
        for step in range(1, dims[axis]):
            place, device = peer(axis, step)
            copies.append(
                pltpu.make_async_remote_copy(
                    src_ref=source(place),
                    dst_ref=target(step - 1),
                    send_sem=send_sems.at[lane, step - 1],
                    recv_sem=recv_sems.at[lane, step - 1],
                    device_id=device,
                    device_id_type=MESH,
                )
            )
        for copy in copies:
            copy.start()
        flying[lane] = copies

    def land(lane):
        for copy in flying.pop(lane):
            copy.wait()

    def joined(own, others):
        total = own.astype(F32)
        for other in others:
            total = total + other.astype(F32)
        return total

    def send(part, level):
        axis, axes = ORDERS[part][level], remaining(part, level)

        def source(place):
            return holders[part][level].at[
                tuple(place if item == axis else slice(None) for item in axes)
            ]

        launch(4 * part + level, axis, source, lambda slot: inboxes[part][level].at[slot])

    def join(part, level):
        land(4 * part + level)
        axis, axes = ORDERS[part][level], remaining(part, level)
        source, box = holders[part][level], inboxes[part][level]
        left = [item for item in axes if item != axis]
        count = dims[axis] - 1
        if not left:
            grad_ref[:, part * cut : (part + 1) * cut] = joined(
                source[mine[axis]], [box[slot] for slot in range(count)]
            )
            return
        spots = [()]
        for item in left[1:]:
            spots = [spot + (place,) for spot in spots for place in range(dims[item])]

        def add(k, carry):
            for spot in spots:
                there = (k,) + spot
                where = dict(zip(left, there))
                where[axis] = mine[axis]
                own = tuple(where[item] for item in axes)
                holders[part][level + 1][there] = joined(
                    source[own], [box[(slot,) + there] for slot in range(count)]
                ).astype(BF16)
            return carry

        lax.fori_loop(0, dims[left[0]], add, 0)
        send(part, level + 1)

    small_order = (3, 1, 2, 0)
    chunks = width // LANES
    span = 8 * min(2, chunks)
    rest = sums_ref.shape[0] - span

    def window(place):
        return pl.ds(pl.multiple_of(8 * window_start(place, width, deep), 8), span)

    tail_lines = pl.ds(8 * chunks, rest)

    def small_send(level):
        axis, lane = small_order[level], 4 * parts + level
        if level < 3:
            launch(lane, axis, lambda place: own_sums.at[level], lambda slot: got_sums.at[level, slot])
            return
        launch(
            lane, axis,
            lambda place: own_sums.at[3, window(place)],
            lambda slot: got_sums.at[3, slot, pl.ds(0, span)],
        )
        launch(
            lane + 1, axis,
            lambda place: own_sums.at[3, tail_lines],
            lambda slot: got_sums.at[3, slot, tail_lines],
        )

    def small_join(level):
        axis, lane = small_order[level], 4 * parts + level
        land(lane)
        slots = range(dims[axis] - 1)
        if level < 3:
            own_sums[level + 1] = joined(own_sums[level], [got_sums[level, slot] for slot in slots])
            small_send(level + 1)
            return
        land(lane + 1)
        sums_ref[0:span] = joined(
            own_sums[3, window(mine[0])], [got_sums[3, slot, 0:span] for slot in slots]
        )
        sums_ref[span:] = joined(
            own_sums[3, tail_lines], [got_sums[3, slot, tail_lines] for slot in slots]
        )

    spans = [(doc, first) for doc in range(docs) for first in range(0, padded, block)]

    def keep(step):
        doc, first = spans[step]
        return pltpu.make_async_copy(
            one_ref.at[doc, pl.ds(first, block), :], kept.at[step % 2], keep_sems.at[step % 2]
        )

    def store(step):
        doc, first = spans[step]
        count = min(block, rows - first)
        return pltpu.make_async_copy(
            stage.at[step % 2, pl.ds(0, count)],
            input_ref.at[doc, pl.ds(first, count)],
            store_sems.at[step % 2],
        )

    def input_step(step):
        doc, first = spans[step]
        if step == 0:
            loads[1 + MATRICES].wait()
            keep(0).start()
        if step + 1 < len(spans):
            keep(step + 1).start()
        keep(step).wait()
        if step >= 2:
            store(step - 2).wait()
        at = pl.ds(doc * padded + first, block)
        total = kept[step % 2]
        for part in range(MATRICES):
            total = total + dot_nt(
                mixed[part, at, :], weights[:, part * width : (part + 1) * width]
            )
        stage[step % 2, :, 0, :] = total
        store(step).start()

    loads[0].wait()
    place = lax.broadcasted_iota(jnp.int32, (8, width), 0)
    eight = jnp.where(
        place == 4, line_ref[:, :width],
        jnp.where(place == 5, line_ref[:, 2 * width :], dense_ref[...]),
    )
    for chunk in range(chunks):
        own_sums[0, 8 * chunk : 8 * chunk + 8] = eight[:, chunk * LANES : (chunk + 1) * LANES]
    ups = up_ref.shape[1] // LANES
    for chunk in range(ups):
        at = 8 * chunks + chunk
        own_sums[0, at : at + 1] = up_ref[:, chunk * LANES : (chunk + 1) * LANES]
    own_sums[0, 8 * chunks + ups :] = bins_ref[...]
    small_send(0)

    def multiply(matrix):
        loads[1 + matrix].wait()
        for part in range(matrix * parts // MATRICES, (matrix + 1) * parts // MATRICES):
            first = part * cut - matrix * width
            block_rows = dot(turned[...], mixed[matrix, :, first : first + cut])
            holders[part][0][...] = block_rows.reshape(holders[part][0].shape).astype(BF16)
            send(part, 0)

    multiply(0)
    small_join(0)
    multiply(1)
    join(0, 0)
    join(1, 0)
    multiply(2)
    small_join(1)
    join(2, 0)
    join(3, 0)
    join(0, 1)
    join(1, 1)
    join(4, 0)
    join(5, 0)
    small_join(2)
    input_step(0)
    join(2, 1)
    join(3, 1)
    join(0, 2)
    join(1, 2)
    input_step(1)
    join(4, 1)
    join(5, 1)
    join(2, 2)
    join(3, 2)
    input_step(2)
    small_join(3)
    join(4, 2)
    join(5, 2)
    input_step(3)
    for part in range(parts):
        join(part, 3)
    for step in range(max(len(spans) - 2, 0), len(spans)):
        store(step).wait()


def split_mesh(dp, fsdp):
    across = 1 << ((dp.bit_length() - 1) // 2)
    across = across if dp % across == 0 else 1
    cores = 2 if fsdp % 2 == 0 else 1
    return dp // across, across, fsdp // cores, cores


def window_start(place, width, deep):
    chunks = width // LANES
    return jnp.minimum(place * (width // deep) // LANES, max(chunks - 2, 0))


def tail(w_mixed, tok, d_mixed, d_one, sums, up_sum, line, bins, rows, dims):
    docs, padded, width = d_one.shape
    parts = len(ORDERS)
    cut = MATRICES * width // parts
    devices = dims[0] * dims[1] * dims[2] * dims[3]
    own = width // devices
    more = up_sum.shape[1] // LANES + bins.shape[0]
    small = (8 * width // LANES + more, LANES)
    lines = 8 * min(2, width // LANES) + more
    any_space = pl.BlockSpec(memory_space=pl.ANY)
    vmem = pl.BlockSpec(memory_space=pltpu.VMEM)
    scratch = []
    for part in range(parts):
        boxes = []
        for level in range(4):
            axes = remaining(part, level)
            axis = ORDERS[part][level]
            scratch.append(pltpu.VMEM(tuple(dims[item] for item in axes) + (own, cut), BF16))
            boxes.append(
                pltpu.VMEM(
                    (max(dims[axis] - 1, 1),)
                    + tuple(dims[item] for item in axes if item != axis)
                    + (own, cut),
                    BF16,
                )
            )
        scratch += boxes
    most = max(max(dims) - 1, 1)
    flat = docs * padded
    scratch += [
        pltpu.VMEM((width, flat), BF16),
        pltpu.VMEM((MATRICES, flat, width), BF16),
        pltpu.VMEM((width, MATRICES * width), BF16),
        pltpu.VMEM((2, DENSE_BLOCK, width), F32),
        pltpu.VMEM((2, DENSE_BLOCK, 1, width), F32),
        pltpu.VMEM((4,) + small, F32),
        pltpu.VMEM((4, most) + small, F32),
        pltpu.SemaphoreType.DMA((4 * parts + 5, most)),
        pltpu.SemaphoreType.DMA((4 * parts + 5, most)),
        pltpu.SemaphoreType.DMA((MATRICES + 2,)),
        pltpu.SemaphoreType.DMA((2,)),
        pltpu.SemaphoreType.DMA((2,)),
    ]
    return pl.pallas_call(
        partial(tail_kernel, dims),
        out_shape=(
            jax.ShapeDtypeStruct((own, MATRICES * width), F32),
            jax.ShapeDtypeStruct((lines, LANES), F32),
            jax.ShapeDtypeStruct((docs, rows, 1, width), F32),
        ),
        in_specs=[any_space] * 4 + [vmem] * 4,
        out_specs=(vmem, vmem, any_space),
        scratch_shapes=scratch,
        compiler_params=pltpu.CompilerParams(
            collective_id=0, has_side_effects=True, vmem_limit_bytes=VMEM_LIMIT
        ),
        name="tail",
    )(w_mixed, tok, d_mixed, d_one, sums, up_sum, line, bins)


def handed_on(rows_out, d_weights, d_qkv):
    docs, count, unused, width = rows_out.shape
    own, fold = d_weights.shape[0], (d_weights.shape[1] // width - 1) // 2
    hidden = fold * width
    pieces = 4
    edges = [count * piece // pieces for piece in range(pieces + 1)]

    def kernel(
        in_ref, w_ref, q_ref, out_ref, branch_ref, up_ref, down_ref, qkv_ref,
        held_ref, in_sems, out_sems,
    ):
        arrivals, departures = [], []
        for doc in range(docs):
            for piece in range(pieces):
                at = pl.ds(edges[piece], edges[piece + 1] - edges[piece])
                held = held_ref.at[doc, at]
                arrivals.append(
                    pltpu.make_async_copy(in_ref.at[doc, at], held, in_sems.at[doc, piece])
                )
                departures.append(
                    pltpu.make_async_copy(held, out_ref.at[doc, at], out_sems.at[doc, piece])
                )
        for copy in arrivals:
            copy.start()
        branch_ref[...] = w_ref[:, :width].astype(F32)
        up_ref[...] = w_ref[:, width : width + hidden].astype(F32)
        for arrival, departure in zip(arrivals, departures):
            arrival.wait()
            departure.start()
        for part in range(fold):
            first = width + hidden + part * width
            down_ref[part * own : (part + 1) * own, :] = w_ref[:, first : first + width].astype(F32)
        qkv_ref[...] = q_ref[...]
        for copy in departures:
            copy.wait()

    away, near = pl.BlockSpec(memory_space=pl.ANY), pl.BlockSpec(memory_space=pltpu.VMEM)
    return pl.pallas_call(
        kernel,
        out_shape=(
            jax.ShapeDtypeStruct(rows_out.shape, rows_out.dtype),
            jax.ShapeDtypeStruct((own, width), F32),
            jax.ShapeDtypeStruct((own, hidden), F32),
            jax.ShapeDtypeStruct((fold * own, width), F32),
            jax.ShapeDtypeStruct(d_qkv.shape, F32),
        ),
        in_specs=[away, near, near],
        out_specs=(away, near, near, near, near),
        scratch_shapes=[
            pltpu.VMEM(rows_out.shape, rows_out.dtype),
            pltpu.SemaphoreType.DMA((docs, pieces)),
            pltpu.SemaphoreType.DMA((docs, pieces)),
        ],
        compiler_params=pltpu.CompilerParams(vmem_limit_bytes=VMEM_LIMIT),
        name="handed_on",
    )(rows_out, d_weights, d_qkv)


def small_results(packed, width, hidden, heads, deep, own, place):
    span, more = 8 * min(2, width // LANES), hidden // LANES
    sums = jnp.transpose(packed[:span].reshape(-1, 8, LANES), (1, 0, 2)).reshape(8, -1)
    depth = place * own // (width // deep)
    first = place * own - LANES * window_start(depth, width, deep)
    sums = lax.dynamic_slice_in_dim(sums, first, own, 1)
    fold = hidden // width * own
    up_sum = packed[span : span + more].reshape(hidden)
    up_sum = lax.dynamic_slice_in_dim(up_sum, place * fold, fold, 0)
    return sums, up_sum, table_grad(packed[span + more :], heads)


def local_step(dims, lengths, pos_buckets, box_buckets, layer_input, cotangent, w_mixed, w_down, vectors, up_row, table):
    heads, width = table.shape[1], layer_input.shape[3]
    docs, rows = layer_input.shape[0], layer_input.shape[2]
    bias = bias_rows(lengths, table_entries(table), pos_buckets, box_buckets, heads)
    qkv, tok = project(layer_input, w_mixed, vectors)
    probs, attended, turned = attend(qkv, bias)
    result, d_one, left, d_upper, d_ffn, d_branch, d_attended, sums, up_sum = dense(
        layer_input, attended, cotangent, w_mixed, w_down, vectors, up_row
    )

    def flat(item):
        return item.reshape(-1, item.shape[-1])

    d_weights = weight_grads(
        turned, flat(d_branch), left, flat(d_upper), flat(d_ffn), dims[0] * dims[1] * dims[2] * dims[3]
    )
    d_mixed, bins, line = attend_back(qkv, probs, d_attended, attended, pos_buckets, box_buckets)
    return result, d_weights, (w_mixed, tok, flat(d_mixed), d_one, sums, up_sum, line, bins, rows, dims)


def body(
    layer_input, text_lengths, pos_buckets, box_buckets, w_qkv, w_out, w_up, w_down,
    norm_gains, norm_shifts, proj_biases, up_bias, rel_tables, cotangent,
):
    axes = ("dp", "fsdp")
    width, hidden = layer_input.shape[3], w_up.shape[1]
    own = norm_gains.shape[1]
    table = lax.all_gather(rel_tables, "fsdp", axis=0, tiled=True)
    heads = table.shape[1]
    small = jnp.concatenate(
        [
            jnp.concatenate([norm_gains, norm_shifts, proj_biases], axis=0).T,
            up_bias.reshape(own, hidden // width),
        ],
        axis=1,
    )
    small = jnp.pad(small, ((0, 0), (0, LANES - small.shape[1])))
    w_mixed = lax.all_gather(
        jnp.concatenate([w_qkv, w_out, w_up, small], axis=1), axes, axis=0, tiled=True
    )
    w_down = lax.all_gather(w_down, axes, axis=0, tiled=True)
    small = w_mixed[:, 4 * width + hidden :].astype(F32)
    vectors = small[:, :8].T
    up_row = small[:, 8 : 8 + hidden // width].reshape(1, hidden)
    dims = split_mesh(lax.axis_size("dp"), lax.axis_size("fsdp"))
    result, d_weights, rest = local_step(
        dims, text_lengths[:, 0], pos_buckets, box_buckets, layer_input, cotangent, w_mixed, w_down,
        vectors, up_row, table,
    )
    d_weights = lax.psum_scatter(
        d_weights.reshape(width, -1), axes, scatter_dimension=0, tiled=True
    )
    d_qkv, packed, input_grad = tail(*rest)
    input_grad, d_out, d_up, d_down, d_qkv = handed_on(input_grad, d_weights, d_qkv)
    sums, up_sum, d_table = small_results(
        packed, width, hidden, heads, dims[0], own, lax.axis_index(axes)
    )
    table_rows = rel_tables.shape[0]
    d_table = lax.dynamic_slice_in_dim(d_table, lax.axis_index("fsdp") * table_rows, table_rows, 0)
    return (
        result, jnp.transpose(input_grad, (0, 2, 1, 3)), d_qkv, d_out, d_up, d_down,
        sums[0:2], sums[2:4], sums[4:8], up_sum, d_table,
    )


def solution(mesh):
    both = ("dp", "fsdp")
    docs = P(None, both, None, None)
    return jax.shard_map(
        body,
        mesh=mesh,
        in_specs=(
            docs, P(None, both), docs, P(None, both, None, None, None),
            P(both, None), P(both, None), P(both, None), P(both, None),
            P(None, both), P(None, both), P(None, both), P(both), P("fsdp", None), docs,
        ),
        out_specs=(
            docs, docs, P(both, None), P(both, None), P(both, None), P(both, None),
            P(None, both), P(None, both), P(None, both), P(both), P("fsdp", None),
        ),
        check_vma=False,
    )
```

```python
from functools import partial

import jax
import jax.numpy as jnp
from jax import lax
from jax.experimental import pallas as pl
from jax.experimental.pallas import tpu as pltpu
from jax.sharding import PartitionSpec as P

HEAD_DIM = 64
POS_BINS = 32
BOX_BINS = 64
TEXT_SLOTS = 512
NEG_FILL = -1000000000.0
NORM_EPS = 1e-05
BLOCK = 256
DENSE_BLOCK = 384
LANES = 128
HALF = 32
SPLIT = 1
LINES = 1
SCALE = 0.125
F32 = jnp.float32
BF16 = jnp.bfloat16
VMEM_LIMIT = 58 << 20


def dot(left, right):
    return jnp.dot(left, right, preferred_element_type=F32)


def dot_nt(left, right):
    return lax.dot_general(left, right, (((1,), (1,)), ((), ())), preferred_element_type=F32)


def params(count):
    return pltpu.CompilerParams(
        dimension_semantics=("arbitrary",) * count, vmem_limit_bytes=VMEM_LIMIT
    )


def resident(shape):
    zeros = (0,) * len(shape)
    return pl.BlockSpec(shape, lambda *_: zeros, pipeline_mode=pl.Buffered(1))


def columns(shape, place):
    return pl.BlockSpec(shape, lambda *_: (0, place), pipeline_mode=pl.Buffered(1))


def live_rows(values, rows, first):
    row = first + lax.broadcasted_iota(jnp.int32, (values.shape[0], 1), 0)
    return jnp.where(row < rows, values, jnp.zeros_like(values))


def bias_kernel(rows, len_ref, tab_ref, pos_ref, box_ref, out_ref):
    heads, chunks = out_ref.shape[1], out_ref.shape[3] // LANES
    block = pl.program_id(1)
    length = len_ref[pl.program_id(0)]
    steps = jnp.minimum(BLOCK, (rows + 7) // 8 * 8 - block * BLOCK) // 8

    def fill(step, carry):
        at = pl.ds(pl.multiple_of(step * 8, 8), 8)
        for chunk in range(chunks):
            cols = slice(chunk * LANES, (chunk + 1) * LANES)
            picks = (
                box_ref[0, 0, 0, at, cols] & (BOX_BINS - 1),
                (box_ref[0, 0, 1, at, cols] & (BOX_BINS - 1)) | BOX_BINS,
                pos_ref[0, 0, at, cols] & (POS_BINS - 1),
            )
            slot = chunk * LANES + lax.broadcasted_iota(jnp.int32, (8, LANES), 1)
            valid = ((slot >= TEXT_SLOTS) & (slot < rows)) | (slot < length)
            totals = [None] * heads
            for which, pick in enumerate(picks):
                for head in range(heads):
                    line = head + (heads if which == 2 else 0)
                    entries = jnp.broadcast_to(tab_ref[line : line + 1, :], (8, LANES))
                    term = jnp.take_along_axis(entries, pick, axis=1)
                    totals[head] = term if which == 0 else totals[head] + term
            for head in range(heads):
                out_ref[0, head, at, cols] = jnp.where(valid, totals[head], NEG_FILL)
        return carry

    def blank(step, carry):
        at = pl.ds(pl.multiple_of(step * 8, 8), 8)
        for head in range(heads):
            out_ref[0, head, at, :] = jnp.zeros((8, chunks * LANES), F32)
        return carry

    lax.fori_loop(0, steps, fill, 0)
    lax.fori_loop(steps, BLOCK // 8, blank, 0)


def bias_rows(lengths, entries, pos_buckets, box_buckets, heads):
    docs, rows = pos_buckets.shape[0], pos_buckets.shape[2]
    padded = pl.cdiv(rows, BLOCK) * BLOCK
    return pl.pallas_call(
        partial(bias_kernel, rows),
        out_shape=jax.ShapeDtypeStruct((docs, heads, padded, padded), F32),
        grid=(docs, padded // BLOCK),
        in_specs=[
            pl.BlockSpec(memory_space=pltpu.SMEM),
            resident(entries.shape),
            pl.BlockSpec((1, 1, BLOCK, padded), lambda d, i: (d, 0, i, 0)),
            pl.BlockSpec((1, 1, 2, BLOCK, padded), lambda d, i: (d, 0, 0, i, 0)),
        ],
        out_specs=pl.BlockSpec((1, heads, BLOCK, padded), lambda d, i: (d, 0, i, 0)),
        compiler_params=params(2),
        cost_estimate=pl.CostEstimate(
            flops=3 * docs * heads * rows * rows,
            transcendentals=0,
            bytes_accessed=docs * padded * padded * (4 * heads + 12),
        ),
        name="bias_rows",
    )(lengths, entries, pos_buckets, box_buckets)


def project_kernel(rows, x_ref, w_ref, vec_ref, out_ref, tok_ref):
    width = x_ref.shape[3]
    block = live_rows(x_ref[0, 0], rows, pl.program_id(1) * x_ref.shape[2])
    tok_ref[...] = block.T
    queries = dot(block, w_ref[:, :width]) + vec_ref[4:5, :]
    out_ref[0, :, :width] = queries.astype(BF16) * BF16(SCALE)
    out_ref[0, :, width : 2 * width] = dot(block, w_ref[:, width : 2 * width]).astype(BF16)
    values = dot(block, w_ref[:, 2 * width :]) + vec_ref[5:6, :]
    out_ref[0, :, 2 * width :] = values.astype(BF16)


def project(layer_input, w_mixed, vectors):
    docs, unused, rows, width = layer_input.shape
    padded = pl.cdiv(rows, BLOCK) * BLOCK
    return pl.pallas_call(
        partial(project_kernel, rows),
        out_shape=(
            jax.ShapeDtypeStruct((docs, padded, 3 * width), BF16),
            jax.ShapeDtypeStruct((width, docs * padded), BF16),
        ),
        grid=(docs, padded // DENSE_BLOCK),
        in_specs=[
            pl.BlockSpec((1, 1, DENSE_BLOCK, width), lambda d, i: (d, 0, i, 0)),
            columns((width, 3 * width), 0),
            resident(vectors.shape),
        ],
        out_specs=(
            pl.BlockSpec((1, DENSE_BLOCK, 3 * width), lambda d, i: (d, i, 0)),
            pl.BlockSpec((width, DENSE_BLOCK), lambda d, i: (0, d * (padded // DENSE_BLOCK) + i)),
        ),
        compiler_params=params(2),
        name="project",
    )(layer_input, w_mixed, vectors)


def attend_kernel(q_ref, k_ref, v_ref, bias_ref, probs_ref, out_ref, turned_ref):
    lane = lax.broadcasted_iota(jnp.int32, (1, LANES), 1)
    for pair in range(q_ref.shape[2] // LANES):
        cols = slice(pair * LANES, (pair + 1) * LANES)
        queries, key_rows, values = q_ref[0, :, cols], k_ref[0, :, cols], v_ref[0, :, cols]
        total = None
        for half in range(2):
            head = 2 * pair + half
            keep = (lane < HEAD_DIM) if half == 0 else (lane >= HEAD_DIM)
            scores = dot_nt(jnp.where(keep, queries, BF16(0)), key_rows) + bias_ref[0, head]
            top = jnp.max(scores, axis=-1, keepdims=True)
            powers = jnp.exp(scores - top)
            share = 1.0 / jnp.sum(powers, axis=-1, keepdims=True)
            probs = (powers * share).astype(BF16)
            probs_ref[0, head] = probs
            part = dot(probs, jnp.where(keep, values, BF16(0)))
            total = part if half == 0 else total + part
        low = total.astype(BF16)
        out_ref[0, :, cols] = low
        turned_ref[cols, :] = low.T


def attend(qkv, bias):
    docs, padded, width = qkv.shape[0], qkv.shape[1], qkv.shape[2] // 3
    heads = bias.shape[1]
    return pl.pallas_call(
        attend_kernel,
        out_shape=(
            jax.ShapeDtypeStruct((docs, heads, padded, padded), BF16),
            jax.ShapeDtypeStruct((docs, padded, width), BF16),
            jax.ShapeDtypeStruct((width, docs * padded), BF16),
        ),
        grid=(docs, padded // BLOCK),
        in_specs=[
            pl.BlockSpec((1, BLOCK, width), lambda d, i: (d, i, 0)),
            pl.BlockSpec((1, padded, width), lambda d, i: (d, 0, 1)),
            pl.BlockSpec((1, padded, width), lambda d, i: (d, 0, 2)),
            pl.BlockSpec((1, heads, BLOCK, padded), lambda d, i: (d, 0, i, 0)),
        ],
        out_specs=(
            pl.BlockSpec((1, heads, BLOCK, padded), lambda d, i: (d, 0, i, 0)),
            pl.BlockSpec((1, BLOCK, width), lambda d, i: (d, i, 0)),
            pl.BlockSpec((width, BLOCK), lambda d, i: (0, d * (padded // BLOCK) + i)),
        ),
        compiler_params=params(2),
        name="attend",
    )(qkv, qkv, qkv, bias)


def norm(rows_in):
    centre = rows_in - jnp.mean(rows_in, axis=-1, keepdims=True)
    inv_std = lax.rsqrt(jnp.mean(centre * centre, axis=-1, keepdims=True) + NORM_EPS)
    return centre * inv_std, inv_std


def norm_back(grad_in, normed, inv_std, gain_row):
    scaled = grad_in * gain_row
    return inv_std * (
        scaled
        - jnp.mean(scaled, axis=-1, keepdims=True)
        - normed * jnp.mean(scaled * normed, axis=-1, keepdims=True)
    )


def dense_kernel(
    rows, x_ref, o_ref, cot_ref, wo_ref, wu_ref, wd_ref, vec_ref, upb_ref,
    y_ref, dr_ref, left_ref, du_ref, df_ref, db_ref, do_ref, sums_ref, upsum_ref,
    slope_ref,
):
    width, hidden = wu_ref.shape
    first = pl.program_id(1) * x_ref.shape[2]
    vec = vec_ref[...]

    @pl.when((pl.program_id(0) == 0) & (pl.program_id(1) == 0))
    def _():
        sums_ref[...] = jnp.zeros_like(sums_ref)
        upsum_ref[...] = jnp.zeros_like(upsum_ref)

    tok = live_rows(x_ref[0, 0], rows, first).astype(F32)
    normed_one, inv_one = norm(tok + dot(o_ref[0], wo_ref[...]) + vec[6:7])
    state = normed_one * vec[0:1] + vec[2:3]
    low = state.astype(BF16)
    left_ref[0:width, :] = low.T
    second = state + vec[7:8]
    for part in range(hidden // width):
        cols = slice(part * width, (part + 1) * width)
        upper = dot(low, wu_ref[:, cols]) + upb_ref[:, cols]
        cdf = 0.5 * (1.0 + lax.erf(upper * (0.5**0.5)))
        slope_ref[:, cols] = cdf + upper * (jnp.exp(-0.5 * upper * upper) * 0.3989422804014327)
        active = (upper * cdf).astype(BF16)
        left_ref[(part + 1) * width : (part + 2) * width, :] = active.T
        second = second + dot(active, wd_ref[cols, :])
    normed_two, inv_two = norm(second)
    y_ref[0, 0] = (normed_two * vec[1:2] + vec[3:4]).astype(BF16)
    grad = live_rows(cot_ref[0, 0], rows, first).astype(F32)
    sums_ref[1:2, :] += jnp.sum(grad * normed_two, axis=0, keepdims=True)
    sums_ref[3:4, :] += jnp.sum(grad, axis=0, keepdims=True)
    d_two = norm_back(grad, normed_two, inv_two, vec[1:2])
    d_ffn = d_two.astype(BF16)
    df_ref[0] = d_ffn
    sums_ref[7:8, :] += jnp.sum(d_ffn.astype(F32), axis=0, keepdims=True)
    back = d_two
    for part in range(hidden // width):
        cols = slice(part * width, (part + 1) * width)
        d_upper = (dot_nt(d_ffn, wd_ref[cols, :]) * slope_ref[:, cols]).astype(BF16)
        du_ref[0, :, cols] = d_upper
        upsum_ref[:, cols] += jnp.sum(d_upper.astype(F32), axis=0, keepdims=True)
        back = back + dot_nt(d_upper, wu_ref[:, cols])
    sums_ref[0:1, :] += jnp.sum(back * normed_one, axis=0, keepdims=True)
    sums_ref[2:3, :] += jnp.sum(back, axis=0, keepdims=True)
    d_one = norm_back(back, normed_one, inv_one, vec[0:1])
    dr_ref[0] = d_one
    d_branch = d_one.astype(BF16)
    db_ref[0] = d_branch
    sums_ref[6:7, :] += jnp.sum(d_branch.astype(F32), axis=0, keepdims=True)
    do_ref[0] = dot_nt(d_branch, wo_ref[...]).astype(BF16)


def dense(layer_input, attended, cotangent, w_mixed, w_down, vectors, up_row):
    docs, unused, rows, width = layer_input.shape
    padded, hidden = attended.shape[1], w_down.shape[0]
    ragged = pl.BlockSpec((1, 1, DENSE_BLOCK, width), lambda d, i: (d, 0, i, 0))
    narrow = pl.BlockSpec((1, DENSE_BLOCK, width), lambda d, i: (d, i, 0))
    wide = pl.BlockSpec((1, DENSE_BLOCK, hidden), lambda d, i: (d, i, 0))

    def turned(lines):
        return pl.BlockSpec(
            (lines, DENSE_BLOCK), lambda d, i: (0, d * (padded // DENSE_BLOCK) + i)
        )

    def rows_of(columns, dtype):
        return jax.ShapeDtypeStruct((docs, padded, columns), dtype)

    return pl.pallas_call(
        partial(dense_kernel, rows),
        out_shape=(
            jax.ShapeDtypeStruct(layer_input.shape, BF16),
            rows_of(width, F32),
            jax.ShapeDtypeStruct((width + hidden, docs * padded), BF16),
            rows_of(hidden, BF16),
            rows_of(width, BF16),
            rows_of(width, BF16),
            rows_of(width, BF16),
            jax.ShapeDtypeStruct((8, width), F32),
            jax.ShapeDtypeStruct((1, hidden), F32),
        ),
        grid=(docs, padded // DENSE_BLOCK),
        in_specs=[
            ragged, narrow, ragged,
            columns((width, width), 3), columns((width, hidden), 4 * width // hidden),
            resident(w_down.shape),
            resident(vectors.shape), resident(up_row.shape),
        ],
        out_specs=(
            ragged, narrow, turned(width + hidden), wide, narrow, narrow, narrow,
            pl.BlockSpec((8, width), lambda d, i: (0, 0)),
            pl.BlockSpec((1, hidden), lambda d, i: (0, 0)),
        ),
        scratch_shapes=[pltpu.VMEM((DENSE_BLOCK, hidden), F32)],
        compiler_params=params(2),
        name="dense",
    )(layer_input, attended, cotangent, w_mixed, w_mixed, w_down, vectors, up_row)


def attend_back_kernel(
    rows, q_ref, k_ref, v_ref, probs_ref, do_ref, o_ref, pos_ref, box_ref, dm_ref, bins_ref, line_ref,
    dk_ref, dv_ref, ds_ref, acc_ref, picks_ref,
):
    block, width = pl.program_id(1), q_ref.shape[2]
    padded = k_ref.shape[1]
    lane = lax.broadcasted_iota(jnp.int32, (1, LANES), 1)

    @pl.when((pl.program_id(0) == 0) & (block == 0))
    def _():
        acc_ref[...] = jnp.zeros_like(acc_ref)
        line_ref[...] = jnp.zeros_like(line_ref)
        ds_ref[...] = jnp.zeros_like(ds_ref)

    @pl.when(block == 0)
    def _():
        dk_ref[...] = jnp.zeros_like(dk_ref)
        dv_ref[...] = jnp.zeros_like(dv_ref)

    own = pl.ds(pl.multiple_of(block * BLOCK, BLOCK), BLOCK)
    for pair in range(width // LANES):
        cols = slice(pair * LANES, (pair + 1) * LANES)
        queries, key_rows, values = q_ref[0, :, cols], k_ref[0, :, cols], v_ref[0, :, cols]
        grads = do_ref[0, :, cols]
        turned_q, turned_g = queries.T, grads.T
        shared = grads.astype(F32) * o_ref[0, :, cols].astype(F32)
        total = None
        for half in range(2):
            head = 2 * pair + half
            keep = (lane < HEAD_DIM) if half == 0 else (lane >= HEAD_DIM)
            part = slice(half * HEAD_DIM, (half + 1) * HEAD_DIM)
            lines = slice(head * HEAD_DIM, (head + 1) * HEAD_DIM)
            low = probs_ref[0, head]
            probs = low.astype(F32)
            dprobs = dot_nt(jnp.where(keep, grads, BF16(0)), values)
            delta = jnp.sum(jnp.where(keep, shared, 0.0), axis=-1, keepdims=True)
            dscore = probs * (dprobs - delta)
            for chunk in range(padded // LANES):
                ds_ref[chunk, pl.ds(head, BLOCK, stride=16), :] = dscore[
                    :, chunk * LANES : (chunk + 1) * LANES
                ]
            dlow = dscore.astype(BF16)
            piece = dot(dlow, jnp.where(keep, key_rows, BF16(0)))
            total = piece if half == 0 else total + piece
            dk_ref[lines, :] += dot(turned_q[part, :], dlow)
            dv_ref[lines, :] += dot(turned_g[part, :], low)
        dm_ref[0, own, cols] = (total * SCALE).astype(BF16)

    group = 32
    low_bins = lax.broadcasted_iota(jnp.int32, (HALF, LANES), 0).astype(BF16)

    def hits(picks, bins):
        low = picks.astype(BF16)
        return jnp.concatenate(
            [
                jnp.where(low_bins[first : first + 16] == low, BF16(1), BF16(0))
                for first in range(0, bins, 16)
            ],
            axis=0,
        )

    for place, (picks, bits) in enumerate(
        (
            (box_ref[0, 0, 0], BOX_BINS),
            (box_ref[0, 0, 1], BOX_BINS),
            (pos_ref[0, 0], POS_BINS),
        )
    ):
        half = bits // 2
        for chunk in range(padded // LANES):
            part = picks[:, chunk * LANES : (chunk + 1) * LANES] & (bits - 1)
            picks_ref[2 * place, chunk] = (part & (half - 1)).astype(F32)
            picks_ref[2 * place + 1, chunk] = (part >> (half.bit_length() - 1)).astype(F32)

    def count(step, carry):
        total = None
        for line in range(0, group, LINES):
            left, right = [], []
            for own in range(LINES):
                row = step * group + line + own
                here = pl.ds(pl.multiple_of(row * 16, 16), 16)
                again = pl.ds(row, 16, stride=0)
                for chunk in range(padded // LANES):
                    base = ds_ref[chunk, here, :]
                    left.append(
                        jnp.concatenate(
                            [base.astype(BF16)]
                            + [
                                (base * picks_ref[2 * place + 1, chunk, again, :]).astype(BF16)
                                for place in range(3)
                            ],
                            axis=0,
                        )
                    )
                    right.append(
                        jnp.concatenate(
                            [
                                hits(picks_ref[2 * place, chunk, again, :], bins)
                                for place, bins in enumerate((HALF, HALF, HALF // 2))
                            ],
                            axis=0,
                        )
                    )
            part = dot_nt(jnp.concatenate(left, axis=1), jnp.concatenate(right, axis=1))
            total = part if total is None else total + part
        acc_ref[0, :, : total.shape[1]] += total
        return carry

    live = jnp.minimum(BLOCK, (rows + group - 1) // group * group - block * BLOCK)
    lax.fori_loop(0, live // group, count, 0)

    @pl.when(block == pl.num_programs(1) - 1)
    def _():
        dm_ref[0, :, width : 2 * width] = dk_ref[...].astype(BF16).T
        dm_ref[0, :, 2 * width :] = dv_ref[...].astype(BF16).T
        bins_ref[...] = jnp.sum(acc_ref[...], axis=0)
        line_ref[...] += dot(jnp.ones((16, padded), BF16), dm_ref[0])[0:8]


def attend_back(qkv, probs, d_attended, attended, pos_buckets, box_buckets):
    docs, padded, width = qkv.shape[0], qkv.shape[1], qkv.shape[2] // 3
    heads, rows = probs.shape[1], pos_buckets.shape[2]
    return pl.pallas_call(
        partial(attend_back_kernel, rows),
        out_shape=(
            jax.ShapeDtypeStruct((docs, padded, 3 * width), BF16),
            jax.ShapeDtypeStruct((64, LANES), F32),
            jax.ShapeDtypeStruct((8, 3 * width), F32),
        ),
        grid=(docs, padded // BLOCK),
        in_specs=[
            pl.BlockSpec((1, BLOCK, width), lambda d, i: (d, i, 0)),
            pl.BlockSpec((1, padded, width), lambda d, i: (d, 0, 1)),
            pl.BlockSpec((1, padded, width), lambda d, i: (d, 0, 2)),
            pl.BlockSpec((1, heads, BLOCK, padded), lambda d, i: (d, 0, i, 0)),
            pl.BlockSpec((1, BLOCK, width), lambda d, i: (d, i, 0)),
            pl.BlockSpec((1, BLOCK, width), lambda d, i: (d, i, 0)),
            pl.BlockSpec((1, 1, BLOCK, padded), lambda d, i: (d, 0, i, 0)),
            pl.BlockSpec((1, 1, 2, BLOCK, padded), lambda d, i: (d, 0, 0, i, 0)),
        ],
        out_specs=(
            pl.BlockSpec((1, padded, 3 * width), lambda d, i: (d, 0, 0)),
            pl.BlockSpec((64, LANES), lambda d, i: (0, 0)),
            pl.BlockSpec((8, 3 * width), lambda d, i: (0, 0)),
        ),
        scratch_shapes=[
            pltpu.VMEM((width, padded), F32),
            pltpu.VMEM((width, padded), F32),
            pltpu.VMEM((padded // LANES, BLOCK * 16, LANES), F32),
            pltpu.VMEM((SPLIT, 64, LANES), F32),
            pltpu.VMEM((6, padded // LANES, BLOCK, LANES), F32),
        ],
        compiler_params=params(2),
        name="attend_back",
    )(qkv, qkv, qkv, probs, d_attended, attended, pos_buckets, box_buckets)


def table_entries(table):
    heads = table.shape[1]
    lines = table.astype(F32).T * SCALE
    boxes = lines[:, POS_BINS:]
    spots = jnp.pad(lines[:, :POS_BINS], ((0, 0), (0, LANES - POS_BINS)))
    return jnp.concatenate([boxes, spots], axis=0).reshape(2 * heads, LANES)


def table_grad(bins, heads):
    base, upper = bins[:heads], (bins[16 : 16 + heads], bins[32 : 32 + heads], bins[48 : 48 + heads])
    pieces = []
    for which, (first, size) in enumerate(((0, HALF), (HALF, HALF), (2 * HALF, HALF // 2))):
        high = upper[which][:, first : first + size]
        pieces.append(jnp.concatenate([base[:, first : first + size] - high, high], axis=1))
    return jnp.concatenate([pieces[2], pieces[0], pieces[1]], axis=1).T * SCALE


def weight_grads(attended, d_branch, left, d_upper, d_ffn, devices):
    width, rows = attended.shape
    own, fold = width // devices, d_upper.shape[1] // width
    share = devices // fold
    steps = 1 + 2 * fold

    def kernel(
        l_ref, u_ref, a_ref, b_ref, f_ref, out_ref,
        attended_ref, branch_ref, ffn_ref, stage_ref, sems, load_sems,
    ):
        step = pl.program_id(0)
        slot = step % 2
        loads = [
            pltpu.make_async_copy(source, target, load_sems.at[place])
            for place, (source, target) in enumerate(
                ((f_ref, ffn_ref), (a_ref, attended_ref), (b_ref, branch_ref))
            )
        ]

        def flat_copy(part, spot):
            cols = pl.ds(pl.multiple_of(part * width, width), width)
            return pltpu.make_async_copy(
                stage_ref.at[spot], out_ref.at[:, :, cols], sems.at[spot, 0]
            )

        def fold_copy(where, spot, part):
            block = where - fold
            cols = pl.ds((1 + fold + part) * width, width)
            return pltpu.make_async_copy(
                stage_ref.at[spot].reshape(share, fold, own, width).at[:, part],
                out_ref.at[pl.ds(block * share, share), :, cols],
                sems.at[spot, part],
            )

        def wait_for(where, spot):
            @pl.when(where < fold)
            def _():
                flat_copy(where + 1, spot).wait()

            @pl.when((where >= fold) & (where < 2 * fold))
            def _():
                for part in range(fold):
                    fold_copy(where, spot, part).wait()

        @pl.when(step == 0)
        def _():
            for load in loads:
                load.start()

        @pl.when(step >= 2)
        def _():
            wait_for(step - 2, slot)

        def put(value):
            stage_ref[slot] = value.reshape(devices, own, width).astype(BF16)

        @pl.when(step < fold)
        def _():
            put(dot(l_ref[...], u_ref[...]))
            flat_copy(step + 1, slot).start()

        @pl.when(step == fold)
        def _():
            loads[0].wait()

        @pl.when((step >= fold) & (step < 2 * fold))
        def _():
            put(dot(l_ref[...], ffn_ref[...]))
            for part in range(fold):
                fold_copy(step, slot, part).start()

        @pl.when(step == 2 * fold)
        def _():
            loads[1].wait()
            loads[2].wait()
            put(dot(attended_ref[...], branch_ref[...]))
            flat_copy(0, slot).start()
            wait_for(step - 1, 1 - slot)
            flat_copy(0, slot).wait()

    away = pl.BlockSpec(memory_space=pl.ANY)
    return pl.pallas_call(
        kernel,
        out_shape=jax.ShapeDtypeStruct((devices, own, (1 + 2 * fold) * width), BF16),
        grid=(steps,),
        in_specs=[
            pl.BlockSpec((width, rows), lambda p: (jnp.clip(p - fold + 1, 0, fold), 0)),
            pl.BlockSpec((rows, width), lambda p: (0, jnp.minimum(p, fold - 1))),
            away,
            away,
            away,
        ],
        out_specs=away,
        scratch_shapes=[
            pltpu.VMEM((width, rows), BF16),
            pltpu.VMEM((rows, width), BF16),
            pltpu.VMEM((rows, width), BF16),
            pltpu.VMEM((2, devices, own, width), BF16),
            pltpu.SemaphoreType.DMA((2, fold)),
            pltpu.SemaphoreType.DMA((3,)),
        ],
        compiler_params=params(1),
        cost_estimate=pl.CostEstimate(
            flops=2 * rows * width * width * steps, transcendentals=0,
            bytes_accessed=2 * rows * width * (steps + 3),
        ),
        name="weight_grads",
    )(left, d_upper, attended, d_branch, d_ffn)


ORDERS = ((3, 1, 2, 0), (3, 2, 1, 0)) * 3
MATRICES = 3
MESH = pl.DeviceIdType.MESH


def remaining(part, level):
    return [axis for axis in range(4) if axis not in ORDERS[part][:level]]


def tail_kernel(
    dims, w_ref, tok_ref, mixed_ref, one_ref, dense_ref, up_ref, line_ref, bins_ref,
    grad_ref, sums_ref, ups_ref, table_ref, input_ref, *scratch
):
    parts, width = len(ORDERS), tok_ref.shape[0]
    cut = MATRICES * width // parts
    holders = [scratch[8 * part : 8 * part + 4] for part in range(parts)]
    inboxes = [scratch[8 * part + 4 : 8 * part + 8] for part in range(parts)]
    (
        turned, mixed, weights, kept, stage, own_sums, got_sums,
        send_sems, recv_sems, load_sems, keep_sems, store_sems,
    ) = scratch[8 * parts :]
    deep, across, along, cores = dims
    dp, fsdp = lax.axis_index("dp"), lax.axis_index("fsdp")
    mine = (dp // across, dp % across, fsdp // cores, fsdp % cores)
    docs, padded = one_ref.shape[0], one_ref.shape[1]
    rows, block = input_ref.shape[1], kept.shape[1]

    def peer(axis, step):
        place = list(mine)
        place[axis] = (place[axis] + step) % dims[axis]
        return place[axis], (place[0] * across + place[1], place[2] * cores + place[3])

    loads = [pltpu.make_async_copy(tok_ref, turned, load_sems.at[0])]
    for part in range(MATRICES):
        loads.append(
            pltpu.make_async_copy(
                mixed_ref.at[:, pl.ds(part * width, width)], mixed.at[part], load_sems.at[1 + part]
            )
        )
    loads.append(
        pltpu.make_async_copy(
            w_ref.at[:, pl.ds(0, MATRICES * width)], weights, load_sems.at[1 + MATRICES]
        )
    )
    for load in loads:
        load.start()

    barrier = pltpu.get_barrier_semaphore()
    partners = 0
    for axis in range(4):
        for step in range(1, dims[axis]):
            pl.semaphore_signal(barrier, inc=1, device_id=peer(axis, step)[1], device_id_type=MESH)
            partners += 1
    pl.semaphore_wait(barrier, partners)

    flying = {}

    def launch(lane, axis, source, target):
        copies = []
        for step in range(1, dims[axis]):
            place, device = peer(axis, step)
            copies.append(
                pltpu.make_async_remote_copy(
                    src_ref=source(place),
                    dst_ref=target(step - 1),
                    send_sem=send_sems.at[lane, step - 1],
                    recv_sem=recv_sems.at[lane, step - 1],
                    device_id=device,
                    device_id_type=MESH,
                )
            )
        for copy in copies:
            copy.start()
        flying[lane] = copies

    def land(lane):
        for copy in flying.pop(lane):
            copy.wait()

    def joined(own, others):
        total = own.astype(F32)
        for other in others:
            total = total + other.astype(F32)
        return total

    def send(part, level):
        axis, axes = ORDERS[part][level], remaining(part, level)

        def source(place):
            return holders[part][level].at[
                tuple(place if item == axis else slice(None) for item in axes)
            ]

        launch(4 * part + level, axis, source, lambda slot: inboxes[part][level].at[slot])

    def join(part, level):
        land(4 * part + level)
        axis, axes = ORDERS[part][level], remaining(part, level)
        source, box = holders[part][level], inboxes[part][level]
        left = [item for item in axes if item != axis]
        count = dims[axis] - 1
        if not left:
            grad_ref[:, part * cut : (part + 1) * cut] = joined(
                source[mine[axis]], [box[slot] for slot in range(count)]
            )
            return
        spots = [()]
        for item in left[1:]:
            spots = [spot + (place,) for spot in spots for place in range(dims[item])]

        def add(k, carry):
            for spot in spots:
                there = (k,) + spot
                where = dict(zip(left, there))
                where[axis] = mine[axis]
                own = tuple(where[item] for item in axes)
                holders[part][level + 1][there] = joined(
                    source[own], [box[(slot,) + there] for slot in range(count)]
                ).astype(BF16)
            return carry

        lax.fori_loop(0, dims[left[0]], add, 0)
        send(part, level + 1)

    small_order = (3, 1, 2, 0)
    chunks = width // LANES
    span = sums_ref.shape[0]
    ups = ups_ref.shape[0]
    rest = ups + table_ref.shape[0]

    def window(place):
        return pl.ds(pl.multiple_of(8 * window_start(place, width, deep), 8), span)

    tail_lines = pl.ds(8 * chunks, rest)

    def small_send(level):
        axis, lane = small_order[level], 4 * parts + level
        if level < 3:
            launch(lane, axis, lambda place: own_sums.at[level], lambda slot: got_sums.at[level, slot])
            return
        launch(
            lane, axis,
            lambda place: own_sums.at[3, window(place)],
            lambda slot: got_sums.at[3, slot, pl.ds(0, span)],
        )
        launch(
            lane + 1, axis,
            lambda place: own_sums.at[3, tail_lines],
            lambda slot: got_sums.at[3, slot, tail_lines],
        )

    def small_join(level):
        axis, lane = small_order[level], 4 * parts + level
        land(lane)
        slots = range(dims[axis] - 1)
        if level < 3:
            own_sums[level + 1] = joined(own_sums[level], [got_sums[level, slot] for slot in slots])
            small_send(level + 1)
            return
        land(lane + 1)
        sums_ref[...] = joined(
            own_sums[3, window(mine[0])], [got_sums[3, slot, 0:span] for slot in slots]
        )
        others = joined(own_sums[3, tail_lines], [got_sums[3, slot, tail_lines] for slot in slots])
        ups_ref[...] = others[:ups]
        table_ref[...] = others[ups:]

    spans = [(doc, first) for doc in range(docs) for first in range(0, padded, block)]

    def keep(step):
        doc, first = spans[step]
        return pltpu.make_async_copy(
            one_ref.at[doc, pl.ds(first, block), :], kept.at[step % 2], keep_sems.at[step % 2]
        )

    def store(step):
        doc, first = spans[step]
        count = min(block, rows - first)
        return pltpu.make_async_copy(
            stage.at[step % 2, pl.ds(0, count)],
            input_ref.at[doc, pl.ds(first, count)],
            store_sems.at[step % 2],
        )

    def input_step(step):
        doc, first = spans[step]
        if step == 0:
            loads[1 + MATRICES].wait()
            keep(0).start()
        if step + 1 < len(spans):
            keep(step + 1).start()
        keep(step).wait()
        if step >= 2:
            store(step - 2).wait()
        at = pl.ds(doc * padded + first, block)
        total = kept[step % 2]
        for part in range(MATRICES):
            total = total + dot_nt(
                mixed[part, at, :], weights[:, part * width : (part + 1) * width]
            )
        stage[step % 2, :, 0, :] = total
        store(step).start()

    loads[0].wait()
    place = lax.broadcasted_iota(jnp.int32, (8, width), 0)
    eight = jnp.where(
        place == 4, line_ref[:, :width],
        jnp.where(place == 5, line_ref[:, 2 * width :], dense_ref[...]),
    )
    for chunk in range(chunks):
        own_sums[0, 8 * chunk : 8 * chunk + 8] = eight[:, chunk * LANES : (chunk + 1) * LANES]
    for chunk in range(ups):
        at = 8 * chunks + chunk
        own_sums[0, at : at + 1] = up_ref[:, chunk * LANES : (chunk + 1) * LANES]
    own_sums[0, 8 * chunks + ups :] = bins_ref[...]
    small_send(0)

    def multiply(matrix):
        loads[1 + matrix].wait()
        for part in range(matrix * parts // MATRICES, (matrix + 1) * parts // MATRICES):
            first = part * cut - matrix * width
            block_rows = dot(turned[...], mixed[matrix, :, first : first + cut])
            holders[part][0][...] = block_rows.reshape(holders[part][0].shape).astype(BF16)
            send(part, 0)

    multiply(0)
    small_join(0)
    multiply(1)
    join(0, 0)
    join(1, 0)
    multiply(2)
    small_join(1)
    join(2, 0)
    join(3, 0)
    join(0, 1)
    join(1, 1)
    join(4, 0)
    join(5, 0)
    small_join(2)
    input_step(0)
    join(2, 1)
    join(3, 1)
    join(0, 2)
    join(1, 2)
    input_step(1)
    join(4, 1)
    join(5, 1)
    join(2, 2)
    join(3, 2)
    input_step(2)
    small_join(3)
    join(4, 2)
    join(5, 2)
    input_step(3)
    for part in range(parts):
        join(part, 3)
    for step in range(max(len(spans) - 2, 0), len(spans)):
        store(step).wait()


def split_mesh(dp, fsdp):
    across = 1 << ((dp.bit_length() - 1) // 2)
    across = across if dp % across == 0 else 1
    cores = 2 if fsdp % 2 == 0 else 1
    return dp // across, across, fsdp // cores, cores


def window_start(place, width, deep):
    chunks = width // LANES
    return jnp.minimum(place * (width // deep) // LANES, max(chunks - 2, 0))


def tail(w_mixed, tok, d_mixed, d_one, sums, up_sum, line, bins, rows, dims):
    docs, padded, width = d_one.shape
    parts = len(ORDERS)
    cut = MATRICES * width // parts
    devices = dims[0] * dims[1] * dims[2] * dims[3]
    own = width // devices
    more = up_sum.shape[1] // LANES + bins.shape[0]
    small = (8 * width // LANES + more, LANES)
    lines = 8 * min(2, width // LANES) + more
    any_space = pl.BlockSpec(memory_space=pl.ANY)
    vmem = pl.BlockSpec(memory_space=pltpu.VMEM)
    scratch = []
    for part in range(parts):
        boxes = []
        for level in range(4):
            axes = remaining(part, level)
            axis = ORDERS[part][level]
            scratch.append(pltpu.VMEM(tuple(dims[item] for item in axes) + (own, cut), BF16))
            boxes.append(
                pltpu.VMEM(
                    (max(dims[axis] - 1, 1),)
                    + tuple(dims[item] for item in axes if item != axis)
                    + (own, cut),
                    BF16,
                )
            )
        scratch += boxes
    most = max(max(dims) - 1, 1)
    flat = docs * padded
    scratch += [
        pltpu.VMEM((width, flat), BF16),
        pltpu.VMEM((MATRICES, flat, width), BF16),
        pltpu.VMEM((width, MATRICES * width), BF16),
        pltpu.VMEM((2, DENSE_BLOCK, width), F32),
        pltpu.VMEM((2, DENSE_BLOCK, 1, width), F32),
        pltpu.VMEM((4,) + small, F32),
        pltpu.VMEM((4, most) + small, F32),
        pltpu.SemaphoreType.DMA((4 * parts + 5, most)),
        pltpu.SemaphoreType.DMA((4 * parts + 5, most)),
        pltpu.SemaphoreType.DMA((MATRICES + 2,)),
        pltpu.SemaphoreType.DMA((2,)),
        pltpu.SemaphoreType.DMA((2,)),
    ]
    return pl.pallas_call(
        partial(tail_kernel, dims),
        out_shape=(
            jax.ShapeDtypeStruct((own, MATRICES * width), F32),
            jax.ShapeDtypeStruct((lines - more, LANES), F32),
            jax.ShapeDtypeStruct((more - bins.shape[0], LANES), F32),
            jax.ShapeDtypeStruct(bins.shape, F32),
            jax.ShapeDtypeStruct((docs, rows, 1, width), F32),
        ),
        in_specs=[any_space] * 4 + [vmem] * 4,
        out_specs=(vmem, vmem, vmem, vmem, any_space),
        scratch_shapes=scratch,
        compiler_params=pltpu.CompilerParams(
            collective_id=0, has_side_effects=True, vmem_limit_bytes=VMEM_LIMIT
        ),
        name="tail",
    )(w_mixed, tok, d_mixed, d_one, sums, up_sum, line, bins)


def handed_on(rows_out, d_weights, d_qkv):
    docs, count, unused, width = rows_out.shape
    own, fold = d_weights.shape[0], (d_weights.shape[1] // width - 1) // 2
    hidden = fold * width
    pieces = 4
    edges = [count * piece // pieces for piece in range(pieces + 1)]

    def kernel(
        in_ref, w_ref, q_ref, out_ref, branch_ref, up_ref, down_ref, qkv_ref,
        held_ref, in_sems, out_sems,
    ):
        arrivals, departures = [], []
        for doc in range(docs):
            for piece in range(pieces):
                at = pl.ds(edges[piece], edges[piece + 1] - edges[piece])
                held = held_ref.at[doc, at]
                arrivals.append(
                    pltpu.make_async_copy(in_ref.at[doc, at], held, in_sems.at[doc, piece])
                )
                departures.append(
                    pltpu.make_async_copy(held, out_ref.at[doc, at], out_sems.at[doc, piece])
                )
        for copy in arrivals:
            copy.start()
        branch_ref[...] = w_ref[:, :width].astype(F32)
        up_ref[...] = w_ref[:, width : width + hidden].astype(F32)
        for arrival, departure in zip(arrivals, departures):
            arrival.wait()
            departure.start()
        for part in range(fold):
            first = width + hidden + part * width
            down_ref[part * own : (part + 1) * own, :] = w_ref[:, first : first + width].astype(F32)
        qkv_ref[...] = q_ref[...]
        for copy in departures:
            copy.wait()

    away, near = pl.BlockSpec(memory_space=pl.ANY), pl.BlockSpec(memory_space=pltpu.VMEM)
    return pl.pallas_call(
        kernel,
        out_shape=(
            jax.ShapeDtypeStruct(rows_out.shape, rows_out.dtype),
            jax.ShapeDtypeStruct((own, width), F32),
            jax.ShapeDtypeStruct((own, hidden), F32),
            jax.ShapeDtypeStruct((fold * own, width), F32),
            jax.ShapeDtypeStruct(d_qkv.shape, F32),
        ),
        in_specs=[away, near, near],
        out_specs=(away, near, near, near, near),
        scratch_shapes=[
            pltpu.VMEM(rows_out.shape, rows_out.dtype),
            pltpu.SemaphoreType.DMA((docs, pieces)),
            pltpu.SemaphoreType.DMA((docs, pieces)),
        ],
        compiler_params=pltpu.CompilerParams(vmem_limit_bytes=VMEM_LIMIT),
        name="handed_on",
    )(rows_out, d_weights, d_qkv)


def small_results(packed, width, hidden, heads, deep, own, place):
    sums = jnp.transpose(packed[0].reshape(-1, 8, LANES), (1, 0, 2)).reshape(8, -1)
    depth = place * own // (width // deep)
    first = place * own - LANES * window_start(depth, width, deep)
    sums = lax.dynamic_slice_in_dim(sums, first, own, 1)
    fold = hidden // width * own
    up_sum = packed[1].reshape(hidden)
    up_sum = lax.dynamic_slice_in_dim(up_sum, place * fold, fold, 0)
    return sums, up_sum, table_grad(packed[2], heads)


def local_step(dims, lengths, pos_buckets, box_buckets, layer_input, cotangent, w_mixed, w_down, vectors, up_row, table):
    heads, width = table.shape[1], layer_input.shape[3]
    docs, rows = layer_input.shape[0], layer_input.shape[2]
    bias = bias_rows(lengths, table_entries(table), pos_buckets, box_buckets, heads)
    qkv, tok = project(layer_input, w_mixed, vectors)
    probs, attended, turned = attend(qkv, bias)
    result, d_one, left, d_upper, d_ffn, d_branch, d_attended, sums, up_sum = dense(
        layer_input, attended, cotangent, w_mixed, w_down, vectors, up_row
    )

    def flat(item):
        return item.reshape(-1, item.shape[-1])

    d_weights = weight_grads(
        turned, flat(d_branch), left, flat(d_upper), flat(d_ffn), dims[0] * dims[1] * dims[2] * dims[3]
    )
    d_mixed, bins, line = attend_back(qkv, probs, d_attended, attended, pos_buckets, box_buckets)
    return result, d_weights, (w_mixed, tok, flat(d_mixed), d_one, sums, up_sum, line, bins, rows, dims)


def body(
    layer_input, text_lengths, pos_buckets, box_buckets, w_qkv, w_out, w_up, w_down,
    norm_gains, norm_shifts, proj_biases, up_bias, rel_tables, cotangent,
):
    axes = ("dp", "fsdp")
    width, hidden = layer_input.shape[3], w_up.shape[1]
    own = norm_gains.shape[1]
    table = lax.all_gather(rel_tables, "fsdp", axis=0, tiled=True)
    heads = table.shape[1]
    small = jnp.concatenate(
        [
            jnp.concatenate([norm_gains, norm_shifts, proj_biases], axis=0).T,
            up_bias.reshape(own, hidden // width),
        ],
        axis=1,
    )
    small = jnp.pad(small, ((0, 0), (0, LANES - small.shape[1])))
    w_mixed = lax.all_gather(
        jnp.concatenate([w_qkv, w_out, w_up, small], axis=1), axes, axis=0, tiled=True
    )
    w_down = lax.all_gather(w_down, axes, axis=0, tiled=True)
    small = w_mixed[:, 4 * width + hidden :].astype(F32)
    vectors = small[:, :8].T
    up_row = small[:, 8 : 8 + hidden // width].reshape(1, hidden)
    dims = split_mesh(lax.axis_size("dp"), lax.axis_size("fsdp"))
    result, d_weights, rest = local_step(
        dims, text_lengths[:, 0], pos_buckets, box_buckets, layer_input, cotangent, w_mixed, w_down,
        vectors, up_row, table,
    )
    d_weights = lax.psum_scatter(
        d_weights.reshape(width, -1), axes, scatter_dimension=0, tiled=True
    )
    d_qkv, *packed, input_grad = tail(*rest)
    input_grad, d_out, d_up, d_down, d_qkv = handed_on(input_grad, d_weights, d_qkv)
    sums, up_sum, d_table = small_results(
        packed, width, hidden, heads, dims[0], own, lax.axis_index(axes)
    )
    table_rows = rel_tables.shape[0]
    d_table = lax.dynamic_slice_in_dim(d_table, lax.axis_index("fsdp") * table_rows, table_rows, 0)
    return (
        result, jnp.transpose(input_grad, (0, 2, 1, 3)), d_qkv, d_out, d_up, d_down,
        sums[0:2], sums[2:4], sums[4:8], up_sum, d_table,
    )


def solution(mesh):
    both = ("dp", "fsdp")
    docs = P(None, both, None, None)
    return jax.shard_map(
        body,
        mesh=mesh,
        in_specs=(
            docs, P(None, both), docs, P(None, both, None, None, None),
            P(both, None), P(both, None), P(both, None), P(both, None),
            P(None, both), P(None, both), P(None, both), P(both), P("fsdp", None), docs,
        ),
        out_specs=(
            docs, docs, P(both, None), P(both, None), P(both, None), P(both, None),
            P(None, both), P(None, both), P(None, both), P(both), P("fsdp", None),
        ),
        check_vma=False,
    )
```
